32 devices in a mesh: seq: 4 (over x, core), batch: 8 (over z, y).
Axes of the slice: x: 2, y: 2, z: 4, core: 2. Of those that a mesh axis runs over, the one named last changes fastest.
Arguments:
- patches: bfloat16 [8, 1024, 768], P('batch', 'seq'), may hold values from -6 to 6
- specials: bfloat16 [8, 16, 768], P('batch', 'seq'), may hold values from -6 to 6
- segment_ids: int32 [8, 1024], P('batch', 'seq'), may hold values from 0 to 7, never falling along the last dimension, each value on 1 to 576 neighbouring positions
- special_order: int32 [8, 16], P('batch', 'seq'), may hold values from 0 to 15, each once within a row
- keep_mask: int32 [8, 16], P('batch'), may hold values 0 or 1
- norm_gains: float32 [2, 768], replicated, may hold values from 0.5 to 1.5
- norm_shifts: float32 [2, 768], replicated, may hold values from -3 to 3
- w_qkv: bfloat16 [768, 2304], replicated, may hold values from -0.21875 to 0.21875
- biases: float32 [4, 768], replicated, may hold values from -3 to 3
- w_out: bfloat16 [768, 768], replicated, may hold values from -0.875 to 0.875
- w_fc1: bfloat16 [768, 3072], replicated, may hold values from -0.21875 to 0.21875
- fc1_bias: float32 [3072], replicated, may hold values from -3 to 3
- w_fc2: bfloat16 [3072, 768], replicated, may hold values from -0.109375 to 0.109375
- cot_patches: bfloat16 [8, 1024, 768], P('batch', 'seq'), may hold values from -6 to 6
- cot_specials: bfloat16 [8, 16, 768], P('batch', 'seq'), may hold values from -6 to 6
Outputs:
- out_patches: bfloat16 [8, 1024, 768], P('batch', 'seq')
- out_specials: bfloat16 [8, 16, 768], P('batch', 'seq')
- grad_patches: float32 [8, 1024, 768], P('batch', 'seq')
- grad_specials: float32 [8, 16, 768], P('batch', 'seq')
- grad_gains: float32 [2, 768], P(None, ('seq', 'batch'))
- grad_shifts: float32 [2, 768], P(None, ('seq', 'batch'))
- grad_w_qkv: float32 [768, 2304], P(('seq', 'batch'))
- grad_biases: float32 [4, 768], P(None, ('seq', 'batch'))
- grad_w_out: float32 [768, 768], P(('seq', 'batch'))
- grad_w_fc1: float32 [768, 3072], P(('seq', 'batch'))
- grad_fc1_bias: float32 [3072], P(('seq', 'batch'))
- grad_w_fc2: float32 [3072, 768], P(('seq', 'batch'))
The draws below stay inside these ranges and needn't reach their ends.
Inputs may be any that keep to these rules, and one draw needn't show every extreme that they name: `segment_ids`: within a row image ids never fall; every image of a row has 1 to 576 patches. `special_order`: each row holds every number once.
All inputs are finite; a program needn't handle non-finite values. No bound on the sum of `keep_mask` on one device may be relied on, other than what follows from the above.
Results may differ from the reference program's by a relative error of at most 0.011.
Values may be sent and summed in bfloat16 or wider, within the bound.
No kernel may reach another device: no remote copies, remote signals or barrier semaphores. Data moves between devices by JAX's collectives and lax.ppermute only.
A program may use at most 192 MiB of HBM per device.

```python
import math
import jax
import jax.numpy as jnp
import numpy as np
from jax import lax

D = 768
HEADS = 12
HEAD = 64
FF = 3072
L = 1024
IMG = 8
MOST = 576
ROWS = 8
SPC = 16


def with_ends(values, stream_key, least, high):
    shape = values.shape
    spot = [jax.random.randint(jax.random.fold_in(stream_key, axis), (), 0, shape[axis]) for axis in range(len(shape))]
    values = values.at[tuple(spot)].set(least)
    longest = shape.index(max(shape))
    spot[longest] = (spot[longest] + 1) % shape[longest]
    return values.at[tuple(spot)].set(high)


def spiked(entries, own_key, source, target, blocks, factor):
    def block_of(position):
        return (jnp.arange(entries.shape[position]) // (entries.shape[position] // blocks)).reshape((-1,) + (1,) * (entries.ndim - 1 - position))

    first = jax.random.permutation(own_key, blocks)[block_of(target)]
    other_side = (block_of(target) + blocks // 2) % blocks
    return jnp.where((block_of(source) == first) | (block_of(source) == other_side), factor * entries, entries)


def shard_levels(rng, shape, pieces, low, largest):
    gain, own = 1.0, jax.random.fold_in(rng, 6)
    for dim, shards_of in pieces:
        heights = jnp.exp(jax.random.uniform(jax.random.fold_in(own, dim), (shards_of,), jnp.float32, low / len(pieces), largest / len(pieces)))
        gain = gain * jnp.repeat(heights, shape[dim] // shards_of).reshape([-1 if axis == dim else 1 for axis in range(len(shape))])
    return gain


def length_profile(number_of, total, most, skew):
    loads = [(1 << 20) // math.isqrt(grade ** skew) + 1 for grade in range(2, number_of + 1)]
    rest, given = total - most - (number_of - 1), [1] * (number_of - 1)
    while rest > 0:
        free = [i for i in range(number_of - 1) if given[i] < most]
        mass, remaining = sum([loads[i] for i in free]), rest
        for i in free:
            extra = min(most - given[i], max(1, remaining * loads[i] // mass), rest)
            given[i] = given[i] + extra
            rest = rest - extra
    return np.array([most] + given)


def ragged(own_key, amount, total, bound, lean):
    if amount == 2:
        one = jax.random.randint(own_key, (), max(1, total - bound), min(bound, total - 1) + 1)
        return jnp.stack([one, total - one])
    lengths = jnp.asarray(length_profile(amount, total, bound, lean), jnp.int32)
    pairs = (amount - 1) // 2
    source_of, receiver = lengths[1:1 + 2 * pairs:2], lengths[2:2 + 2 * pairs:2]
    room = jnp.minimum(source_of - 1, bound - receiver)
    moved = jax.random.randint(jax.random.fold_in(own_key, 1), (pairs,), 0, 1 << 20) % (room + 1)
    lengths = lengths.at[1:1 + 2 * pairs:2].set(source_of - moved).at[2:2 + 2 * pairs:2].set(receiver + moved)
    return lengths[jax.random.permutation(jax.random.fold_in(own_key, 2), amount)]


def gaussian(key, shape, scale, limit, pieces=(), held_as=jnp.bfloat16):
    gain = shard_levels(key, shape, pieces, -0.22, 0.18) if pieces else 1.0
    result = jax.random.normal(key, shape, jnp.float32) * scale * gain
    return jnp.minimum(jnp.maximum(result, -limit), limit).astype(held_as)


def heavy_noise(key, extent, scale, most, pieces, heavy, kind=jnp.bfloat16):
    values = scale * jax.random.normal(key, extent, jnp.float32)
    if pieces:
        values = values * shard_levels(key, extent, pieces, -0.22, 0.18)
    return jnp.clip(spiked(values, jax.random.fold_in(key, 3), *heavy), -most, most).astype(kind)


def setup_inputs(seed: int = 0) -> dict:
    streams_of = jax.random.split(jax.random.key(seed), 16)
    return {
        "patches": gaussian(streams_of[0], (ROWS, L, D), 1.0, 6.0, ((0, 8), (1, 4))),
        "specials": gaussian(streams_of[1], (ROWS, SPC, D), 1.0, 6.0, ((0, 8), (1, 4))),
        "segment_ids": jax.vmap(lambda own: jnp.searchsorted(jnp.cumsum(ragged(own, IMG, L, MOST, 2)), jnp.arange(L), side="right"))(jax.random.split(streams_of[2], ROWS)).reshape((ROWS, L)).astype(jnp.int32),
        "special_order": jax.vmap(lambda own: jax.random.permutation(own, SPC))(jax.random.split(streams_of[3], ROWS)).reshape((ROWS, SPC)).astype(jnp.int32),
        "keep_mask": with_ends((jax.random.randint(streams_of[4], (ROWS, 2 * IMG), 0, 4) < 3).astype(jnp.int32), jax.random.fold_in(streams_of[4], 1), 0, 1),
        "norm_gains": jnp.clip(1.0 + 0.1 * jax.random.normal(streams_of[5], (2, D), jnp.float32), 0.5, 1.5),
        "norm_shifts": gaussian(streams_of[6], (2, D), 0.5, 3.0, (), jnp.float32),
        "w_qkv": gaussian(streams_of[7], (D, 3 * D), D ** -0.5, 0.21875),
        "biases": gaussian(streams_of[8], (4, D), 0.5, 3.0, (), jnp.float32),
        "w_out": gaussian(streams_of[9], (D, D), (D // 16) ** -0.5, 0.875),
        "w_fc1": gaussian(streams_of[10], (D, FF), D ** -0.5, 0.21875),
        "fc1_bias": gaussian(streams_of[11], (FF,), 0.5, 3.0, (), jnp.float32),
        "w_fc2": gaussian(streams_of[12], (FF, D), FF ** -0.5, 0.109375),
        "cot_patches": heavy_noise(streams_of[13], (ROWS, L, D), 1.0, 6.0, ((0, 8), (1, 4)), (0, 2, 8, 2.0)),
        "cot_specials": gaussian(streams_of[14], (ROWS, SPC, D), 1.0, 6.0, ((0, 8), (1, 4))),
    }


PRECISE = lax.Precision.HIGHEST

@jax.custom_vjp
def low(v):
    return lax.optimization_barrier(v.astype(jnp.bfloat16)).astype(jnp.float32)

@jax.custom_vjp
def low_back(v):
    return v

def low_keep(v):
    return (low(v), None)

def low_pass(kept, grad):
    return (grad,)

def back_keep(v):
    return (v, None)

def back_low(kept, grad):
    return (low(grad),)
low.defvjp(low_keep, low_pass)
low_back.defvjp(back_keep, back_low)

def both_ways(inputs):
    return low(low_back(inputs))

def layer_norm(inputs, norm_gain, norm_shift):
    center = inputs - lax.optimization_barrier(jnp.mean(inputs, axis=-1, keepdims=True))
    spread = lax.optimization_barrier(jnp.mean(center * center, axis=-1, keepdims=True))
    return center * lax.rsqrt(spread + 1e-06) * norm_gain + norm_shift

def row_layer(params, tokens, row_segs, keep_first, keep_second):
    norm_gains, norm_shifts, w_qkv, biases, w_out, w_fc1, fc1_bias, w_fc2 = params
    token_count = tokens.shape[0]
    model_width = tokens.shape[1]
    normed = low(layer_norm(tokens, norm_gains[0], norm_shifts[0]))
    qkv_proj = jnp.dot(normed, w_qkv, precision=PRECISE)
    query_proj = both_ways(qkv_proj[:, :model_width] + biases[0])
    key_proj = both_ways(qkv_proj[:, model_width:2 * model_width])
    value_proj = both_ways(qkv_proj[:, 2 * model_width:] + biases[1])
    query_heads = query_proj.reshape(token_count, HEADS, HEAD)
    key_heads = key_proj.reshape(token_count, HEADS, HEAD)
    value_heads = value_proj.reshape(token_count, HEADS, HEAD)
    scores = jnp.einsum('qhd,khd->hqk', query_heads, key_heads, precision=PRECISE) * HEAD ** (-0.5)
    scores = low_back(scores)
    same_image = row_segs[:, None] == row_segs[None, :]
    scores = jnp.where(same_image[None], scores, -1e+30)
    row_top = lax.optimization_barrier(jnp.max(scores, axis=-1, keepdims=True))
    exponent = jnp.exp(scores - row_top)
    attn_probs = low(exponent / lax.optimization_barrier(jnp.sum(exponent, axis=-1, keepdims=True)))
    attended = jnp.einsum('hqk,khd->qhd', attn_probs, value_heads, precision=PRECISE)
    attended = both_ways(attended.reshape(token_count, model_width))
    branch = low_back(jnp.dot(attended, w_out, precision=PRECISE) + biases[2])
    middle = tokens + (keep_first / 0.75)[:, None] * branch
    normed2 = low(layer_norm(middle, norm_gains[1], norm_shifts[1]))
    hidden_pre = low_back(jnp.dot(normed2, w_fc1, precision=PRECISE) + fc1_bias)
    active = low(jax.nn.gelu(hidden_pre, approximate=False))
    branch2 = low_back(jnp.dot(active, w_fc2, precision=PRECISE) + biases[3])
    return middle + (keep_second / 0.75)[:, None] * branch2

def reference(patches, specials, segment_ids, special_order, keep_mask, norm_gains, norm_shifts, w_qkv, biases, w_out, w_fc1, fc1_bias, w_fc2, cot_patches, cot_specials):
    params = (norm_gains.astype(jnp.float32), norm_shifts.astype(jnp.float32), w_qkv.astype(jnp.float32), biases.astype(jnp.float32), w_out.astype(jnp.float32), w_fc1.astype(jnp.float32), fc1_bias.astype(jnp.float32), w_fc2.astype(jnp.float32))
    tokens = jnp.concatenate([patches, specials], axis=1).astype(jnp.float32)
    seg_all = jnp.concatenate([segment_ids, special_order // 2], axis=1).astype(jnp.int32)
    onehot = (seg_all[..., None] == jnp.arange(IMG, dtype=jnp.int32)).astype(jnp.float32)
    keep_float = keep_mask.astype(jnp.float32)
    keep_first = lax.optimization_barrier(jnp.sum(onehot * keep_float[:, None, :IMG], axis=-1))
    keep_second = lax.optimization_barrier(jnp.sum(onehot * keep_float[:, None, IMG:], axis=-1))
    cotangent = jnp.concatenate([cot_patches, cot_specials], axis=1).astype(jnp.float32)
    zero_grads = jax.tree.map(jnp.zeros_like, params)

    def row_step(running, row_data):
        row_tokens, row_segs, row_first, row_second, row_cot = row_data
        row_out, pullback = jax.vjp(lambda par, tok: row_layer(par, tok, row_segs, row_first, row_second), params, row_tokens)
        grad_params, row_grad = pullback(row_cot)
        running = jax.tree.map(jnp.add, running, grad_params)
        return (running, (row_out, row_grad))
    totals, (outputs, grads) = lax.scan(row_step, zero_grads, (tokens, seg_all, keep_first, keep_second, cotangent))
    return (outputs[:, :L].astype(jnp.bfloat16), outputs[:, L:].astype(jnp.bfloat16), grads[:, :L], grads[:, L:], totals[0], totals[1], totals[2], totals[3], totals[4], totals[5], totals[6], totals[7])
```

```python
import jax
import jax.numpy as jnp
from jax import lax
from jax.sharding import PartitionSpec as P

HEADS = 12
HEAD = 64
PAD = 16
LANES = 128
FAR = -(2.0**100)
F32 = jnp.float32
BF16 = jnp.bfloat16


def dot(a, b):
    return jnp.dot(a, b, preferred_element_type=F32)


def dot_t(a, b):
    return lax.dot_general(a, b, (((1,), (1,)), ((), ())), preferred_element_type=F32)


def dot_lt(a, b):
    return lax.dot_general(a, b, (((0,), (0,)), ((), ())), preferred_element_type=F32)


def normalize(v):
    center = v - jnp.mean(v, axis=-1, keepdims=True)
    spread = jnp.mean(center * center, axis=-1, keepdims=True)
    scale = lax.rsqrt(spread + 1e-06)
    return center * scale, scale


def normalize_back(grad_hat, hat, scale):
    mean_g = jnp.mean(grad_hat, axis=-1, keepdims=True)
    mean_gh = jnp.mean(grad_hat * hat, axis=-1, keepdims=True)
    return scale * (grad_hat - mean_g - hat * mean_gh)


def gelu_pair(v):
    half = 0.5 * (1.0 + lax.erf(v * 0.5**0.5))
    slope = half + v * jnp.exp(-0.5 * v * v) * 0.3989422804014327
    return v * half, slope


def pick(arr, index, axis):
    return lax.dynamic_index_in_dim(arr, index, axis, keepdims=False)


def total(parts):
    out = parts[0].astype(F32)
    for part in parts[1:]:
        out = out + part.astype(F32)
    return out


def swap_seq(v, mask):
    return lax.ppermute(v, "seq", [(i, i ^ mask) for i in range(lax.axis_size("seq"))])


def swap_batch(v, mask):
    return lax.ppermute(v, "batch", [(i, i ^ mask) for i in range(lax.axis_size("batch"))])


def halve(parts, axis, bit, kind, dtype=BF16):
    own = (lax.axis_index(kind) >> bit) & 1
    send = total([pick(p, 1 - own, axis) for p in parts]).astype(dtype)
    swap = swap_seq if kind == "seq" else swap_batch
    return [pick(p, own, axis) for p in parts] + [swap(send, 1 << bit)]


def bits_of(kind):
    return lax.axis_size(kind).bit_length() - 1


def split_bits(arr, axis, count):
    shape = arr.shape
    return arr.reshape(shape[:axis] + (2,) * count + shape[axis + 1 :])


def halve_batch(parts, axis, dtype=BF16, skip=()):
    left = [b for b in range(bits_of("batch")) if b not in skip]
    while left:
        bit = left.pop(0)
        parts = halve(parts, axis + len(left), bit, "batch", dtype)
    return parts


def body(
    patches,
    specials,
    segment_ids,
    special_order,
    keep_mask,
    norm_gains,
    norm_shifts,
    w_qkv,
    biases,
    w_out,
    w_fc1,
    fc1_bias,
    w_fc2,
    cot_patches,
    cot_specials,
):
    rows, count, width = patches.shape
    extra = specials.shape[1]
    images = keep_mask.shape[1] // 2
    block = count + PAD
    own_heads = HEADS // 4
    cols = own_heads * HEAD
    hidden = w_fc1.shape[1] // 4
    s = lax.axis_index("seq")
    nb = lax.axis_size("batch")
    nbits = bits_of("batch")

    zeros = jnp.zeros((PAD - extra, width), BF16)
    mine = jnp.concatenate([patches[0], specials[0], zeros], axis=0)
    segs = jnp.concatenate([segment_ids[0], special_order[0] // 2, jnp.full((PAD - extra,), -1, jnp.int32)])
    onehot = (segs[:, None] == jnp.arange(LANES, dtype=jnp.int32)).astype(BF16)
    pay = jnp.concatenate([mine, onehot], axis=1)
    cot = jnp.concatenate([cot_patches[0], cot_specials[0], zeros], axis=0)
    pay_c = swap_seq(pay, 1)
    pay_x = swap_seq(pay, 2)
    pay_d = swap_seq(pay_x, 1)
    cot_c = swap_seq(cot, 1)
    allpay = jnp.concatenate([pay, pay_c, pay_x, pay_d], axis=0)
    cots = jnp.concatenate([cot, cot_c], axis=0)
    tok = allpay[:, :width].astype(F32)
    hot = allpay[:, width:]
    hot_chip = hot[: 2 * block].astype(F32)
    keep = keep_mask[0].astype(F32) / 0.75
    keep_a = hot_chip[:, :images] @ keep[:images, None]
    keep_m = hot_chip[:, :images] @ keep[images:, None]

    hat1, scale1 = normalize(tok)
    normed = (hat1 * norm_gains[0] + norm_shifts[0]).astype(BF16)
    w_own = [lax.dynamic_slice(w_qkv, (0, j * width + s * cols), (width, cols)) for j in range(3)]
    bias_own = [lax.dynamic_slice(biases, (j, s * cols), (1, cols)) for j in range(2)]
    query = ((dot(normed, w_own[0]) + bias_own[0]).astype(BF16).astype(F32) * HEAD**-0.5).astype(BF16)
    key = dot(normed, w_own[1]).astype(BF16)
    value = (dot(normed, w_own[2]) + bias_own[1]).astype(BF16)
    far = jnp.where(hot[:, :images] > 0, 0.0, FAR).astype(BF16)

    def head(v, h):
        return v[:, h * HEAD : (h + 1) * HEAD]

    attended, tops = [], []
    for h in range(own_heads):
        q = jnp.concatenate([head(query, h), hot[:, :images]], axis=1)
        k = jnp.concatenate([head(key, h), far], axis=1)
        sc = dot_t(q, k)
        top = jnp.max(sc, axis=-1, keepdims=True)
        e = jnp.exp(sc - top)
        tot = jnp.sum(e, axis=-1, keepdims=True)
        attended.append(dot((e / tot).astype(BF16), head(value, h)))
        tops.append((top, tot))
    attended = jnp.concatenate(attended, axis=1).astype(BF16)

    chip = 2 * block
    att_x = swap_seq(attended[chip:], 2)
    six = jnp.concatenate([attended[:chip], att_x], axis=1)
    six_c = swap_seq(six, 1)
    six_c = jnp.concatenate([six_c[block:], six_c[:block]], axis=0)
    w_out_own = jnp.concatenate(
        [lax.dynamic_slice(w_out, ((s ^ j) * cols, 0), (cols, width)) for j in (0, 2)], axis=0
    )
    w_out_oth = jnp.concatenate(
        [lax.dynamic_slice(w_out, ((s ^ j) * cols, 0), (cols, width)) for j in (1, 3)], axis=0
    )
    branch = dot(six, w_out_own) + dot(six_c, w_out_oth) + biases[2]
    middle = tok[:chip] + keep_a * branch
    hat2, scale2 = normalize(middle)
    normed2 = (hat2 * norm_gains[1] + norm_shifts[1]).astype(BF16)
    gout = cots.astype(F32)
    gb2 = (keep_m * gout).astype(BF16)

    fc1 = [lax.dynamic_slice(w_fc1, (0, (s ^ j) * hidden), (width, hidden)) for j in (0, 2)]
    fc2 = [lax.dynamic_slice(w_fc2, ((s ^ j) * hidden, 0), (hidden, width)) for j in (0, 2)]
    f_bias = [lax.dynamic_slice(fc1_bias, ((s ^ j) * hidden,), (hidden,)) for j in (0, 2)]
    g_fc2, g_fc1, g_fb = [], [], []
    branch2 = 0.0
    gn2 = 0.0
    for j in range(2):
        pre = dot(normed2, fc1[j]) + f_bias[j]
        act, slope = gelu_pair(pre)
        act = act.astype(BF16)
        g_fc2.append(dot_lt(act, gb2).astype(BF16))
        gh = (dot_t(gb2, fc2[j]) * slope).astype(BF16)
        g_fc1.append(dot_lt(normed2, gh).astype(BF16))
        g_fb.append(jnp.sum(gh.astype(F32), axis=0))
        branch2 = branch2 + dot(act, fc2[j])
        gn2 = gn2 + dot_t(gh, fc1[j])

    keep2 = g_fc2[0].reshape(nb, -1, width)
    got2 = swap_seq(g_fc2[1], 2).reshape(nb, -1, width)
    parts2 = [split_bits(p, 0, nbits) for p in (keep2, got2)]
    out_fc2 = total(halve_batch(parts2, 0))

    arr = jnp.stack(g_fc1, axis=1).reshape(2, 2, nb, -1, 2, hidden)
    parts1 = [split_bits(arr, 2, nbits)]
    parts1 = halve(parts1, 2 + nbits - 1, 0, "batch")
    parts1 = halve(parts1, 0, 1, "seq")
    parts1[-1] = jnp.flip(parts1[-1], axis=-2)
    parts1 = halve_batch(parts1, 1, skip=(0,))
    sum1 = total(parts1)
    own_c = s & 1
    sent = pick(sum1, 1 - own_c, 0).astype(BF16)
    kept = pick(sum1, own_c, 0)
    got = swap_seq(sent, 1).astype(F32)
    rel = jnp.stack([kept[:, 0], got[:, 0], kept[:, 1], got[:, 1]], axis=0)
    out_fc1 = jnp.concatenate([pick(rel, s ^ a, 0) for a in range(4)], axis=1)

    b2_c = swap_seq(branch2[block:].astype(BF16), 1).astype(F32)
    result = middle[:block] + keep_m[:block] * (branch2[:block] + b2_c + biases[3])

    gn2_c = swap_seq(gn2.astype(BF16), 1).astype(F32)
    gn2 = gn2 + jnp.concatenate([gn2_c[block:], gn2_c[:block]], axis=0)
    gmid = gout + normalize_back(gn2 * norm_gains[1], hat2, scale2)
    gbr = (keep_a * gmid).astype(BF16)
    own = slice(0, block)
    small = [
        jnp.sum(gn2[own] * hat2[own], axis=0),
        jnp.sum(gn2[own], axis=0),
        jnp.sum(gb2[own].astype(F32), axis=0),
        jnp.sum(gbr[own].astype(F32), axis=0),
    ]
    g_out = [dot_lt(six[:, j * cols : (j + 1) * cols], gbr).astype(BF16) for j in range(2)]
    keep_o = g_out[0].reshape(nb, -1, width)
    got_o = swap_seq(g_out[1], 2).reshape(nb, -1, width)
    out_out = total(halve_batch([split_bits(p, 0, nbits) for p in (keep_o, got_o)], 0))

    gatt6 = dot_t(gbr, w_out_own).astype(BF16)
    gatt_x = swap_seq(gatt6[:, cols:], 2)
    gatt = jnp.concatenate([gatt6[:, :cols], gatt_x], axis=0)

    gq, gk, gv = [], [], []
    for h in range(own_heads):
        q = jnp.concatenate([head(query, h), hot[:, :images]], axis=1)
        k = jnp.concatenate([head(key, h), far], axis=1)
        top, tot = tops[h]
        prob = jnp.exp(dot_t(q, k) - top) / tot
        go = head(gatt, h)
        gp = dot_t(go, head(value, h))
        inner = jnp.sum(gp * prob, axis=-1, keepdims=True)
        gs = (prob * (gp - inner)).astype(BF16)
        gq.append(dot(gs, head(key, h)) * HEAD**-0.5)
        gk.append(dot_lt(gs, head(query, h)))
        gv.append(dot_lt(prob.astype(BF16), go))
    gq, gk, gv = [jnp.concatenate(v, axis=1).astype(BF16) for v in (gq, gk, gv)]
    gqkv = jnp.concatenate([gq, gk, gv], axis=1)
    w_cat = jnp.concatenate(w_own, axis=1)
    gn1 = dot_t(gqkv, w_cat)
    g_qkv = dot_lt(normed, gqkv).astype(BF16)
    small = small + [jnp.sum(gn1 * hat1, axis=0), jnp.sum(gn1, axis=0)]
    own_small = jnp.stack([jnp.sum(gq.astype(F32), axis=0), jnp.sum(gv.astype(F32), axis=0)])

    blocks = gn1.reshape(2, 2, block, width)
    got_n = swap_seq(blocks[:, 1].astype(BF16), 1)
    half_n = blocks[:, 0] + got_n.astype(F32)
    fin = half_n[0] + swap_seq(half_n[1].astype(BF16), 2).astype(F32)
    gtok = gmid[:block] + normalize_back(fin * norm_gains[0], hat1[:block], scale1[:block])

    arr = g_qkv.reshape(4, nb, -1, 3 * cols)
    sum_q = total(halve_batch([split_bits(arr, 1, nbits)], 1))
    pieces = [pick(sum_q, s, 0)] + [
        swap_seq(pick(sum_q, s ^ j, 0).astype(BF16), j).astype(F32) for j in (1, 2, 3)
    ]
    rel = jnp.stack(pieces, axis=0)
    absolute = jnp.stack([pick(rel, s ^ a, 0) for a in range(4)], axis=1)
    out_qkv = absolute.reshape(-1, 4, 3, cols).transpose(0, 2, 1, 3).reshape(-1, 3 * width)

    sm = jnp.stack(small).reshape(6, 2, 2, nb, -1)
    parts = [split_bits(sm, 3, nbits)]
    parts = halve(parts, 1, 1, "seq", F32)
    parts = halve(parts, 1, 0, "seq", F32)
    sums = total(halve_batch(parts, 1, F32))
    sums_own = total(halve_batch([split_bits(own_small.reshape(2, nb, -1), 1, nbits)], 1, F32))
    fb_keep = g_fb[0].reshape(nb, -1)
    fb_got = swap_seq(g_fb[1], 2).reshape(nb, -1)
    out_fb = total(halve_batch([split_bits(p, 0, nbits) for p in (fb_keep, fb_got)], 0, F32))

    grad_gains = jnp.stack([sums[4], sums[0]])
    grad_shifts = jnp.stack([sums[5], sums[1]])
    grad_biases = jnp.stack([sums_own[0], sums_own[1], sums[3], sums[2]])
    return (
        result[None, :count].astype(BF16),
        result[None, count : count + extra].astype(BF16),
        gtok[None, :count],
        gtok[None, count : count + extra],
        grad_gains,
        grad_shifts,
        out_qkv,
        grad_biases,
        out_out,
        out_fc1,
        out_fb,
        out_fc2,
    )


def solution(mesh):
    tok = P("batch", "seq", None)
    ids = P("batch", "seq")
    split = P(None, ("seq", "batch"))
    rows = P(("seq", "batch"), None)
    return jax.shard_map(
        body,
        mesh=mesh,
        in_specs=(tok, tok, ids, ids, P("batch", None)) + (P(),) * 8 + (tok, tok),
        out_specs=(tok, tok, tok, tok, split, split, rows, split, rows, rows, P(("seq", "batch")), rows),
        check_vma=False,
    )
```

```python
import functools

import jax
import jax.numpy as jnp
from jax import lax
from jax.experimental import pallas as pl
from jax.experimental.pallas import tpu as pltpu
from jax.sharding import PartitionSpec as P

HEADS = 12
HEAD = 64
PAD = 32
LANES = 128
OWN = 3
FAR = -(2.0**100)
F32 = jnp.float32
BF16 = jnp.bfloat16
SDS = jax.ShapeDtypeStruct


def dot(a, b):
    return jnp.dot(a, b, preferred_element_type=F32)


def dot_t(a, b):
    return lax.dot_general(a, b, (((1,), (1,)), ((), ())), preferred_element_type=F32)


def dot_lt(a, b):
    return lax.dot_general(a, b, (((0,), (0,)), ((), ())), preferred_element_type=F32)


def normalize(v):
    center = v - jnp.mean(v, axis=-1, keepdims=True)
    spread = jnp.mean(center * center, axis=-1, keepdims=True)
    scale = lax.rsqrt(spread + 1e-06)
    return center * scale, scale


def normalize_back(grad_hat, hat, scale):
    mean_g = jnp.mean(grad_hat, axis=-1, keepdims=True)
    mean_gh = jnp.mean(grad_hat * hat, axis=-1, keepdims=True)
    return scale * (grad_hat - mean_g - hat * mean_gh)


def gelu_pair(v):
    half = 0.5 * (1.0 + lax.erf(v * 0.5**0.5))
    slope = half + v * jnp.exp(-0.5 * v * v) * 0.3989422804014327
    return v * half, slope


def lane_of(rows):
    return lax.broadcasted_iota(jnp.int32, (rows, LANES), 1)


def unpack_head(tiles, e):
    tile = tiles[:, (e // 2) * LANES : (e // 2 + 1) * LANES]
    return tile if e % 2 == 0 else pltpu.roll(tile, HEAD, 1)


def pack_pair(low, high):
    return jnp.where(lane_of(low.shape[0]) < HEAD, low, pltpu.roll(high, HEAD, 1))


def vmem():
    return pl.BlockSpec(memory_space=pltpu.VMEM)


def smem():
    return pl.BlockSpec(memory_space=pltpu.SMEM)


def call(kernel, outs, args, scratch=(), flops=0, scalars=0):
    nbytes = sum(a.size * a.dtype.itemsize for a in args)
    nbytes += sum(o.size * o.dtype.itemsize for o in outs)
    return pl.pallas_call(
        kernel,
        out_shape=outs,
        in_specs=[smem()] * scalars + [vmem()] * (len(args) - scalars),
        out_specs=[vmem()] * len(outs),
        scratch_shapes=list(scratch),
        cost_estimate=pl.CostEstimate(flops=flops, bytes_accessed=nbytes, transcendentals=0),
    )(*args)


def attend_kernel(p0, p1, p2, p3, gain, shift, w, bias, qa, ka, va, lse, keep, send, normed, oacc):
    rows = p0.shape[0]
    width = gain.shape[1]
    whole = 4 * rows
    lane = lane_of(rows)
    for i, p in enumerate((p0, p1, p2, p3)):
        at = pl.ds(i * rows, rows)
        hat, _ = normalize(p[:, :width].astype(F32))
        nrm = (hat * gain[...] + shift[...]).astype(BF16)
        normed[at, :] = nrm
        qkv = dot(nrm, w[...]) + bias[...]
        hot = p[:, width:].astype(F32)
        far = jnp.where((lane >= HEAD) & (lane < HEAD + 8) & (hot == 0.0), FAR, 0.0)
        one = jnp.where(lane == HEAD, 1.0, 0.0)
        for h in range(OWN):
            q = unpack_head(qkv, 3 * h) * HEAD**-0.5
            qa[h, at, :] = jnp.where(lane < HEAD, q, hot).astype(BF16)
            ka[h, at, :] = jnp.where(lane < HEAD, unpack_head(qkv, 3 * h + 1), far).astype(BF16)
            va[h, at, :] = jnp.where(lane < HEAD, unpack_head(qkv, 3 * h + 2), one).astype(BF16)
    step = whole // 3

    def block(i, carry):
        h, b = i // 3, i % 3
        at = pl.ds(pl.multiple_of(b * step, step), step)
        sc = dot_t(qa[h, at, :], ka[h])
        top = jnp.max(sc, axis=-1, keepdims=True)
        e = jnp.exp(sc - top).astype(BF16)
        o = dot(e, va[h])
        tot = o[:, HEAD : HEAD + 1]
        oacc[h, at, :] = o * (1.0 / tot)
        col = jnp.broadcast_to(top + jnp.log(tot), (step, LANES))
        lse[h, b] = col.T[:8]
        return carry

    lax.fori_loop(0, 3 * OWN, block, 0)
    for out, start in ((keep, 0), (send, 2 * rows)):
        at = pl.ds(start, 2 * rows)
        out[:, :LANES] = pack_pair(oacc[0, at, :], oacc[1, at, :]).astype(BF16)
        out[:, LANES:] = oacc[2, at, :HEAD].astype(BF16)


def keep_column(p0, p1, table, width):
    hot = jnp.concatenate([p0[:, width:], p1[:, width:]], axis=0).astype(F32)
    return jnp.sum(hot * table, axis=-1, keepdims=True)


def middle_kernel(sref, a0, a1, a2, a3, p0, p1, c0, c1, table, w_out, bias, gain, shift, middle, normed2, gb2):
    s = sref[0]
    rows, width = c0.shape
    cols = a0.shape[1]
    acc = jnp.zeros((2 * rows, width), F32) + bias[...]
    for j, a in ((0, a0), (2, a2)):
        w = w_out[pl.ds(pl.multiple_of((s ^ j) * cols, HEAD), cols), :]
        acc = acc + dot(a[...], w)
    for j, a in ((1, a1), (3, a3)):
        w = w_out[pl.ds(pl.multiple_of((s ^ j) * cols, HEAD), cols), :]
        part = dot(a[...], w)
        acc = acc + jnp.concatenate([part[rows:], part[:rows]], axis=0)
    keep_a = keep_column(p0, p1, table[0:1, :], width)
    keep_m = keep_column(p0, p1, table[1:2, :], width)
    tok = jnp.concatenate([p0[:, :width], p1[:, :width]], axis=0).astype(F32)
    mid = tok + keep_a * acc
    middle[...] = mid
    hat, _ = normalize(mid)
    normed2[...] = (hat * gain[...] + shift[...]).astype(BF16)
    gout = jnp.concatenate([c0[...], c1[...]], axis=0).astype(F32)
    gb2[...] = (keep_m * gout).astype(BF16)


def feed_kernel(last, sref, bref, normed2, gb2, fc1, bias, fc2, *refs):
    if last:
        b2_in, gn_in, g2, g1_send, g1_keep, gb, b2_keep, b2_send, gn_keep, gn_send, wide, b2, gn = refs
    else:
        g2a, g2b, g1_send, g1_keep, gb, b2, gn, wide = refs
    i = pl.program_id(0)
    half = b2.shape[0] // 2
    pre = dot(normed2[...], fc1[...]) + bias[...]
    gact = dot_t(gb2[...], fc2[...])
    act, slope = gelu_pair(pre)
    act = act.astype(BF16)
    gh = (gact * slope).astype(BF16)
    grad2 = dot_lt(act, gb2[...]).astype(BF16)
    if last:
        g2[...] = grad2
    else:

        @pl.when(i == 0)
        def _():
            g2a[...] = grad2

        @pl.when(i == 1)
        def _():
            g2b[...] = grad2

    split_rows(dot_lt(normed2[...], gh), wide, bref[0] & 1, g1_send, g1_keep)
    gb[...] = jnp.sum(gh.astype(F32), axis=0, keepdims=True)
    part2 = dot(act, fc2[...])
    partn = dot_t(gh, fc1[...])

    @pl.when(i == 0)
    def _():
        if last:
            b2[...] = b2_in[...] + part2
            gn[...] = gn_in[...] + partn
        else:
            b2[...] = part2
            gn[...] = partn

    @pl.when(i > 0)
    def _():
        b2[...] += part2
        gn[...] += partn

    if last:

        @pl.when(i == pl.num_programs(0) - 1)
        def _():
            b2_keep[...] = b2[:half]
            b2_send[...] = b2[half:].astype(BF16)
            gn_keep[...] = gn[...]
            gn_send[:half] = gn[half:].astype(BF16)
            gn_send[half:] = gn[:half].astype(BF16)


def split_rows(value, wide, bit, send, keep):
    if len(send.shape) == 2:
        rows = value.shape[0] // 2
        send[...] = value[:rows].astype(BF16)
        keep[...] = value[rows:].astype(BF16)
        return
    wide[...] = value
    rows = send.shape[1]
    for m in range(send.shape[0]):
        base = 2 * m * rows
        send[m] = wide[pl.ds(pl.multiple_of(base + (1 - bit) * rows, 8), rows), :].astype(BF16)
        keep[m] = wide[pl.ds(pl.multiple_of(base + bit * rows, 8), rows), :].astype(BF16)


def feed(last, pick, per, sidx, bidx, normed2, gb2, w_fc1, bias, w_fc2, prev=()):
    tokens, width = normed2.shape
    hidden = w_fc1.shape[1] // 4
    chunk = hidden // 2
    steps = 2
    const = lambda i, s, b: (0, 0)
    full = pl.BlockSpec((tokens, width), const)
    half = pl.BlockSpec((tokens // 2, width), const)
    in_specs = [
        full,
        full,
        pl.BlockSpec((width, chunk), lambda i, s, b: (0, (s[0] ^ pick) * steps + i)),
        pl.BlockSpec((1, chunk), lambda i, s, b: (0, (s[0] ^ pick) * steps + i)),
        pl.BlockSpec((chunk, width), lambda i, s, b: ((s[0] ^ pick) * steps + i, 0)),
    ] + [full] * len(prev)
    if last:
        out_specs = [pl.BlockSpec((chunk, width), lambda i, s, b: (i, 0))]
        outs = [SDS((hidden, width), BF16)]
    else:
        out_specs = [pl.BlockSpec((chunk, width), const)] * 2
        outs = [SDS((chunk, width), BF16)] * 2
    if per % 8 == 0:
        pairs = width // (2 * per)
        out_specs += [pl.BlockSpec((pairs, per, chunk), lambda i, s, b: (0, 0, i))] * 2
        outs += [SDS((pairs, per, hidden), BF16)] * 2
    else:
        out_specs += [pl.BlockSpec((width // 2, chunk), lambda i, s, b: (0, i))] * 2
        outs += [SDS((width // 2, hidden), BF16)] * 2
    out_specs += [pl.BlockSpec((1, chunk), lambda i, s, b: (0, i))]
    outs += [SDS((1, hidden), F32)]
    scratch = [pltpu.VMEM((width, chunk), F32)]
    if last:
        out_specs += [half, half, full, full]
        outs += [SDS((tokens // 2, width), F32), SDS((tokens // 2, width), BF16)]
        outs += [SDS((tokens, width), F32), SDS((tokens, width), BF16)]
        scratch += [pltpu.VMEM((tokens, width), F32)] * 2
    else:
        out_specs += [full, full]
        outs += [SDS((tokens, width), F32)] * 2
    out = pl.pallas_call(
        functools.partial(feed_kernel, last),
        grid_spec=pltpu.PrefetchScalarGridSpec(
            num_scalar_prefetch=2,
            grid=(steps,),
            in_specs=in_specs,
            out_specs=out_specs,
            scratch_shapes=scratch,
        ),
        out_shape=outs,
        cost_estimate=pl.CostEstimate(
            flops=12 * tokens * width * hidden, bytes_accessed=10 * width * hidden, transcendentals=0
        ),
    )(sidx, bidx, normed2, gb2, w_fc1, bias, w_fc2, *prev)
    at = 1 if last else 2
    out = list(out)
    if per % 8:
        out[at : at + 2] = by_batch_bit(jnp.concatenate(out[at : at + 2], axis=0), per)
    return out


def by_batch_bit(arr, per):
    arr = arr.reshape(-1, 2, per, arr.shape[-1])
    own = lax.axis_index("batch") & 1
    return [pick(arr, 1 - own, 1), pick(arr, own, 1)]


def branch_back_kernel(
    sref, gn_keep, gn_got, middle, p0, p1, c0, c1, table, w_out, gain, shift, a0, a2, gb2,
    b2_keep, b2_got, bias, gain1, shift1, fb_own, fb_oth,
    gmid_own, gatt, gatt_send, go_keep, go_send, early, opat, ospe, fcol,
):
    s = sref[0]
    rows, width = c0.shape
    cols = a0.shape[1]
    mid = middle[...]
    hat, scale = normalize(mid)
    g = gn_keep[...] + gn_got[...].astype(F32)
    gout = jnp.concatenate([c0[...], c1[...]], axis=0).astype(F32)
    gmid = gout + normalize_back(g * gain[...], hat, scale)
    gmid_own[...] = gmid[:rows]
    keep_a = keep_column(p0, p1, table[0:1, :], width)
    gbr = (keep_a * gmid).astype(BF16)
    w_own = w_out[pl.ds(pl.multiple_of(s * cols, HEAD), cols), :]
    w_oth = w_out[pl.ds(pl.multiple_of((s ^ 2) * cols, HEAD), cols), :]
    gatt_send[...] = dot_t(gbr, w_oth).astype(BF16)
    gatt[...] = dot_t(gbr, w_own).astype(BF16)
    go_send[...] = dot_lt(a2[...], gbr).astype(BF16)
    go_keep[...] = dot_lt(a0[...], gbr).astype(BF16)

    hot = p0[:, width:].astype(F32)
    keep_m = jnp.sum(hot * table[1:2, :], axis=-1, keepdims=True)
    res = (mid[:rows] + keep_m * (b2_keep[...] + b2_got[...].astype(F32) + bias[...])).astype(BF16)
    opat[...] = res[: opat.shape[0]]
    ospe[...] = res[opat.shape[0] : opat.shape[0] + ospe.shape[0]]

    own = slice(0, rows)
    blank = functools.partial(jnp.zeros, dtype=F32)
    lines = [
        gain1[...],
        shift1[...],
        blank((HEAD + 2, width)),
        jnp.sum(g[own] * hat[own], axis=0, keepdims=True),
        jnp.sum(g[own], axis=0, keepdims=True),
        jnp.sum(gb2[own, :].astype(F32), axis=0, keepdims=True),
        jnp.sum(gbr[own].astype(F32), axis=0, keepdims=True),
        blank((LANES - HEAD - 8, width)),
    ]
    early[...] = jnp.concatenate(lines, axis=0).T
    lane = lane_of(cols)
    for j, ref in ((0, fb_own), (2, fb_oth)):
        fcol[...] = jnp.broadcast_to(ref[...], (LANES, ref.shape[1])).T
        at = pl.ds(pl.multiple_of((s ^ j) * cols, HEAD), cols)
        val = early[at, :]
        for k in range(4):
            val = jnp.where(lane == HEAD + 8 + k, fcol[pl.ds(k, cols, stride=4), :], val)
        early[at, :] = val


def attend_back_kernel(first, heads, qa, ka, va, lse, ga, gx, out, sums, goa, dq, dk, dv):
    whole = qa.shape[1]
    half = ga.shape[0]
    lane = lane_of(half)
    for i in range(heads):
        h = first + i
        for ref, start in ((ga, 0), (gx, half)):
            if h < 2:
                t = ref[:, :LANES].astype(F32)
                t = jnp.where(lane < HEAD, t if h == 0 else pltpu.roll(t, HEAD, 1), 0.0)
            else:
                t = ref[:, LANES:].astype(F32)
                t = jnp.concatenate([t, jnp.zeros_like(t)], axis=1)
            goa[i, pl.ds(start, half), :] = t.astype(BF16)
    step = whole // 3

    def block(n, carry):
        i, b = n // 3, n % 3
        h = first + i
        at = pl.ds(pl.multiple_of(b * step, step), step)
        q, go = qa[h, at, :], goa[i, at, :]
        prob = jnp.exp(dot_t(ka[h], q) - lse[h, b][0:1, :])
        gp = dot_t(va[h], go)
        inner = jnp.sum(gp * prob, axis=0, keepdims=True)
        gs = (prob * (gp - inner)).astype(BF16)
        pv = dot(prob.astype(BF16), go)
        pk = dot(gs, q)
        dq[i, at, :] = dot_lt(gs, ka[h])

        @pl.when(b == 0)
        def _():
            dv[i] = pv
            dk[i] = pk

        @pl.when(b > 0)
        def _():
            dv[i] += pv
            dk[i] += pk

        return carry

    lax.fori_loop(0, 3 * heads, block, 0)
    for i in range(heads):
        out[i, :, :LANES] = pack_pair(dq[i] * HEAD**-0.5, dk[i]).astype(BF16)
        out[i, :, LANES:] = dv[i, :, :HEAD].astype(BF16)
        sums[i] = jnp.sum(out[i].astype(F32), axis=0, keepdims=True)


def attend_back(first, heads, qa, ka, va, lse, ga, gx):
    whole = qa.shape[1]
    return call(
        functools.partial(attend_back_kernel, first, heads),
        [SDS((heads, whole, 3 * HEAD), BF16), SDS((heads, 1, 3 * HEAD), F32)],
        (qa, ka, va, lse, ga, gx),
        [pltpu.VMEM((heads, whole, LANES), BF16)] + [pltpu.VMEM((heads, whole, LANES), F32)] * 3,
        flops=10 * heads * whole * whole * LANES,
    )


def norm1_kernel(g0, g12, w, keep, send):
    rows = keep.shape[0] // 2
    cols = g0.shape[2]
    for i in range(4):
        at = pl.ds(i * rows, rows)
        part = dot_t(g0[0, at, :], w[:, :cols])
        part = part + dot_t(g12[0, at, :], w[:, cols : 2 * cols])
        part = part + dot_t(g12[1, at, :], w[:, 2 * cols : 3 * cols])
        to = pl.ds((i // 2) * rows, rows)
        if i % 2 == 0:
            keep[to, :] = part
        else:
            send[to, :] = part.astype(BF16)


def qkv_grad_kernel(sref, bref, normed, g0, g12, s0, s12, w, early, send, keep, tile, wide):
    width, cols = w.shape[0], g0.shape[2]
    every = (g0[0], g12[0], g12[1])
    parts = [dot_lt(normed[...], g) for g in every]
    g = jnp.concatenate(parts, axis=1)
    w32 = w[:, : 3 * cols].astype(F32)
    rows = jnp.concatenate([s0[0], s12[0], s12[1]], axis=1)
    both = jnp.sum(g * w32, axis=-1, keepdims=True)
    gshift = jnp.sum(w32 * rows, axis=-1, keepdims=True)
    ggain = (both - early[:, 1:2] * gshift) / early[:, 0:1]
    lane = lane_of(width)
    tail = jnp.concatenate([g[:, 4 * LANES :], jnp.zeros((width, LANES - HEAD), F32)], axis=1)
    tail = jnp.where(lane == HEAD, ggain, tail)
    tail = jnp.where(lane == HEAD + 1, gshift, tail)
    tile[...] = jnp.where(lane >= HEAD + 4, early[...], tail)
    ones = jnp.ones((g0.shape[1], LANES), BF16)
    at = pl.multiple_of(sref[0] * cols, HEAD)
    for h, part in enumerate(every):
        col = dot_lt(part, ones)
        here = pl.ds(at + h * HEAD, HEAD)
        lanes = lane_of(HEAD)
        row = tile[here, :]
        row = jnp.where(lanes == HEAD + 2, col[:HEAD], row)
        tile[here, :] = jnp.where(lanes == HEAD + 3, col[2 * HEAD :], row)
    split_rows(jnp.concatenate([g[:, : 4 * LANES], tile[...]], axis=1), wide, bref[0] & 1, send, keep)


def wide_sum(*parts):
    return sum(p.astype(F32) for p in parts[1:]) + parts[0].astype(F32)


def stage1_kernel(sref, keep_own, got_own, keep_oth, got_oth, send):
    x = sref[0] >> 1
    n, _, width = send.shape
    width = width // 2
    for i in range(n):
        m = (1 - x) * n + i
        send[i, :, :width] = wide_sum(keep_own[m], got_own[m]).astype(BF16)
        send[i, :, width:] = wide_sum(keep_oth[m], got_oth[m]).astype(BF16)


def stage2_kernel(
    sref, bref, keep_own, got_own, keep_oth, got_oth, got_b, fc2, got2a, got2b, out, got_o,
    send_a, zb1, zb2, zb3, keep_b,
):
    x, y, q = sref[0] >> 1, bref[0] & 1, bref[0] >> 1
    n = got_b.shape[0] // 4
    width = keep_own.shape[2]
    deep = fc2.shape[1]
    for c in range(2):
        for k, ref in enumerate((keep_b, zb1, zb2, zb3)):
            i = c * 4 + (q ^ k)
            m = x * 8 + i
            ref[c, :, :width] = wide_sum(keep_own[m], got_own[m], got_b[i, :, width:]).astype(ref.dtype)
            ref[c, :, width:] = wide_sum(keep_oth[m], got_oth[m], got_b[i, :, :width]).astype(ref.dtype)
    for j in range(4):
        b = 2 * j + 1 - y
        got = got2a if j < 2 else got2b
        send_a[j, :deep] = wide_sum(fc2[b], got[b - 4 * (j // 2)]).astype(BF16)
        send_a[j, deep:] = wide_sum(out[b], got_o[b]).astype(BF16)


def stage3_kernel(
    sref, bref, fc2, got2, out, got_o, got_a, keep_b, zb1, zb2, zb3, gn_keep, gn_got,
    za1, za2, za3, keep_a, swap_send, swap_keep, xsend,
):
    c, y, q = sref[0] & 1, bref[0] & 1, bref[0] >> 1
    deep = fc2.shape[1]
    for k, ref in enumerate((keep_a, za1, za2, za3)):
        j = q ^ k
        b = 2 * j + y
        ref[:deep] = wide_sum(fc2[b], got2[b], got_a[j, :deep]).astype(ref.dtype)
        ref[deep:] = wide_sum(out[b], got_o[b], got_a[j, deep:]).astype(ref.dtype)
    swap_send[...] = wide_sum(keep_b[1 - c], zb1[1 - c], zb2[1 - c], zb3[1 - c]).astype(BF16)
    swap_keep[...] = wide_sum(keep_b[c], zb1[c], zb2[c], zb3[c])
    rows = xsend.shape[0]
    xsend[...] = wide_sum(gn_keep[rows:], gn_got[rows:]).astype(BF16)


def final_kernel(
    sref, k0, c0, x0, p0, gmid, gain, keep_a, za1, za2, za3, swap_keep, swap_got,
    gpat, gspe, fc2, out, fc1,
):
    s = sref[0]
    rows, width = x0.shape
    count = gpat.shape[0]
    extra = gspe.shape[0]
    hat, scale = normalize(p0[:, :width].astype(F32))
    g = wide_sum(k0[:rows], c0[:rows], x0[...])
    res = gmid[...] + normalize_back(g * gain[...], hat, scale)
    gpat[...] = res[:count]
    gspe[...] = res[count : count + extra]
    sums = wide_sum(keep_a[...], za1[...], za2[...], za3[...])
    deep = fc2.shape[0]
    fc2[...] = sums[:deep]
    out[...] = sums[deep:]
    hidden = swap_keep.shape[1] // 2

    def place(j, value):
        fc1[:, pl.ds(pl.multiple_of((s ^ j) * hidden, LANES), hidden)] = value

    place(0, swap_keep[:, :hidden])
    place(2, swap_keep[:, hidden:])
    place(1, swap_got[:, :hidden].astype(F32))
    place(3, swap_got[:, hidden:].astype(F32))


def norm_only_kernel(k0, c0, x0, p0, gmid, gain, gpat, gspe):
    rows, width = x0.shape
    count = gpat.shape[0]
    hat, scale = normalize(p0[:, :width].astype(F32))
    g = wide_sum(k0[:rows], c0[:rows], x0[...])
    res = gmid[...] + normalize_back(g * gain[...], hat, scale)
    gpat[...] = res[:count]
    gspe[...] = res[count : count + gspe.shape[0]]


def quarter_kernel(bref, keep, got, z1, z2, z3, kept):
    q = bref[0] >> 1
    for r in range(4):
        for k, ref in enumerate((kept, z1, z2, z3)):
            m = r * 4 + (q ^ k)
            ref[r] = wide_sum(keep[m], got[m]).astype(ref.dtype)


def owner_kernel(sref, kept, z1, z2, z3, s1, s2, s3, own):
    s = sref[0]
    for k, ref in enumerate((own, s1, s2, s3)):
        m = s ^ k
        ref[...] = wide_sum(kept[m], z1[m], z2[m], z3[m]).astype(ref.dtype)


def collect_kernel(sref, own, g1, g2, g3, out, vec, every):
    s = sref[0]
    for k, ref in enumerate((own, g1, g2, g3)):
        every[k] = ref[...].astype(F32)
    pieces = [every[s ^ a] for a in range(4)]

    def part(u):
        j, a, h = u // 12, (u // 3) % 4, u % 3
        e = 3 * h + j
        return pieces[a][:, (e // 2) * LANES : (e // 2 + 1) * LANES], e % 2

    lane = lane_of(out.shape[0])
    for t in range(out.shape[1] // LANES):
        (low, lo), (high, hi) = part(2 * t), part(2 * t + 1)
        low = pltpu.roll(low, HEAD, 1) if lo else low
        high = high if hi else pltpu.roll(high, HEAD, 1)
        out[:, t * LANES : (t + 1) * LANES] = jnp.where(lane < HEAD, low, high)
    tail = 4 * LANES
    vec[...] = wide_sum(*[every[k, :, tail:] for k in range(4)])


def pick(arr, index, axis):
    return lax.dynamic_index_in_dim(arr, index, axis, keepdims=False)


def total(parts):
    out = parts[0].astype(F32)
    for part in parts[1:]:
        out = out + part.astype(F32)
    return out


def swap(kind, v, mask):
    return lax.ppermute(v, kind, [(i, i ^ mask) for i in range(lax.axis_size(kind))])


def swap_seq(v, mask):
    return swap("seq", v, mask)


def after(value, *first):
    return lax.optimization_barrier((value, first))[0]


def bits_of(kind):
    return lax.axis_size(kind).bit_length() - 1


def split_bits(arr, axis, count):
    shape = arr.shape
    return arr.reshape(shape[:axis] + (2,) * count + shape[axis + 1 :])


def to_send(parts, axis, bit, kind):
    own = (lax.axis_index(kind) >> bit) & 1
    send = total([pick(p, 1 - own, axis) for p in parts]).astype(BF16)
    return send, [pick(p, own, axis) for p in parts]


def send_four(parts, axis, low):
    own = (lax.axis_index("batch") >> low) & 3

    def quarter(p, k):
        return pick(pick(p, k >> 1, axis), k & 1, axis)

    sends = [total([quarter(p, own ^ k) for p in parts]).astype(BF16) for k in (1, 2, 3)]
    return sends, [quarter(p, own) for p in parts]


def swap_four(sends, low):
    return [swap("batch", v, k << low) for k, v in zip((1, 2, 3), sends)]


def sum_rest(parts, axis, low):
    top = bits_of("batch")
    while low < top:
        if low + 1 < top:
            sends, kept = send_four(parts, axis + top - low - 2, low)
            parts, low = kept + swap_four(sends, low), low + 2
        else:
            send, kept = to_send(parts, axis, low, "batch")
            parts, low = kept + [swap("batch", send, 1 << low)], low + 1
    return total(parts)


def body(
    patches,
    specials,
    segment_ids,
    special_order,
    keep_mask,
    norm_gains,
    norm_shifts,
    w_qkv,
    biases,
    w_out,
    w_fc1,
    fc1_bias,
    w_fc2,
    cot_patches,
    cot_specials,
):
    count, width = patches.shape[1:]
    extra = specials.shape[1]
    images = keep_mask.shape[1] // 2
    block = count + PAD
    chip = 2 * block
    whole = 4 * block
    cols = OWN * HEAD
    hidden = w_fc1.shape[1] // 4
    s = lax.axis_index("seq")
    sidx = s.astype(jnp.int32).reshape(1)
    bidx = lax.axis_index("batch").astype(jnp.int32).reshape(1)
    nb = lax.axis_size("batch")
    nbits = bits_of("batch")

    zeros = jnp.zeros((PAD - extra, width), BF16)
    mine = jnp.concatenate([patches[0], specials[0], zeros], axis=0)
    segs = jnp.concatenate(
        [segment_ids[0], special_order[0] // 2, jnp.full((PAD - extra,), -1, jnp.int32)]
    )
    marks = jnp.arange(LANES, dtype=jnp.int32) - HEAD
    hot = ((segs[:, None] == marks) & (marks >= 0)).astype(BF16)
    pay = jnp.concatenate([mine, hot], axis=1)
    cot = jnp.concatenate([cot_patches[0], cot_specials[0], zeros], axis=0)
    pay_c = swap_seq(pay, 1)
    pay_x = swap_seq(pay, 2)
    cot_c = swap_seq(cot, 1)
    keep = keep_mask[0].astype(F32).reshape(2, images) / 0.75
    table = jnp.pad(keep, ((0, 6), (HEAD, LANES - HEAD - images)))

    order = [(h, j) for h in range(OWN) for j in range(3)]
    w_own = [lax.dynamic_slice(w_qkv, (0, j * width + s * cols + h * HEAD), (width, HEAD)) for h, j in order]
    w_own = jnp.concatenate(w_own + [jnp.zeros((width, HEAD), BF16)], axis=1)
    sides = {0: biases[0], 1: jnp.zeros((width,), F32), 2: biases[1]}
    bias_own = [lax.dynamic_slice(sides[j], (s * cols + h * HEAD,), (HEAD,)) for h, j in order]
    bias_own = jnp.concatenate(bias_own + [jnp.zeros((HEAD,), F32)])[None]
    pay_x, w_own, bias_own, table = lax.optimization_barrier((pay_x, w_own, bias_own, table))
    pay_d = swap_seq(pay_x, 1)
    gain1, gain2 = norm_gains[0:1], norm_gains[1:2]
    shift1, shift2 = norm_shifts[0:1], norm_shifts[1:2]
    fb = fc1_bias.reshape(1, -1)

    headed = SDS((OWN, whole, LANES), BF16)
    qa, ka, va, lse, a0, att_send, normed = call(
        attend_kernel,
        [headed] * 3
        + [SDS((OWN, 3, 8, whole // 3), F32), SDS((chip, cols), BF16), SDS((chip, cols), BF16)]
        + [SDS((whole, width), BF16)],
        (pay, pay_c, pay_x, pay_d, gain1, shift1, w_own, bias_own),
        [pltpu.VMEM((OWN, whole, LANES), F32)],
        flops=2 * whole * width * 3 * cols + 4 * OWN * whole * whole * LANES,
    )
    a2 = swap_seq(att_send, 2)
    a1 = swap_seq(a0, 1)
    a3 = swap_seq(a2, 1)

    middle, normed2, gb2 = call(
        middle_kernel,
        [SDS((chip, width), F32), SDS((chip, width), BF16), SDS((chip, width), BF16)],
        (sidx, a0, a1, a2, a3, pay, pay_c, cot, cot_c, table, w_out, biases[2:3], gain2, shift2),
        flops=2 * chip * width * width,
        scalars=1,
    )
    per = width // (4 * nb)
    fc2_a, fc2_b, oth_y, keep_oth, fb_oth, b2, gn = feed(
        False, 2, per, sidx, bidx, normed2, gb2, w_fc1, fb, w_fc2
    )
    got2a = swap_seq(fc2_a, 2)
    got_oth = swap("batch", oth_y, 1)
    fc2_keep, own_y, keep_own, fb_own, b2_keep, b2_send, gn_keep, gn_send = feed(
        True, 0, per, sidx, bidx, normed2, gb2, w_fc1, fb, w_fc2, (b2, gn)
    )
    gn_send, b2_send, fc2_b, own_y, got2a, got_oth = lax.optimization_barrier(
        (gn_send, b2_send, fc2_b, own_y, got2a, got_oth)
    )
    gn_got = swap_seq(gn_send, 1)
    b2_got = swap_seq(b2_send, 1)
    got2b = swap_seq(fc2_b, 2)
    got_own = swap("batch", own_y, 1)

    gmid, gatt, gatt_send, go_keep, go_send, early, opat, ospe = call(
        branch_back_kernel,
        [SDS((block, width), F32), SDS((chip, cols), BF16), SDS((chip, cols), BF16)]
        + [SDS((cols, width), BF16), SDS((cols, width), BF16), SDS((width, LANES), F32)]
        + [SDS((count, width), BF16), SDS((extra, width), BF16)],
        (sidx, gn_keep, gn_got, middle, pay, pay_c, cot, cot_c, table, w_out, gain2, shift2, a0, a2, gb2)
        + (b2_keep, b2_got, biases[3:4], gain1, shift1, fb_own, fb_oth),
        [pltpu.VMEM((hidden, LANES), F32)],
        flops=8 * chip * width * cols,
        scalars=1,
    )
    gatt_x = swap_seq(gatt_send, 2)
    got_own = after(got_own, gatt_send)
    pairs = (keep_own, got_own, keep_oth, got_oth)

    def head_grads(first, heads, lse):
        return attend_back(first, heads, qa, ka, va, lse, gatt, gatt_x)

    def norm_part(g0, g12):
        return call(
            norm1_kernel,
            [SDS((chip, width), F32), SDS((chip, width), BF16)],
            (g0, g12, w_own),
            flops=2 * whole * width * 5 * LANES,
        )

    def qkv_part(g0, s0, g12, s12, early):
        wide = 5 * LANES
        if per % 8 == 0:
            outs = [SDS((width // (2 * per), per, wide), BF16)] * 2
        else:
            outs = [SDS((width // 2, wide), BF16)] * 2
        out = call(
            qkv_grad_kernel,
            outs,
            (sidx, bidx, normed, g0, g12, s0, s12, w_own, early),
            [pltpu.VMEM((width, LANES), F32), pltpu.VMEM((width, wide), F32)],
            flops=2 * whole * width * wide,
            scalars=2,
        )
        return out if per % 8 == 0 else by_batch_bit(jnp.concatenate(out, axis=0), per)

    rest = (sidx, bidx, per, block, chip, hidden, cols, count, extra, width)
    reduce_all = reduce_eight if nb == 8 else reduce_any
    out_fc2, out_out, out_fc1, out_qkv, vec, gpat, gspe = reduce_all(
        rest, pairs, (fc2_keep, got2a, got2b), (go_keep, go_send), lse, gatt_x, early,
        head_grads, norm_part, qkv_part, pay, gmid, gain1,
    )
    grad_gains = jnp.stack([vec[:, 0], vec[:, 4]])
    grad_shifts = jnp.stack([vec[:, 1], vec[:, 5]])
    grad_biases = jnp.stack([vec[:, 2], vec[:, 3], vec[:, 7], vec[:, 6]])
    return (
        opat[None],
        ospe[None],
        gpat[None],
        gspe[None],
        grad_gains,
        grad_shifts,
        out_qkv,
        grad_biases,
        out_out,
        out_fc1,
        vec[:, 8:12].reshape(-1),
        out_fc2,
    )


def reduce_eight(
    rest, pairs, twos, outs, lse, gatt_x, early, head_grads, norm_part, qkv_part, pay, gmid, gain1
):
    sidx, bidx, per, block, chip, hidden, cols, count, extra, width = rest
    fc2_keep, got2a, got2b = twos
    go_keep, go_send = outs
    wide = 5 * LANES
    deep = hidden // 8
    (send_b,) = call(stage1_kernel, [SDS((8, per, 2 * hidden), BF16)], (sidx,) + pairs, scalars=1)
    go_send, send_b, lse, got2b = lax.optimization_barrier((go_send, send_b, after(lse, gatt_x), got2b))
    got_b = swap_seq(send_b, 2)
    got_o = swap_seq(go_send, 2)
    g0, s0 = head_grads(0, 1, lse)
    g0, got_b, got_o = lax.optimization_barrier((g0, got_b, got_o))

    fc2_keep = fc2_keep.reshape(8, deep, width)
    got2a = got2a.reshape(4, deep, width)
    got2b = got2b.reshape(4, deep, width)
    go_keep = go_keep.reshape(8, per, width)
    got_o = got_o.reshape(8, per, width)
    quarter = SDS((2, per, 2 * hidden), BF16)
    send_a, zb1, zb2, zb3, keep_b = call(
        stage2_kernel,
        [SDS((4, deep + per, width), BF16), quarter, quarter, quarter, SDS(quarter.shape, F32)],
        (sidx, bidx) + pairs + (got_b, fc2_keep, got2a, got2b, go_keep, got_o),
        scalars=2,
    )
    send_a, zb, lse = lax.optimization_barrier((send_a, (zb1, zb2, zb3), after(lse, g0)))
    got_a = swap("batch", send_a, 1)
    got_zb = swap_four(zb, 1)
    g12, s12 = head_grads(1, 2, lse)
    g12, got_a, got_zb = lax.optimization_barrier((g12, got_a, got_zb))

    gn1_keep, gn1_send = norm_part(g0, g12)
    gn1_c = swap_seq(gn1_send, 1)
    got2 = jnp.concatenate([got2a, got2b], axis=0)
    quarter = SDS((deep + per, width), BF16)
    za1, za2, za3, keep_a, swap_send, swap_keep, xsend = call(
        stage3_kernel,
        [quarter, quarter, quarter, SDS(quarter.shape, F32)]
        + [SDS((per, 2 * hidden), BF16), SDS((per, 2 * hidden), F32), SDS((block, width), BF16)],
        (sidx, bidx, fc2_keep, got2, go_keep, got_o, got_a, keep_b, *got_zb, gn1_keep, gn1_c),
        scalars=2,
    )
    xsend, za, swap_send, early = lax.optimization_barrier((xsend, (za1, za2, za3), swap_send, early))
    gn1_x = swap_seq(xsend, 2)
    got_za = swap_four(za, 1)
    swap_got = swap_seq(swap_send, 1)
    q_send, q_keep = qkv_part(g0, s0, g12, s12, early)
    q_send, gn1_x, got_za, swap_got = lax.optimization_barrier((q_send, gn1_x, got_za, swap_got))
    got_q = swap("batch", q_send, 1)
    gpat, gspe, out_fc2, out_out, out_fc1 = call(
        final_kernel,
        [SDS((count, width), F32), SDS((extra, width), F32), SDS((deep, width), F32)]
        + [SDS((per, width), F32), SDS((per, 4 * hidden), F32)],
        (sidx, gn1_keep, gn1_c, gn1_x, pay, gmid, gain1, keep_a, *got_za, swap_keep, swap_got),
        scalars=1,
    )
    got_q = after(got_q, gpat)
    quarter = SDS((4, per, wide), BF16)
    z1, z2, z3, kept = call(
        quarter_kernel, [quarter, quarter, quarter, SDS(quarter.shape, F32)], (bidx, q_keep, got_q), scalars=1
    )
    got_z = swap_four((z1, z2, z3), 1)
    row = SDS((per, wide), BF16)
    s1, s2, s3, own = call(
        owner_kernel, [row, row, row, SDS(row.shape, F32)], (sidx, kept, *got_z), scalars=1
    )
    gots = [swap_seq(v, k) for k, v in ((1, s1), (2, s2), (3, s3))]
    out_qkv, vec = call(
        collect_kernel,
        [SDS((per, 3 * width), F32), SDS((per, LANES), F32)],
        (sidx, own, *gots),
        [pltpu.VMEM((4, per, wide), F32)],
        scalars=1,
    )
    return out_fc2, out_out, out_fc1, out_qkv, vec[:, HEAD:], gpat, gspe


def reduce_any(
    rest, pairs, twos, outs, lse, gatt_x, early, head_grads, norm_part, qkv_part, pay, gmid, gain1
):
    sidx, bidx, per, block, chip, hidden, cols, count, extra, width = rest
    s = lax.axis_index("seq")
    nb = lax.axis_size("batch")
    nbits = bits_of("batch")
    low = nbits - 1
    fc2_keep, got2a, got2b = twos
    go_keep, go_send = outs
    keep_own, got_own, keep_oth, got_oth = [
        split_bits(p.reshape(2, 2, nb // 2, per, hidden), 2, low) for p in pairs
    ]
    g0, s0 = head_grads(0, 1, lse)
    g12, s12 = head_grads(1, 2, lse)
    send_own, parts_own = to_send([keep_own, got_own], 0, 1, "seq")
    send_oth, parts_oth = to_send([keep_oth, got_oth], 0, 1, "seq")
    got_b = swap_seq(jnp.concatenate([send_own, send_oth], axis=-1), 2)
    sum_own = sum_rest(parts_own + [got_b[..., hidden:]], 1, 1)
    sum_oth = sum_rest(parts_oth + [got_b[..., :hidden]], 1, 1)
    own_c = s & 1
    other = jnp.concatenate([pick(sum_own, 1 - own_c, 0), pick(sum_oth, 1 - own_c, 0)], axis=-1)
    got = swap_seq(other.astype(BF16), 1).astype(F32)
    rel = jnp.stack([pick(sum_own, own_c, 0), got[:, :hidden], pick(sum_oth, own_c, 0), got[:, hidden:]])
    out_fc1 = jnp.concatenate([pick(rel, s ^ a, 0) for a in range(4)], axis=1)
    got2 = jnp.concatenate([got2a, got2b], axis=0)
    got_o = swap_seq(go_send, 2)
    both = []
    for keep, got in ((fc2_keep, got2), (go_keep, got_o)):
        parts = [split_bits(p.reshape(nb, -1, width), 0, nbits) for p in (keep, got)]
        both.append(sum_rest(parts, 0, 0))
    gn1_keep, gn1_send = norm_part(g0, g12)
    gn1_c = swap_seq(gn1_send, 1)
    gn1_x = swap_seq((gn1_keep[block:] + gn1_c[block:].astype(F32)).astype(BF16), 2)
    gpat, gspe = call(
        norm_only_kernel,
        [SDS((count, width), F32), SDS((extra, width), F32)],
        (gn1_keep, gn1_c, gn1_x, pay, gmid, gain1),
    )
    q_send, q_keep = qkv_part(g0, s0, g12, s12, early)
    wide = 5 * LANES
    parts = [split_bits(p.reshape(4, nb // 2, per, wide), 1, low) for p in (q_keep, swap("batch", q_send, 1))]
    sum_q = sum_rest(parts, 1, 1)
    pieces = [pick(sum_q, s, 0)] + [
        swap_seq(pick(sum_q, s ^ j, 0).astype(BF16), j).astype(F32) for j in (1, 2, 3)
    ]
    rel = jnp.stack([p[:, : 3 * cols] for p in pieces])
    absolute = jnp.stack([pick(rel, s ^ a, 0) for a in range(4)], axis=1)
    out_qkv = absolute.reshape(-1, 4, OWN, 3, HEAD).transpose(0, 3, 1, 2, 4).reshape(-1, 3 * width)
    vec = total([p[:, 3 * cols :] for p in pieces])
    return both[0], both[1], out_fc1, out_qkv, vec, gpat, gspe


def solution(mesh):
    tok = P("batch", "seq", None)
    ids = P("batch", "seq")
    split = P(None, ("seq", "batch"))
    rows = P(("seq", "batch"), None)
    return jax.shard_map(
        body,
        mesh=mesh,
        in_specs=(tok, tok, ids, ids, P("batch", None)) + (P(),) * 8 + (tok, tok),
        out_specs=(tok, tok, tok, tok, split, split, rows, split, rows, rows, P(("seq", "batch")), rows),
        check_vma=False,
    )
```

```python
import functools

import jax
import jax.numpy as jnp
from jax import lax
from jax.experimental import pallas as pl
from jax.experimental.pallas import tpu as pltpu
from jax.sharding import PartitionSpec as P

HEADS = 12
HEAD = 64
PAD = 32
LANES = 128
OWN = 3
FAR = -(2.0**100)
F32 = jnp.float32
BF16 = jnp.bfloat16
SDS = jax.ShapeDtypeStruct


def dot(a, b):
    return jnp.dot(a, b, preferred_element_type=F32)


def dot_t(a, b):
    return lax.dot_general(a, b, (((1,), (1,)), ((), ())), preferred_element_type=F32)


def dot_lt(a, b):
    return lax.dot_general(a, b, (((0,), (0,)), ((), ())), preferred_element_type=F32)


def normalize(v):
    center = v - jnp.mean(v, axis=-1, keepdims=True)
    spread = jnp.mean(center * center, axis=-1, keepdims=True)
    scale = lax.rsqrt(spread + 1e-06)
    return center * scale, scale


def normalize_back(grad_hat, hat, scale):
    mean_g = jnp.mean(grad_hat, axis=-1, keepdims=True)
    mean_gh = jnp.mean(grad_hat * hat, axis=-1, keepdims=True)
    return scale * (grad_hat - mean_g - hat * mean_gh)


def gelu_pair(v):
    half = 0.5 * (1.0 + lax.erf(v * 0.5**0.5))
    slope = half + v * jnp.exp(-0.5 * v * v) * 0.3989422804014327
    return v * half, slope


def lane_of(rows):
    return lax.broadcasted_iota(jnp.int32, (rows, LANES), 1)


def unpack_head(tiles, e):
    tile = tiles[:, (e // 2) * LANES : (e // 2 + 1) * LANES]
    return tile if e % 2 == 0 else pltpu.roll(tile, HEAD, 1)


def pack_pair(low, high):
    return jnp.where(lane_of(low.shape[0]) < HEAD, low, pltpu.roll(high, HEAD, 1))


def vmem():
    return pl.BlockSpec(memory_space=pltpu.VMEM)


def smem():
    return pl.BlockSpec(memory_space=pltpu.SMEM)


def call(kernel, outs, args, scratch=(), flops=0, scalars=0, room=24):
    nbytes = sum(a.size * a.dtype.itemsize for a in args)
    nbytes += sum(o.size * o.dtype.itemsize for o in outs)
    return pl.pallas_call(
        kernel,
        out_shape=outs,
        in_specs=[smem()] * scalars + [vmem()] * (len(args) - scalars),
        out_specs=[vmem()] * len(outs),
        scratch_shapes=list(scratch),
        compiler_params=pltpu.CompilerParams(vmem_limit_bytes=room << 20),
        cost_estimate=pl.CostEstimate(flops=flops, bytes_accessed=nbytes, transcendentals=0),
    )(*args)


def attend_block(h, b, step, qa, ka, va, lse, oacc):
    at = pl.ds(pl.multiple_of(b * step, step), step)
    sc = dot_t(qa[h, at, :], ka[h])
    top = jnp.max(sc, axis=-1, keepdims=True)
    e = jnp.exp(sc - top).astype(BF16)
    o = dot(e, va[h])
    tot = o[:, HEAD : HEAD + 1]
    oacc[h, at, :] = o * (1.0 / tot)
    col = jnp.broadcast_to(top + jnp.log(tot), (step, LANES))
    lse[h, b] = col.T[:8]


def attend_first_kernel(p0, p1, p2, p3, gain, shift, w, bias, qa, ka, va, lse, part, send, normed, oacc):
    rows = p0.shape[0]
    width = gain.shape[1]
    step = 4 * rows // 3
    lane = lane_of(rows)
    for i, p in enumerate((p0, p1, p2, p3)):
        at = pl.ds(i * rows, rows)
        hat, _ = normalize(p[:, :width].astype(F32))
        nrm = (hat * gain[...] + shift[...]).astype(BF16)
        normed[at, :] = nrm
        qkv = dot(nrm, w[...]) + bias[...]
        hot = p[:, width:].astype(F32)
        far = jnp.where((lane >= HEAD) & (lane < HEAD + 8) & (hot == 0.0), FAR, 0.0)
        one = jnp.where(lane == HEAD, 1.0, 0.0)
        for h in range(OWN):
            q = unpack_head(qkv, 3 * h) * HEAD**-0.5
            qa[h, at, :] = jnp.where(lane < HEAD, q, hot).astype(BF16)
            ka[h, at, :] = jnp.where(lane < HEAD, unpack_head(qkv, 3 * h + 1), far).astype(BF16)
            va[h, at, :] = jnp.where(lane < HEAD, unpack_head(qkv, 3 * h + 2), one).astype(BF16)

    def block(i, carry):
        attend_block(i // 2, 1 + i % 2, step, qa, ka, va, lse, oacc)
        return carry

    lax.fori_loop(0, 2 * OWN, block, 0)
    gather_heads(oacc, step, 2 * rows - step, part, 0)
    gather_heads(oacc, 2 * rows, 2 * rows, send, 0)


def gather_heads(oacc, start, size, out, to):
    at, dst = pl.ds(start, size), pl.ds(to, size)
    out[dst, :LANES] = pack_pair(oacc[0, at, :], oacc[1, at, :]).astype(BF16)
    out[dst, LANES:] = oacc[2, at, :HEAD].astype(BF16)


def attend_second_kernel(qa, ka, va, lse_in, part, keep, lse, oacc):
    step = oacc.shape[1]
    lse[...] = lse_in[...]

    def block(h, carry):
        attend_block(h, 0, step, qa, ka, va, lse, oacc)
        return carry

    lax.fori_loop(0, OWN, block, 0)
    gather_heads(oacc, 0, step, keep, 0)
    keep[pl.ds(step, part.shape[0]), :] = part[...]


def keep_column(p0, p1, table, width):
    hot = jnp.concatenate([p0[:, width:], p1[:, width:]], axis=0).astype(F32)
    return jnp.sum(hot * table, axis=-1, keepdims=True)


def middle_kernel(sref, a0, a1, a2, a3, p0, p1, c0, c1, table, w_out, bias, gain, shift, middle, normed2, gb2):
    s = sref[0]
    rows, width = c0.shape
    cols = a0.shape[1]
    acc = jnp.zeros((2 * rows, width), F32) + bias[...]
    for j, a in ((0, a0), (2, a2)):
        w = w_out[pl.ds(pl.multiple_of((s ^ j) * cols, HEAD), cols), :]
        acc = acc + dot(a[...], w)
    for j, a in ((1, a1), (3, a3)):
        w = w_out[pl.ds(pl.multiple_of((s ^ j) * cols, HEAD), cols), :]
        part = dot(a[...], w)
        acc = acc + jnp.concatenate([part[rows:], part[:rows]], axis=0)
    keep_a = keep_column(p0, p1, table[0:1, :], width)
    keep_m = keep_column(p0, p1, table[1:2, :], width)
    tok = jnp.concatenate([p0[:, :width], p1[:, :width]], axis=0).astype(F32)
    mid = tok + keep_a * acc
    middle[...] = mid
    hat, _ = normalize(mid)
    normed2[...] = (hat * gain[...] + shift[...]).astype(BF16)
    gout = jnp.concatenate([c0[...], c1[...]], axis=0).astype(F32)
    gb2[...] = (keep_m * gout).astype(BF16)


def feed_kernel(last, fast, sref, bref, normed2, gb2, fc1, bias, fc2, *refs):
    if last:
        b2_in, gn_in, y_in, g2, y_send, g1_keep, gb, b2_keep, b2_send, gn_keep, gn_send, wide = refs
    else:
        g2a, g2b, y_first, y_second, g1_keep, gb, b2, gn, wide = refs
    tokens = normed2.shape[0]
    half = tokens // 2
    pre = dot(normed2[...], fc1[...]) + bias[...]
    gact = dot_t(gb2[...], fc2[...])
    act, slope = gelu_pair(pre)
    act = act.astype(BF16)
    gh = (gact * slope).astype(BF16)
    grad1 = dot_lt(normed2[...], gh)
    if not fast:
        rows = grad1.shape[0] // 2
        if last:
            y_send[...] = grad1[:rows].astype(BF16)
            g1_keep[...] = grad1[rows:].astype(BF16)
        else:
            y_first[...] = grad1[:rows].astype(BF16)
            g1_keep[...] = grad1[rows:].astype(BF16)
    else:
        x, y = sref[0] >> 1, bref[0] & 1
        wide[...] = grad1
        n, rows = g1_keep.shape[:2]
        n = n // 2
        for m in range(2 * n):
            base = 2 * rows * (((1 - x) if m < n else x) * n + m % n)
            piece = wide[pl.ds(pl.multiple_of(base + (1 - y) * rows, 8), rows), :].astype(BF16)
            if last:
                y_send[n + m] = piece
            elif m < n:
                y_first[m] = piece
            else:
                y_second[m - n] = piece
            g1_keep[m] = wide[pl.ds(pl.multiple_of(base + y * rows, 8), rows), :].astype(BF16)
        if last:
            for m in range(n):
                y_send[m] = y_in[m]
    gb[...] = jnp.sum(gh.astype(F32), axis=0, keepdims=True)
    partn = dot_t(gh, fc1[...])
    part2 = dot(act, fc2[...])
    if last:
        partn = partn + gn_in[...]
        part2 = part2 + b2_in[...]
        b2_keep[...] = part2[:half]
        b2_send[...] = part2[half:].astype(BF16)
        gn_keep[...] = partn
        gn_send[:half] = partn[half:].astype(BF16)
        gn_send[half:] = partn[:half].astype(BF16)
        g2[...] = dot_lt(act, gb2[...]).astype(BF16)
    else:
        b2[...] = part2
        gn[...] = partn
        grad2 = dot_lt(act, gb2[...]).astype(BF16)
        rows = g2a.shape[0]
        g2a[...] = grad2[:rows]
        g2b[...] = grad2[rows:]


def split_rows(value, wide, bit, send, keep):
    if len(send.shape) == 2:
        rows = value.shape[0] // 2
        send[...] = value[:rows].astype(BF16)
        keep[...] = value[rows:].astype(BF16)
        return
    wide[...] = value
    rows = send.shape[1]
    for m in range(send.shape[0]):
        base = 2 * m * rows
        send[m] = wide[pl.ds(pl.multiple_of(base + (1 - bit) * rows, 8), rows), :].astype(BF16)
        keep[m] = wide[pl.ds(pl.multiple_of(base + bit * rows, 8), rows), :].astype(BF16)


def feed(last, fast, per, sidx, bidx, normed2, gb2, fc1, bias, fc2, prev=()):
    tokens, width = normed2.shape
    hidden = fc1.shape[1]
    pairs = width // (2 * per)
    if last:
        outs = [SDS((hidden, width), BF16)]
        send = [SDS((3 * pairs // 2, per, hidden), BF16)]
    else:
        outs = [SDS((hidden // 4, width), BF16), SDS((3 * hidden // 4, width), BF16)]
        send = [SDS((pairs // 2, per, hidden), BF16)] * 2
    keep = SDS((pairs, per, hidden), BF16)
    if not fast:
        keep = SDS((width // 2, hidden), BF16)
        send = [keep] if last else [keep, SDS((8, LANES), BF16)]
    outs += send + [keep, SDS((1, hidden), F32)]
    if last:
        outs += [SDS((tokens // 2, width), F32), SDS((tokens // 2, width), BF16)]
        outs += [SDS((tokens, width), F32), SDS((tokens, width), BF16)]
    else:
        outs += [SDS((tokens, width), F32)] * 2
    return call(
        functools.partial(feed_kernel, last, fast),
        outs,
        (sidx, bidx, normed2, gb2, fc1, bias, fc2) + tuple(prev),
        [pltpu.VMEM((width, hidden), F32)],
        flops=12 * tokens * width * hidden,
        scalars=2,
    )


def by_batch_bit(arr, per):
    arr = arr.reshape(-1, 2, per, arr.shape[-1])
    own = lax.axis_index("batch") & 1
    return [pick(arr, 1 - own, 1), pick(arr, own, 1)]


def middle_back_kernel(
    sref, gn_keep, gn_got, middle, p0, p1, c0, c1, table, w_out, gain, gb2, gmid_own, gbr_out, gatt_send, sums
):
    s = sref[0]
    rows, width = c0.shape
    cols = gatt_send.shape[1]
    hat, scale = normalize(middle[...])
    g = gn_keep[...] + gn_got[...].astype(F32)
    gout = jnp.concatenate([c0[...], c1[...]], axis=0).astype(F32)
    gmid = gout + normalize_back(g * gain[...], hat, scale)
    keep_a = keep_column(p0, p1, table[0:1, :], width)
    gbr = (keep_a * gmid).astype(BF16)
    gbr_out[...] = gbr
    w_oth = w_out[pl.ds(pl.multiple_of((s ^ 2) * cols, HEAD), cols), :]
    gatt_send[...] = dot_t(gbr, w_oth).astype(BF16)
    gmid_own[...] = gmid[:rows]
    own = slice(0, rows)
    lines = [
        jnp.sum(g[own] * hat[own], axis=0, keepdims=True),
        jnp.sum(g[own], axis=0, keepdims=True),
        jnp.sum(gb2[own, :].astype(F32), axis=0, keepdims=True),
        jnp.sum(gbr[own].astype(F32), axis=0, keepdims=True),
        jnp.zeros((4, width), F32),
    ]
    sums[...] = jnp.concatenate(lines, axis=0)


def branch_back_kernel(
    sref, bref, gbr, w_out, a0, a2, middle, p0, table, b2_keep, b2_got, bias, gain1, shift1, sums, fb_own, fb_oth,
    gatt, go_send, go_keep, early, opat, ospe, fcol, wide,
):
    s = sref[0]
    cols = a0.shape[1]
    rows, width = b2_keep.shape
    w_own = w_out[pl.ds(pl.multiple_of(s * cols, HEAD), cols), :]
    gatt[...] = dot_t(gbr[...], w_own).astype(BF16)
    for j, a in enumerate((a0, a2)):
        split_rows(dot_lt(a[...], gbr[...]), wide, bref[0] & 1, go_send.at[j], go_keep.at[j])
    hot = p0[:, width:].astype(F32)
    keep_m = jnp.sum(hot * table[1:2, :], axis=-1, keepdims=True)
    res = middle[:rows, :] + keep_m * (b2_keep[...] + b2_got[...].astype(F32) + bias[...])
    res = res.astype(BF16)
    opat[...] = res[: opat.shape[0]]
    ospe[...] = res[opat.shape[0] : opat.shape[0] + ospe.shape[0]]
    blank = functools.partial(jnp.zeros, dtype=F32)
    lines = [gain1[...], shift1[...], blank((HEAD + 2, width)), sums[:4, :], blank((LANES - HEAD - 8, width))]
    early[...] = jnp.concatenate(lines, axis=0).T
    lane = lane_of(cols)
    for j, ref in ((0, fb_own), (2, fb_oth)):
        fcol[...] = jnp.broadcast_to(ref[...], (LANES, ref.shape[1])).T
        at = pl.ds(pl.multiple_of((s ^ j) * cols, HEAD), cols)
        val = early[at, :]
        for k in range(4):
            val = jnp.where(lane == HEAD + 8 + k, fcol[pl.ds(k, cols, stride=4), :], val)
        early[at, :] = val


def attend_back_kernel(first, heads, qa, ka, va, lse, ga, gx, out, sums, goa, dq, dk, dv):
    whole = qa.shape[1]
    half = ga.shape[0]
    lane = lane_of(half)
    for i in range(heads):
        h = first + i
        for ref, start in ((ga, 0), (gx, half)):
            if h < 2:
                t = ref[:, :LANES].astype(F32)
                t = jnp.where(lane < HEAD, t if h == 0 else pltpu.roll(t, HEAD, 1), 0.0)
            else:
                t = ref[:, LANES:].astype(F32)
                t = jnp.concatenate([t, jnp.zeros_like(t)], axis=1)
            goa[i, pl.ds(start, half), :] = t.astype(BF16)
    step = whole // 3

    def block(n, carry):
        i, b = n // 3, n % 3
        h = first + i
        at = pl.ds(pl.multiple_of(b * step, step), step)
        q, go = qa[h, at, :], goa[i, at, :]
        prob = jnp.exp(dot_t(ka[h], q) - lse[h, b][0:1, :])
        gp = dot_t(va[h], go)
        inner = jnp.sum(gp * prob, axis=0, keepdims=True)
        gs = (prob * (gp - inner)).astype(BF16)
        pv = dot(prob.astype(BF16), go)
        pk = dot(gs, q)
        dq[i, at, :] = dot_lt(gs, ka[h])

        @pl.when(b == 0)
        def _():
            dv[i] = pv
            dk[i] = pk

        @pl.when(b > 0)
        def _():
            dv[i] += pv
            dk[i] += pk

        return carry

    lax.fori_loop(0, 3 * heads, block, 0)
    for i in range(heads):
        out[i, :, :LANES] = pack_pair(dq[i] * HEAD**-0.5, dk[i]).astype(BF16)
        out[i, :, LANES:] = dv[i, :, :HEAD].astype(BF16)
        sums[i] = jnp.sum(out[i].astype(F32), axis=0, keepdims=True)


def attend_back(first, heads, qa, ka, va, lse, ga, gx):
    whole = qa.shape[1]
    return call(
        functools.partial(attend_back_kernel, first, heads),
        [SDS((heads, whole, 3 * HEAD), BF16), SDS((heads, 1, 3 * HEAD), F32)],
        (qa, ka, va, lse, ga, gx),
        [pltpu.VMEM((heads, whole, LANES), BF16)] + [pltpu.VMEM((heads, whole, LANES), F32)] * 3,
        flops=10 * heads * whole * whole * LANES,
    )


def norm1_kernel(g0, g12, w, keep, send):
    rows = keep.shape[0] // 2
    cols = g0.shape[2]
    for i in range(4):
        at = pl.ds(i * rows, rows)
        part = dot_t(g0[0, at, :], w[:, :cols])
        part = part + dot_t(g12[0, at, :], w[:, cols : 2 * cols])
        part = part + dot_t(g12[1, at, :], w[:, 2 * cols : 3 * cols])
        to = pl.ds((i // 2) * rows, rows)
        if i % 2 == 0:
            keep[to, :] = part
        else:
            send[to, :] = part.astype(BF16)


def qkv_grad_kernel(sref, bref, normed, g0, g12, s0, s12, w, early, send, keep, tile, wide):
    width, cols = w.shape[0], g0.shape[2]
    every = (g0[0], g12[0], g12[1])
    parts = [dot_lt(normed[...], g) for g in every]
    g = jnp.concatenate(parts, axis=1)
    w32 = w[:, : 3 * cols].astype(F32)
    rows = jnp.concatenate([s0[0], s12[0], s12[1]], axis=1)
    both = jnp.sum(g * w32, axis=-1, keepdims=True)
    gshift = jnp.sum(w32 * rows, axis=-1, keepdims=True)
    ggain = (both - early[:, 1:2] * gshift) / early[:, 0:1]
    lane = lane_of(width)
    tail = jnp.concatenate([g[:, 4 * LANES :], jnp.zeros((width, LANES - HEAD), F32)], axis=1)
    tail = jnp.where(lane == HEAD, ggain, tail)
    tail = jnp.where(lane == HEAD + 1, gshift, tail)
    tile[...] = jnp.where(lane >= HEAD + 4, early[...], tail)
    ones = jnp.ones((g0.shape[1], LANES), BF16)
    at = pl.multiple_of(sref[0] * cols, HEAD)
    for h, part in enumerate(every):
        col = dot_lt(part, ones)
        here = pl.ds(at + h * HEAD, HEAD)
        lanes = lane_of(HEAD)
        row = tile[here, :]
        row = jnp.where(lanes == HEAD + 2, col[:HEAD], row)
        tile[here, :] = jnp.where(lanes == HEAD + 3, col[2 * HEAD :], row)
    split_rows(jnp.concatenate([g[:, : 4 * LANES], tile[...]], axis=1), wide, bref[0] & 1, send, keep)


def wide_sum(*parts):
    return sum(p.astype(F32) for p in parts[1:]) + parts[0].astype(F32)


def stage1_kernel(
    bref, keep_own, keep_oth, y1, y2, fc2, got2a, got2b, out, y3, msg_x, msg_a, part_b, part_o, part_a
):
    y = bref[0] & 1
    n = keep_own.shape[0] // 2
    for i in range(n):
        msg_x[2 * i] = wide_sum(keep_own[i], y2[n + i]).astype(BF16)
        msg_x[2 * i + 1] = wide_sum(keep_oth[i], y1[i]).astype(BF16)
        part_b[2 * i] = wide_sum(keep_own[n + i], y2[2 * n + i])
        part_b[2 * i + 1] = wide_sum(keep_oth[n + i], y2[i])
    for j in range(4):
        msg_x[2 * n + j] = wide_sum(out[1, j], y3[1, j]).astype(BF16)
        part_o[j] = wide_sum(out[0, j], y3[0, j])
        for bit, ref in ((1 - y, msg_a), (y, part_a)):
            got = got2a[bit] if j == 0 else got2b[2 * j - 2 + bit]
            ref[j] = wide_sum(fc2[2 * j + bit], got).astype(ref.dtype)


def stage2_kernel(bref, part_b, part_o, part_a, got_x, got_a, z1, z2, z3, kept):
    q = bref[0] >> 1
    per = part_o.shape[1]
    n = part_b.shape[0]
    deep = part_a.shape[1]
    for k, ref in enumerate((kept, z1, z2, z3)):
        j = q ^ k
        for c in range(2):
            i = 2 * (c * 4 + j)
            for half in range(2):
                at = pl.ds((2 * c + half) * per, per)
                ref[at, :] = wide_sum(part_b[i + half], got_x[i + 1 - half]).astype(ref.dtype)
        ref[pl.ds(4 * per, deep), :] = wide_sum(part_a[j], got_a[j]).astype(ref.dtype)
        ref[pl.ds(4 * per + deep, per), :] = wide_sum(part_o[j], got_x[n + j]).astype(ref.dtype)


def shift_kernel(keep, got, send):
    rows = send.shape[0]
    send[...] = wide_sum(keep[rows:, :], got[rows:, :]).astype(BF16)


def quarter_kernel(bref, keep, got, z1, z2, z3, kept):
    q = bref[0] >> 1
    for r in range(4):
        for k, ref in enumerate((kept, z1, z2, z3)):
            m = r * 4 + (q ^ k)
            ref[r] = wide_sum(keep[m], got[m]).astype(ref.dtype)


def sums_kernel(sref, kept, z1, z2, z3, swap_send, swap_keep, fc2, out):
    c = sref[0] & 1
    rows = swap_send.shape[0]
    deep = fc2.shape[0]
    for pos, ref in ((1 - c, swap_send), (c, swap_keep)):
        at = pl.ds(pl.multiple_of(pos * rows, 8), rows)
        ref[...] = wide_sum(kept[at, :], z1[at, :], z2[at, :], z3[at, :]).astype(ref.dtype)
    for lo, ref in ((2 * rows, fc2), (2 * rows + deep, out)):
        at = pl.ds(lo, ref.shape[0])
        ref[...] = wide_sum(kept[at, :], z1[at, :], z2[at, :], z3[at, :])


def owner_kernel(sref, kept, z1, z2, z3, s1, s2, s3, own):
    s = sref[0]
    for k, ref in enumerate((own, s1, s2, s3)):
        m = s ^ k
        ref[...] = wide_sum(kept[m], z1[m], z2[m], z3[m]).astype(ref.dtype)


def final_kernel(k0, c0, x0, p0, gmid, gain, gpat, gspe):
    rows, width = x0.shape
    count = gpat.shape[0]
    hat, scale = normalize(p0[:, :width].astype(F32))
    g = wide_sum(k0[:rows], c0[:rows], x0[...])
    res = gmid[...] + normalize_back(g * gain[...], hat, scale)
    gpat[...] = res[:count]
    gspe[...] = res[count : count + gspe.shape[0]]


def collect_kernel(sref, own, g1, g2, g3, swap_keep, swap_got, out, vec, fc1, every):
    s = sref[0]
    per, hidden = swap_keep.shape[0] // 2, swap_keep.shape[1]
    for j, value in ((0, swap_keep[:per]), (2, swap_keep[per:]), (1, swap_got[:per]), (3, swap_got[per:])):
        fc1[:, pl.ds(pl.multiple_of((s ^ j) * hidden, LANES), hidden)] = value.astype(F32)
    for k, ref in enumerate((own, g1, g2, g3)):
        every[k] = ref[...].astype(F32)
    pieces = [every[s ^ a] for a in range(4)]

    def part(u):
        j, a, h = u // 12, (u // 3) % 4, u % 3
        e = 3 * h + j
        return pieces[a][:, (e // 2) * LANES : (e // 2 + 1) * LANES], e % 2

    lane = lane_of(out.shape[0])
    for t in range(out.shape[1] // LANES):
        (low, lo), (high, hi) = part(2 * t), part(2 * t + 1)
        low = pltpu.roll(low, HEAD, 1) if lo else low
        high = high if hi else pltpu.roll(high, HEAD, 1)
        out[:, t * LANES : (t + 1) * LANES] = jnp.where(lane < HEAD, low, high)
    tail = 4 * LANES
    vec[...] = wide_sum(*[every[k, :, tail:] for k in range(4)])


def pick(arr, index, axis):
    return lax.dynamic_index_in_dim(arr, index, axis, keepdims=False)


def total(parts):
    out = parts[0].astype(F32)
    for part in parts[1:]:
        out = out + part.astype(F32)
    return out


def swap(kind, v, mask):
    return lax.ppermute(v, kind, [(i, i ^ mask) for i in range(lax.axis_size(kind))])


def swap_seq(v, mask):
    return swap("seq", v, mask)


def after(value, *first):
    return lax.optimization_barrier((value, first))[0]


def bits_of(kind):
    return lax.axis_size(kind).bit_length() - 1


def split_bits(arr, axis, count):
    shape = arr.shape
    return arr.reshape(shape[:axis] + (2,) * count + shape[axis + 1 :])


def to_send(parts, axis, bit, kind):
    own = (lax.axis_index(kind) >> bit) & 1
    send = total([pick(p, 1 - own, axis) for p in parts]).astype(BF16)
    return send, [pick(p, own, axis) for p in parts]


def send_four(parts, axis, low):
    own = (lax.axis_index("batch") >> low) & 3

    def quarter(p, k):
        return pick(pick(p, k >> 1, axis), k & 1, axis)

    sends = [total([quarter(p, own ^ k) for p in parts]).astype(BF16) for k in (1, 2, 3)]
    return sends, [quarter(p, own) for p in parts]


def swap_four(sends, low):
    return [swap("batch", v, k << low) for k, v in zip((1, 2, 3), sends)]


def sum_rest(parts, axis, low):
    top = bits_of("batch")
    while low < top:
        if low + 1 < top:
            sends, kept = send_four(parts, axis + top - low - 2, low)
            parts, low = kept + swap_four(sends, low), low + 2
        else:
            send, kept = to_send(parts, axis, low, "batch")
            parts, low = kept + [swap("batch", send, 1 << low)], low + 1
    return total(parts)


def body(
    patches,
    specials,
    segment_ids,
    special_order,
    keep_mask,
    norm_gains,
    norm_shifts,
    w_qkv,
    biases,
    w_out,
    w_fc1,
    fc1_bias,
    w_fc2,
    cot_patches,
    cot_specials,
):
    count, width = patches.shape[1:]
    extra = specials.shape[1]
    images = keep_mask.shape[1] // 2
    block = count + PAD
    chip = 2 * block
    whole = 4 * block
    cols = OWN * HEAD
    hidden = w_fc1.shape[1] // 4
    s = lax.axis_index("seq")
    sidx = s.astype(jnp.int32).reshape(1)
    bidx = lax.axis_index("batch").astype(jnp.int32).reshape(1)
    nb = lax.axis_size("batch")
    nbits = bits_of("batch")

    zeros = jnp.zeros((PAD - extra, width), BF16)
    mine = jnp.concatenate([patches[0], specials[0], zeros], axis=0)
    segs = jnp.concatenate(
        [segment_ids[0], special_order[0] // 2, jnp.full((PAD - extra,), -1, jnp.int32)]
    )
    marks = jnp.arange(LANES, dtype=jnp.int32) - HEAD
    hot = ((segs[:, None] == marks) & (marks >= 0)).astype(BF16)
    pay = jnp.concatenate([mine, hot], axis=1)
    cot = jnp.concatenate([cot_patches[0], cot_specials[0], zeros], axis=0)
    pay_c = swap_seq(pay, 1)
    pay_x = swap_seq(pay, 2)
    cot_c = swap_seq(cot, 1)
    keep = keep_mask[0].astype(F32).reshape(2, images) / 0.75
    table = jnp.pad(keep, ((0, 6), (HEAD, LANES - HEAD - images)))

    order = [(h, j) for h in range(OWN) for j in range(3)]
    w_own = [lax.dynamic_slice(w_qkv, (0, j * width + s * cols + h * HEAD), (width, HEAD)) for h, j in order]
    w_own = jnp.concatenate(w_own + [jnp.zeros((width, HEAD), BF16)], axis=1)
    sides = {0: biases[0], 1: jnp.zeros((width,), F32), 2: biases[1]}
    bias_own = [lax.dynamic_slice(sides[j], (s * cols + h * HEAD,), (HEAD,)) for h, j in order]
    bias_own = jnp.concatenate(bias_own + [jnp.zeros((HEAD,), F32)])[None]
    w1 = [lax.dynamic_slice(w_fc1, (0, (s ^ j) * hidden), (width, hidden)) for j in (2, 0)]
    w2 = [lax.dynamic_slice(w_fc2, ((s ^ j) * hidden, 0), (hidden, width)) for j in (2, 0)]
    fb = [lax.dynamic_slice(fc1_bias, ((s ^ j) * hidden,), (hidden,))[None] for j in (2, 0)]
    pay_x, w_own, bias_own, table, w1, w2, fb = lax.optimization_barrier(
        (pay_x, w_own, bias_own, table, w1, w2, fb)
    )
    pay_d = swap_seq(pay_x, 1)
    gain1, gain2 = norm_gains[0:1], norm_gains[1:2]
    shift1, shift2 = norm_shifts[0:1], norm_shifts[1:2]

    headed = SDS((OWN, whole, LANES), BF16)
    tops = SDS((OWN, 3, 8, whole // 3), F32)
    step = whole // 3
    qa, ka, va, lse, part, att_send, normed = call(
        attend_first_kernel,
        [headed] * 3
        + [tops, SDS((chip - step, cols), BF16), SDS((chip, cols), BF16), SDS((whole, width), BF16)],
        (pay, pay_c, pay_x, pay_d, gain1, shift1, w_own, bias_own),
        [pltpu.VMEM((OWN, whole, LANES), F32)],
        flops=2 * whole * width * 3 * cols + 3 * OWN * whole * whole * LANES,
    )
    a2 = swap_seq(att_send, 2)
    a0, lse = call(
        attend_second_kernel,
        [SDS((chip, cols), BF16), tops],
        (qa, ka, va, lse, part),
        [pltpu.VMEM((OWN, step, LANES), F32)],
        flops=OWN * whole * whole * LANES,
    )
    a1 = swap_seq(a0, 1)
    a3 = swap_seq(a2, 1)

    middle, normed2, gb2 = call(
        middle_kernel,
        [SDS((chip, width), F32), SDS((chip, width), BF16), SDS((chip, width), BF16)],
        (sidx, a0, a1, a2, a3, pay, pay_c, cot, cot_c, table, w_out, biases[2:3], gain2, shift2),
        flops=2 * chip * width * width,
        scalars=1,
    )
    per = width // (4 * nb)
    fast = nb == 8
    fc2_a, fc2_b, y1, y_rest, keep_oth, fb_oth, b2, gn = feed(
        False, fast, per, sidx, bidx, normed2, gb2, w1[0], fb[0], w2[0]
    )
    got2a = swap_seq(fc2_a, 2)
    if fast:
        got_y1 = swap("batch", y1, 1)
        ahead = (got2a, got_y1)
    else:
        y1, keep_oth = by_batch_bit(jnp.concatenate([y1, keep_oth], axis=0), per)
        got_y1 = swap("batch", y1, 1)
        ahead = (got2a, got_y1)
    fc2_keep, y2, keep_own, fb_own, b2_keep, b2_send, gn_keep, gn_send = feed(
        True, fast, per, sidx, bidx, normed2, gb2, w1[1], fb[1], w2[1], (b2, gn, y_rest)
    )
    if not fast:
        y2, keep_own = by_batch_bit(jnp.concatenate([y2, keep_own], axis=0), per)
    gn_send, b2_send, fc2_b, y2, (got2a, got_y1) = lax.optimization_barrier((gn_send, b2_send, fc2_b, y2, ahead))
    gn_got = swap_seq(gn_send, 1)
    b2_got = swap_seq(b2_send, 1)
    got2b = swap_seq(fc2_b, 2)
    got_y2 = swap("batch", y2, 1)

    gmid, gbr, gatt_send, line_sums = call(
        middle_back_kernel,
        [SDS((block, width), F32), SDS((chip, width), BF16), SDS((chip, cols), BF16), SDS((8, width), F32)],
        (sidx, gn_keep, gn_got, middle, pay, pay_c, cot, cot_c, table, w_out, gain2, gb2),
        flops=2 * chip * width * cols,
        scalars=1,
    )
    gatt_x = swap_seq(gatt_send, 2)
    if fast:
        split = SDS((2, cols // (2 * per), per, width), BF16)
    else:
        split = SDS((2, cols // 2, width), BF16)
    gatt, go_send, go_keep, early, opat, ospe = call(
        branch_back_kernel,
        [SDS((chip, cols), BF16), split, split, SDS((width, LANES), F32)]
        + [SDS((count, width), BF16), SDS((extra, width), BF16)],
        (sidx, bidx, gbr, w_out, a0, a2, middle, pay, table, b2_keep, b2_got, biases[3:4], gain1, shift1)
        + (line_sums, fb_own, fb_oth),
        [pltpu.VMEM((hidden, LANES), F32), pltpu.VMEM((cols, width), F32)],
        flops=6 * chip * width * cols,
        scalars=2,
    )
    if not fast:
        halves = [by_batch_bit(jnp.concatenate([go_send[j], go_keep[j]], axis=0), per) for j in range(2)]
        go_send, go_keep = [jnp.stack([halves[j][k] for j in range(2)]) for k in range(2)]
    got_o = swap("batch", go_send, 1)
    got_y2, got2b = after((got_y2, got2b), gatt_send)
    gatt_x = after(gatt_x, go_send)
    pairs = (keep_own, keep_oth, got_y1, got_y2)

    def head_grads(first, heads, lse):
        return attend_back(first, heads, qa, ka, va, lse, gatt, gatt_x)

    def norm_part(g0, g12):
        return call(
            norm1_kernel,
            [SDS((chip, width), F32), SDS((chip, width), BF16)],
            (g0, g12, w_own),
            flops=2 * whole * width * 5 * LANES,
        )

    def qkv_part(g0, s0, g12, s12, early):
        wide = 5 * LANES
        if fast:
            outs = [SDS((width // (2 * per), per, wide), BF16)] * 2
        else:
            outs = [SDS((width // 2, wide), BF16)] * 2
        out = call(
            qkv_grad_kernel,
            outs,
            (sidx, bidx, normed, g0, g12, s0, s12, w_own, early),
            [pltpu.VMEM((width, LANES), F32), pltpu.VMEM((width, wide), F32)],
            flops=2 * whole * width * wide,
            scalars=2,
        )
        return out if fast else by_batch_bit(jnp.concatenate(out, axis=0), per)

    rest = (sidx, bidx, per, block, chip, hidden, cols, count, extra, width)
    reduce_all = reduce_eight if fast else reduce_any
    out_fc2, out_out, out_fc1, out_qkv, vec, gpat, gspe = reduce_all(
        rest, pairs, (fc2_keep, got2a, got2b), (go_keep, got_o), lse, gatt_x, early,
        head_grads, norm_part, qkv_part, pay, gmid, gain1,
    )
    grad_gains = jnp.stack([vec[:, 0], vec[:, 4]])
    grad_shifts = jnp.stack([vec[:, 1], vec[:, 5]])
    grad_biases = jnp.stack([vec[:, 2], vec[:, 3], vec[:, 7], vec[:, 6]])
    return (
        opat[None],
        ospe[None],
        gpat[None],
        gspe[None],
        grad_gains,
        grad_shifts,
        out_qkv,
        grad_biases,
        out_out,
        out_fc1,
        vec[:, 8:12].reshape(-1),
        out_fc2,
    )


def reduce_eight(
    rest, pairs, twos, outs, lse, gatt_x, early, head_grads, norm_part, qkv_part, pay, gmid, gain1
):
    sidx, bidx, per, block, chip, hidden, cols, count, extra, width = rest
    fc2_keep, got2a, got2b = twos
    go_keep, got_o = outs
    wide = 5 * LANES
    deep = hidden // 8
    fc2_keep = fc2_keep.reshape(8, deep, width)
    got2a = got2a.reshape(2, deep, width)
    got2b = got2b.reshape(6, deep, width)
    g0, s0 = head_grads(0, 1, after(lse, gatt_x))
    g0, got_y2, got2b, got_o = lax.optimization_barrier((g0, pairs[3], got2b, got_o))
    keep_own, keep_oth, got_y1 = pairs[:3]
    msg_x, msg_a, part_b, part_o, part_a = call(
        stage1_kernel,
        [SDS((20, per, width), BF16), SDS((4, deep, width), BF16)]
        + [SDS((16, per, width), F32), SDS((4, per, width), F32), SDS((4, deep, width), F32)],
        (bidx, keep_own, keep_oth, got_y1, got_y2, fc2_keep, got2a, got2b, go_keep, got_o),
        scalars=1,
    )
    msg_x, msg_a, lse = lax.optimization_barrier((msg_x, msg_a, after(lse, g0)))
    got_x = swap_seq(msg_x, 2)
    got_a = swap("batch", msg_a, 1)
    g12, s12 = head_grads(1, 2, lse)
    g12, got_x, got_a = lax.optimization_barrier((g12, got_x, got_a))

    gn1_keep, gn1_send = norm_part(g0, g12)
    gn1_c = swap_seq(gn1_send, 1)
    q_send, q_keep = qkv_part(g0, s0, g12, s12, after(early, gn1_send))
    q_send, gn1_c, got_x, got_a = lax.optimization_barrier((q_send, gn1_c, got_x, got_a))
    got_q = swap("batch", q_send, 1)
    (xsend,) = call(shift_kernel, [SDS((block, width), BF16)], (gn1_keep, gn1_c))
    gn1_x = swap_seq(xsend, 2)
    quarter = SDS((5 * per + deep, width), BF16)
    z1, z2, z3, kept = call(
        stage2_kernel,
        [quarter, quarter, quarter, SDS(quarter.shape, F32)],
        (bidx, part_b, part_o, part_a, got_x, got_a),
        scalars=1,
    )
    got_z = swap_four((z1, z2, z3), 1)
    gpat, gspe = call(
        final_kernel,
        [SDS((count, width), F32), SDS((extra, width), F32)],
        (gn1_keep, gn1_c, after(gn1_x, z1), pay, gmid, gain1),
    )
    got_q = after(got_q, gpat)
    quarter = SDS((4, per, wide), BF16)
    q1, q2, q3, q_kept = call(
        quarter_kernel, [quarter, quarter, quarter, SDS(quarter.shape, F32)], (bidx, q_keep, got_q), scalars=1
    )
    (q1, q2, q3), got_z = lax.optimization_barrier(((q1, q2, q3), got_z))
    got_qz = swap_four((q1, q2, q3), 1)
    swap_send, swap_keep, out_fc2, out_out = call(
        sums_kernel,
        [SDS((2 * per, width), BF16), SDS((2 * per, width), F32), SDS((deep, width), F32), SDS((per, width), F32)],
        (sidx, kept, *got_z),
        scalars=1,
    )
    swap_got = swap_seq(swap_send, 1)
    row = SDS((per, wide), BF16)
    s1, s2, s3, own = call(
        owner_kernel, [row, row, row, SDS(row.shape, F32)], (sidx, q_kept, *after(got_qz, out_out)), scalars=1
    )
    gots = [swap_seq(v, k) for k, v in ((1, s1), (2, s2), (3, s3))]
    out_qkv, vec, out_fc1 = call(
        collect_kernel,
        [SDS((per, 3 * width), F32), SDS((per, LANES), F32), SDS((per, 4 * hidden), F32)],
        (sidx, own, *gots, swap_keep, swap_got),
        [pltpu.VMEM((4, per, wide), F32)],
        scalars=1,
    )
    return out_fc2, out_out, out_fc1, out_qkv, vec[:, HEAD:], gpat, gspe


def reduce_any(
    rest, pairs, twos, outs, lse, gatt_x, early, head_grads, norm_part, qkv_part, pay, gmid, gain1
):
    sidx, bidx, per, block, chip, hidden, cols, count, extra, width = rest
    s = lax.axis_index("seq")
    nb = lax.axis_size("batch")
    nbits = bits_of("batch")
    low = nbits - 1
    fc2_keep, got2a, got2b = twos
    go_keep, got_o = outs
    keep_own, keep_oth, got_oth, got_own = [
        split_bits(p.reshape(2, 2, nb // 2, per, hidden), 2, low) for p in pairs
    ]
    g0, s0 = head_grads(0, 1, lse)
    g12, s12 = head_grads(1, 2, lse)
    send_own, parts_own = to_send([keep_own, got_own], 0, 1, "seq")
    send_oth, parts_oth = to_send([keep_oth, got_oth], 0, 1, "seq")
    got_b = swap_seq(jnp.concatenate([send_own, send_oth], axis=-1), 2)
    sum_own = sum_rest(parts_own + [got_b[..., hidden:]], 1, 1)
    sum_oth = sum_rest(parts_oth + [got_b[..., :hidden]], 1, 1)
    own_c = s & 1
    other = jnp.concatenate([pick(sum_own, 1 - own_c, 0), pick(sum_oth, 1 - own_c, 0)], axis=-1)
    got = swap_seq(other.astype(BF16), 1).astype(F32)
    rel = jnp.stack([pick(sum_own, own_c, 0), got[:, :hidden], pick(sum_oth, own_c, 0), got[:, hidden:]])
    out_fc1 = jnp.concatenate([pick(rel, s ^ a, 0) for a in range(4)], axis=1)
    got2 = jnp.concatenate([got2a, got2b], axis=0)
    parts = [split_bits(p.reshape(nb, -1, width), 0, nbits) for p in (fc2_keep, got2)]
    out_fc2 = sum_rest(parts, 0, 0)
    parts = [split_bits(p.reshape(2, nb // 2, per, width), 1, low) for p in (go_keep, got_o)]
    parts = [p[0] for p in parts] + [swap_seq(total([p[1] for p in parts]).astype(BF16), 2)]
    out_out = sum_rest(parts, 0, 1)
    gn1_keep, gn1_send = norm_part(g0, g12)
    gn1_c = swap_seq(gn1_send, 1)
    gn1_x = swap_seq((gn1_keep[block:] + gn1_c[block:].astype(F32)).astype(BF16), 2)
    gpat, gspe = call(
        final_kernel,
        [SDS((count, width), F32), SDS((extra, width), F32)],
        (gn1_keep, gn1_c, gn1_x, pay, gmid, gain1),
    )
    q_send, q_keep = qkv_part(g0, s0, g12, s12, early)
    wide = 5 * LANES
    parts = [split_bits(p.reshape(4, nb // 2, per, wide), 1, low) for p in (q_keep, swap("batch", q_send, 1))]
    sum_q = sum_rest(parts, 1, 1)
    pieces = [pick(sum_q, s, 0)] + [
        swap_seq(pick(sum_q, s ^ j, 0).astype(BF16), j).astype(F32) for j in (1, 2, 3)
    ]
    rel = jnp.stack([p[:, : 3 * cols] for p in pieces])
    absolute = jnp.stack([pick(rel, s ^ a, 0) for a in range(4)], axis=1)
    out_qkv = absolute.reshape(-1, 4, OWN, 3, HEAD).transpose(0, 3, 1, 2, 4).reshape(-1, 3 * width)
    vec = total([p[:, 3 * cols :] for p in pieces])
    return out_fc2, out_out, out_fc1, out_qkv, vec, gpat, gspe


def solution(mesh):
    tok = P("batch", "seq", None)
    ids = P("batch", "seq")
    split = P(None, ("seq", "batch"))
    rows = P(("seq", "batch"), None)
    return jax.shard_map(
        body,
        mesh=mesh,
        in_specs=(tok, tok, ids, ids, P("batch", None)) + (P(),) * 8 + (tok, tok),
        out_specs=(tok, tok, tok, tok, split, split, rows, split, rows, rows, P(("seq", "batch")), rows),
        check_vma=False,
    )
```

```python
import functools

import jax
import jax.numpy as jnp
from jax import lax
from jax.experimental import pallas as pl
from jax.experimental.pallas import tpu as pltpu
from jax.sharding import PartitionSpec as P

HEADS = 12
HEAD = 64
PAD = 32
LANES = 128
OWN = 3
FAR = -(2.0**100)
F32 = jnp.float32
BF16 = jnp.bfloat16
SDS = jax.ShapeDtypeStruct


def dot(a, b):
    return jnp.dot(a, b, preferred_element_type=F32)


def dot_t(a, b):
    return lax.dot_general(a, b, (((1,), (1,)), ((), ())), preferred_element_type=F32)


def dot_lt(a, b):
    return lax.dot_general(a, b, (((0,), (0,)), ((), ())), preferred_element_type=F32)


def normalize(v):
    center = v - jnp.mean(v, axis=-1, keepdims=True)
    spread = jnp.mean(center * center, axis=-1, keepdims=True)
    scale = lax.rsqrt(spread + 1e-06)
    return center * scale, scale


def normalize_back(grad_hat, hat, scale):
    mean_g = jnp.mean(grad_hat, axis=-1, keepdims=True)
    mean_gh = jnp.mean(grad_hat * hat, axis=-1, keepdims=True)
    return scale * (grad_hat - mean_g - hat * mean_gh)


def gelu_pair(v):
    half = 0.5 * (1.0 + lax.erf(v * 0.5**0.5))
    slope = half + v * jnp.exp(-0.5 * v * v) * 0.3989422804014327
    return v * half, slope


def lane_of(rows):
    return lax.broadcasted_iota(jnp.int32, (rows, LANES), 1)


def unpack_head(tiles, e):
    tile = tiles[:, (e // 2) * LANES : (e // 2 + 1) * LANES]
    return tile if e % 2 == 0 else pltpu.roll(tile, HEAD, 1)


def pack_pair(low, high):
    return jnp.where(lane_of(low.shape[0]) < HEAD, low, pltpu.roll(high, HEAD, 1))


def vmem():
    return pl.BlockSpec(memory_space=pltpu.VMEM)


def smem():
    return pl.BlockSpec(memory_space=pltpu.SMEM)


def call(kernel, outs, args, scratch=(), flops=0, scalars=0, room=24):
    nbytes = sum(a.size * a.dtype.itemsize for a in args)
    nbytes += sum(o.size * o.dtype.itemsize for o in outs)
    return pl.pallas_call(
        kernel,
        out_shape=outs,
        in_specs=[smem()] * scalars + [vmem()] * (len(args) - scalars),
        out_specs=[vmem()] * len(outs),
        scratch_shapes=list(scratch),
        compiler_params=pltpu.CompilerParams(vmem_limit_bytes=room << 20),
        cost_estimate=pl.CostEstimate(flops=flops, bytes_accessed=nbytes, transcendentals=0),
    )(*args)


def attend_block(h, b, step, qa, ka, va, lse, oacc):
    at = pl.ds(pl.multiple_of(b * step, step), step)
    sc = dot_t(qa[h, at, :], ka[h])
    top = jnp.max(sc, axis=-1, keepdims=True)
    e = jnp.exp(sc - top).astype(BF16)
    o = dot(e, va[h])
    tot = o[:, HEAD : HEAD + 1]
    oacc[h, at, :] = o * (1.0 / tot)
    col = jnp.broadcast_to(top + jnp.log(tot), (step, LANES))
    lse[h, b] = col.T[:8]


def attend_first_kernel(p0, p1, p2, p3, gain, shift, w, bias, qa, ka, va, lse, part, send, normed, oacc):
    rows = p0.shape[0]
    width = gain.shape[1]
    step = 4 * rows // 3
    lane = lane_of(rows)
    for i, p in enumerate((p0, p1, p2, p3)):
        at = pl.ds(i * rows, rows)
        hat, _ = normalize(p[:, :width].astype(F32))
        nrm = (hat * gain[...] + shift[...]).astype(BF16)
        normed[at, :] = nrm
        qkv = dot(nrm, w[...]) + bias[...]
        hot = p[:, width:].astype(F32)
        far = jnp.where((lane >= HEAD) & (lane < HEAD + 8) & (hot == 0.0), FAR, 0.0)
        one = jnp.where(lane == HEAD, 1.0, 0.0)
        for h in range(OWN):
            q = unpack_head(qkv, 3 * h) * HEAD**-0.5
            qa[h, at, :] = jnp.where(lane < HEAD, q, hot).astype(BF16)
            ka[h, at, :] = jnp.where(lane < HEAD, unpack_head(qkv, 3 * h + 1), far).astype(BF16)
            va[h, at, :] = jnp.where(lane < HEAD, unpack_head(qkv, 3 * h + 2), one).astype(BF16)

    def block(i, carry):
        attend_block(i // 2, 1 + i % 2, step, qa, ka, va, lse, oacc)
        return carry

    lax.fori_loop(0, 2 * OWN, block, 0)
    gather_heads(oacc, step, 2 * rows - step, part, 0)
    gather_heads(oacc, 2 * rows, 2 * rows, send, 0)


def gather_heads(oacc, start, size, out, to):
    at, dst = pl.ds(start, size), pl.ds(to, size)
    out[dst, :LANES] = pack_pair(oacc[0, at, :], oacc[1, at, :]).astype(BF16)
    out[dst, LANES:] = oacc[2, at, :HEAD].astype(BF16)


def attend_second_kernel(qa, ka, va, lse_in, part, keep, lse, oacc):
    step = oacc.shape[1]
    lse[...] = lse_in[...]

    def block(h, carry):
        attend_block(h, 0, step, qa, ka, va, lse, oacc)
        return carry

    lax.fori_loop(0, OWN, block, 0)
    gather_heads(oacc, 0, step, keep, 0)
    keep[pl.ds(step, part.shape[0]), :] = part[...]


def keep_column(p0, p1, table, width):
    hot = jnp.concatenate([p0[:, width:], p1[:, width:]], axis=0).astype(F32)
    return jnp.sum(hot * table, axis=-1, keepdims=True)


def middle_kernel(sref, a0, a1, a2, a3, p0, p1, c0, c1, table, w_out, bias, gain, shift, middle, normed2, gb2):
    s = sref[0]
    rows, width = c0.shape
    cols = a0.shape[1]
    acc = jnp.zeros((2 * rows, width), F32) + bias[...]
    for j, a in ((0, a0), (2, a2)):
        w = w_out[pl.ds(pl.multiple_of((s ^ j) * cols, HEAD), cols), :]
        acc = acc + dot(a[...], w)
    for j, a in ((1, a1), (3, a3)):
        w = w_out[pl.ds(pl.multiple_of((s ^ j) * cols, HEAD), cols), :]
        part = dot(a[...], w)
        acc = acc + jnp.concatenate([part[rows:], part[:rows]], axis=0)
    keep_a = keep_column(p0, p1, table[0:1, :], width)
    keep_m = keep_column(p0, p1, table[1:2, :], width)
    tok = jnp.concatenate([p0[:, :width], p1[:, :width]], axis=0).astype(F32)
    mid = tok + keep_a * acc
    middle[...] = mid
    hat, _ = normalize(mid)
    normed2[...] = (hat * gain[...] + shift[...]).astype(BF16)
    gout = jnp.concatenate([c0[...], c1[...]], axis=0).astype(F32)
    gb2[...] = (keep_m * gout).astype(BF16)


def feed_kernel(last, fast, sref, bref, normed2, gb2, fc1, bias, fc2, *refs):
    if last:
        b2_in, gn_in, y_in, g2, y_send, g1_keep, gb, b2_keep, b2_send, gn_keep, gn_send, wide = refs
    else:
        g2a, g2m, g2b, y_first, y_second, g1_keep, gb, b2, gn, wide = refs
    tokens = normed2.shape[0]
    half = tokens // 2
    pre = dot(normed2[...], fc1[...]) + bias[...]
    gact = dot_t(gb2[...], fc2[...])
    act, slope = gelu_pair(pre)
    act = act.astype(BF16)
    gh = (gact * slope).astype(BF16)
    grad1 = dot_lt(normed2[...], gh)
    if not fast:
        rows = grad1.shape[0] // 2
        (y_send if last else y_first)[...] = grad1[:rows].astype(BF16)
        g1_keep[...] = grad1[rows:].astype(BF16)
    else:
        x, c = sref[0] >> 1, sref[0] & 1
        y, z1, z2 = bref[0] & 1, (bref[0] >> 1) & 1, bref[0] >> 2
        wide[...] = grad1
        n, rows = g1_keep.shape[:2]
        for m in range(2 * n):
            near = [(m >> k) & 1 for k in (4, 3, 2, 1, 0)]
            yy, zz1, xx, zz2, cc = [own if r else 1 - own for own, r in zip((y, z1, x, z2, c), near)]
            base = rows * (16 * xx + 8 * cc + 4 * zz2 + 2 * zz1 + yy)
            piece = wide[pl.ds(pl.multiple_of(base, 8), rows), :].astype(BF16)
            if m >= n:
                g1_keep[m - n] = piece
            elif last:
                y_send[n // 2 + m] = piece
            elif m < n // 2:
                y_first[m] = piece
            else:
                y_second[m - n // 2] = piece
        if last:
            for m in range(n // 2):
                y_send[m] = y_in[m]
    gb[...] = jnp.sum(gh.astype(F32), axis=0, keepdims=True)
    partn = dot_t(gh, fc1[...])
    part2 = dot(act, fc2[...])
    if last:
        partn = partn + gn_in[...]
        part2 = part2 + b2_in[...]
        b2_keep[...] = part2[:half]
        b2_send[...] = part2[half:].astype(BF16)
        gn_keep[...] = partn
        gn_send[:half] = partn[half:].astype(BF16)
        gn_send[half:] = partn[:half].astype(BF16)
        g2[...] = dot_lt(act, gb2[...]).astype(BF16)
    else:
        b2[...] = part2
        gn[...] = partn
        grad2 = dot_lt(act, gb2[...]).astype(BF16)
        if not fast:
            rows = g2a.shape[0]
            g2a[...] = grad2[:rows]
            g2m[...] = grad2[rows : 2 * rows]
            g2b[...] = grad2[2 * rows :]
        else:
            n, rows = g2a.shape[:2]
            for m in range(n):
                base = 4 * rows * m
                g2a[m] = grad2[base : base + rows]
                g2m[m] = grad2[base + rows : base + 2 * rows]
                g2b[m] = grad2[base + 2 * rows : base + 4 * rows]


def split_rows(value, wide, bit, send, keep):
    if len(send.shape) == 2:
        rows = value.shape[0] // 2
        send[...] = value[:rows].astype(BF16)
        keep[...] = value[rows:].astype(BF16)
        return
    wide[...] = value
    rows = send.shape[1]
    for m in range(send.shape[0]):
        base = 2 * m * rows
        send[m] = wide[pl.ds(pl.multiple_of(base + (1 - bit) * rows, 8), rows), :].astype(BF16)
        keep[m] = wide[pl.ds(pl.multiple_of(base + bit * rows, 8), rows), :].astype(BF16)


def feed(last, fast, per, sidx, bidx, normed2, gb2, fc1, bias, fc2, prev=()):
    tokens, width = normed2.shape
    hidden = fc1.shape[1]
    pairs = width // (2 * per)
    if last:
        outs = [SDS((hidden, width), BF16)]
        send = [SDS((3 * pairs // 2, per, hidden), BF16)]
    else:
        deep = hidden // 8
        if fast:
            outs = [SDS((8, deep // 4, width), BF16)] * 2 + [SDS((8, deep // 2, width), BF16)]
        else:
            outs = [SDS((hidden // 4, width), BF16)] * 2 + [SDS((hidden // 2, width), BF16)]
        send = [SDS((pairs // 2, per, hidden), BF16)] * 2
    keep = SDS((pairs, per, hidden), BF16)
    if not fast:
        keep = SDS((width // 2, hidden), BF16)
        send = [keep] if last else [keep, SDS((8, LANES), BF16)]
    outs += send + [keep, SDS((1, hidden), F32)]
    if last:
        outs += [SDS((tokens // 2, width), F32), SDS((tokens // 2, width), BF16)]
        outs += [SDS((tokens, width), F32), SDS((tokens, width), BF16)]
    else:
        outs += [SDS((tokens, width), F32)] * 2
    return call(
        functools.partial(feed_kernel, last, fast),
        outs,
        (sidx, bidx, normed2, gb2, fc1, bias, fc2) + tuple(prev),
        [pltpu.VMEM((width, hidden), F32)],
        flops=12 * tokens * width * hidden,
        scalars=2,
    )


def by_batch_bit(arr, per):
    arr = arr.reshape(-1, 2, per, arr.shape[-1])
    own = lax.axis_index("batch") & 1
    return [pick(arr, 1 - own, 1), pick(arr, own, 1)]


def middle_back_kernel(
    sref, gn_keep, gn_got, middle, p0, p1, c0, c1, table, w_out, gain, gb2, gmid_own, gbr_out, gatt_send, sums
):
    s = sref[0]
    rows, width = c0.shape
    cols = gatt_send.shape[1]
    hat, scale = normalize(middle[...])
    g = gn_keep[...] + gn_got[...].astype(F32)
    gout = jnp.concatenate([c0[...], c1[...]], axis=0).astype(F32)
    gmid = gout + normalize_back(g * gain[...], hat, scale)
    keep_a = keep_column(p0, p1, table[0:1, :], width)
    gbr = (keep_a * gmid).astype(BF16)
    gbr_out[...] = gbr
    w_oth = w_out[pl.ds(pl.multiple_of((s ^ 2) * cols, HEAD), cols), :]
    gatt_send[...] = dot_t(gbr, w_oth).astype(BF16)
    gmid_own[...] = gmid[:rows]
    own = slice(0, rows)
    lines = [
        jnp.sum(g[own] * hat[own], axis=0, keepdims=True),
        jnp.sum(g[own], axis=0, keepdims=True),
        jnp.sum(gb2[own, :].astype(F32), axis=0, keepdims=True),
        jnp.sum(gbr[own].astype(F32), axis=0, keepdims=True),
        jnp.zeros((4, width), F32),
    ]
    sums[...] = jnp.concatenate(lines, axis=0)


def branch_back_kernel(
    sref, bref, gbr, w_out, a0, a2, middle, p0, table, b2_keep, b2_got, bias, gain1, shift1, sums, fb_own, fb_oth,
    gatt, go_send, go_keep, early, opat, ospe, fcol, wide,
):
    s = sref[0]
    cols = a0.shape[1]
    rows, width = b2_keep.shape
    w_own = w_out[pl.ds(pl.multiple_of(s * cols, HEAD), cols), :]
    gatt[...] = dot_t(gbr[...], w_own).astype(BF16)
    for j, a in enumerate((a0, a2)):
        split_rows(dot_lt(a[...], gbr[...]), wide, bref[0] & 1, go_send.at[j], go_keep.at[j])
    hot = p0[:, width:].astype(F32)
    keep_m = jnp.sum(hot * table[1:2, :], axis=-1, keepdims=True)
    res = middle[:rows, :] + keep_m * (b2_keep[...] + b2_got[...].astype(F32) + bias[...])
    res = res.astype(BF16)
    opat[...] = res[: opat.shape[0]]
    ospe[...] = res[opat.shape[0] : opat.shape[0] + ospe.shape[0]]
    blank = functools.partial(jnp.zeros, dtype=F32)
    lines = [gain1[...], shift1[...], blank((HEAD + 2, width)), sums[:4, :], blank((LANES - HEAD - 8, width))]
    early[...] = jnp.concatenate(lines, axis=0).T
    lane = lane_of(cols)
    for j, ref in ((0, fb_own), (2, fb_oth)):
        fcol[...] = jnp.broadcast_to(ref[...], (LANES, ref.shape[1])).T
        at = pl.ds(pl.multiple_of((s ^ j) * cols, HEAD), cols)
        val = early[at, :]
        for k in range(4):
            val = jnp.where(lane == HEAD + 8 + k, fcol[pl.ds(k, cols, stride=4), :], val)
        early[at, :] = val


def attend_back_kernel(first, heads, qa, ka, va, lse, ga, gx, out, sums, goa, dq, dk, dv):
    whole = qa.shape[1]
    half = ga.shape[0]
    lane = lane_of(half)
    for i in range(heads):
        h = first + i
        for ref, start in ((ga, 0), (gx, half)):
            if h < 2:
                t = ref[:, :LANES].astype(F32)
                t = jnp.where(lane < HEAD, t if h == 0 else pltpu.roll(t, HEAD, 1), 0.0)
            else:
                t = ref[:, LANES:].astype(F32)
                t = jnp.concatenate([t, jnp.zeros_like(t)], axis=1)
            goa[i, pl.ds(start, half), :] = t.astype(BF16)
    step = whole // 3

    def block(n, carry):
        i, b = n // 3, n % 3
        h = first + i
        at = pl.ds(pl.multiple_of(b * step, step), step)
        q, go = qa[h, at, :], goa[i, at, :]
        prob = jnp.exp(dot_t(ka[h], q) - lse[h, b][0:1, :])
        gp = dot_t(va[h], go)
        inner = jnp.sum(gp * prob, axis=0, keepdims=True)
        gs = (prob * (gp - inner)).astype(BF16)
        pv = dot(prob.astype(BF16), go)
        pk = dot(gs, q)
        dq[i, at, :] = dot_lt(gs, ka[h])

        @pl.when(b == 0)
        def _():
            dv[i] = pv
            dk[i] = pk

        @pl.when(b > 0)
        def _():
            dv[i] += pv
            dk[i] += pk

        return carry

    lax.fori_loop(0, 3 * heads, block, 0)
    for i in range(heads):
        out[i, :, :LANES] = pack_pair(dq[i] * HEAD**-0.5, dk[i]).astype(BF16)
        out[i, :, LANES:] = dv[i, :, :HEAD].astype(BF16)
        sums[i] = jnp.sum(out[i].astype(F32), axis=0, keepdims=True)


def attend_back(first, heads, qa, ka, va, lse, ga, gx):
    whole = qa.shape[1]
    return call(
        functools.partial(attend_back_kernel, first, heads),
        [SDS((heads, whole, 3 * HEAD), BF16), SDS((heads, 1, 3 * HEAD), F32)],
        (qa, ka, va, lse, ga, gx),
        [pltpu.VMEM((heads, whole, LANES), BF16)] + [pltpu.VMEM((heads, whole, LANES), F32)] * 3,
        flops=10 * heads * whole * whole * LANES,
    )


def norm1_kernel(g01, g2, w, keep, send):
    rows = keep.shape[0] // 2
    cols = g2.shape[2]
    for i in range(4):
        at = pl.ds(i * rows, rows)
        part = dot_t(g01[0, at, :], w[:, :cols])
        part = part + dot_t(g01[1, at, :], w[:, cols : 2 * cols])
        part = part + dot_t(g2[0, at, :], w[:, 2 * cols : 3 * cols])
        to = pl.ds((i // 2) * rows, rows)
        if i % 2 == 0:
            keep[to, :] = part
        else:
            send[to, :] = part.astype(BF16)


def qkv_grad_kernel(sref, bref, normed, g01, g2, s01, s2, w, early, send, keep, tile, wide):
    width, cols = w.shape[0], g2.shape[2]
    every = (g01[0], g01[1], g2[0])
    parts = [dot_lt(normed[...], g) for g in every]
    g = jnp.concatenate(parts, axis=1)
    w32 = w[:, : 3 * cols].astype(F32)
    rows = jnp.concatenate([s01[0], s01[1], s2[0]], axis=1)
    both = jnp.sum(g * w32, axis=-1, keepdims=True)
    gshift = jnp.sum(w32 * rows, axis=-1, keepdims=True)
    ggain = (both - early[:, 1:2] * gshift) / early[:, 0:1]
    lane = lane_of(width)
    tail = jnp.concatenate([g[:, 4 * LANES :], jnp.zeros((width, LANES - HEAD), F32)], axis=1)
    tail = jnp.where(lane == HEAD, ggain, tail)
    tail = jnp.where(lane == HEAD + 1, gshift, tail)
    tile[...] = jnp.where(lane >= HEAD + 4, early[...], tail)
    ones = jnp.ones((g2.shape[1], LANES), BF16)
    at = pl.multiple_of(sref[0] * cols, HEAD)
    for h, part in enumerate(every):
        col = dot_lt(part, ones)
        here = pl.ds(at + h * HEAD, HEAD)
        lanes = lane_of(HEAD)
        row = tile[here, :]
        row = jnp.where(lanes == HEAD + 2, col[:HEAD], row)
        tile[here, :] = jnp.where(lanes == HEAD + 3, col[2 * HEAD :], row)
    split_rows(jnp.concatenate([g[:, : 4 * LANES], tile[...]], axis=1), wide, bref[0] & 1, send, keep)


def wide_sum(*parts):
    return sum(p.astype(F32) for p in parts[1:]) + parts[0].astype(F32)


def stage1_kernel(
    bref, keep_own, keep_oth, y1, y2, fc2, g2a, g2m, g2b, out, y3,
    msg_z, msg_y, msg_x, part_f, part_a, part_o,
):
    y, z1, z2 = bref[0] & 1, (bref[0] >> 1) & 1, bref[0] >> 2
    n = keep_own.shape[0] // 2
    for i in range(n):
        msg_z[i] = wide_sum(keep_own[i], y2[n + i]).astype(BF16)
        msg_z[n + i] = wide_sum(keep_oth[i], y1[i]).astype(BF16)
        part_f[i] = wide_sum(keep_own[n + i], y2[2 * n + i])
        part_f[n + i] = wide_sum(keep_oth[n + i], y2[i])
    rows = g2a.shape[1]
    for i in range(4):
        zz1 = z1 if i >> 1 else 1 - z1
        zz2 = z2 if i & 1 else 1 - z2
        m = 2 * zz2 + zz1
        msg_x[i] = wide_sum(out[1, m], y3[1, m]).astype(BF16)
        part_o[i] = wide_sum(out[0, m], y3[0, m])
        for bit, ref in ((1 - y, msg_y), (y, part_a)):
            b = 2 * m + bit
            ref[i, :rows] = wide_sum(fc2[b, :rows], g2a[b]).astype(ref.dtype)
            ref[i, rows : 2 * rows] = wide_sum(fc2[b, rows : 2 * rows], g2m[b]).astype(ref.dtype)
            ref[i, 2 * rows :] = wide_sum(fc2[b, 2 * rows :], g2b[b]).astype(ref.dtype)


def stage2_kernel(part_f, got_z, part_a, got_y, part_o, got_x, msg_x, msg_z, part_g, part_c):
    for half in range(2):
        for i in range(4):
            k = 8 * half + i
            msg_x[4 * half + i] = wide_sum(part_f[k], got_z[k]).astype(BF16)
            part_g[4 * half + i] = wide_sum(part_f[k + 4], got_z[k + 4])
    deep = part_a.shape[1]
    for i in range(2):
        for k, ref in ((i, msg_z), (2 + i, part_c)):
            ref[i, :deep] = wide_sum(part_a[k], got_y[k]).astype(ref.dtype)
            ref[i, deep:] = wide_sum(part_o[k], got_x[k]).astype(ref.dtype)


def stage3_kernel(part_g, got_x, part_c, got_z, msg, kept):
    per = part_g.shape[1]
    for half in range(2):
        for i in range(2):
            at = pl.ds((2 * half + i) * per, per)
            k, other = 4 * half + i, 4 * (1 - half) + i
            msg[at, :] = wide_sum(part_g[k], got_x[other]).astype(BF16)
            kept[at, :] = wide_sum(part_g[k + 2], got_x[other + 2])
    at = pl.ds(4 * per, part_c.shape[1])
    msg[at, :] = wide_sum(part_c[0], got_z[0]).astype(BF16)
    kept[at, :] = wide_sum(part_c[1], got_z[1])


def shift_kernel(keep, got, send):
    rows = send.shape[0]
    send[...] = wide_sum(keep[rows:, :], got[rows:, :]).astype(BF16)


def quarter_kernel(bref, keep, got, z1, z2, z3, kept):
    q = bref[0] >> 1
    for r in range(4):
        for k, ref in enumerate((kept, z1, z2, z3)):
            m = r * 4 + (q ^ k)
            ref[r] = wide_sum(keep[m], got[m]).astype(ref.dtype)


def sums_kernel(kept, got, swap_send, swap_keep, fc2, out):
    per = out.shape[0]
    for half in range(2):
        for i, ref in ((0, swap_send), (1, swap_keep)):
            at = pl.ds((2 * half + i) * per, per)
            ref[pl.ds(half * per, per), :] = wide_sum(kept[at, :], got[at, :]).astype(ref.dtype)
    deep = fc2.shape[0]
    for lo, ref in ((4 * per, fc2), (4 * per + deep, out)):
        at = pl.ds(lo, ref.shape[0])
        ref[...] = wide_sum(kept[at, :], got[at, :])


def owner_kernel(sref, kept, z1, z2, z3, s1, s2, s3, own):
    s = sref[0]
    for k, ref in enumerate((own, s1, s2, s3)):
        m = s ^ k
        ref[...] = wide_sum(kept[m], z1[m], z2[m], z3[m]).astype(ref.dtype)


def tail_kernel(
    sref, bref, qa, ka, va, lse, ga, gx, normed, g01, s01, w, early, gn_keep, gn_send, send, keep,
    g2, s2, goa, dq, dk, dv, tile, wide,
):
    attend_back_kernel(2, 1, qa, ka, va, lse, ga, gx, g2, s2, goa, dq, dk, dv)
    norm1_kernel(g01, g2, w, gn_keep, gn_send)
    qkv_grad_kernel(sref, bref, normed, g01, g2, s01, s2, w, early, send, keep, tile, wide)


def final_kernel(k0, c0, x0, p0, gmid, gain, gpat, gspe):
    rows, width = x0.shape
    count = gpat.shape[0]
    hat, scale = normalize(p0[:, :width].astype(F32))
    g = wide_sum(k0[:rows], c0[:rows], x0[...])
    res = gmid[...] + normalize_back(g * gain[...], hat, scale)
    gpat[...] = res[:count]
    gspe[...] = res[count : count + gspe.shape[0]]


def collect_kernel(sref, own, g1, g2, g3, swap_keep, swap_got, out, vec, fc1, every):
    s = sref[0]
    per, hidden = swap_keep.shape[0] // 2, swap_keep.shape[1]
    for j, value in ((0, swap_keep[:per]), (2, swap_keep[per:]), (1, swap_got[:per]), (3, swap_got[per:])):
        fc1[:, pl.ds(pl.multiple_of((s ^ j) * hidden, LANES), hidden)] = value.astype(F32)
    for k, ref in enumerate((own, g1, g2, g3)):
        every[k] = ref[...].astype(F32)
    pieces = [every[s ^ a] for a in range(4)]

    def part(u):
        j, a, h = u // 12, (u // 3) % 4, u % 3
        e = 3 * h + j
        return pieces[a][:, (e // 2) * LANES : (e // 2 + 1) * LANES], e % 2

    lane = lane_of(out.shape[0])
    for t in range(out.shape[1] // LANES):
        (low, lo), (high, hi) = part(2 * t), part(2 * t + 1)
        low = pltpu.roll(low, HEAD, 1) if lo else low
        high = high if hi else pltpu.roll(high, HEAD, 1)
        out[:, t * LANES : (t + 1) * LANES] = jnp.where(lane < HEAD, low, high)
    tail = 4 * LANES
    vec[...] = wide_sum(*[every[k, :, tail:] for k in range(4)])


def pick(arr, index, axis):
    return lax.dynamic_index_in_dim(arr, index, axis, keepdims=False)


def total(parts):
    out = parts[0].astype(F32)
    for part in parts[1:]:
        out = out + part.astype(F32)
    return out


def swap(kind, v, mask):
    return lax.ppermute(v, kind, [(i, i ^ mask) for i in range(lax.axis_size(kind))])


def swap_seq(v, mask):
    return swap("seq", v, mask)


def after(value, *first):
    return lax.optimization_barrier((value, first))[0]


def bits_of(kind):
    return lax.axis_size(kind).bit_length() - 1


def split_bits(arr, axis, count):
    shape = arr.shape
    return arr.reshape(shape[:axis] + (2,) * count + shape[axis + 1 :])


def to_send(parts, axis, bit, kind):
    own = (lax.axis_index(kind) >> bit) & 1
    send = total([pick(p, 1 - own, axis) for p in parts]).astype(BF16)
    return send, [pick(p, own, axis) for p in parts]


def send_four(parts, axis, low):
    own = (lax.axis_index("batch") >> low) & 3

    def quarter(p, k):
        return pick(pick(p, k >> 1, axis), k & 1, axis)

    sends = [total([quarter(p, own ^ k) for p in parts]).astype(BF16) for k in (1, 2, 3)]
    return sends, [quarter(p, own) for p in parts]


def swap_four(sends, low):
    return [swap("batch", v, k << low) for k, v in zip((1, 2, 3), sends)]


def sum_rest(parts, axis, low):
    top = bits_of("batch")
    while low < top:
        if low + 1 < top:
            sends, kept = send_four(parts, axis + top - low - 2, low)
            parts, low = kept + swap_four(sends, low), low + 2
        else:
            send, kept = to_send(parts, axis, low, "batch")
            parts, low = kept + [swap("batch", send, 1 << low)], low + 1
    return total(parts)


def body(
    patches,
    specials,
    segment_ids,
    special_order,
    keep_mask,
    norm_gains,
    norm_shifts,
    w_qkv,
    biases,
    w_out,
    w_fc1,
    fc1_bias,
    w_fc2,
    cot_patches,
    cot_specials,
):
    count, width = patches.shape[1:]
    extra = specials.shape[1]
    images = keep_mask.shape[1] // 2
    block = count + PAD
    chip = 2 * block
    whole = 4 * block
    cols = OWN * HEAD
    hidden = w_fc1.shape[1] // 4
    s = lax.axis_index("seq")
    sidx = s.astype(jnp.int32).reshape(1)
    bidx = lax.axis_index("batch").astype(jnp.int32).reshape(1)
    nb = lax.axis_size("batch")
    nbits = bits_of("batch")

    zeros = jnp.zeros((PAD - extra, width), BF16)
    mine = jnp.concatenate([patches[0], specials[0], zeros], axis=0)
    segs = jnp.concatenate(
        [segment_ids[0], special_order[0] // 2, jnp.full((PAD - extra,), -1, jnp.int32)]
    )
    marks = jnp.arange(LANES, dtype=jnp.int32) - HEAD
    hot = ((segs[:, None] == marks) & (marks >= 0)).astype(BF16)
    pay = jnp.concatenate([mine, hot], axis=1)
    cot = jnp.concatenate([cot_patches[0], cot_specials[0], zeros], axis=0)
    pay_c = swap_seq(pay, 1)
    pay_x = swap_seq(pay, 2)
    cot_c = swap_seq(cot, 1)
    keep = keep_mask[0].astype(F32).reshape(2, images) / 0.75
    table = jnp.pad(keep, ((0, 6), (HEAD, LANES - HEAD - images)))

    order = [(h, j) for h in range(OWN) for j in range(3)]
    w_own = [lax.dynamic_slice(w_qkv, (0, j * width + s * cols + h * HEAD), (width, HEAD)) for h, j in order]
    w_own = jnp.concatenate(w_own + [jnp.zeros((width, HEAD), BF16)], axis=1)
    sides = {0: biases[0], 1: jnp.zeros((width,), F32), 2: biases[1]}
    bias_own = [lax.dynamic_slice(sides[j], (s * cols + h * HEAD,), (HEAD,)) for h, j in order]
    bias_own = jnp.concatenate(bias_own + [jnp.zeros((HEAD,), F32)])[None]
    w1 = [lax.dynamic_slice(w_fc1, (0, (s ^ j) * hidden), (width, hidden)) for j in (2, 0)]
    w2 = [lax.dynamic_slice(w_fc2, ((s ^ j) * hidden, 0), (hidden, width)) for j in (2, 0)]
    fb = [lax.dynamic_slice(fc1_bias, ((s ^ j) * hidden,), (hidden,))[None] for j in (2, 0)]
    pay_x, w_own, bias_own, table, w1, w2, fb = lax.optimization_barrier(
        (pay_x, w_own, bias_own, table, w1, w2, fb)
    )
    pay_d = swap_seq(pay_x, 1)
    gain1, gain2 = norm_gains[0:1], norm_gains[1:2]
    shift1, shift2 = norm_shifts[0:1], norm_shifts[1:2]

    headed = SDS((OWN, whole, LANES), BF16)
    tops = SDS((OWN, 3, 8, whole // 3), F32)
    step = whole // 3
    qa, ka, va, lse, part, att_send, normed = call(
        attend_first_kernel,
        [headed] * 3
        + [tops, SDS((chip - step, cols), BF16), SDS((chip, cols), BF16), SDS((whole, width), BF16)],
        (pay, pay_c, pay_x, pay_d, gain1, shift1, w_own, bias_own),
        [pltpu.VMEM((OWN, whole, LANES), F32)],
        flops=2 * whole * width * 3 * cols + 3 * OWN * whole * whole * LANES,
    )
    a2 = swap_seq(att_send, 2)
    a0, lse = call(
        attend_second_kernel,
        [SDS((chip, cols), BF16), tops],
        (qa, ka, va, lse, part),
        [pltpu.VMEM((OWN, step, LANES), F32)],
        flops=OWN * whole * whole * LANES,
    )
    a1 = swap_seq(a0, 1)
    a3 = swap_seq(a2, 1)

    middle, normed2, gb2 = call(
        middle_kernel,
        [SDS((chip, width), F32), SDS((chip, width), BF16), SDS((chip, width), BF16)],
        (sidx, a0, a1, a2, a3, pay, pay_c, cot, cot_c, table, w_out, biases[2:3], gain2, shift2),
        flops=2 * chip * width * width,
        scalars=1,
    )
    per = width // (4 * nb)
    fast = nb == 8
    fc2_a, fc2_m, fc2_b, y1, y_rest, keep_oth, fb_oth, b2, gn = feed(
        False, fast, per, sidx, bidx, normed2, gb2, w1[0], fb[0], w2[0]
    )
    got2a = swap_seq(fc2_a, 2)
    if not fast:
        y1, keep_oth = by_batch_bit(jnp.concatenate([y1, keep_oth], axis=0), per)
    got_y1 = swap("batch", y1, 1)
    ahead = (got2a, got_y1)
    fc2_keep, y2, keep_own, fb_own, b2_keep, b2_send, gn_keep, gn_send = feed(
        True, fast, per, sidx, bidx, normed2, gb2, w1[1], fb[1], w2[1], (b2, gn, y_rest)
    )
    if not fast:
        y2, keep_own = by_batch_bit(jnp.concatenate([y2, keep_own], axis=0), per)
    gn_send, b2_send, fc2_m, y2, (got2a, got_y1) = lax.optimization_barrier((gn_send, b2_send, fc2_m, y2, ahead))
    gn_got = swap_seq(gn_send, 1)
    b2_got = swap_seq(b2_send, 1)
    got2m = swap_seq(fc2_m, 2)
    got_y2 = swap("batch", y2, 1)

    gmid, gbr, gatt_send, line_sums = call(
        middle_back_kernel,
        [SDS((block, width), F32), SDS((chip, width), BF16), SDS((chip, cols), BF16), SDS((8, width), F32)],
        (sidx, gn_keep, gn_got, middle, pay, pay_c, cot, cot_c, table, w_out, gain2, gb2),
        flops=2 * chip * width * cols,
        scalars=1,
    )
    gatt_x = swap_seq(gatt_send, 2)
    if fast:
        split = SDS((2, cols // (2 * per), per, width), BF16)
    else:
        split = SDS((2, cols // 2, width), BF16)
    gatt, go_send, go_keep, early, opat, ospe = call(
        branch_back_kernel,
        [SDS((chip, cols), BF16), split, split, SDS((width, LANES), F32)]
        + [SDS((count, width), BF16), SDS((extra, width), BF16)],
        (sidx, bidx, gbr, w_out, a0, a2, middle, pay, table, b2_keep, b2_got, biases[3:4], gain1, shift1)
        + (line_sums, fb_own, fb_oth),
        [pltpu.VMEM((hidden, LANES), F32), pltpu.VMEM((cols, width), F32)],
        flops=6 * chip * width * cols,
        scalars=2,
    )
    if not fast:
        halves = [by_batch_bit(jnp.concatenate([go_send[j], go_keep[j]], axis=0), per) for j in range(2)]
        go_send, go_keep = [jnp.stack([halves[j][k] for j in range(2)]) for k in range(2)]
    got_o = swap("batch", go_send, 1)
    gatt_x, fc2_b = lax.optimization_barrier((after(gatt_x, go_send), fc2_b))
    got2b = swap_seq(fc2_b, 2)
    pairs = (keep_own, keep_oth, got_y1, got_y2)

    def first_heads(lse):
        return attend_back(0, 2, qa, ka, va, lse, gatt, gatt_x)

    def tail_part(lse, g01, s01):
        wide = 5 * LANES
        if fast:
            outs = [SDS((width // (2 * per), per, wide), BF16)] * 2
        else:
            outs = [SDS((width // 2, wide), BF16)] * 2
        out = call(
            tail_kernel,
            [SDS((chip, width), F32), SDS((chip, width), BF16)] + outs,
            (sidx, bidx, qa, ka, va, lse, gatt, gatt_x, normed, g01, s01, w_own, early),
            [pltpu.VMEM((1, whole, cols), BF16), pltpu.VMEM((1, 1, cols), F32)]
            + [pltpu.VMEM((1, whole, LANES), BF16)]
            + [pltpu.VMEM((1, whole, LANES), F32)] * 3
            + [pltpu.VMEM((width, LANES), F32), pltpu.VMEM((width, wide), F32)],
            flops=10 * whole * whole * LANES + 4 * whole * width * wide,
            scalars=2,
            room=28,
        )
        if fast:
            return out
        return list(out[:2]) + by_batch_bit(jnp.concatenate(out[2:], axis=0), per)

    rest = (sidx, bidx, per, block, chip, hidden, cols, count, extra, width)
    reduce_all = reduce_eight if fast else reduce_any
    out_fc2, out_out, out_fc1, out_qkv, vec, gpat, gspe = reduce_all(
        rest, pairs, (fc2_keep, got2a, got2m, got2b), (go_keep, got_o), lse, gatt_x,
        first_heads, tail_part, pay, gmid, gain1,
    )
    grad_gains = jnp.stack([vec[:, 0], vec[:, 4]])
    grad_shifts = jnp.stack([vec[:, 1], vec[:, 5]])
    grad_biases = jnp.stack([vec[:, 2], vec[:, 3], vec[:, 7], vec[:, 6]])
    return (
        opat[None],
        ospe[None],
        gpat[None],
        gspe[None],
        grad_gains,
        grad_shifts,
        out_qkv,
        grad_biases,
        out_out,
        out_fc1,
        vec[:, 8:12].reshape(-1),
        out_fc2,
    )


def reduce_eight(
    rest, pairs, twos, outs, lse, gatt_x, first_heads, tail_part, pay, gmid, gain1
):
    sidx, bidx, per, block, chip, hidden, cols, count, extra, width = rest
    fc2_keep, got2a, got2m, got2b = twos
    go_keep, got_o = outs
    wide = 5 * LANES
    deep = hidden // 8
    fc2_keep = fc2_keep.reshape(8, deep, width)
    g01, s01 = first_heads(after(lse, gatt_x))
    g01, got_y2, got2m, got2b, got_o = lax.optimization_barrier((g01, pairs[3], got2m, got2b, got_o))
    keep_own, keep_oth, got_y1 = pairs[:3]
    msg_z, msg_y, msg_x, part_f, part_a, part_o = call(
        stage1_kernel,
        [SDS((16, per, width), BF16), SDS((4, deep, width), BF16), SDS((4, per, width), BF16)]
        + [SDS((16, per, width), F32), SDS((4, deep, width), F32), SDS((4, per, width), F32)],
        (bidx, keep_own, keep_oth, got_y1, got_y2, fc2_keep, got2a, got2m, got2b, go_keep, got_o),
        scalars=1,
    )
    msg_z, msg_y, msg_x, lse = lax.optimization_barrier((msg_z, msg_y, msg_x, after(lse, g01)))
    got_z = swap("batch", msg_z, 2)
    got_y = swap("batch", msg_y, 1)
    got_x = swap_seq(msg_x, 2)
    gn1_keep, gn1_send, q_send, q_keep = tail_part(lse, g01, s01)
    gn1_send, q_send, got_x, got_y, got_z = lax.optimization_barrier((gn1_send, q_send, got_x, got_y, got_z))
    gn1_c = swap_seq(gn1_send, 1)
    got_q = swap("batch", q_send, 1)
    msg_x, msg_z, part_g, part_c = call(
        stage2_kernel,
        [SDS((8, per, width), BF16), SDS((2, per + deep, width), BF16)]
        + [SDS((8, per, width), F32), SDS((2, per + deep, width), F32)],
        (part_f, got_z, part_a, got_y, part_o, got_x),
    )
    got_x = swap_seq(msg_x, 2)
    got_z = swap("batch", msg_z, 2)
    (xsend,) = call(shift_kernel, [SDS((block, width), BF16)], (after(gn1_keep, msg_x), gn1_c))
    gn1_x = swap_seq(xsend, 2)
    msg, kept = call(
        stage3_kernel,
        [SDS((5 * per + deep, width), BF16), SDS((5 * per + deep, width), F32)],
        (part_g, after(got_x, xsend), part_c, got_z),
    )
    got_last = swap("batch", msg, 4)
    got_q = after(got_q, msg)
    quarter = SDS((4, per, wide), BF16)
    q1, q2, q3, q_kept = call(
        quarter_kernel, [quarter, quarter, quarter, SDS(quarter.shape, F32)], (bidx, q_keep, got_q), scalars=1
    )
    got_qz = swap_four((q1, q2, q3), 1)
    gpat, gspe = call(
        final_kernel,
        [SDS((count, width), F32), SDS((extra, width), F32)],
        (gn1_keep, gn1_c, after(gn1_x, q1), pay, gmid, gain1),
    )
    got_last = after(got_last, gpat)
    swap_send, swap_keep, out_fc2, out_out = call(
        sums_kernel,
        [SDS((2 * per, width), BF16), SDS((2 * per, width), F32), SDS((deep, width), F32), SDS((per, width), F32)],
        (kept, got_last),
    )
    swap_got = swap_seq(swap_send, 1)
    row = SDS((per, wide), BF16)
    s1, s2, s3, own = call(
        owner_kernel, [row, row, row, SDS(row.shape, F32)], (sidx, q_kept, *after(got_qz, out_out)), scalars=1
    )
    gots = [swap_seq(v, k) for k, v in ((1, s1), (2, s2), (3, s3))]
    out_qkv, vec, out_fc1 = call(
        collect_kernel,
        [SDS((per, 3 * width), F32), SDS((per, LANES), F32), SDS((per, 4 * hidden), F32)],
        (sidx, own, *gots, swap_keep, swap_got),
        [pltpu.VMEM((4, per, wide), F32)],
        scalars=1,
    )
    return out_fc2, out_out, out_fc1, out_qkv, vec[:, HEAD:], gpat, gspe


def reduce_any(
    rest, pairs, twos, outs, lse, gatt_x, first_heads, tail_part, pay, gmid, gain1
):
    sidx, bidx, per, block, chip, hidden, cols, count, extra, width = rest
    s = lax.axis_index("seq")
    nb = lax.axis_size("batch")
    nbits = bits_of("batch")
    low = nbits - 1
    fc2_keep, got2a, got2m, got2b = twos
    go_keep, got_o = outs
    keep_own, keep_oth, got_oth, got_own = [
        split_bits(p.reshape(2, 2, nb // 2, per, hidden), 2, low) for p in pairs
    ]
    g01, s01 = first_heads(lse)
    send_own, parts_own = to_send([keep_own, got_own], 0, 1, "seq")
    send_oth, parts_oth = to_send([keep_oth, got_oth], 0, 1, "seq")
    got_b = swap_seq(jnp.concatenate([send_own, send_oth], axis=-1), 2)
    sum_own = sum_rest(parts_own + [got_b[..., hidden:]], 1, 1)
    sum_oth = sum_rest(parts_oth + [got_b[..., :hidden]], 1, 1)
    own_c = s & 1
    other = jnp.concatenate([pick(sum_own, 1 - own_c, 0), pick(sum_oth, 1 - own_c, 0)], axis=-1)
    got = swap_seq(other.astype(BF16), 1).astype(F32)
    rel = jnp.stack([pick(sum_own, own_c, 0), got[:, :hidden], pick(sum_oth, own_c, 0), got[:, hidden:]])
    out_fc1 = jnp.concatenate([pick(rel, s ^ a, 0) for a in range(4)], axis=1)
    got2 = jnp.concatenate([got2a, got2m, got2b], axis=0)
    parts = [split_bits(p.reshape(nb, -1, width), 0, nbits) for p in (fc2_keep, got2)]
    out_fc2 = sum_rest(parts, 0, 0)
    parts = [split_bits(p.reshape(2, nb // 2, per, width), 1, low) for p in (go_keep, got_o)]
    parts = [p[0] for p in parts] + [swap_seq(total([p[1] for p in parts]).astype(BF16), 2)]
    out_out = sum_rest(parts, 0, 1)
    gn1_keep, gn1_send, q_send, q_keep = tail_part(lse, g01, s01)
    gn1_c = swap_seq(gn1_send, 1)
    gn1_x = swap_seq((gn1_keep[block:] + gn1_c[block:].astype(F32)).astype(BF16), 2)
    gpat, gspe = call(
        final_kernel,
        [SDS((count, width), F32), SDS((extra, width), F32)],
        (gn1_keep, gn1_c, gn1_x, pay, gmid, gain1),
    )
    wide = 5 * LANES
    parts = [split_bits(p.reshape(4, nb // 2, per, wide), 1, low) for p in (q_keep, swap("batch", q_send, 1))]
    sum_q = sum_rest(parts, 1, 1)
    pieces = [pick(sum_q, s, 0)] + [
        swap_seq(pick(sum_q, s ^ j, 0).astype(BF16), j).astype(F32) for j in (1, 2, 3)
    ]
    rel = jnp.stack([p[:, : 3 * cols] for p in pieces])
    absolute = jnp.stack([pick(rel, s ^ a, 0) for a in range(4)], axis=1)
    out_qkv = absolute.reshape(-1, 4, OWN, 3, HEAD).transpose(0, 3, 1, 2, 4).reshape(-1, 3 * width)
    vec = total([p[:, 3 * cols :] for p in pieces])
    return out_fc2, out_out, out_fc1, out_qkv, vec, gpat, gspe


def solution(mesh):
    tok = P("batch", "seq", None)
    ids = P("batch", "seq")
    split = P(None, ("seq", "batch"))
    rows = P(("seq", "batch"), None)
    return jax.shard_map(
        body,
        mesh=mesh,
        in_specs=(tok, tok, ids, ids, P("batch", None)) + (P(),) * 8 + (tok, tok),
        out_specs=(tok, tok, tok, tok, split, split, rows, split, rows, rows, P(("seq", "batch")), rows),
        check_vma=False,
    )
```

```python
import functools

import jax
import jax.numpy as jnp
from jax import lax
from jax.experimental import pallas as pl
from jax.experimental.pallas import tpu as pltpu
from jax.sharding import PartitionSpec as P

HEADS = 12
HEAD = 64
PAD = 32
LANES = 128
OWN = 3
FAR = -(2.0**100)
F32 = jnp.float32
BF16 = jnp.bfloat16
SDS = jax.ShapeDtypeStruct


def dot(a, b):
    return jnp.dot(a, b, preferred_element_type=F32)


def dot_t(a, b):
    return lax.dot_general(a, b, (((1,), (1,)), ((), ())), preferred_element_type=F32)


def dot_lt(a, b):
    return lax.dot_general(a, b, (((0,), (0,)), ((), ())), preferred_element_type=F32)


def normalize(v):
    center = v - jnp.mean(v, axis=-1, keepdims=True)
    spread = jnp.mean(center * center, axis=-1, keepdims=True)
    scale = lax.rsqrt(spread + 1e-06)
    return center * scale, scale


def normalize_back(grad_hat, hat, scale):
    mean_g = jnp.mean(grad_hat, axis=-1, keepdims=True)
    mean_gh = jnp.mean(grad_hat * hat, axis=-1, keepdims=True)
    return scale * (grad_hat - mean_g - hat * mean_gh)


def gelu_pair(v):
    half = 0.5 * (1.0 + lax.erf(v * 0.5**0.5))
    slope = half + v * jnp.exp(-0.5 * v * v) * 0.3989422804014327
    return v * half, slope


def lane_of(rows):
    return lax.broadcasted_iota(jnp.int32, (rows, LANES), 1)


def unpack_head(tiles, e):
    tile = tiles[:, (e // 2) * LANES : (e // 2 + 1) * LANES]
    return tile if e % 2 == 0 else pltpu.roll(tile, HEAD, 1)


def pack_pair(low, high):
    return jnp.where(lane_of(low.shape[0]) < HEAD, low, pltpu.roll(high, HEAD, 1))


def vmem():
    return pl.BlockSpec(memory_space=pltpu.VMEM)


def smem():
    return pl.BlockSpec(memory_space=pltpu.SMEM)


def call(kernel, outs, args, scratch=(), flops=0, scalars=0, room=16, far=()):
    args = [pltpu.with_memory_space_constraint(a, pltpu.HBM) if i in far else a for i, a in enumerate(args)]
    nbytes = sum(a.size * a.dtype.itemsize for a in args)
    nbytes += sum(o.size * o.dtype.itemsize for o in outs)
    return pl.pallas_call(
        kernel,
        out_shape=outs,
        in_specs=[
            smem() if i < scalars else pl.BlockSpec(memory_space=pltpu.HBM) if i in far else vmem()
            for i in range(len(args))
        ],
        out_specs=[vmem()] * len(outs),
        scratch_shapes=list(scratch),
        compiler_params=pltpu.CompilerParams(vmem_limit_bytes=room << 20),
        cost_estimate=pl.CostEstimate(flops=flops, bytes_accessed=nbytes, transcendentals=0),
    )(*args)


def prep_kernel(sref, w, biases, w_own, bias_own):
    width = w.shape[0]
    per = width // HEAD
    line = lax.broadcasted_iota(jnp.int32, (1, LANES), 1)
    for t in range((3 * OWN + 1) // 2):
        out, bias = jnp.zeros((width, LANES), F32), jnp.zeros((1, LANES), F32)
        for dest in range(2):
            e = 2 * t + dest
            if e == 3 * OWN:
                continue
            h, j = e // 3, e % 3
            u = per * j + OWN * sref[0] + h
            side = (lane_of(width) >= HEAD) == (dest == 1)
            moved = jnp.broadcast_to((u & 1) != dest, (1, LANES))
            tile = w[:, pl.ds(pl.multiple_of((u >> 1) * LANES, LANES), LANES)].astype(F32)
            tile = jnp.where(moved, pltpu.roll(tile, HEAD, 1), tile)
            out = jnp.where(side, tile, out)
            if j != 1:
                v = per * 0 + OWN * sref[0] + h
                tile = biases[j // 2 : j // 2 + 1, pl.ds(pl.multiple_of((v >> 1) * LANES, LANES), LANES)]
                tile = jnp.broadcast_to(tile, (8, LANES))
                away = jnp.broadcast_to((v & 1) != dest, (8, LANES))
                tile = jnp.where(away, pltpu.roll(tile, HEAD, 1), tile)[:1]
                bias = jnp.where((line >= HEAD) == (dest == 1), tile, bias)
        w_own[:, t * LANES : (t + 1) * LANES] = out.astype(BF16)
        bias_own[:, t * LANES : (t + 1) * LANES] = bias


def tokens_of(patches, small):
    parts = [patches[...].astype(F32), small[:16, :].astype(F32)]
    return jnp.concatenate(parts + [jnp.zeros((PAD - 16, patches.shape[1]), F32)], axis=0)


def cots_of(patches, small):
    parts = [patches[...].astype(F32), small[16:, :].astype(F32)]
    return jnp.concatenate(parts + [jnp.zeros((PAD - 16, patches.shape[1]), F32)], axis=0)


def images_of(small, rows):
    size = -(-rows // LANES) * LANES
    line = small[:16, :size].astype(F32)[4:5]
    return jnp.broadcast_to(line, (LANES, size)).T[:rows]


def project(patches, small, gain, shift, w, bias, at, qa, ka, va, normed):
    tok = tokens_of(patches, small)
    rows = tok.shape[0]
    lane = lane_of(rows)
    hat, _ = normalize(tok)
    nrm = (hat * gain[...] + shift[...]).astype(BF16)
    normed[at, :] = nrm
    qkv = dot(nrm, w[...]) + bias[...]
    image = images_of(small, rows)
    hot = jnp.where((lane >= HEAD) & (image == (lane - HEAD).astype(F32)), 1.0, 0.0)
    far = jnp.where((lane >= HEAD) & (lane < HEAD + 8) & (hot == 0.0), FAR, 0.0)
    one = jnp.where(lane == HEAD, 1.0, 0.0)
    for h in range(OWN):
        q = unpack_head(qkv, 3 * h) * HEAD**-0.5
        qa[h, at, :] = jnp.where(lane < HEAD, q, hot).astype(BF16)
        ka[h, at, :] = jnp.where(lane < HEAD, unpack_head(qkv, 3 * h + 1), far).astype(BF16)
        va[h, at, :] = jnp.where(lane < HEAD, unpack_head(qkv, 3 * h + 2), one).astype(BF16)
    return tok, image


def project_kernel(flags, p0, s0, p1, s1, gain, shift, w, bias, qa, ka, va, normed, toks, keeps):
    rows = normed.shape[0] // 2
    lane = lane_of(rows)
    for i, (p, small) in enumerate(((p0, s0), (p1, s1))):
        at = pl.ds(i * rows, rows)
        tok, image = project(p, small, gain, shift, w, bias, at, qa, ka, va, normed)
        toks[at, :] = tok.astype(BF16)
        keep = jnp.zeros((rows, LANES), F32)
        half = flags.shape[1] // 2
        for j in range(half):
            first = flags[0, j].astype(F32) / 0.75
            second = flags[0, half + j].astype(F32) / 0.75
            keep = jnp.where(image == float(j), jnp.where(lane == 0, first, second), keep)
        keeps[at, :] = keep


def attend_block(h, at, keys, values, queries, oacc):
    sc = dot_t(queries[h, at, :], keys[h])
    top = jnp.max(sc, axis=-1, keepdims=True)
    e = jnp.exp(sc - top).astype(BF16)
    o = dot(e, values[h])
    tot = o[:, HEAD : HEAD + 1]
    mark = jnp.where(lane_of(o.shape[0]) == HEAD + 1, top + jnp.log(tot), o * (1.0 / tot))
    return mark


def attend_first_kernel(
    q0, k0, v0, n0, p2, s2, p3, s3, gain, shift, w, bias, qa, ka, va, send, oacc, normed
):
    half = n0.shape[0]
    rows = half // 2
    own = pl.ds(0, half)
    for h in range(OWN):
        qa[h, own, :] = q0[h]
        ka[h, own, :] = k0[h]
        va[h, own, :] = v0[h]
    normed[own, :] = n0[...]
    for i, (p, small) in enumerate(((p2, s2), (p3, s3))):
        project(p, small, gain, shift, w, bias, pl.ds(half + i * rows, rows), qa, ka, va, normed)

    def block(i, carry):
        h, b = i // 2, i % 2
        at = pl.ds(pl.multiple_of(half + b * rows, 16), rows)
        oacc[h, pl.ds(pl.multiple_of(b * rows, 16), rows), :] = attend_block(h, at, ka, va, qa, oacc)
        return carry

    lax.fori_loop(0, 2 * OWN, block, 0)
    gather_heads(oacc, send)


def gather_heads(oacc, out):
    out[:, :LANES] = pack_pair(oacc[0], oacc[1]).astype(BF16)
    out[:, LANES:] = oacc[2, :, :HEAD].astype(BF16)


def attend_second_kernel(qa, ka, va, other, keep, lse, oacc):
    half = oacc.shape[1]
    rows = half // 2

    def block(i, carry):
        h, b = i // 2, i % 2
        at = pl.ds(pl.multiple_of(b * rows, 16), rows)
        oacc[h, at, :] = attend_block(h, at, ka, va, qa, oacc)
        return carry

    lax.fori_loop(0, 2 * OWN, block, 0)
    gather_heads(oacc, keep)
    step = 2 * half // 3
    for h in range(OWN):
        parts = [
            oacc[h, :step, :],
            jnp.concatenate([oacc[h, step:, :], other[h, : step - (half - step), :]], axis=0),
            other[h, half - step :, :],
        ]
        for b in range(3):
            lse[h, b] = jnp.broadcast_to(parts[b].T[HEAD + 1 : HEAD + 2], (8, step))


def middle_kernel(
    sref, a0, a1, a2, a3, toks, keeps, cp0, cp1, c0, c1, w_out, bias, gain, shift, w_fc1, w_fc2,
    middle, normed2, gb2, w1, w2, sems,
):
    s = sref[0]
    copies = fetch(s ^ 2, w_fc1, w_fc2, w1, w2, sems)
    chip, width = toks.shape
    rows = chip // 2
    cols = a0.shape[1]
    acc = jnp.zeros((chip, width), F32) + bias[...]
    for j, a in ((0, a0), (2, a2)):
        w = w_out[pl.ds(pl.multiple_of((s ^ j) * cols, HEAD), cols), :]
        acc = acc + dot(a[...], w)
    for j, a in ((1, a1), (3, a3)):
        w = w_out[pl.ds(pl.multiple_of((s ^ j) * cols, HEAD), cols), :]
        part = dot(a[...], w)
        acc = acc + jnp.concatenate([part[rows:], part[:rows]], axis=0)
    mid = toks[...].astype(F32) + keeps[:, 0:1] * acc
    middle[...] = mid
    hat, _ = normalize(mid)
    normed2[...] = (hat * gain[...] + shift[...]).astype(BF16)
    gout = jnp.concatenate([cots_of(cp0, c0), cots_of(cp1, c1)], axis=0)
    gb2[...] = (keeps[:, 1:2] * gout).astype(BF16)
    for copy in copies:
        copy.wait()


def fetch(block, w_fc1, w_fc2, w1, w2, sems):
    size = w1.shape[1]
    at = pl.ds(pl.multiple_of(block * size, LANES), size)
    copies = [
        pltpu.make_async_copy(w_fc1.at[:, at], w1, sems.at[0]),
        pltpu.make_async_copy(w_fc2.at[at, :], w2, sems.at[1]),
    ]
    for copy in copies:
        copy.start()
    return copies


def feed_kernel(last, fast, sref, bref, normed2, gb2, fc1, bias, fc2, *refs):
    copies = []
    if last:
        b2_in, gn_in, y_in, g2, zb_send, zb_keep, y_send, g1_keep, gb, b2_keep, b2_send, gn_keep, gn_send, wide, wide2 = refs
    else:
        w_fc1, w_fc2, g2a, g2m, zb_send, zb_keep, y_first, y_second, g1_keep, gb, b2, gn = refs[:12]
        w1, w2, wide, wide2, sems = refs[12:]
        copies = fetch(sref[0], w_fc1, w_fc2, w1, w2, sems)
    tokens = normed2.shape[0]
    half = tokens // 2
    pre = dot(normed2[...], fc1[...]) + bias[...]
    gact = dot_t(gb2[...], fc2[...])
    act, slope = gelu_pair(pre)
    act = act.astype(BF16)
    gh = (gact * slope).astype(BF16)
    grad1 = dot_lt(normed2[...], gh)
    if not fast:
        rows = grad1.shape[0] // 2
        (y_send if last else y_first)[...] = grad1[:rows].astype(BF16)
        g1_keep[...] = grad1[rows:].astype(BF16)
    else:
        x, c = sref[0] >> 1, sref[0] & 1
        y, z1, z2 = bref[0] & 1, (bref[0] >> 1) & 1, bref[0] >> 2
        wide[...] = grad1
        n, rows = g1_keep.shape[:2]
        for m in range(2 * n):
            near = [(m >> k) & 1 for k in (4, 3, 2, 1, 0)]
            yy, zz1, xx, zz2, cc = [own if r else 1 - own for own, r in zip((y, z1, x, z2, c), near)]
            base = rows * (16 * xx + 8 * cc + 4 * zz2 + 2 * zz1 + yy)
            piece = wide[pl.ds(pl.multiple_of(base, 8), rows), :].astype(BF16)
            if m >= n:
                g1_keep[m - n] = piece
            elif last:
                y_send[n // 2 + m] = piece
            elif m < n // 2:
                y_first[m] = piece
            else:
                y_second[m - n // 2] = piece
        if last:
            for m in range(n // 2):
                y_send[m] = y_in[m]
    gb[...] = jnp.sum(gh.astype(F32), axis=0, keepdims=True)
    partn = dot_t(gh, fc1[...])
    part2 = dot(act, fc2[...])
    if last:
        partn = partn + gn_in[...]
        part2 = part2 + b2_in[...]
        b2_keep[...] = part2[:half]
        b2_send[...] = part2[half:].astype(BF16)
        gn_keep[...] = partn
        gn_send[:half] = partn[half:].astype(BF16)
        gn_send[half:] = partn[:half].astype(BF16)
    else:
        b2[...] = part2
        gn[...] = partn
    grad2 = dot_lt(act, gb2[...])
    if not fast:
        rows = zb_send.shape[0]
        if last:
            g2[...] = grad2[: 2 * rows].astype(BF16)
        else:
            g2a[...] = grad2[:rows].astype(BF16)
            g2m[...] = grad2[rows : 2 * rows].astype(BF16)
        zb_send[...] = grad2[2 * rows : 3 * rows].astype(BF16)
        zb_keep[...] = grad2[3 * rows :].astype(BF16)
    else:
        deep = grad2.shape[0] // 8
        half = deep // 2
        for m in range(8):
            if last:
                g2[m] = grad2[m * deep : m * deep + half].astype(BF16)
            else:
                mid = m * deep + half // 2
                g2a[m] = grad2[m * deep : mid].astype(BF16)
                g2m[m] = grad2[mid : mid + half // 2].astype(BF16)
            wide2[pl.ds(m * half, half), :] = grad2[m * deep + half : (m + 1) * deep]
        for m in range(8):
            near = [(m >> k) & 1 for k in (2, 1, 0)]
            zz1, zz2, yy = [own if r else 1 - own for own, r in zip((z1, z2, y), near)]
            base = half * (4 * zz2 + 2 * zz1 + yy)
            piece = wide2[pl.ds(pl.multiple_of(base, 8), half), :].astype(BF16)
            (zb_keep if m >= 4 else zb_send)[m % 4] = piece
    for copy in copies:
        copy.wait()


def split_rows(value, wide, bit, send, keep):
    if len(send.shape) == 2:
        rows = value.shape[0] // 2
        send[...] = value[:rows].astype(BF16)
        keep[...] = value[rows:].astype(BF16)
        return
    wide[...] = value
    rows = send.shape[1]
    for m in range(send.shape[0]):
        base = 2 * m * rows
        send[m] = wide[pl.ds(pl.multiple_of(base + (1 - bit) * rows, 8), rows), :].astype(BF16)
        keep[m] = wide[pl.ds(pl.multiple_of(base + bit * rows, 8), rows), :].astype(BF16)


def feed(last, fast, per, sidx, bidx, normed2, gb2, fc1, bias, fc2, prev=()):
    tokens, width = normed2.shape
    hidden = fc1.shape[1]
    pairs = width // (2 * per)
    deep = hidden // 8
    if fast:
        outs = [SDS((8, deep // 2, width), BF16)] if last else [SDS((8, deep // 4, width), BF16)] * 2
        outs += [SDS((4, deep // 2, width), BF16)] * 2
    else:
        outs = [SDS((hidden // 2, width), BF16)] if last else [SDS((hidden // 4, width), BF16)] * 2
        outs += [SDS((hidden // 4, width), BF16)] * 2
    send = [SDS((3 * pairs // 2, per, hidden), BF16)] if last else [SDS((pairs // 2, per, hidden), BF16)] * 2
    keep = SDS((pairs, per, hidden), BF16)
    if not fast:
        keep = SDS((width // 2, hidden), BF16)
        send = [keep] if last else [keep, SDS((8, LANES), BF16)]
    outs += send + [keep, SDS((1, hidden), F32)]
    if last:
        outs += [SDS((tokens // 2, width), F32), SDS((tokens // 2, width), BF16)]
        outs += [SDS((tokens, width), F32), SDS((tokens, width), BF16)]
    else:
        outs += [SDS((tokens, width), F32)] * 2 + [SDS((width, hidden), BF16), SDS((hidden, width), BF16)]
    return call(
        functools.partial(feed_kernel, last, fast),
        outs,
        (sidx, bidx, normed2, gb2, fc1, bias, fc2) + tuple(prev),
        [pltpu.VMEM((width, hidden), F32), pltpu.VMEM((hidden // 2, width), F32)]
        + ([] if last else [pltpu.SemaphoreType.DMA((2,))]),
        flops=12 * tokens * width * hidden,
        scalars=2,
        far=() if last else (7, 8),
    )


def by_batch_bit(arr, per):
    arr = arr.reshape(-1, 2, per, arr.shape[-1])
    own = lax.axis_index("batch") & 1
    return [pick(arr, 1 - own, 1), pick(arr, own, 1)]


def middle_back_kernel(
    sref, gn_keep, gn_got, middle, keeps, cp0, cp1, c0, c1, w_out, gain, gb2, gmid_own, gbr_out, gatt_send, sums
):
    s = sref[0]
    rows, width = gmid_own.shape
    cols = gatt_send.shape[1]
    hat, scale = normalize(middle[...])
    g = gn_keep[...] + gn_got[...].astype(F32)
    gout = jnp.concatenate([cots_of(cp0, c0), cots_of(cp1, c1)], axis=0)
    gmid = gout + normalize_back(g * gain[...], hat, scale)
    gbr = (keeps[:, 0:1] * gmid).astype(BF16)
    gbr_out[...] = gbr
    w_oth = w_out[pl.ds(pl.multiple_of((s ^ 2) * cols, HEAD), cols), :]
    gatt_send[...] = dot_t(gbr, w_oth).astype(BF16)
    gmid_own[...] = gmid[:rows]
    own = slice(0, rows)
    lines = [
        jnp.sum(g[own] * hat[own], axis=0, keepdims=True),
        jnp.sum(g[own], axis=0, keepdims=True),
        jnp.sum(gb2[own, :].astype(F32), axis=0, keepdims=True),
        jnp.sum(gbr[own].astype(F32), axis=0, keepdims=True),
        jnp.zeros((4, width), F32),
    ]
    sums[...] = jnp.concatenate(lines, axis=0)


def branch_back_kernel(
    sref, bref, gbr, w_out, a0, a2, middle, keeps, b2_keep, b2_got, bias, gain1, shift1, sums, fb_own, fb_oth,
    gatt, go_send, go_keep, early, opat, ospe, fcol, wide,
):
    s = sref[0]
    cols = a0.shape[1]
    rows, width = b2_keep.shape
    w_own = w_out[pl.ds(pl.multiple_of(s * cols, HEAD), cols), :]
    gatt[...] = dot_t(gbr[...], w_own).astype(BF16)
    for j, a in enumerate((a0, a2)):
        split_rows(dot_lt(a[...], gbr[...]), wide, bref[0] & 1, go_send.at[j], go_keep.at[j])
    res = middle[:rows, :] + keeps[:rows, 1:2] * (b2_keep[...] + b2_got[...].astype(F32) + bias[...])
    res = res.astype(BF16)
    opat[...] = res[: opat.shape[0]]
    ospe[...] = res[opat.shape[0] : opat.shape[0] + ospe.shape[0]]
    blank = functools.partial(jnp.zeros, dtype=F32)
    lines = [gain1[...], shift1[...], blank((HEAD + 2, width)), sums[:4, :], blank((LANES - HEAD - 8, width))]
    early[...] = jnp.concatenate(lines, axis=0).T
    lane = lane_of(cols)
    for j, ref in ((0, fb_own), (2, fb_oth)):
        fcol[...] = jnp.broadcast_to(ref[...], (LANES, ref.shape[1])).T
        at = pl.ds(pl.multiple_of((s ^ j) * cols, HEAD), cols)
        val = early[at, :]
        for k in range(4):
            val = jnp.where(lane == HEAD + 8 + k, fcol[pl.ds(k, cols, stride=4), :], val)
        early[at, :] = val


def attend_back_kernel(first, heads, qa, ka, va, lse, ga, gx, out, sums, goa, dq, dk, dv):
    whole = qa.shape[1]
    half = ga.shape[0]
    lane = lane_of(half)
    for i in range(heads):
        h = first + i
        for ref, start in ((ga, 0), (gx, half)):
            if h < 2:
                t = ref[:, :LANES].astype(F32)
                t = jnp.where(lane < HEAD, t if h == 0 else pltpu.roll(t, HEAD, 1), 0.0)
            else:
                t = ref[:, LANES:].astype(F32)
                t = jnp.concatenate([t, jnp.zeros_like(t)], axis=1)
            goa[i, pl.ds(start, half), :] = t.astype(BF16)
    step = whole // 3

    def block(n, carry):
        i, b = n // 3, n % 3
        h = first + i
        at = pl.ds(pl.multiple_of(b * step, step), step)
        q, go = qa[h, at, :], goa[i, at, :]
        prob = jnp.exp(dot_t(ka[h], q) - lse[h, b][0:1, :])
        gp = dot_t(va[h], go)
        inner = jnp.sum(gp * prob, axis=0, keepdims=True)
        gs = (prob * (gp - inner)).astype(BF16)
        pv = dot(prob.astype(BF16), go)
        pk = dot(gs, q)
        dq[i, at, :] = dot_lt(gs, ka[h])

        @pl.when(b == 0)
        def _():
            dv[i] = pv
            dk[i] = pk

        @pl.when(b > 0)
        def _():
            dv[i] += pv
            dk[i] += pk

        return carry

    lax.fori_loop(0, 3 * heads, block, 0)
    for i in range(heads):
        out[i, :, :LANES] = pack_pair(dq[i] * HEAD**-0.5, dk[i]).astype(BF16)
        out[i, :, LANES:] = dv[i, :, :HEAD].astype(BF16)
        sums[i] = jnp.sum(out[i].astype(F32), axis=0, keepdims=True)


def attend_back(first, heads, qa, ka, va, lse, ga, gx):
    whole = qa.shape[1]
    return call(
        functools.partial(attend_back_kernel, first, heads),
        [SDS((heads, whole, 3 * HEAD), BF16), SDS((heads, 1, 3 * HEAD), F32)],
        (qa, ka, va, lse, ga, gx),
        [pltpu.VMEM((heads, whole, LANES), BF16)] + [pltpu.VMEM((heads, whole, LANES), F32)] * 3,
        flops=10 * heads * whole * whole * LANES,
    )


def norm1_kernel(g01, g2, w, keep, send):
    rows = keep.shape[0] // 2
    cols = g2.shape[2]
    for i in range(4):
        at = pl.ds(i * rows, rows)
        part = dot_t(g01[0, at, :], w[:, :cols])
        part = part + dot_t(g01[1, at, :], w[:, cols : 2 * cols])
        part = part + dot_t(g2[0, at, :], w[:, 2 * cols : 3 * cols])
        to = pl.ds((i // 2) * rows, rows)
        if i % 2 == 0:
            keep[to, :] = part
        else:
            send[to, :] = part.astype(BF16)


def qkv_grad(sref, normed, grads, sums, w, first, tile, bound):
    width, cols = w.shape[0], grads[0].shape[1]
    g = jnp.concatenate([dot_lt(normed[...], v) for v in grads], axis=1)
    w32 = w[:, first * cols : (first + len(grads)) * cols].astype(F32)
    rows = jnp.concatenate(sums, axis=1)
    both = jnp.sum(g * w32, axis=-1, keepdims=True)
    gshift = jnp.sum(w32 * rows, axis=-1, keepdims=True)
    lane = lane_of(width)
    old = bound[...]
    tile[...] = jnp.where(lane == HEAD, old + both, jnp.where(lane == HEAD + 1, old + gshift, old))
    ones = jnp.ones((grads[0].shape[0], LANES), BF16)
    at = pl.multiple_of(sref[0] * cols, HEAD)
    lanes = lane_of(HEAD)
    for i, v in enumerate(grads):
        col = dot_lt(v, ones)
        here = pl.ds(at + (first + i) * HEAD, HEAD)
        row = tile[here, :]
        row = jnp.where(lanes == HEAD + 2, col[:HEAD], row)
        tile[here, :] = jnp.where(lanes == HEAD + 3, col[2 * HEAD :], row)
    return g


def heads_kernel(
    fast, sref, bref, qa, ka, va, lse, ga, gx, normed, w, early, g01, send, keep, tile,
    s01, goa, dq, dk, dv, wide,
):
    attend_back_kernel(0, 2, qa, ka, va, lse, ga, gx, g01, s01, goa, dq, dk, dv)
    g = qkv_grad(sref, normed, (g01[0], g01[1]), (s01[0], s01[1]), w, 0, tile, early)
    if not fast:
        rows = g.shape[0] // 2
        send[...] = g[:rows].astype(BF16)
        keep[...] = g[rows:].astype(BF16)
        return
    wide[...] = g
    y, z1, z2 = bref[0] & 1, (bref[0] >> 1) & 1, bref[0] >> 2
    per, cols = send.shape[1], g.shape[1]
    for m in range(8):
        zz1 = z1 if m & 4 else 1 - z1
        zz2 = z2 if m & 2 else 1 - z2
        for j in range(2):
            base = per * ((2 * (m & 1) + j) * 8 + 4 * zz2 + 2 * zz1)
            to = slice(j * cols, (j + 1) * cols)
            send[m, :, to] = wide[pl.ds(pl.multiple_of(base + (1 - y) * per, 8), per), :].astype(BF16)
            keep[m, :, to] = wide[pl.ds(pl.multiple_of(base + y * per, 8), per), :].astype(BF16)


def tail_kernel(
    sref, bref, qa, ka, va, lse, ga, gx, normed, g01, w, early, gn_keep, gn_send, send, keep,
    g2, s2, goa, dq, dk, dv, tile, wide,
):
    attend_back_kernel(2, 1, qa, ka, va, lse, ga, gx, g2, s2, goa, dq, dk, dv)
    norm1_kernel(g01, g2, w, gn_keep, gn_send)
    g = qkv_grad(sref, normed, (g2[0],), (s2[0],), w, 2, tile, early)
    width = g.shape[0]
    lane = lane_of(width)
    val = tile[...]
    gshift = val[:, HEAD + 1 : HEAD + 2]
    ggain = (val[:, HEAD : HEAD + 1] - val[:, 1:2] * gshift) / val[:, 0:1]
    val = jnp.where(lane == HEAD, ggain, val)
    last = jnp.concatenate([g[:, LANES:], jnp.zeros((width, LANES - HEAD), F32)], axis=1)
    out = jnp.concatenate([g[:, :LANES], jnp.where(lane < HEAD, last, val)], axis=1)
    split_rows(out, wide, bref[0] & 1, send, keep)


def wide_sum(*parts):
    return sum(p.astype(F32) for p in parts[1:]) + parts[0].astype(F32)


def stage0_kernel(own_keep, own_got, oth_keep, oth_got, msg, part):
    for i in range(2):
        msg[i] = wide_sum(own_keep[i], own_got[i]).astype(BF16)
        msg[2 + i] = wide_sum(oth_keep[i], oth_got[i]).astype(BF16)
        part[i] = wide_sum(own_keep[2 + i], own_got[2 + i])
        part[2 + i] = wide_sum(oth_keep[2 + i], oth_got[2 + i])


def stage1_kernel(
    bref, keep_own, keep_oth, y1, y2, fc2, g2a, g2m, out, y3, part_0, got_0, q_send,
    msg_z, msg_y, msg_x, part_f, part_a, part_o, part_p,
):
    y, z1, z2 = bref[0] & 1, (bref[0] >> 1) & 1, bref[0] >> 2
    n = keep_own.shape[0] // 2
    for i in range(n):
        msg_z[i] = wide_sum(keep_own[i], y2[n + i]).astype(BF16)
        msg_z[n + i] = wide_sum(keep_oth[i], y1[i]).astype(BF16)
        part_f[i] = wide_sum(keep_own[n + i], y2[2 * n + i])
        part_f[n + i] = wide_sum(keep_oth[n + i], y2[i])
        msg_y[8 + i] = q_send[i]
    rows = g2a.shape[1]
    for i in range(4):
        zz1 = z1 if i >> 1 else 1 - z1
        zz2 = z2 if i & 1 else 1 - z2
        m = 2 * zz2 + zz1
        msg_x[i] = wide_sum(out[1, m], y3[1, m]).astype(BF16)
        part_o[i] = wide_sum(out[0, m], y3[0, m])
        for k, got in enumerate((g2a, g2m)):
            at = slice(k * rows, (k + 1) * rows)
            b = 2 * m + 1 - y
            msg_y[2 * i + k] = wide_sum(fc2[b, at], got[b]).astype(BF16)
            b = 2 * m + y
            part_a[2 * i + k] = wide_sum(fc2[b, at], got[b])
    for i in range(2):
        for k in range(2):
            at = slice(k * rows, (k + 1) * rows)
            msg_x[4 + 2 * i + k] = wide_sum(part_0[2 + i, at], got_0[2 + i, at]).astype(BF16)
            part_p[2 * i + k] = wide_sum(part_0[i, at], got_0[i, at])


def stage2_kernel(
    part_f, got_z, part_a, got_y, part_o, got_x, part_p, q_keep, msg_x, msg_z, msg_y, part_g, part_c, part_q
):
    for half in range(2):
        for i in range(4):
            k = 8 * half + i
            msg_x[4 * half + i] = wide_sum(part_f[k], got_z[k]).astype(BF16)
            part_g[4 * half + i] = wide_sum(part_f[k + 4], got_z[k + 4])
    for i in range(4):
        msg_z[i] = wide_sum(part_a[i], got_y[i]).astype(BF16)
        part_c[i] = wide_sum(part_a[4 + i], got_y[4 + i])
        msg_z[6 + i] = wide_sum(q_keep[i], got_y[8 + i]).astype(BF16)
        part_c[6 + i] = wide_sum(q_keep[4 + i], got_y[12 + i])
    for i in range(2):
        msg_z[4 + i] = wide_sum(part_o[i], got_x[i]).astype(BF16)
        part_c[4 + i] = wide_sum(part_o[2 + i], got_x[2 + i])
        msg_y[i] = wide_sum(part_p[i], got_x[4 + i]).astype(BF16)
        part_q[i] = wide_sum(part_p[2 + i], got_x[6 + i])


def stage3_kernel(part_g, got_x, part_c, got_z, msg, kept):
    for half in range(2):
        for i in range(2):
            k, other = 4 * half + i, 4 * (1 - half) + i
            msg[2 * half + i] = wide_sum(part_g[k], got_x[other]).astype(BF16)
            kept[2 * half + i] = wide_sum(part_g[k + 2], got_x[other + 2])
    for to, a, b in ((4, 0, 2), (5, 1, 3), (6, 4, 5), (7, 6, 8), (8, 7, 9)):
        msg[to] = wide_sum(part_c[a], got_z[a]).astype(BF16)
        kept[to] = wide_sum(part_c[b], got_z[b])


def shift_kernel(keep, got, send):
    rows = send.shape[0]
    send[...] = wide_sum(keep[rows:, :], got[rows:, :]).astype(BF16)


def quarter_kernel(bref, keep, got, z1, z2, z3, kept):
    q = bref[0] >> 1
    for r in range(4):
        for k, ref in enumerate((kept, z1, z2, z3)):
            m = r * 4 + (q ^ k)
            ref[r] = wide_sum(keep[m], got[m]).astype(ref.dtype)


def sums_kernel(kept, got, part_q, got_q, swap_send, swap_keep, fc2, out):
    per = out.shape[0]
    for half in range(2):
        at = pl.ds(half * per, per)
        swap_send[at, :] = wide_sum(kept[2 * half], got[2 * half]).astype(BF16)
        swap_keep[at, :] = wide_sum(kept[2 * half + 1], got[2 * half + 1])
        fc2[at, :] = wide_sum(kept[4 + half], got[4 + half])
        fc2[pl.ds((2 + half) * per, per), :] = wide_sum(part_q[half], got_q[half])
    out[...] = wide_sum(kept[6], got[6])


def owner_kernel(sref, most, got, kept, z1, z2, z3, s1, s2, s3, own, every):
    s = sref[0]
    cols = most.shape[2] // 2
    for m in range(4):
        at = slice((m % 2) * cols, (m % 2 + 1) * cols)
        every[m, :, :cols] = wide_sum(most[7 + m // 2, :, at], got[7 + m // 2, :, at])
        every[m, :, cols:] = wide_sum(kept[m], z1[m], z2[m], z3[m])
    for k, ref in enumerate((own, s1, s2, s3)):
        ref[...] = every[s ^ k].astype(ref.dtype)


def final_kernel(k0, c0, x0, p0, s0, gmid, gain, gpat, gspe):
    rows, width = x0.shape
    count = gpat.shape[0]
    hat, scale = normalize(tokens_of(p0, s0))
    g = wide_sum(k0[:rows], c0[:rows], x0[...])
    res = gmid[...] + normalize_back(g * gain[...], hat, scale)
    gpat[...] = res[:count]
    gspe[...] = res[count : count + gspe.shape[0]]


def collect_kernel(sref, own, g1, g2, g3, swap_keep, swap_got, out, vec, fc1, every):
    s = sref[0]
    per, hidden = swap_keep.shape[0] // 2, swap_keep.shape[1]
    for j, value in ((0, swap_keep[:per]), (2, swap_keep[per:]), (1, swap_got[:per]), (3, swap_got[per:])):
        fc1[:, pl.ds(pl.multiple_of((s ^ j) * hidden, LANES), hidden)] = value.astype(F32)
    for k, ref in enumerate((own, g1, g2, g3)):
        every[k] = ref[...].astype(F32)
    pieces = [every[s ^ a] for a in range(4)]

    def part(u):
        j, a, h = u // 12, (u // 3) % 4, u % 3
        e = 3 * h + j
        return pieces[a][:, (e // 2) * LANES : (e // 2 + 1) * LANES], e % 2

    lane = lane_of(out.shape[0])
    for t in range(out.shape[1] // LANES):
        (low, lo), (high, hi) = part(2 * t), part(2 * t + 1)
        low = pltpu.roll(low, HEAD, 1) if lo else low
        high = high if hi else pltpu.roll(high, HEAD, 1)
        out[:, t * LANES : (t + 1) * LANES] = jnp.where(lane < HEAD, low, high)
    tail = 4 * LANES
    vec[...] = wide_sum(*[every[k, :, tail:] for k in range(4)])


def pick(arr, index, axis):
    return lax.dynamic_index_in_dim(arr, index, axis, keepdims=False)


def total(parts):
    out = parts[0].astype(F32)
    for part in parts[1:]:
        out = out + part.astype(F32)
    return out


def swap(kind, v, mask):
    return lax.ppermute(v, kind, [(i, i ^ mask) for i in range(lax.axis_size(kind))])


def swap_seq(v, mask):
    return swap("seq", v, mask)


def after(value, *first):
    return lax.optimization_barrier((value, first))[0]


def bits_of(kind):
    return lax.axis_size(kind).bit_length() - 1


def split_bits(arr, axis, count):
    shape = arr.shape
    return arr.reshape(shape[:axis] + (2,) * count + shape[axis + 1 :])


def to_send(parts, axis, bit, kind):
    own = (lax.axis_index(kind) >> bit) & 1
    send = total([pick(p, 1 - own, axis) for p in parts]).astype(BF16)
    return send, [pick(p, own, axis) for p in parts]


def send_four(parts, axis, low):
    own = (lax.axis_index("batch") >> low) & 3

    def quarter(p, k):
        return pick(pick(p, k >> 1, axis), k & 1, axis)

    sends = [total([quarter(p, own ^ k) for p in parts]).astype(BF16) for k in (1, 2, 3)]
    return sends, [quarter(p, own) for p in parts]


def swap_four(sends, low):
    return [swap("batch", v, k << low) for k, v in zip((1, 2, 3), sends)]


def sum_rest(parts, axis, low):
    top = bits_of("batch")
    while low < top:
        if low + 1 < top:
            sends, kept = send_four(parts, axis + top - low - 2, low)
            parts, low = kept + swap_four(sends, low), low + 2
        else:
            send, kept = to_send(parts, axis, low, "batch")
            parts, low = kept + [swap("batch", send, 1 << low)], low + 1
    return total(parts)


def body(
    patches,
    specials,
    segment_ids,
    special_order,
    keep_mask,
    norm_gains,
    norm_shifts,
    w_qkv,
    biases,
    w_out,
    w_fc1,
    fc1_bias,
    w_fc2,
    cot_patches,
    cot_specials,
):
    count, width = patches.shape[1:]
    extra = specials.shape[1]
    images = keep_mask.shape[1] // 2
    block = count + PAD
    chip = 2 * block
    whole = 4 * block
    cols = OWN * HEAD
    hidden = w_fc1.shape[1] // 4
    s = lax.axis_index("seq")
    sidx = s.astype(jnp.int32).reshape(1)
    bidx = lax.axis_index("batch").astype(jnp.int32).reshape(1)
    nb = lax.axis_size("batch")
    nbits = bits_of("batch")

    own_p, own_cot = patches[0], cot_patches[0]
    got_px = swap_seq(own_p, 2)
    got_pc = swap_seq(own_p, 1)
    ids = jnp.concatenate([segment_ids[0], special_order[0] // 2])
    line = jnp.full((width,), -1, jnp.int32).at[: count + extra].set(ids).astype(BF16)
    blank = jnp.zeros((16, width), BF16)
    small = jnp.concatenate(
        [specials[0], line[None], blank[: 15 - extra], cot_specials[0], blank[: 16 - extra]], axis=0
    )
    got_sx = swap_seq(small, 2)
    got_sc = swap_seq(small, 1)
    cot_c = swap_seq(own_cot, 1)
    gain1, gain2 = norm_gains[0:1], norm_gains[1:2]
    shift1, shift2 = norm_shifts[0:1], norm_shifts[1:2]
    fb = [lax.dynamic_slice(fc1_bias, ((s ^ j) * hidden,), (hidden,))[None] for j in (2, 0)]
    sidx, bidx, fb, small = lax.optimization_barrier((sidx, bidx, fb, small))
    w_own, bias_own = call(
        prep_kernel,
        [SDS((width, 5 * LANES), BF16), SDS((1, 5 * LANES), F32)],
        (sidx, w_qkv, biases),
        scalars=1,
    )
    headed = SDS((OWN, chip, LANES), BF16)
    q0, k0, v0, n0, toks, keeps = call(
        project_kernel,
        [headed] * 3 + [SDS((chip, width), BF16), SDS((chip, width), BF16), SDS((chip, LANES), F32)],
        (keep_mask, own_p, small, got_pc, got_sc, gain1, shift1, w_own, bias_own),
        flops=2 * chip * width * 3 * cols,
        scalars=1,
    )
    got_px, got_sx, n0 = lax.optimization_barrier((got_px, got_sx, n0))
    got_pd = swap_seq(got_px, 1)
    got_sd = swap_seq(got_sx, 1)

    headed = SDS((OWN, whole, LANES), BF16)
    heads32 = SDS((OWN, chip, LANES), F32)
    qa, ka, va, att_send, other, normed = call(
        attend_first_kernel,
        [headed] * 3 + [SDS((chip, cols), BF16), heads32, SDS((whole, width), BF16)],
        (q0, k0, v0, n0, got_px, got_sx, got_pd, got_sd, gain1, shift1, w_own, bias_own),
        flops=2 * chip * width * 3 * cols + 2 * OWN * whole * whole * LANES,
    )
    a2 = swap_seq(att_send, 2)
    a0, lse = call(
        attend_second_kernel,
        [SDS((chip, cols), BF16), SDS((OWN, 3, 8, whole // 3), F32)],
        (qa, ka, va, other),
        [pltpu.VMEM((OWN, chip, LANES), F32)],
        flops=2 * OWN * whole * whole * LANES,
    )
    a1 = swap_seq(a0, 1)
    a3 = swap_seq(a2, 1)

    middle, normed2, gb2, w1, w2 = call(
        middle_kernel,
        [SDS((chip, width), F32), SDS((chip, width), BF16), SDS((chip, width), BF16)]
        + [SDS((width, hidden), BF16), SDS((hidden, width), BF16)],
        (sidx, a0, a1, a2, a3, toks, keeps, own_cot, cot_c, small, got_sc, w_out, biases[2:3], gain2, shift2)
        + (w_fc1, w_fc2),
        [pltpu.SemaphoreType.DMA((2,))],
        flops=2 * chip * width * width,
        scalars=1,
        far=(15, 16),
    )
    per = width // (4 * nb)
    fast = nb == 8
    fc2_a, fc2_m, zo_send, zo_keep, y1, y_rest, keep_oth, fb_oth, b2, gn, w1, w2 = feed(
        False, fast, per, sidx, bidx, normed2, gb2, w1, fb[0], w2, (w_fc1, w_fc2)
    )
    got2a = swap_seq(fc2_a, 2)
    if not fast:
        y1, keep_oth = by_batch_bit(jnp.concatenate([y1, keep_oth], axis=0), per)
    got_y1 = swap("batch", y1, 1)
    got_zo = swap("batch", zo_send, 2) if fast else zo_send
    ahead = (got2a, got_y1, got_zo)
    fc2_keep, zn_send, zn_keep, y2, keep_own, fb_own, b2_keep, b2_send, gn_keep, gn_send = feed(
        True, fast, per, sidx, bidx, normed2, gb2, w1, fb[1], w2, (b2, gn, y_rest)
    )
    if not fast:
        y2, keep_own = by_batch_bit(jnp.concatenate([y2, keep_own], axis=0), per)
    gn_send, b2_send, zn_send, y2, (got2a, got_y1, got_zo) = lax.optimization_barrier(
        (gn_send, b2_send, zn_send, y2, ahead)
    )
    gn_got = swap_seq(gn_send, 1)
    b2_got = swap_seq(b2_send, 1)
    got_zn = swap("batch", zn_send, 2) if fast else zn_send
    got_y2 = swap("batch", y2, 1)

    gmid, gbr, gatt_send, line_sums = call(
        middle_back_kernel,
        [SDS((block, width), F32), SDS((chip, width), BF16), SDS((chip, cols), BF16), SDS((8, width), F32)],
        (sidx, gn_keep, gn_got, middle, keeps, own_cot, cot_c, small, got_sc, w_out, gain2, gb2),
        flops=2 * chip * width * cols,
        scalars=1,
    )
    gatt_x = swap_seq(gatt_send, 2)
    if fast:
        split = SDS((2, cols // (2 * per), per, width), BF16)
    else:
        split = SDS((2, cols // 2, width), BF16)
    gatt, go_send, go_keep, early, opat, ospe = call(
        branch_back_kernel,
        [SDS((chip, cols), BF16), split, split, SDS((width, LANES), F32)]
        + [SDS((count, width), BF16), SDS((extra, width), BF16)],
        (sidx, bidx, gbr, w_out, a0, a2, middle, keeps, b2_keep, b2_got, biases[3:4], gain1, shift1)
        + (line_sums, fb_own, fb_oth),
        [pltpu.VMEM((hidden, LANES), F32), pltpu.VMEM((cols, width), F32)],
        flops=6 * chip * width * cols,
        scalars=2,
    )
    if not fast:
        halves = [by_batch_bit(jnp.concatenate([go_send[j], go_keep[j]], axis=0), per) for j in range(2)]
        go_send, go_keep = [jnp.stack([halves[j][k] for j in range(2)]) for k in range(2)]
    got_o = swap("batch", go_send, 1)
    msg_0, part_0 = None, None
    if fast:
        msg_0, part_0 = call(
            stage0_kernel,
            [SDS(zn_keep.shape, BF16), SDS(zn_keep.shape, F32)],
            (zn_keep, after(got_zn, go_send), zo_keep, got_zo),
        )
        gatt_x = after(gatt_x, msg_0)
    gatt_x, fc2_m = lax.optimization_barrier((after(gatt_x, go_send), fc2_m))
    got2m = swap_seq(fc2_m, 2)
    pairs = (keep_own, keep_oth, got_y1, got_y2)

    def heads_scratch(heads):
        return [pltpu.VMEM((heads, whole, LANES), BF16)] + [pltpu.VMEM((heads, whole, LANES), F32)] * 3

    def first_heads(lse):
        if fast:
            split = [SDS((8, per, 4 * cols), BF16)] * 2
        else:
            split = [SDS((width // 2, 2 * cols), BF16)] * 2
        return call(
            functools.partial(heads_kernel, fast),
            [SDS((2, whole, cols), BF16)] + split + [SDS((width, LANES), F32)],
            (sidx, bidx, qa, ka, va, lse, gatt, gatt_x, normed, w_own, early),
            [pltpu.VMEM((2, 1, cols), F32)] + heads_scratch(2) + [pltpu.VMEM((width, 2 * cols), F32)],
            flops=20 * whole * whole * LANES,
            scalars=2,
            room=20,
        )

    def tail_part(lse, g01, tile):
        wide = cols + HEAD
        if fast:
            outs = [SDS((width // (2 * per), per, wide), BF16)] * 2
        else:
            outs = [SDS((width // 2, wide), BF16)] * 2
        return call(
            tail_kernel,
            [SDS((chip, width), F32), SDS((chip, width), BF16)] + outs,
            (sidx, bidx, qa, ka, va, lse, gatt, gatt_x, normed, g01, w_own, tile),
            [pltpu.VMEM((1, whole, cols), BF16), pltpu.VMEM((1, 1, cols), F32)]
            + heads_scratch(1)
            + [pltpu.VMEM((width, LANES), F32), pltpu.VMEM((width, wide), F32)],
            flops=10 * whole * whole * LANES,
            scalars=2,
            room=20,
        )

    rest = (sidx, bidx, per, block, chip, hidden, cols, count, extra, width)
    zs = (zn_send, zn_keep, zo_send, zo_keep, msg_0, part_0)
    reduce_all = reduce_eight if fast else reduce_any
    out_fc2, out_out, out_fc1, out_qkv, vec, gpat, gspe = reduce_all(
        rest, pairs, (fc2_keep, got2a, got2m, zs), (go_keep, got_o), lse, gatt_x,
        first_heads, tail_part, (own_p, small), gmid, gain1,
    )
    grad_gains = jnp.stack([vec[:, 0], vec[:, 4]])
    grad_shifts = jnp.stack([vec[:, 1], vec[:, 5]])
    grad_biases = jnp.stack([vec[:, 2], vec[:, 3], vec[:, 7], vec[:, 6]])
    return (
        opat[None],
        ospe[None],
        gpat[None],
        gspe[None],
        grad_gains,
        grad_shifts,
        out_qkv,
        grad_biases,
        out_out,
        out_fc1,
        vec[:, 8:12].reshape(-1),
        out_fc2,
    )


def reduce_eight(
    rest, pairs, twos, outs, lse, gatt_x, first_heads, tail_part, pay, gmid, gain1
):
    sidx, bidx, per, block, chip, hidden, cols, count, extra, width = rest
    fc2_keep, got2a, got2m, zs = twos
    go_keep, got_o = outs
    deep = hidden // 8
    got_0 = swap("batch", zs[4], 4)
    part_0 = zs[5]
    g01, q01_send, q01_keep, tile = first_heads(after(lse, gatt_x))
    g01, got_y2, got2m, got_o, got_0 = lax.optimization_barrier((g01, pairs[3], got2m, got_o, got_0))
    keep_own, keep_oth, got_y1 = pairs[:3]

    def blocks(n, dtype=BF16):
        return SDS((n, per, width), dtype)

    msg_z, msg_y, msg_x, part_f, part_a, part_o, part_p = call(
        stage1_kernel,
        [blocks(16), blocks(16), blocks(8), blocks(16, F32), blocks(8, F32), blocks(4, F32), blocks(4, F32)],
        (bidx, keep_own, keep_oth, got_y1, got_y2, fc2_keep, got2a, got2m, go_keep, got_o, part_0, got_0)
        + (q01_send,),
        scalars=1,
    )
    msg_z, msg_y, msg_x, lse = lax.optimization_barrier((msg_z, msg_y, msg_x, after(lse, g01)))
    got_z = swap("batch", msg_z, 2)
    got_y = swap("batch", msg_y, 1)
    got_x = swap_seq(msg_x, 2)
    gn1_keep, gn1_send, q_send, q_keep = tail_part(lse, g01, tile)
    gn1_send, q_send, got_x, got_y, got_z = lax.optimization_barrier((gn1_send, q_send, got_x, got_y, got_z))
    gn1_c = swap_seq(gn1_send, 1)
    got_q = swap("batch", q_send, 1)
    msg_x, msg_z, msg_y, part_g, part_c, part_q = call(
        stage2_kernel,
        [blocks(8), blocks(10), blocks(2), blocks(8, F32), blocks(10, F32), blocks(2, F32)],
        (part_f, got_z, part_a, got_y, part_o, got_x, part_p, q01_keep),
    )
    got_x = swap_seq(msg_x, 2)
    got_z = swap("batch", msg_z, 2)
    (xsend,) = call(shift_kernel, [SDS((block, width), BF16)], (after(gn1_keep, msg_x), gn1_c))
    gn1_x = swap_seq(xsend, 2)
    msg, kept = call(
        stage3_kernel, [blocks(9), blocks(9, F32)], (part_g, after(got_x, xsend, got_q), part_c, got_z)
    )
    got_last = swap("batch", msg, 4)
    got_q = after(got_q, msg)
    quarter = SDS((4, per, cols + HEAD), BF16)
    q1, q2, q3, q_kept = call(
        quarter_kernel, [quarter, quarter, quarter, SDS(quarter.shape, F32)], (bidx, q_keep, got_q), scalars=1
    )
    got_qz = swap_four((q1, q2, q3), 1)
    got_yb = swap("batch", after(msg_y, q1), 1)
    gpat, gspe = call(
        final_kernel,
        [SDS((count, width), F32), SDS((extra, width), F32)],
        (gn1_keep, gn1_c, after(gn1_x, q1), *pay, gmid, gain1),
    )
    got_last = after(got_last, gpat)
    swap_send, swap_keep, out_fc2, out_out = call(
        sums_kernel,
        [SDS((2 * per, width), BF16), SDS((2 * per, width), F32), SDS((deep, width), F32), SDS((per, width), F32)],
        (kept, got_last, part_q, got_yb),
    )
    swap_got = swap_seq(swap_send, 1)
    row = SDS((per, 5 * LANES), BF16)
    s1, s2, s3, own = call(
        owner_kernel,
        [row, row, row, SDS(row.shape, F32)],
        (sidx, kept, got_last, q_kept, *after(got_qz, out_out)),
        [pltpu.VMEM((4, per, 5 * LANES), F32)],
        scalars=1,
    )
    gots = [swap_seq(v, k) for k, v in ((1, s1), (2, s2), (3, s3))]
    out_qkv, vec, out_fc1 = call(
        collect_kernel,
        [SDS((per, 3 * width), F32), SDS((per, LANES), F32), SDS((per, 4 * hidden), F32)],
        (sidx, own, *gots, swap_keep, swap_got),
        [pltpu.VMEM((4, per, 5 * LANES), F32)],
        scalars=1,
    )
    return out_fc2, out_out, out_fc1, out_qkv, vec[:, HEAD:], gpat, gspe


def reduce_any(
    rest, pairs, twos, outs, lse, gatt_x, first_heads, tail_part, pay, gmid, gain1
):
    sidx, bidx, per, block, chip, hidden, cols, count, extra, width = rest
    s = lax.axis_index("seq")
    nb = lax.axis_size("batch")
    nbits = bits_of("batch")
    low = nbits - 1
    fc2_keep, got2a, got2m, zs = twos
    go_keep, got_o = outs
    keep_own, keep_oth, got_oth, got_own = [
        split_bits(p.reshape(2, 2, nb // 2, per, hidden), 2, low) for p in pairs
    ]
    g01, q01_top, q01_low, tile = first_heads(lse)
    send_own, parts_own = to_send([keep_own, got_own], 0, 1, "seq")
    send_oth, parts_oth = to_send([keep_oth, got_oth], 0, 1, "seq")
    got_b = swap_seq(jnp.concatenate([send_own, send_oth], axis=-1), 2)
    sum_own = sum_rest(parts_own + [got_b[..., hidden:]], 1, 1)
    sum_oth = sum_rest(parts_oth + [got_b[..., :hidden]], 1, 1)
    own_c = s & 1
    other = jnp.concatenate([pick(sum_own, 1 - own_c, 0), pick(sum_oth, 1 - own_c, 0)], axis=-1)
    got = swap_seq(other.astype(BF16), 1).astype(F32)
    rel = jnp.stack([pick(sum_own, own_c, 0), got[:, :hidden], pick(sum_oth, own_c, 0), got[:, hidden:]])
    out_fc1 = jnp.concatenate([pick(rel, s ^ a, 0) for a in range(4)], axis=1)
    zn_send, zn_keep, zo_send, zo_keep = zs[:4]
    got2 = jnp.concatenate([got2a, got2m, swap_seq(jnp.concatenate([zo_send, zo_keep], axis=0), 2)], axis=0)
    fc2_keep = jnp.concatenate([fc2_keep, zn_send, zn_keep], axis=0)
    parts = [split_bits(p.reshape(nb, -1, width), 0, nbits) for p in (fc2_keep, got2)]
    out_fc2 = sum_rest(parts, 0, 0)
    parts = [split_bits(p.reshape(2, nb // 2, per, width), 1, low) for p in (go_keep, got_o)]
    parts = [p[0] for p in parts] + [swap_seq(total([p[1] for p in parts]).astype(BF16), 2)]
    out_out = sum_rest(parts, 0, 1)
    gn1_keep, gn1_send, q2_top, q2_low = tail_part(lse, g01, tile)
    q_all = [jnp.concatenate(v, axis=1) for v in ((q01_top, q2_top), (q01_low, q2_low))]
    q_send, q_keep = by_batch_bit(jnp.concatenate(q_all, axis=0), per)
    gn1_c = swap_seq(gn1_send, 1)
    gn1_x = swap_seq((gn1_keep[block:] + gn1_c[block:].astype(F32)).astype(BF16), 2)
    gpat, gspe = call(
        final_kernel,
        [SDS((count, width), F32), SDS((extra, width), F32)],
        (gn1_keep, gn1_c, gn1_x, *pay, gmid, gain1),
    )
    wide = 5 * LANES
    parts = [split_bits(p.reshape(4, nb // 2, per, wide), 1, low) for p in (q_keep, swap("batch", q_send, 1))]
    sum_q = sum_rest(parts, 1, 1)
    pieces = [pick(sum_q, s, 0)] + [
        swap_seq(pick(sum_q, s ^ j, 0).astype(BF16), j).astype(F32) for j in (1, 2, 3)
    ]
    rel = jnp.stack([p[:, : 3 * cols] for p in pieces])
    absolute = jnp.stack([pick(rel, s ^ a, 0) for a in range(4)], axis=1)
    out_qkv = absolute.reshape(-1, 4, OWN, 3, HEAD).transpose(0, 3, 1, 2, 4).reshape(-1, 3 * width)
    vec = total([p[:, 3 * cols :] for p in pieces])
    return out_fc2, out_out, out_fc1, out_qkv, vec, gpat, gspe


def solution(mesh):
    tok = P("batch", "seq", None)
    ids = P("batch", "seq")
    split = P(None, ("seq", "batch"))
    rows = P(("seq", "batch"), None)
    return jax.shard_map(
        body,
        mesh=mesh,
        in_specs=(tok, tok, ids, ids, P("batch", None)) + (P(),) * 8 + (tok, tok),
        out_specs=(tok, tok, tok, tok, split, split, rows, split, rows, rows, P(("seq", "batch")), rows),
        check_vma=False,
    )
```

```python
import functools

import jax
import jax.numpy as jnp
from jax import lax
from jax.experimental import pallas as pl
from jax.experimental.pallas import tpu as pltpu
from jax.sharding import PartitionSpec as P

HEADS = 12
HEAD = 64
PAD = 32
SPECIAL = 4
LANES = 128
OWN = 3
FAR = -(2.0**100)
F32 = jnp.float32
BF16 = jnp.bfloat16
SDS = jax.ShapeDtypeStruct


def dot(a, b):
    return jnp.dot(a, b, preferred_element_type=F32)


def dot_t(a, b):
    return lax.dot_general(a, b, (((1,), (1,)), ((), ())), preferred_element_type=F32)


def dot_lt(a, b):
    return lax.dot_general(a, b, (((0,), (0,)), ((), ())), preferred_element_type=F32)


def normalize(v):
    center = v - jnp.mean(v, axis=-1, keepdims=True)
    spread = jnp.mean(center * center, axis=-1, keepdims=True)
    scale = lax.rsqrt(spread + 1e-06)
    return center * scale, scale


def normalize_back(grad_hat, hat, scale):
    mean_g = jnp.mean(grad_hat, axis=-1, keepdims=True)
    mean_gh = jnp.mean(grad_hat * hat, axis=-1, keepdims=True)
    return scale * (grad_hat - mean_g - hat * mean_gh)


def gelu_pair(v):
    half = 0.5 * (1.0 + lax.erf(v * 0.5**0.5))
    slope = half + v * jnp.exp(-0.5 * v * v) * 0.3989422804014327
    return v * half, slope


def lane_of(rows):
    return lax.broadcasted_iota(jnp.int32, (rows, LANES), 1)


def unpack_head(tiles, e):
    tile = tiles[:, (e // 2) * LANES : (e // 2 + 1) * LANES]
    return tile if e % 2 == 0 else pltpu.roll(tile, HEAD, 1)


def pack_pair(low, high):
    return jnp.where(lane_of(low.shape[0]) < HEAD, low, pltpu.roll(high, HEAD, 1))


def vmem():
    return pl.BlockSpec(memory_space=pltpu.VMEM)


def smem():
    return pl.BlockSpec(memory_space=pltpu.SMEM)


def call(kernel, outs, args, scratch=(), flops=0, scalars=0, room=16, far=()):
    args = [pltpu.with_memory_space_constraint(a, pltpu.HBM) if i in far else a for i, a in enumerate(args)]
    nbytes = sum(a.size * a.dtype.itemsize for a in args)
    nbytes += sum(o.size * o.dtype.itemsize for o in outs)
    return pl.pallas_call(
        kernel,
        out_shape=outs,
        in_specs=[
            smem() if i < scalars else pl.BlockSpec(memory_space=pltpu.HBM) if i in far else vmem()
            for i in range(len(args))
        ],
        out_specs=[vmem()] * len(outs),
        scratch_shapes=list(scratch),
        compiler_params=pltpu.CompilerParams(vmem_limit_bytes=room << 20),
        cost_estimate=pl.CostEstimate(flops=flops, bytes_accessed=nbytes, transcendentals=0),
    )(*args)


def prep_kernel(sref, w, biases, w_own, bias_own, tiles, lines, sems):
    width = w.shape[0]
    per = width // HEAD
    spots = [per * (e % 3) + OWN * sref[0] + e // 3 for e in range(3 * OWN)]
    copies = [pltpu.make_async_copy(biases, lines, sems.at[3 * OWN])]
    for e, u in enumerate(spots):
        tile = w.at[:, pl.ds(pl.multiple_of((u >> 1) * LANES, LANES), LANES)]
        copies.append(pltpu.make_async_copy(tile, tiles.at[e], sems.at[e]))
    for copy in copies:
        copy.start()
    copies[0].wait()
    line = lax.broadcasted_iota(jnp.int32, (1, LANES), 1)
    for t in range((3 * OWN + 1) // 2):
        out, bias = jnp.zeros((width, LANES), F32), jnp.zeros((1, LANES), F32)
        for dest in range(2):
            e = 2 * t + dest
            if e == 3 * OWN:
                continue
            copies[1 + e].wait()
            u, j = spots[e], e % 3
            side = (lane_of(width) >= HEAD) == (dest == 1)
            moved = jnp.broadcast_to((u & 1) != dest, (1, LANES))
            tile = tiles[e].astype(F32)
            tile = jnp.where(moved, pltpu.roll(tile, HEAD, 1), tile)
            out = jnp.where(side, tile, out)
            if j != 1:
                v = OWN * sref[0] + e // 3
                tile = lines[j // 2 : j // 2 + 1, pl.ds(pl.multiple_of((v >> 1) * LANES, LANES), LANES)]
                tile = jnp.broadcast_to(tile, (8, LANES))
                away = jnp.broadcast_to((v & 1) != dest, (8, LANES))
                tile = jnp.where(away, pltpu.roll(tile, HEAD, 1), tile)[:1]
                bias = jnp.where((line >= HEAD) == (dest == 1), tile, bias)
        w_own[:, t * LANES : (t + 1) * LANES] = out.astype(BF16)
        bias_own[:, t * LANES : (t + 1) * LANES] = bias


def small_kernel(specials_in, segments_in, order_in, cots_in, small, specials, segments, order, cots, wide, sems):
    pairs = ((specials_in, specials), (segments_in, segments), (order_in, order), (cots_in, cots))
    copies = [pltpu.make_async_copy(src, dst, sems.at[i]) for i, (src, dst) in enumerate(pairs)]
    for copy in copies:
        copy.start()
    extra, width = specials.shape
    count = segments.shape[1]
    wide[...] = jnp.zeros_like(wide)
    wide[extra : extra + 1, :] = jnp.full((1, width), -1.0, F32)
    for copy in copies:
        copy.wait()
    wide[:extra, :] = specials[...].astype(F32)
    wide[16 : 16 + extra, :] = cots[...].astype(F32)
    wide[extra : extra + 1, :count] = segments[...].astype(F32)
    wide[extra : extra + 1, count : count + extra] = (order[...] >> 1).astype(F32)
    small[...] = wide[...].astype(BF16)


def tokens_of(patches, small):
    parts = [patches[...].astype(F32), small[:16, :].astype(F32)]
    return jnp.concatenate(parts + [jnp.zeros((PAD - 16, patches.shape[1]), F32)], axis=0)


def cots_of(patches, small):
    parts = [patches[...].astype(F32), small[16:, :].astype(F32)]
    return jnp.concatenate(parts + [jnp.zeros((PAD - 16, patches.shape[1]), F32)], axis=0)


def images_of(small, rows):
    size = -(-rows // LANES) * LANES
    line = small[:16, :size].astype(F32)[SPECIAL : SPECIAL + 1]
    return jnp.broadcast_to(line, (LANES, size)).T[:rows]


def project(patches, small, gain, shift, w, bias, at, qa, ka, va, normed):
    tok = tokens_of(patches, small)
    rows = tok.shape[0]
    lane = lane_of(rows)
    hat, _ = normalize(tok)
    nrm = (hat * gain[0:1, :] + shift[0:1, :]).astype(BF16)
    normed[at, :] = nrm
    qkv = dot(nrm, w[...]) + bias[...]
    image = images_of(small, rows)
    hot = jnp.where((lane >= HEAD) & (image == (lane - HEAD).astype(F32)), 1.0, 0.0)
    far = jnp.where((lane >= HEAD) & (lane < HEAD + 8) & (hot == 0.0), FAR, 0.0)
    one = jnp.where(lane == HEAD, 1.0, 0.0)
    for h in range(OWN):
        q = unpack_head(qkv, 3 * h) * HEAD**-0.5
        qa[h, at, :] = jnp.where(lane < HEAD, q, hot).astype(BF16)
        ka[h, at, :] = jnp.where(lane < HEAD, unpack_head(qkv, 3 * h + 1), far).astype(BF16)
        va[h, at, :] = jnp.where(lane < HEAD, unpack_head(qkv, 3 * h + 2), one).astype(BF16)
    return tok, image


def project_kernel(flags, p0, s0, p1, s1, gain, shift, w, bias, qa, ka, va, normed, toks, keeps):
    rows = normed.shape[0] // 2
    lane = lane_of(rows)
    for i, (p, small) in enumerate(((p0, s0), (p1, s1))):
        at = pl.ds(i * rows, rows)
        tok, image = project(p, small, gain, shift, w, bias, at, qa, ka, va, normed)
        toks[at, :] = tok.astype(BF16)
        keep = jnp.zeros((rows, LANES), F32)
        half = flags.shape[1] // 2
        for j in range(half):
            first = flags[0, j].astype(F32) / 0.75
            second = flags[0, half + j].astype(F32) / 0.75
            keep = jnp.where(image == float(j), jnp.where(lane == 0, first, second), keep)
        keeps[at, :] = keep


def attend_block(h, at, keys, values, queries, oacc):
    sc = dot_t(queries[h, at, :], keys[h])
    top = jnp.max(sc, axis=-1, keepdims=True)
    e = jnp.exp(sc - top).astype(BF16)
    o = dot(e, values[h])
    tot = o[:, HEAD : HEAD + 1]
    mark = jnp.where(lane_of(o.shape[0]) == HEAD + 1, top + jnp.log(tot), o * (1.0 / tot))
    return mark


def attend_first_kernel(
    q0, k0, v0, n0, p2, s2, p3, s3, gain, shift, w, bias, qa, ka, va, send, oacc, normed
):
    half = n0.shape[0]
    rows = half // 2
    own = pl.ds(0, half)
    for h in range(OWN):
        qa[h, own, :] = q0[h]
        ka[h, own, :] = k0[h]
        va[h, own, :] = v0[h]
    normed[own, :] = n0[...]
    for i, (p, small) in enumerate(((p2, s2), (p3, s3))):
        project(p, small, gain, shift, w, bias, pl.ds(half + i * rows, rows), qa, ka, va, normed)

    def block(i, carry):
        h, b = i // 2, i % 2
        at = pl.ds(pl.multiple_of(half + b * rows, 16), rows)
        oacc[h, pl.ds(pl.multiple_of(b * rows, 16), rows), :] = attend_block(h, at, ka, va, qa, oacc)
        return carry

    lax.fori_loop(0, 2 * OWN, block, 0, unroll=3)
    gather_heads(oacc, send)


def gather_heads(oacc, out):
    out[:, :LANES] = pack_pair(oacc[0], oacc[1]).astype(BF16)
    out[:, LANES:] = oacc[2, :, :HEAD].astype(BF16)


def attend_second_kernel(qa, ka, va, other, keep, lse, oacc):
    half = oacc.shape[1]
    rows = half // 2

    def block(i, carry):
        h, b = i // 2, i % 2
        at = pl.ds(pl.multiple_of(b * rows, 16), rows)
        oacc[h, at, :] = attend_block(h, at, ka, va, qa, oacc)
        return carry

    lax.fori_loop(0, 2 * OWN, block, 0, unroll=3)
    gather_heads(oacc, keep)
    step = 2 * half // 3
    for h in range(OWN):
        parts = [
            oacc[h, :step, :],
            jnp.concatenate([oacc[h, step:, :], other[h, : step - (half - step), :]], axis=0),
            other[h, half - step :, :],
        ]
        for b in range(3):
            lse[h, b] = jnp.broadcast_to(parts[b].T[HEAD + 1 : HEAD + 2], (8, step))


def middle_kernel(
    sref, a0, a1, a2, a3, toks, keeps, cp0, cp1, c0, c1, w_out, bias, gain, shift, w_fc1, w_fc2,
    middle, normed2, gb2, w1, w2, sems,
):
    s = sref[0]
    copies = fetch(s ^ 2, w_fc1, w_fc2, w1, w2, sems)
    chip, width = toks.shape
    rows = chip // 2
    cols = a0.shape[1]
    acc = jnp.zeros((chip, width), F32) + bias[2:3, :]
    for j, a in ((0, a0), (2, a2)):
        w = w_out[pl.ds(pl.multiple_of((s ^ j) * cols, HEAD), cols), :]
        acc = acc + dot(a[...], w)
    for j, a in ((1, a1), (3, a3)):
        w = w_out[pl.ds(pl.multiple_of((s ^ j) * cols, HEAD), cols), :]
        part = dot(a[...], w)
        acc = acc + jnp.concatenate([part[rows:], part[:rows]], axis=0)
    mid = toks[...].astype(F32) + keeps[:, 0:1] * acc
    middle[...] = mid
    hat, _ = normalize(mid)
    normed2[...] = (hat * gain[1:2, :] + shift[1:2, :]).astype(BF16)
    gout = jnp.concatenate([cots_of(cp0, c0), cots_of(cp1, c1)], axis=0)
    gb2[...] = (keeps[:, 1:2] * gout).astype(BF16)
    for copy in copies:
        copy.wait()


def fetch(block, w_fc1, w_fc2, w1, w2, sems):
    size = w1.shape[1]
    at = pl.ds(pl.multiple_of(block * size, LANES), size)
    copies = [
        pltpu.make_async_copy(w_fc1.at[:, at], w1, sems.at[0]),
        pltpu.make_async_copy(w_fc2.at[at, :], w2, sems.at[1]),
    ]
    for copy in copies:
        copy.start()
    return copies


def feed_kernel(last, fast, sref, bref, normed2, gb2, fc1, bias, fc2, *refs):
    copies = []
    if last:
        b2_in, gn_in, y_in, g2, zb_send, zb_keep, y_send, g1_keep, gb, b2_keep, b2_send, gn_keep, gn_send, wide, wide2 = refs
    else:
        w_fc1, w_fc2, g2a, g2m, zb_send, zb_keep, y_first, y_second, g1_keep, gb, b2, gn = refs[:12]
        w1, w2, wide, wide2, sems = refs[12:]
        copies = fetch(sref[0], w_fc1, w_fc2, w1, w2, sems)
    tokens = normed2.shape[0]
    half = tokens // 2
    block = sref[0] if last else sref[0] ^ 2
    pre = dot(normed2[...], fc1[...]) + bias[:, pl.ds(pl.multiple_of(block * fc1.shape[1], LANES), fc1.shape[1])]
    gact = dot_t(gb2[...], fc2[...])
    act, slope = gelu_pair(pre)
    act = act.astype(BF16)
    gh = (gact * slope).astype(BF16)
    grad1 = dot_lt(normed2[...], gh)
    if not fast:
        rows = grad1.shape[0] // 2
        (y_send if last else y_first)[...] = grad1[:rows].astype(BF16)
        g1_keep[...] = grad1[rows:].astype(BF16)
    else:
        x, c = sref[0] >> 1, sref[0] & 1
        y, z1, z2 = bref[0] & 1, (bref[0] >> 1) & 1, bref[0] >> 2
        wide[...] = grad1
        n, rows = g1_keep.shape[:2]
        for m in range(2 * n):
            near = [(m >> k) & 1 for k in (4, 3, 2, 1, 0)]
            yy, zz1, xx, zz2, cc = [own if r else 1 - own for own, r in zip((y, z1, x, z2, c), near)]
            base = rows * (16 * xx + 8 * cc + 4 * zz2 + 2 * zz1 + yy)
            piece = wide[pl.ds(pl.multiple_of(base, 8), rows), :].astype(BF16)
            if m >= n:
                g1_keep[m - n] = piece
            elif last:
                y_send[n // 4 + m] = piece
            elif m < 3 * n // 4:
                y_first[m] = piece
            else:
                y_second[m - 3 * n // 4] = piece
        if last:
            for m in range(n // 4):
                y_send[m] = y_in[m]
    gb[...] = jnp.sum(gh.astype(F32), axis=0, keepdims=True)
    partn = dot_t(gh, fc1[...])
    part2 = dot(act, fc2[...])
    if last:
        partn = partn + gn_in[...]
        part2 = part2 + b2_in[...]
        b2_keep[...] = part2[:half]
        b2_send[...] = part2[half:].astype(BF16)
        gn_keep[...] = partn
        gn_send[:half] = partn[half:].astype(BF16)
        gn_send[half:] = partn[:half].astype(BF16)
    else:
        b2[...] = part2
        gn[...] = partn
    grad2 = dot_lt(act, gb2[...])
    if not fast:
        rows = zb_send.shape[0]
        if last:
            g2[...] = grad2[: 2 * rows].astype(BF16)
        else:
            g2a[...] = grad2[:rows].astype(BF16)
            g2m[...] = grad2[rows : 2 * rows].astype(BF16)
        zb_send[...] = grad2[2 * rows : 3 * rows].astype(BF16)
        zb_keep[...] = grad2[3 * rows :].astype(BF16)
    else:
        deep = grad2.shape[0] // 8
        half = deep // 2
        for m in range(8):
            if last:
                g2[m] = grad2[m * deep : m * deep + half].astype(BF16)
            else:
                mid = m * deep + half // 2
                g2a[m] = grad2[m * deep : mid].astype(BF16)
                g2m[m] = grad2[mid : mid + half // 2].astype(BF16)
            wide2[pl.ds(m * half, half), :] = grad2[m * deep + half : (m + 1) * deep]
        for m in range(8):
            near = [(m >> k) & 1 for k in (2, 1, 0)]
            zz1, zz2, yy = [own if r else 1 - own for own, r in zip((z1, z2, y), near)]
            base = half * (4 * zz2 + 2 * zz1 + yy)
            piece = wide2[pl.ds(pl.multiple_of(base, 8), half), :].astype(BF16)
            (zb_keep if m >= 4 else zb_send)[m % 4] = piece
    for copy in copies:
        copy.wait()


def split_rows(value, wide, bit, send, keep):
    if len(send.shape) == 2:
        rows = value.shape[0] // 2
        send[...] = value[:rows].astype(BF16)
        keep[...] = value[rows:].astype(BF16)
        return
    wide[...] = value
    rows = send.shape[1]
    for m in range(send.shape[0]):
        base = 2 * m * rows
        send[m] = wide[pl.ds(pl.multiple_of(base + (1 - bit) * rows, 8), rows), :].astype(BF16)
        keep[m] = wide[pl.ds(pl.multiple_of(base + bit * rows, 8), rows), :].astype(BF16)


def feed(last, fast, per, sidx, bidx, normed2, gb2, fc1, bias, fc2, prev=()):
    tokens, width = normed2.shape
    hidden = fc1.shape[1]
    pairs = width // (2 * per)
    deep = hidden // 8
    if fast:
        outs = [SDS((8, deep // 2, width), BF16)] if last else [SDS((8, deep // 4, width), BF16)] * 2
        outs += [SDS((4, deep // 2, width), BF16)] * 2
    else:
        outs = [SDS((hidden // 2, width), BF16)] if last else [SDS((hidden // 4, width), BF16)] * 2
        outs += [SDS((hidden // 4, width), BF16)] * 2
    if last:
        send = [SDS((5 * pairs // 4, per, hidden), BF16)]
    else:
        send = [SDS((n, per, hidden), BF16) for n in (3 * pairs // 4, pairs // 4)]
    keep = SDS((pairs, per, hidden), BF16)
    if not fast:
        keep = SDS((width // 2, hidden), BF16)
        send = [keep] if last else [keep, SDS((8, LANES), BF16)]
    outs += send + [keep, SDS((1, hidden), F32)]
    if last:
        outs += [SDS((tokens // 2, width), F32), SDS((tokens // 2, width), BF16)]
        outs += [SDS((tokens, width), F32), SDS((tokens, width), BF16)]
    else:
        outs += [SDS((tokens, width), F32)] * 2 + [SDS((width, hidden), BF16), SDS((hidden, width), BF16)]
    return call(
        functools.partial(feed_kernel, last, fast),
        outs,
        (sidx, bidx, normed2, gb2, fc1, bias, fc2) + tuple(prev),
        [pltpu.VMEM((width, hidden), F32), pltpu.VMEM((hidden // 2, width), F32)]
        + ([] if last else [pltpu.SemaphoreType.DMA((2,))]),
        flops=12 * tokens * width * hidden,
        scalars=2,
        far=() if last else (7, 8),
    )


def by_batch_bit(arr, per):
    arr = arr.reshape(-1, 2, per, arr.shape[-1])
    own = lax.axis_index("batch") & 1
    return [pick(arr, 1 - own, 1), pick(arr, own, 1)]


def middle_back_kernel(
    sref, gn_keep, gn_got, middle, keeps, cp0, cp1, c0, c1, w_out, gain, gb2, gmid_own, gbr_out, gatt_send, sums
):
    s = sref[0]
    rows, width = gmid_own.shape
    cols = gatt_send.shape[1]
    hat, scale = normalize(middle[...])
    g = gn_keep[...] + gn_got[...].astype(F32)
    gout = jnp.concatenate([cots_of(cp0, c0), cots_of(cp1, c1)], axis=0)
    gmid = gout + normalize_back(g * gain[1:2, :], hat, scale)
    gbr = (keeps[:, 0:1] * gmid).astype(BF16)
    gbr_out[...] = gbr
    w_oth = w_out[pl.ds(pl.multiple_of((s ^ 2) * cols, HEAD), cols), :]
    gatt_send[...] = dot_t(gbr, w_oth).astype(BF16)
    gmid_own[...] = gmid[:rows]
    own = slice(0, rows)
    lines = [
        jnp.sum(g[own] * hat[own], axis=0, keepdims=True),
        jnp.sum(g[own], axis=0, keepdims=True),
        jnp.sum(gb2[own, :].astype(F32), axis=0, keepdims=True),
        jnp.sum(gbr[own].astype(F32), axis=0, keepdims=True),
        jnp.zeros((4, width), F32),
    ]
    sums[...] = jnp.concatenate(lines, axis=0)


def branch_back_kernel(
    per, sref, bref, gbr, w_out, a0, a2, middle, keeps, b2_keep, b2_got, bias, gain1, shift1, sums, fb_own, fb_oth,
    gatt, go_send, go_keep, early, opat, ospe, fcol, wide,
):
    s = sref[0]
    cols = a0.shape[1]
    rows, width = b2_keep.shape
    w_own = w_out[pl.ds(pl.multiple_of(s * cols, HEAD), cols), :]
    gatt[...] = dot_t(gbr[...], w_own).astype(BF16)
    for j, a in enumerate((a0, a2)):
        split_rows(dot_lt(a[...], gbr[...]), wide, bref[0] & 1, go_send.at[j], go_keep.at[j])
    res = middle[:rows, :] + keeps[:rows, 1:2] * (b2_keep[...] + b2_got[...].astype(F32) + bias[3:4, :])
    res = res.astype(BF16)
    opat[...] = res[: opat.shape[0]]
    ospe[...] = res[opat.shape[0] : opat.shape[0] + ospe.shape[0]]
    blank = functools.partial(jnp.zeros, dtype=F32)
    lines = [gain1[0:1, :], shift1[0:1, :], blank((HEAD + 2, width)), sums[:4, :], blank((LANES - HEAD - 8, width))]
    early[...] = jnp.concatenate(lines, axis=0).T
    lane = lane_of(cols)
    for j, ref in ((0, fb_own), (2, fb_oth)):
        fcol[...] = jnp.broadcast_to(ref[...], (LANES, ref.shape[1])).T
        at = pl.ds(pl.multiple_of((s ^ j) * cols, HEAD), cols)
        val = early[at, :]
        for k in range(4):
            lines = [fcol[(4 * b + k) * per : (4 * b + k + 1) * per, :] for b in range(cols // per)]
            val = jnp.where(lane == HEAD + 8 + k, jnp.concatenate(lines, axis=0), val)
        early[at, :] = val


def attend_back_kernel(first, heads, unroll, qa, ka, va, lse, ga, gx, out, sums, goa, dq, dk, dv):
    whole = qa.shape[1]
    half = ga.shape[0]
    lane = lane_of(half)
    for i in range(heads):
        h = first + i
        for ref, start in ((ga, 0), (gx, half)):
            if h < 2:
                t = ref[:, :LANES].astype(F32)
                t = jnp.where(lane < HEAD, t if h == 0 else pltpu.roll(t, HEAD, 1), 0.0)
            else:
                t = ref[:, LANES:].astype(F32)
                t = jnp.concatenate([t, jnp.zeros_like(t)], axis=1)
            goa[i, pl.ds(start, half), :] = t.astype(BF16)
    step = whole // 3

    def block(n, carry):
        i, b = n // 3, n % 3
        h = first + i
        at = pl.ds(pl.multiple_of(b * step, step), step)
        q, go = qa[h, at, :], goa[i, at, :]
        prob = jnp.exp(dot_t(ka[h], q) - lse[h, b][0:1, :])
        gp = dot_t(va[h], go)
        inner = jnp.sum(gp * prob, axis=0, keepdims=True)
        gs = (prob * (gp - inner)).astype(BF16)
        pv = dot(prob.astype(BF16), go)
        pk = dot(gs, q)
        dq[i, at, :] = dot_lt(gs, ka[h])

        dv[i] = jnp.where(b == 0, pv, dv[i] + pv)
        dk[i] = jnp.where(b == 0, pk, dk[i] + pk)
        return carry

    lax.fori_loop(0, 3 * heads, block, 0, unroll=unroll)
    for i in range(heads):
        out[i, :, :LANES] = pack_pair(dq[i] * HEAD**-0.5, dk[i]).astype(BF16)
        out[i, :, LANES:] = dv[i, :, :HEAD].astype(BF16)
        sums[i] = jnp.sum(out[i].astype(F32), axis=0, keepdims=True)


def attend_back(first, heads, qa, ka, va, lse, ga, gx):
    whole = qa.shape[1]
    return call(
        functools.partial(attend_back_kernel, first, heads),
        [SDS((heads, whole, 3 * HEAD), BF16), SDS((heads, 1, 3 * HEAD), F32)],
        (qa, ka, va, lse, ga, gx),
        [pltpu.VMEM((heads, whole, LANES), BF16)] + [pltpu.VMEM((heads, whole, LANES), F32)] * 3,
        flops=10 * heads * whole * whole * LANES,
    )


def norm1_kernel(g01, g2, w, keep, send):
    rows = keep.shape[0] // 2
    cols = g2.shape[2]
    for i in range(4):
        at = pl.ds(i * rows, rows)
        part = dot_t(g01[0, at, :], w[:, :cols])
        part = part + dot_t(g01[1, at, :], w[:, cols : 2 * cols])
        part = part + dot_t(g2[0, at, :], w[:, 2 * cols : 3 * cols])
        to = pl.ds((i // 2) * rows, rows)
        if i % 2 == 0:
            keep[to, :] = part
        else:
            send[to, :] = part.astype(BF16)


def qkv_grad(sref, normed, grads, sums, w, first, tile, bound):
    width, cols = w.shape[0], grads[0].shape[1]
    g = jnp.concatenate([dot_lt(normed[...], v) for v in grads], axis=1)
    w32 = w[:, first * cols : (first + len(grads)) * cols].astype(F32)
    rows = jnp.concatenate(sums, axis=1)
    both = jnp.sum(g * w32, axis=-1, keepdims=True)
    gshift = jnp.sum(w32 * rows, axis=-1, keepdims=True)
    lane = lane_of(width)
    old = bound[...]
    tile[...] = jnp.where(lane == HEAD, old + both, jnp.where(lane == HEAD + 1, old + gshift, old))
    ones = jnp.ones((grads[0].shape[0], LANES), BF16)
    at = pl.multiple_of(sref[0] * cols, HEAD)
    lanes = lane_of(HEAD)
    for i, v in enumerate(grads):
        col = dot_lt(v, ones)
        here = pl.ds(at + (first + i) * HEAD, HEAD)
        row = tile[here, :]
        row = jnp.where(lanes == HEAD + 2, col[:HEAD], row)
        tile[here, :] = jnp.where(lanes == HEAD + 3, col[2 * HEAD :], row)
    return g


def heads_kernel(
    fast, sref, bref, qa, ka, va, lse, ga, gx, normed, w, early, g01, send, keep, tile,
    s01, goa, dq, dk, dv, wide,
):
    attend_back_kernel(0, 2, 2, qa, ka, va, lse, ga, gx, g01, s01, goa, dq, dk, dv)
    g = qkv_grad(sref, normed, (g01[0], g01[1]), (s01[0], s01[1]), w, 0, tile, early)
    if not fast:
        rows = g.shape[0] // 2
        send[...] = g[:rows].astype(BF16)
        keep[...] = g[rows:].astype(BF16)
        return
    wide[...] = g
    y, z1, z2 = bref[0] & 1, (bref[0] >> 1) & 1, bref[0] >> 2
    per, cols = send.shape[1], g.shape[1]
    for m in range(8):
        zz1 = z1 if m & 4 else 1 - z1
        zz2 = z2 if m & 2 else 1 - z2
        for j in range(2):
            base = per * ((2 * (m & 1) + j) * 8 + 4 * zz2 + 2 * zz1)
            to = slice(j * cols, (j + 1) * cols)
            send[m, :, to] = wide[pl.ds(pl.multiple_of(base + (1 - y) * per, 8), per), :].astype(BF16)
            keep[m, :, to] = wide[pl.ds(pl.multiple_of(base + y * per, 8), per), :].astype(BF16)


def tail_kernel(
    sref, bref, qa, ka, va, lse, ga, gx, normed, g01, w, early, gn_keep, gn_send, send, keep,
    g2, s2, goa, dq, dk, dv, tile, wide,
):
    attend_back_kernel(2, 1, 1, qa, ka, va, lse, ga, gx, g2, s2, goa, dq, dk, dv)
    norm1_kernel(g01, g2, w, gn_keep, gn_send)
    g = qkv_grad(sref, normed, (g2[0],), (s2[0],), w, 2, tile, early)
    width = g.shape[0]
    lane = lane_of(width)
    val = tile[...]
    gshift = val[:, HEAD + 1 : HEAD + 2]
    ggain = (val[:, HEAD : HEAD + 1] - val[:, 1:2] * gshift) / val[:, 0:1]
    val = jnp.where(lane == HEAD, ggain, val)
    last = jnp.concatenate([g[:, LANES:], jnp.zeros((width, LANES - HEAD), F32)], axis=1)
    out = jnp.concatenate([g[:, :LANES], jnp.where(lane < HEAD, last, val)], axis=1)
    split_rows(out, wide, bref[0] & 1, send, keep)


def wide_sum(*parts):
    return sum(p.astype(F32) for p in parts[1:]) + parts[0].astype(F32)


def stage0_kernel(own_keep, own_got, oth_keep, oth_got, msg, part):
    for i in range(2):
        msg[i] = wide_sum(own_keep[i], own_got[i]).astype(BF16)
        msg[2 + i] = wide_sum(oth_keep[i], oth_got[i]).astype(BF16)
        part[i] = wide_sum(own_keep[2 + i], own_got[2 + i])
        part[2 + i] = wide_sum(oth_keep[2 + i], oth_got[2 + i])


def stage1_kernel(
    bref, keep_own, keep_oth, y1, y2, fc2, g2a, g2m, out, y3, part_0, got_0, q_send,
    msg_z, msg_y, msg_x, part_f, part_a, part_o, part_p,
):
    y, z1, z2 = bref[0] & 1, (bref[0] >> 1) & 1, bref[0] >> 2
    n = keep_own.shape[0] // 2
    for i in range(n):
        more = n // 2
        msg_z[i] = wide_sum(keep_own[i], y2[more + i]).astype(BF16)
        msg_z[n + i] = wide_sum(keep_oth[i], y1[i]).astype(BF16)
        part_f[i] = wide_sum(keep_own[n + i], y2[more + n + i])
        part_f[n + i] = wide_sum(keep_oth[n + i], y1[n + i] if i < more else y2[i - more])
        msg_y[8 + i] = q_send[i]
    rows = g2a.shape[1]
    for i in range(4):
        zz1 = z1 if i >> 1 else 1 - z1
        zz2 = z2 if i & 1 else 1 - z2
        m = 2 * zz2 + zz1
        msg_x[i] = wide_sum(out[1, m], y3[1, m]).astype(BF16)
        part_o[i] = wide_sum(out[0, m], y3[0, m])
        for k, got in enumerate((g2a, g2m)):
            at = slice(k * rows, (k + 1) * rows)
            b = 2 * m + 1 - y
            msg_y[2 * i + k] = wide_sum(fc2[b, at], got[b]).astype(BF16)
            b = 2 * m + y
            part_a[2 * i + k] = wide_sum(fc2[b, at], got[b])
    for i in range(2):
        for k in range(2):
            at = slice(k * rows, (k + 1) * rows)
            msg_x[4 + 2 * i + k] = wide_sum(part_0[2 + i, at], got_0[2 + i, at]).astype(BF16)
            part_p[2 * i + k] = wide_sum(part_0[i, at], got_0[i, at])


def stage2_kernel(
    part_f, got_z, part_a, got_y, part_o, got_x, part_p, q_keep, q2_send, msg_x, msg_z, msg_y, part_g, part_c, part_q
):
    n, _, cols = q2_send.shape
    for i in range(n):
        msg_y[i] = q2_send[i]
    for half in range(2):
        for i in range(4):
            k = 8 * half + i
            msg_x[4 * half + i] = wide_sum(part_f[k], got_z[k]).astype(BF16)
            part_g[4 * half + i] = wide_sum(part_f[k + 4], got_z[k + 4])
    for i in range(4):
        msg_z[i] = wide_sum(part_a[i], got_y[i]).astype(BF16)
        part_c[i] = wide_sum(part_a[4 + i], got_y[4 + i])
        msg_z[6 + i] = wide_sum(q_keep[i], got_y[8 + i]).astype(BF16)
        part_c[6 + i] = wide_sum(q_keep[4 + i], got_y[12 + i])
    for i in range(2):
        msg_z[4 + i] = wide_sum(part_o[i], got_x[i]).astype(BF16)
        part_c[4 + i] = wide_sum(part_o[2 + i], got_x[2 + i])
        rest = wide_sum(part_p[i], got_x[4 + i]).astype(BF16)
        for k in range(3):
            msg_y[n + 3 * i + k] = rest[:, k * cols : (k + 1) * cols]
        part_q[i] = wide_sum(part_p[2 + i], got_x[6 + i])


def stage3_kernel(bref, part_g, got_x, part_c, got_z, q_keep, got_y, msg, kept, z1, z2, z3, q_kept):
    for half in range(2):
        for i in range(2):
            k, other = 4 * half + i, 4 * (1 - half) + i
            msg[2 * half + i] = wide_sum(part_g[k], got_x[other]).astype(BF16)
            kept[2 * half + i] = wide_sum(part_g[k + 2], got_x[other + 2])
    for to, a, b in ((4, 0, 2), (5, 1, 3), (6, 4, 5), (7, 6, 8), (8, 7, 9)):
        msg[to] = wide_sum(part_c[a], got_z[a]).astype(BF16)
        kept[to] = wide_sum(part_c[b], got_z[b])
    q = bref[0] >> 1
    for r in range(4):
        for k, ref in enumerate((q_kept, z1, z2, z3)):
            m = r * 4 + (q ^ k)
            ref[r] = wide_sum(q_keep[m], got_y[m]).astype(ref.dtype)


def shift_kernel(keep, got, send):
    rows = send.shape[0]
    send[...] = wide_sum(keep[rows:, :], got[rows:, :]).astype(BF16)


def sums_kernel(kept, got, part_q, got_q, swap_send, swap_keep, fc2, out):
    per = out.shape[0]
    for half in range(2):
        at = pl.ds(half * per, per)
        swap_send[at, :] = wide_sum(kept[2 * half], got[2 * half]).astype(BF16)
        swap_keep[at, :] = wide_sum(kept[2 * half + 1], got[2 * half + 1])
        fc2[at, :] = wide_sum(kept[4 + half], got[4 + half])
        cols = got_q.shape[2]
        for k in range(3):
            at3 = slice(k * cols, (k + 1) * cols)
            fc2[pl.ds((2 + half) * per, per), at3] = wide_sum(part_q[half, :, at3], got_q[16 + 3 * half + k])
    out[...] = wide_sum(kept[6], got[6])


def owner_kernel(sref, most, got, kept, z1, z2, z3, s1, s2, s3, own, every):
    s = sref[0]
    cols = most.shape[2] // 2
    for m in range(4):
        at = slice((m % 2) * cols, (m % 2 + 1) * cols)
        every[m, :, :cols] = wide_sum(most[7 + m // 2, :, at], got[7 + m // 2, :, at])
        every[m, :, cols:] = wide_sum(kept[m], z1[m], z2[m], z3[m])
    for k, ref in enumerate((own, s1, s2, s3)):
        ref[...] = every[s ^ k].astype(ref.dtype)


def final_kernel(k0, c0, x0, p0, s0, gmid, gain, gpat, gspe):
    rows, width = x0.shape
    count = gpat.shape[0]
    hat, scale = normalize(tokens_of(p0, s0))
    g = wide_sum(k0[:rows], c0[:rows], x0[...])
    res = gmid[...] + normalize_back(g * gain[0:1, :], hat, scale)
    gpat[...] = res[:count]
    gspe[...] = res[count : count + gspe.shape[0]]


def collect_kernel(
    sref, own, g1, g2, g3, swap_keep, swap_got, out, gains, shifts, biases, fc1_bias, fc1, every
):
    s = sref[0]
    per, hidden = swap_keep.shape[0] // 2, swap_keep.shape[1]
    for j, value in ((0, swap_keep[:per]), (2, swap_keep[per:]), (1, swap_got[:per]), (3, swap_got[per:])):
        fc1[:, pl.ds(pl.multiple_of((s ^ j) * hidden, LANES), hidden)] = value.astype(F32)
    for k, ref in enumerate((own, g1, g2, g3)):
        every[k] = ref[...].astype(F32)
    pieces = [every[s ^ a] for a in range(4)]

    def part(u):
        j, a, h = u // 12, (u // 3) % 4, u % 3
        e = 3 * h + j
        return pieces[a][:, (e // 2) * LANES : (e // 2 + 1) * LANES], e % 2

    lane = lane_of(out.shape[0])
    for t in range(out.shape[1] // LANES):
        (low, lo), (high, hi) = part(2 * t), part(2 * t + 1)
        low = pltpu.roll(low, HEAD, 1) if lo else low
        high = high if hi else pltpu.roll(high, HEAD, 1)
        out[:, t * LANES : (t + 1) * LANES] = jnp.where(lane < HEAD, low, high)
    tail = 4 * LANES
    vec = wide_sum(*[every[k, :, tail:] for k in range(4)])
    vec = jnp.concatenate([vec, jnp.zeros((LANES - per, LANES), F32)], axis=0).T[:, :per]
    for ref, lines in ((gains, (0, 4)), (shifts, (1, 5)), (biases, (2, 3, 7, 6)), (fc1_bias, (8, 9, 10, 11))):
        for i, k in enumerate(lines):
            ref[i : i + 1, :] = vec[HEAD + k : HEAD + k + 1]


def pick(arr, index, axis):
    return lax.dynamic_index_in_dim(arr, index, axis, keepdims=False)


def total(parts):
    out = parts[0].astype(F32)
    for part in parts[1:]:
        out = out + part.astype(F32)
    return out


def swap(kind, v, mask):
    return lax.ppermute(v, kind, [(i, i ^ mask) for i in range(lax.axis_size(kind))])


def swap_seq(v, mask):
    return swap("seq", v, mask)


def after(value, *first):
    return lax.optimization_barrier((value, first))[0]


def bits_of(kind):
    return lax.axis_size(kind).bit_length() - 1


def split_bits(arr, axis, count):
    shape = arr.shape
    return arr.reshape(shape[:axis] + (2,) * count + shape[axis + 1 :])


def to_send(parts, axis, bit, kind):
    own = (lax.axis_index(kind) >> bit) & 1
    send = total([pick(p, 1 - own, axis) for p in parts]).astype(BF16)
    return send, [pick(p, own, axis) for p in parts]


def send_four(parts, axis, low):
    own = (lax.axis_index("batch") >> low) & 3

    def quarter(p, k):
        return pick(pick(p, k >> 1, axis), k & 1, axis)

    sends = [total([quarter(p, own ^ k) for p in parts]).astype(BF16) for k in (1, 2, 3)]
    return sends, [quarter(p, own) for p in parts]


def swap_four(sends, low):
    return [swap("batch", v, k << low) for k, v in zip((1, 2, 3), sends)]


def sum_rest(parts, axis, low):
    top = bits_of("batch")
    while low < top:
        if low + 1 < top:
            sends, kept = send_four(parts, axis + top - low - 2, low)
            parts, low = kept + swap_four(sends, low), low + 2
        else:
            send, kept = to_send(parts, axis, low, "batch")
            parts, low = kept + [swap("batch", send, 1 << low)], low + 1
    return total(parts)


def body(
    patches,
    specials,
    segment_ids,
    special_order,
    keep_mask,
    norm_gains,
    norm_shifts,
    w_qkv,
    biases,
    w_out,
    w_fc1,
    fc1_bias,
    w_fc2,
    cot_patches,
    cot_specials,
):
    count, width = patches.shape[1:]
    extra = specials.shape[1]
    images = keep_mask.shape[1] // 2
    block = count + PAD
    chip = 2 * block
    whole = 4 * block
    cols = OWN * HEAD
    hidden = w_fc1.shape[1] // 4
    s = lax.axis_index("seq")
    sidx = s.astype(jnp.int32).reshape(1)
    bidx = lax.axis_index("batch").astype(jnp.int32).reshape(1)
    nb = lax.axis_size("batch")
    nbits = bits_of("batch")

    own_p, own_cot = patches[0], cot_patches[0]
    got_px = swap_seq(own_p, 2)
    got_pc = swap_seq(own_p, 1)
    (small,) = call(
        small_kernel,
        [SDS((32, width), BF16)],
        (specials[0], segment_ids, special_order, cot_specials[0]),
        [pltpu.VMEM((extra, width), BF16), pltpu.VMEM((1, count), jnp.int32), pltpu.VMEM((1, extra), jnp.int32)]
        + [pltpu.VMEM((extra, width), BF16), pltpu.VMEM((32, width), F32), pltpu.SemaphoreType.DMA((4,))],
        far=(0, 1, 2, 3),
    )
    got_sx = swap_seq(small, 2)
    got_sc = swap_seq(small, 1)
    cot_c = swap_seq(own_cot, 1)
    fb = fc1_bias.reshape(1, -1)
    sidx, bidx, small = lax.optimization_barrier((sidx, bidx, small))
    w_own, bias_own = call(
        prep_kernel,
        [SDS((width, 5 * LANES), BF16), SDS((1, 5 * LANES), F32)],
        (sidx, w_qkv, biases),
        [pltpu.VMEM((3 * OWN, width, LANES), BF16), pltpu.VMEM(biases.shape, F32)]
        + [pltpu.SemaphoreType.DMA((3 * OWN + 1,))],
        scalars=1,
        far=(1, 2),
    )
    headed = SDS((OWN, chip, LANES), BF16)
    q0, k0, v0, n0, toks, keeps = call(
        project_kernel,
        [headed] * 3 + [SDS((chip, width), BF16), SDS((chip, width), BF16), SDS((chip, LANES), F32)],
        (keep_mask, own_p, small, got_pc, got_sc, norm_gains, norm_shifts, w_own, bias_own),
        flops=2 * chip * width * 3 * cols,
        scalars=1,
    )
    got_px, got_sx, n0 = lax.optimization_barrier((got_px, got_sx, n0))
    got_pd = swap_seq(got_px, 1)
    got_sd = swap_seq(got_sx, 1)

    headed = SDS((OWN, whole, LANES), BF16)
    heads32 = SDS((OWN, chip, LANES), F32)
    qa, ka, va, att_send, other, normed = call(
        attend_first_kernel,
        [headed] * 3 + [SDS((chip, cols), BF16), heads32, SDS((whole, width), BF16)],
        (q0, k0, v0, n0, got_px, got_sx, got_pd, got_sd, norm_gains, norm_shifts, w_own, bias_own),
        flops=2 * chip * width * 3 * cols + 2 * OWN * whole * whole * LANES,
    )
    a2 = swap_seq(att_send, 2)
    a0, lse = call(
        attend_second_kernel,
        [SDS((chip, cols), BF16), SDS((OWN, 3, 8, whole // 3), F32)],
        (qa, ka, va, other),
        [pltpu.VMEM((OWN, chip, LANES), F32)],
        flops=2 * OWN * whole * whole * LANES,
    )
    a1 = swap_seq(a0, 1)
    a3 = swap_seq(a2, 1)

    middle, normed2, gb2, w1, w2 = call(
        middle_kernel,
        [SDS((chip, width), F32), SDS((chip, width), BF16), SDS((chip, width), BF16)]
        + [SDS((width, hidden), BF16), SDS((hidden, width), BF16)],
        (sidx, a0, a1, a2, a3, toks, keeps, own_cot, cot_c, small, got_sc, w_out, biases, norm_gains, norm_shifts)
        + (w_fc1, w_fc2),
        [pltpu.SemaphoreType.DMA((2,))],
        flops=2 * chip * width * width,
        scalars=1,
        far=(15, 16),
    )
    per = width // (4 * nb)
    fast = nb == 8
    fc2_a, fc2_m, zo_send, zo_keep, y1, y_rest, keep_oth, fb_oth, b2, gn, w1, w2 = feed(
        False, fast, per, sidx, bidx, normed2, gb2, w1, fb, w2, (w_fc1, w_fc2)
    )
    got2a = swap_seq(fc2_a, 2)
    if not fast:
        y1, keep_oth = by_batch_bit(jnp.concatenate([y1, keep_oth], axis=0), per)
    got_y1 = swap("batch", y1, 1)
    got_zo = swap("batch", zo_send, 2) if fast else zo_send
    ahead = (got2a, got_y1, got_zo)
    fc2_keep, zn_send, zn_keep, y2, keep_own, fb_own, b2_keep, b2_send, gn_keep, gn_send = feed(
        True, fast, per, sidx, bidx, normed2, gb2, w1, fb, w2, (b2, gn, y_rest)
    )
    if not fast:
        y2, keep_own = by_batch_bit(jnp.concatenate([y2, keep_own], axis=0), per)
    gn_send, b2_send, zn_send, y2, (got2a, got_y1, got_zo) = lax.optimization_barrier(
        (gn_send, b2_send, zn_send, y2, ahead)
    )
    gn_got = swap_seq(gn_send, 1)
    b2_got = swap_seq(b2_send, 1)
    got_zn = swap("batch", zn_send, 2) if fast else zn_send
    got_y2 = swap("batch", y2, 1)

    gmid, gbr, gatt_send, line_sums = call(
        middle_back_kernel,
        [SDS((block, width), F32), SDS((chip, width), BF16), SDS((chip, cols), BF16), SDS((8, width), F32)],
        (sidx, gn_keep, gn_got, middle, keeps, own_cot, cot_c, small, got_sc, w_out, norm_gains, gb2),
        flops=2 * chip * width * cols,
        scalars=1,
    )
    gatt_x = swap_seq(gatt_send, 2)
    if fast:
        split = SDS((2, cols // (2 * per), per, width), BF16)
    else:
        split = SDS((2, cols // 2, width), BF16)
    gatt, go_send, go_keep, early, opat, ospe = call(
        functools.partial(branch_back_kernel, per),
        [SDS((chip, cols), BF16), split, split, SDS((width, LANES), F32)]
        + [SDS((count, width), BF16), SDS((extra, width), BF16)],
        (sidx, bidx, gbr, w_out, a0, a2, middle, keeps, b2_keep, b2_got, biases, norm_gains, norm_shifts)
        + (line_sums, fb_own, fb_oth),
        [pltpu.VMEM((hidden, LANES), F32), pltpu.VMEM((cols, width), F32)],
        flops=6 * chip * width * cols,
        scalars=2,
    )
    if not fast:
        halves = [by_batch_bit(jnp.concatenate([go_send[j], go_keep[j]], axis=0), per) for j in range(2)]
        go_send, go_keep = [jnp.stack([halves[j][k] for j in range(2)]) for k in range(2)]
    got_o = swap("batch", go_send, 1)
    msg_0, part_0 = None, None
    if fast:
        msg_0, part_0 = call(
            stage0_kernel,
            [SDS(zn_keep.shape, BF16), SDS(zn_keep.shape, F32)],
            (zn_keep, after(got_zn, go_send), zo_keep, got_zo),
        )
        gatt_x = after(gatt_x, msg_0)
    gatt_x, fc2_m = lax.optimization_barrier((after(gatt_x, go_send), fc2_m))
    got2m = swap_seq(fc2_m, 2)
    pairs = (keep_own, keep_oth, got_y1, got_y2)

    def heads_scratch(heads):
        return [pltpu.VMEM((heads, whole, LANES), BF16)] + [pltpu.VMEM((heads, whole, LANES), F32)] * 3

    def first_heads(lse):
        if fast:
            split = [SDS((8, per, 4 * cols), BF16)] * 2
        else:
            split = [SDS((width // 2, 2 * cols), BF16)] * 2
        return call(
            functools.partial(heads_kernel, fast),
            [SDS((2, whole, cols), BF16)] + split + [SDS((width, LANES), F32)],
            (sidx, bidx, qa, ka, va, lse, gatt, gatt_x, normed, w_own, early),
            [pltpu.VMEM((2, 1, cols), F32)] + heads_scratch(2) + [pltpu.VMEM((width, 2 * cols), F32)],
            flops=20 * whole * whole * LANES,
            scalars=2,
            room=20,
        )

    def tail_part(lse, g01, tile):
        wide = cols + HEAD
        if fast:
            outs = [SDS((width // (2 * per), per, wide), BF16)] * 2
        else:
            outs = [SDS((width // 2, wide), BF16)] * 2
        return call(
            tail_kernel,
            [SDS((chip, width), F32), SDS((chip, width), BF16)] + outs,
            (sidx, bidx, qa, ka, va, lse, gatt, gatt_x, normed, g01, w_own, tile),
            [pltpu.VMEM((1, whole, cols), BF16), pltpu.VMEM((1, 1, cols), F32)]
            + heads_scratch(1)
            + [pltpu.VMEM((width, LANES), F32), pltpu.VMEM((width, wide), F32)],
            flops=10 * whole * whole * LANES,
            scalars=2,
            room=20,
        )

    rest = (sidx, bidx, per, block, chip, hidden, cols, count, extra, width)
    zs = (zn_send, zn_keep, zo_send, zo_keep, msg_0, part_0)
    reduce_all = reduce_eight if fast else reduce_any
    out_fc2, out_out, out_fc1, out_qkv, smalls, gpat, gspe = reduce_all(
        rest, pairs, (fc2_keep, got2a, got2m, zs), (go_keep, got_o), lse, gatt_x,
        first_heads, tail_part, (own_p, small), gmid, norm_gains,
    )
    grad_gains, grad_shifts, grad_biases, grad_fc1_bias = smalls
    return (
        opat[None],
        ospe[None],
        gpat[None],
        gspe[None],
        grad_gains,
        grad_shifts,
        out_qkv,
        grad_biases,
        out_out,
        out_fc1,
        grad_fc1_bias.reshape(-1),
        out_fc2,
    )


def reduce_eight(
    rest, pairs, twos, outs, lse, gatt_x, first_heads, tail_part, pay, gmid, gains
):
    sidx, bidx, per, block, chip, hidden, cols, count, extra, width = rest
    fc2_keep, got2a, got2m, zs = twos
    go_keep, got_o = outs
    deep = hidden // 8
    got_0 = swap("batch", zs[4], 4)
    part_0 = zs[5]
    g01, q01_send, q01_keep, tile = first_heads(after(lse, gatt_x))
    g01, got_y2, got2m, got_o, got_0 = lax.optimization_barrier((g01, pairs[3], got2m, got_o, got_0))
    keep_own, keep_oth, got_y1 = pairs[:3]

    def blocks(n, dtype=BF16):
        return SDS((n, per, width), dtype)

    msg_z, msg_y, msg_x, part_f, part_a, part_o, part_p = call(
        stage1_kernel,
        [blocks(16), blocks(16), blocks(8), blocks(16, F32), blocks(8, F32), blocks(4, F32), blocks(4, F32)],
        (bidx, keep_own, keep_oth, got_y1, got_y2, fc2_keep, got2a, got2m, go_keep, got_o, part_0, got_0)
        + (q01_send,),
        scalars=1,
    )
    msg_z, msg_y, msg_x, lse = lax.optimization_barrier((msg_z, msg_y, msg_x, after(lse, g01)))
    got_z = swap("batch", msg_z, 2)
    got_y = swap("batch", msg_y, 1)
    got_x = swap_seq(msg_x, 2)
    gn1_keep, gn1_send, q_send, q_keep = tail_part(lse, g01, tile)
    gn1_send, got_x, got_y, got_z = lax.optimization_barrier((gn1_send, got_x, got_y, got_z))
    gn1_c = swap_seq(gn1_send, 1)
    part = SDS((22, per, cols + HEAD), BF16)
    msg_x, msg_z, msg_y, part_g, part_c, part_q = call(
        stage2_kernel,
        [blocks(8), blocks(10), part, blocks(8, F32), blocks(10, F32), blocks(2, F32)],
        (part_f, got_z, part_a, got_y, part_o, got_x, part_p, q01_keep, q_send),
    )
    got_x = swap_seq(msg_x, 2)
    got_z = swap("batch", msg_z, 2)
    got_y = swap("batch", msg_y, 1)
    (xsend,) = call(shift_kernel, [SDS((block, width), BF16)], (after(gn1_keep, msg_x), gn1_c))
    gn1_x = swap_seq(xsend, 2)
    quarter = SDS((4, per, cols + HEAD), BF16)
    msg, kept, q1, q2, q3, q_kept = call(
        stage3_kernel,
        [blocks(9), blocks(9, F32), quarter, quarter, quarter, SDS(quarter.shape, F32)],
        (bidx, part_g, after(got_x, xsend), part_c, got_z, q_keep, got_y),
        scalars=1,
    )
    got_last = swap("batch", msg, 4)
    got_qz = swap_four((q1, q2, q3), 1)
    gpat, gspe = call(
        final_kernel,
        [SDS((count, width), F32), SDS((extra, width), F32)],
        (gn1_keep, gn1_c, after(gn1_x, q1), *pay, gmid, gains),
    )
    got_last = after(got_last, gpat)
    row = SDS((per, 5 * LANES), BF16)
    s1, s2, s3, own = call(
        owner_kernel,
        [row, row, row, SDS(row.shape, F32)],
        (sidx, kept, got_last, q_kept, *got_qz),
        [pltpu.VMEM((4, per, 5 * LANES), F32)],
        scalars=1,
    )
    swap_send, swap_keep, out_fc2, out_out = call(
        sums_kernel,
        [SDS((2 * per, width), BF16), SDS((2 * per, width), F32), SDS((deep, width), F32), SDS((per, width), F32)],
        (kept, after(got_last, s1), part_q, got_y),
    )
    swap_got = swap_seq(swap_send, 1)
    gots = [swap_seq(v, k) for k, v in ((1, s1), (2, s2), (3, s3))]
    lines = [SDS((n, per), F32) for n in (2, 2, 4, 4)]
    out_qkv, *smalls, out_fc1 = call(
        collect_kernel,
        [SDS((per, 3 * width), F32), *lines, SDS((per, 4 * hidden), F32)],
        (sidx, own, *gots, swap_keep, swap_got),
        [pltpu.VMEM((4, per, 5 * LANES), F32)],
        scalars=1,
    )
    return out_fc2, out_out, out_fc1, out_qkv, smalls, gpat, gspe


def reduce_any(
    rest, pairs, twos, outs, lse, gatt_x, first_heads, tail_part, pay, gmid, gains
):
    sidx, bidx, per, block, chip, hidden, cols, count, extra, width = rest
    s = lax.axis_index("seq")
    nb = lax.axis_size("batch")
    nbits = bits_of("batch")
    low = nbits - 1
    fc2_keep, got2a, got2m, zs = twos
    go_keep, got_o = outs
    keep_own, keep_oth, got_oth, got_own = [
        split_bits(p.reshape(2, 2, nb // 2, per, hidden), 2, low) for p in pairs
    ]
    g01, q01_top, q01_low, tile = first_heads(lse)
    send_own, parts_own = to_send([keep_own, got_own], 0, 1, "seq")
    send_oth, parts_oth = to_send([keep_oth, got_oth], 0, 1, "seq")
    got_b = swap_seq(jnp.concatenate([send_own, send_oth], axis=-1), 2)
    sum_own = sum_rest(parts_own + [got_b[..., hidden:]], 1, 1)
    sum_oth = sum_rest(parts_oth + [got_b[..., :hidden]], 1, 1)
    own_c = s & 1
    other = jnp.concatenate([pick(sum_own, 1 - own_c, 0), pick(sum_oth, 1 - own_c, 0)], axis=-1)
    got = swap_seq(other.astype(BF16), 1).astype(F32)
    rel = jnp.stack([pick(sum_own, own_c, 0), got[:, :hidden], pick(sum_oth, own_c, 0), got[:, hidden:]])
    out_fc1 = jnp.concatenate([pick(rel, s ^ a, 0) for a in range(4)], axis=1)
    zn_send, zn_keep, zo_send, zo_keep = zs[:4]
    got2 = jnp.concatenate([got2a, got2m, swap_seq(jnp.concatenate([zo_send, zo_keep], axis=0), 2)], axis=0)
    fc2_keep = jnp.concatenate([fc2_keep, zn_send, zn_keep], axis=0)
    parts = [split_bits(p.reshape(nb, -1, width), 0, nbits) for p in (fc2_keep, got2)]
    out_fc2 = sum_rest(parts, 0, 0)
    parts = [split_bits(p.reshape(2, nb // 2, per, width), 1, low) for p in (go_keep, got_o)]
    parts = [p[0] for p in parts] + [swap_seq(total([p[1] for p in parts]).astype(BF16), 2)]
    out_out = sum_rest(parts, 0, 1)
    gn1_keep, gn1_send, q2_top, q2_low = tail_part(lse, g01, tile)
    q_all = [jnp.concatenate(v, axis=1) for v in ((q01_top, q2_top), (q01_low, q2_low))]
    q_send, q_keep = by_batch_bit(jnp.concatenate(q_all, axis=0), per)
    gn1_c = swap_seq(gn1_send, 1)
    gn1_x = swap_seq((gn1_keep[block:] + gn1_c[block:].astype(F32)).astype(BF16), 2)
    gpat, gspe = call(
        final_kernel,
        [SDS((count, width), F32), SDS((extra, width), F32)],
        (gn1_keep, gn1_c, gn1_x, *pay, gmid, gains),
    )
    wide = 5 * LANES
    parts = [split_bits(p.reshape(4, nb // 2, per, wide), 1, low) for p in (q_keep, swap("batch", q_send, 1))]
    sum_q = sum_rest(parts, 1, 1)
    pieces = [pick(sum_q, s, 0)] + [
        swap_seq(pick(sum_q, s ^ j, 0).astype(BF16), j).astype(F32) for j in (1, 2, 3)
    ]
    rel = jnp.stack([p[:, : 3 * cols] for p in pieces])
    absolute = jnp.stack([pick(rel, s ^ a, 0) for a in range(4)], axis=1)
    out_qkv = absolute.reshape(-1, 4, OWN, 3, HEAD).transpose(0, 3, 1, 2, 4).reshape(-1, 3 * width)
    vec = total([p[:, 3 * cols :] for p in pieces]).T
    smalls = [vec[jnp.array(k)] for k in ((0, 4), (1, 5), (2, 3, 7, 6), (8, 9, 10, 11))]
    return out_fc2, out_out, out_fc1, out_qkv, smalls, gpat, gspe


def solution(mesh):
    tok = P("batch", "seq", None)
    ids = P("batch", "seq")
    split = P(None, ("seq", "batch"))
    rows = P(("seq", "batch"), None)
    return jax.shard_map(
        body,
        mesh=mesh,
        in_specs=(tok, tok, ids, ids, P("batch", None)) + (P(),) * 8 + (tok, tok),
        out_specs=(tok, tok, tok, tok, split, split, rows, split, rows, rows, P(("seq", "batch")), rows),
        check_vma=False,
    )
```

```python
import functools

import jax
import jax.numpy as jnp
from jax import lax
from jax.experimental import pallas as pl
from jax.experimental.pallas import tpu as pltpu
from jax.sharding import PartitionSpec as P

HEADS = 12
HEAD = 64
PAD = 32
SPECIAL = 4
LANES = 128
OWN = 3
FAR = -(2.0**100)
F32 = jnp.float32
BF16 = jnp.bfloat16
SDS = jax.ShapeDtypeStruct


def dot(a, b):
    return jnp.dot(a, b, preferred_element_type=F32)


def dot_t(a, b):
    return lax.dot_general(a, b, (((1,), (1,)), ((), ())), preferred_element_type=F32)


def dot_lt(a, b):
    return lax.dot_general(a, b, (((0,), (0,)), ((), ())), preferred_element_type=F32)


def normalize(v):
    center = v - jnp.mean(v, axis=-1, keepdims=True)
    spread = jnp.mean(center * center, axis=-1, keepdims=True)
    scale = lax.rsqrt(spread + 1e-06)
    return center * scale, scale


def normalize_back(grad_hat, hat, scale):
    mean_g = jnp.mean(grad_hat, axis=-1, keepdims=True)
    mean_gh = jnp.mean(grad_hat * hat, axis=-1, keepdims=True)
    return scale * (grad_hat - mean_g - hat * mean_gh)


def gelu_pair(v):
    half = 0.5 * (1.0 + lax.erf(v * 0.5**0.5))
    slope = half + v * jnp.exp(-0.5 * v * v) * 0.3989422804014327
    return v * half, slope


def lane_of(rows):
    return lax.broadcasted_iota(jnp.int32, (rows, LANES), 1)


def unpack_head(tiles, e):
    tile = tiles[:, (e // 2) * LANES : (e // 2 + 1) * LANES]
    return tile if e % 2 == 0 else pltpu.roll(tile, HEAD, 1)


def pack_pair(low, high):
    return jnp.where(lane_of(low.shape[0]) < HEAD, low, pltpu.roll(high, HEAD, 1))


def vmem():
    return pl.BlockSpec(memory_space=pltpu.VMEM)


def smem():
    return pl.BlockSpec(memory_space=pltpu.SMEM)


def call(kernel, outs, args, scratch=(), flops=0, scalars=0, room=16, far=()):
    args = [pltpu.with_memory_space_constraint(a, pltpu.HBM) if i in far else a for i, a in enumerate(args)]
    nbytes = sum(a.size * a.dtype.itemsize for a in args)
    nbytes += sum(o.size * o.dtype.itemsize for o in outs)
    return pl.pallas_call(
        kernel,
        out_shape=outs,
        in_specs=[
            smem() if i < scalars else pl.BlockSpec(memory_space=pltpu.HBM) if i in far else vmem()
            for i in range(len(args))
        ],
        out_specs=[vmem()] * len(outs),
        scratch_shapes=list(scratch),
        compiler_params=pltpu.CompilerParams(vmem_limit_bytes=room << 20),
        cost_estimate=pl.CostEstimate(flops=flops, bytes_accessed=nbytes, transcendentals=0),
    )(*args)


def prep_kernel(sref, w, biases, w_own, bias_own, tiles, lines, sems):
    width = w.shape[0]
    per = width // HEAD
    spots = [per * (e % 3) + OWN * sref[0] + e // 3 for e in range(3 * OWN)]
    copies = [pltpu.make_async_copy(biases, lines, sems.at[3 * OWN])]
    for e, u in enumerate(spots):
        tile = w.at[:, pl.ds(pl.multiple_of((u >> 1) * LANES, LANES), LANES)]
        copies.append(pltpu.make_async_copy(tile, tiles.at[e], sems.at[e]))
    for copy in copies:
        copy.start()
    copies[0].wait()
    line = lax.broadcasted_iota(jnp.int32, (1, LANES), 1)
    for t in range((3 * OWN + 1) // 2):
        out, bias = jnp.zeros((width, LANES), F32), jnp.zeros((1, LANES), F32)
        for dest in range(2):
            e = 2 * t + dest
            if e == 3 * OWN:
                continue
            copies[1 + e].wait()
            u, j = spots[e], e % 3
            side = (lane_of(width) >= HEAD) == (dest == 1)
            moved = jnp.broadcast_to((u & 1) != dest, (1, LANES))
            tile = tiles[e].astype(F32)
            tile = jnp.where(moved, pltpu.roll(tile, HEAD, 1), tile)
            out = jnp.where(side, tile, out)
            if j != 1:
                v = OWN * sref[0] + e // 3
                tile = lines[j // 2 : j // 2 + 1, pl.ds(pl.multiple_of((v >> 1) * LANES, LANES), LANES)]
                tile = jnp.broadcast_to(tile, (8, LANES))
                away = jnp.broadcast_to((v & 1) != dest, (8, LANES))
                tile = jnp.where(away, pltpu.roll(tile, HEAD, 1), tile)[:1]
                bias = jnp.where((line >= HEAD) == (dest == 1), tile, bias)
        w_own[:, t * LANES : (t + 1) * LANES] = out.astype(BF16)
        bias_own[:, t * LANES : (t + 1) * LANES] = bias


def small_kernel(specials_in, segments_in, order_in, cots_in, small, specials, segments, order, cots, wide, sems):
    pairs = ((specials_in, specials), (segments_in, segments), (order_in, order), (cots_in, cots))
    copies = [pltpu.make_async_copy(src, dst, sems.at[i]) for i, (src, dst) in enumerate(pairs)]
    for copy in copies:
        copy.start()
    extra, width = specials.shape
    count = segments.shape[1]
    wide[...] = jnp.zeros_like(wide)
    wide[extra : extra + 1, :] = jnp.full((1, width), -1.0, F32)
    for copy in copies:
        copy.wait()
    wide[:extra, :] = specials[...].astype(F32)
    wide[16 : 16 + extra, :] = cots[...].astype(F32)
    wide[extra : extra + 1, :count] = segments[...].astype(F32)
    wide[extra : extra + 1, count : count + extra] = (order[...] >> 1).astype(F32)
    small[...] = wide[...].astype(BF16)


def tokens_of(patches, small):
    parts = [patches[...].astype(F32), small[:16, :].astype(F32)]
    return jnp.concatenate(parts + [jnp.zeros((PAD - 16, patches.shape[1]), F32)], axis=0)


def cots_of(patches, small):
    parts = [patches[...].astype(F32), small[16:, :].astype(F32)]
    return jnp.concatenate(parts + [jnp.zeros((PAD - 16, patches.shape[1]), F32)], axis=0)


def images_of(small, rows):
    size = -(-rows // LANES) * LANES
    line = small[:16, :size].astype(F32)[SPECIAL : SPECIAL + 1]
    return jnp.broadcast_to(line, (LANES, size)).T[:rows]


def project(patches, small, gain, shift, w, bias, at, qa, ka, va, normed):
    tok = tokens_of(patches, small)
    rows = tok.shape[0]
    lane = lane_of(rows)
    hat, _ = normalize(tok)
    nrm = (hat * gain[0:1, :] + shift[0:1, :]).astype(BF16)
    normed[at, :] = nrm
    qkv = dot(nrm, w[...]) + bias[...]
    image = images_of(small, rows)
    hot = jnp.where((lane >= HEAD) & (image == (lane - HEAD).astype(F32)), 1.0, 0.0)
    far = jnp.where((lane >= HEAD) & (lane < HEAD + 8) & (hot == 0.0), FAR, 0.0)
    one = jnp.where(lane == HEAD, 1.0, 0.0)
    for h in range(OWN):
        q = unpack_head(qkv, 3 * h) * HEAD**-0.5
        qa[h, at, :] = jnp.where(lane < HEAD, q, hot).astype(BF16)
        ka[h, at, :] = jnp.where(lane < HEAD, unpack_head(qkv, 3 * h + 1), far).astype(BF16)
        va[h, at, :] = jnp.where(lane < HEAD, unpack_head(qkv, 3 * h + 2), one).astype(BF16)
    return tok, image


def project_kernel(flags, p0, s0, p1, s1, gain, shift, w, bias, qa, ka, va, normed, toks, keeps):
    rows = normed.shape[0] // 2
    lane = lane_of(rows)
    for i, (p, small) in enumerate(((p0, s0), (p1, s1))):
        at = pl.ds(i * rows, rows)
        tok, image = project(p, small, gain, shift, w, bias, at, qa, ka, va, normed)
        toks[at, :] = tok.astype(BF16)
        keep = jnp.zeros((rows, LANES), F32)
        half = flags.shape[1] // 2
        for j in range(half):
            first = flags[0, j].astype(F32) / 0.75
            second = flags[0, half + j].astype(F32) / 0.75
            keep = jnp.where(image == float(j), jnp.where(lane == 0, first, second), keep)
        keeps[at, :] = keep


def attend_block(h, at, keys, values, queries, oacc):
    sc = dot_t(queries[h, at, :], keys[h])
    top = jnp.max(sc, axis=-1, keepdims=True)
    e = jnp.exp(sc - top).astype(BF16)
    o = dot(e, values[h])
    tot = o[:, HEAD : HEAD + 1]
    mark = jnp.where(lane_of(o.shape[0]) == HEAD + 1, top + jnp.log(tot), o * (1.0 / tot))
    return mark


def attend_first_kernel(
    q0, k0, v0, n0, p2, s2, p3, s3, gain, shift, w, bias, qa, ka, va, send, oacc, normed
):
    half = n0.shape[0]
    rows = half // 2
    own = pl.ds(0, half)
    for h in range(OWN):
        qa[h, own, :] = q0[h]
        ka[h, own, :] = k0[h]
        va[h, own, :] = v0[h]
    normed[own, :] = n0[...]
    for i, (p, small) in enumerate(((p2, s2), (p3, s3))):
        project(p, small, gain, shift, w, bias, pl.ds(half + i * rows, rows), qa, ka, va, normed)

    def block(i, carry):
        h, b = i // 2, i % 2
        at = pl.ds(pl.multiple_of(half + b * rows, 16), rows)
        oacc[h, pl.ds(pl.multiple_of(b * rows, 16), rows), :] = attend_block(h, at, ka, va, qa, oacc)
        return carry

    lax.fori_loop(0, 2 * OWN, block, 0, unroll=3)
    gather_heads(oacc, send)


def gather_heads(oacc, out):
    out[:, :LANES] = pack_pair(oacc[0], oacc[1]).astype(BF16)
    out[:, LANES:] = oacc[2, :, :HEAD].astype(BF16)


def attend_second_kernel(qa, ka, va, other, keep, lse, oacc):
    half = oacc.shape[1]
    rows = half // 2

    def block(i, carry):
        h, b = i // 2, i % 2
        at = pl.ds(pl.multiple_of(b * rows, 16), rows)
        oacc[h, at, :] = attend_block(h, at, ka, va, qa, oacc)
        return carry

    lax.fori_loop(0, 2 * OWN, block, 0, unroll=3)
    gather_heads(oacc, keep)
    step = 2 * half // 3
    for h in range(OWN):
        parts = [
            oacc[h, :step, :],
            jnp.concatenate([oacc[h, step:, :], other[h, : step - (half - step), :]], axis=0),
            other[h, half - step :, :],
        ]
        for b in range(3):
            lse[h, b] = jnp.broadcast_to(parts[b].T[HEAD + 1 : HEAD + 2], (8, step))


def middle_kernel(
    sref, a0, a1, a2, a3, toks, keeps, cp0, cp1, c0, c1, w_out, bias, gain, shift, w_fc1, w_fc2,
    middle, normed2, gb2, w1, w2, w3, w4, sems,
):
    s = sref[0]
    copies = fetch(s ^ 2, w_fc1, w_fc2, w1, w2, sems.at[0]) + fetch(s, w_fc1, w_fc2, w3, w4, sems.at[1])
    chip, width = toks.shape
    rows = chip // 2
    cols = a0.shape[1]
    acc = jnp.zeros((chip, width), F32) + bias[2:3, :]
    for j, a in ((0, a0), (2, a2)):
        w = w_out[pl.ds(pl.multiple_of((s ^ j) * cols, HEAD), cols), :]
        acc = acc + dot(a[...], w)
    for j, a in ((1, a1), (3, a3)):
        w = w_out[pl.ds(pl.multiple_of((s ^ j) * cols, HEAD), cols), :]
        part = dot(a[...], w)
        acc = acc + jnp.concatenate([part[rows:], part[:rows]], axis=0)
    mid = toks[...].astype(F32) + keeps[:, 0:1] * acc
    middle[...] = mid
    hat, _ = normalize(mid)
    normed2[...] = (hat * gain[1:2, :] + shift[1:2, :]).astype(BF16)
    gout = jnp.concatenate([cots_of(cp0, c0), cots_of(cp1, c1)], axis=0)
    gb2[...] = (keeps[:, 1:2] * gout).astype(BF16)
    for copy in copies:
        copy.wait()


def fetch(block, w_fc1, w_fc2, w1, w2, sems):
    size = w1.shape[1]
    at = pl.ds(pl.multiple_of(block * size, LANES), size)
    copies = [
        pltpu.make_async_copy(w_fc1.at[:, at], w1, sems.at[0]),
        pltpu.make_async_copy(w_fc2.at[at, :], w2, sems.at[1]),
    ]
    for copy in copies:
        copy.start()
    return copies


def feed_kernel(last, fast, sref, bref, normed2, gb2, fc1, bias, fc2, *refs):
    if last:
        b2_in, gn_in, y_in, g2, zb_send, zb_keep, y_send, g1_keep, gb, b2_keep, b2_send, gn_keep, gn_send, wide, wide2 = refs
    else:
        g2a, g2m, zb_send, zb_keep, y_first, y_second, g1_keep, gb, b2, gn, wide, wide2 = refs
    tokens = normed2.shape[0]
    half = tokens // 2
    block = sref[0] if last else sref[0] ^ 2
    pre = dot(normed2[...], fc1[...]) + bias[:, pl.ds(pl.multiple_of(block * fc1.shape[1], LANES), fc1.shape[1])]
    gact = dot_t(gb2[...], fc2[...])
    act, slope = gelu_pair(pre)
    act = act.astype(BF16)
    gh = (gact * slope).astype(BF16)
    grad1 = dot_lt(normed2[...], gh)
    if not fast:
        rows = grad1.shape[0] // 2
        (y_send if last else y_first)[...] = grad1[:rows].astype(BF16)
        g1_keep[...] = grad1[rows:].astype(BF16)
    else:
        x, c = sref[0] >> 1, sref[0] & 1
        y, z1, z2 = bref[0] & 1, (bref[0] >> 1) & 1, bref[0] >> 2
        wide[...] = grad1
        n, rows = g1_keep.shape[:2]
        for m in range(2 * n):
            near = [(m >> k) & 1 for k in (4, 3, 2, 1, 0)]
            yy, zz1, xx, zz2, cc = [own if r else 1 - own for own, r in zip((y, z1, x, z2, c), near)]
            base = rows * (16 * xx + 8 * cc + 4 * zz2 + 2 * zz1 + yy)
            piece = wide[pl.ds(pl.multiple_of(base, 8), rows), :].astype(BF16)
            if m >= n:
                g1_keep[m - n] = piece
            elif last:
                y_send[n // 4 + m] = piece
            elif m < 3 * n // 4:
                y_first[m] = piece
            else:
                y_second[m - 3 * n // 4] = piece
        if last:
            for m in range(n // 4):
                y_send[m] = y_in[m]
    gb[...] = jnp.sum(gh.astype(F32), axis=0, keepdims=True)
    partn = dot_t(gh, fc1[...])
    part2 = dot(act, fc2[...])
    if last:
        partn = partn + gn_in[...]
        part2 = part2 + b2_in[...]
        b2_keep[...] = part2[:half]
        b2_send[...] = part2[half:].astype(BF16)
        gn_keep[...] = partn
        gn_send[:half] = partn[half:].astype(BF16)
        gn_send[half:] = partn[:half].astype(BF16)
    else:
        b2[...] = part2
        gn[...] = partn
    grad2 = dot_lt(act, gb2[...])
    if not fast:
        rows = zb_send.shape[0]
        if last:
            g2[...] = grad2[: 2 * rows].astype(BF16)
        else:
            g2a[...] = grad2[:rows].astype(BF16)
            g2m[...] = grad2[rows : 2 * rows].astype(BF16)
        zb_send[...] = grad2[2 * rows : 3 * rows].astype(BF16)
        zb_keep[...] = grad2[3 * rows :].astype(BF16)
    else:
        deep = grad2.shape[0] // 8
        half = deep // 2
        for m in range(8):
            if last:
                g2[m] = grad2[m * deep : m * deep + half].astype(BF16)
            else:
                mid = m * deep + half // 2
                g2a[m] = grad2[m * deep : mid].astype(BF16)
                g2m[m] = grad2[mid : mid + half // 2].astype(BF16)
            wide2[pl.ds(m * half, half), :] = grad2[m * deep + half : (m + 1) * deep]
        for m in range(8):
            near = [(m >> k) & 1 for k in (2, 1, 0)]
            zz1, zz2, yy = [own if r else 1 - own for own, r in zip((z1, z2, y), near)]
            base = half * (4 * zz2 + 2 * zz1 + yy)
            piece = wide2[pl.ds(pl.multiple_of(base, 8), half), :].astype(BF16)
            (zb_keep if m >= 4 else zb_send)[m % 4] = piece


def split_rows(value, wide, bit, send, keep):
    if len(send.shape) == 2:
        rows = value.shape[0] // 2
        send[...] = value[:rows].astype(BF16)
        keep[...] = value[rows:].astype(BF16)
        return
    wide[...] = value
    rows = send.shape[1]
    for m in range(send.shape[0]):
        base = 2 * m * rows
        send[m] = wide[pl.ds(pl.multiple_of(base + (1 - bit) * rows, 8), rows), :].astype(BF16)
        keep[m] = wide[pl.ds(pl.multiple_of(base + bit * rows, 8), rows), :].astype(BF16)


def feed(last, fast, per, sidx, bidx, normed2, gb2, fc1, bias, fc2, prev=()):
    tokens, width = normed2.shape
    hidden = fc1.shape[1]
    pairs = width // (2 * per)
    deep = hidden // 8
    if fast:
        outs = [SDS((8, deep // 2, width), BF16)] if last else [SDS((8, deep // 4, width), BF16)] * 2
        outs += [SDS((4, deep // 2, width), BF16)] * 2
    else:
        outs = [SDS((hidden // 2, width), BF16)] if last else [SDS((hidden // 4, width), BF16)] * 2
        outs += [SDS((hidden // 4, width), BF16)] * 2
    if last:
        send = [SDS((5 * pairs // 4, per, hidden), BF16)]
    else:
        send = [SDS((n, per, hidden), BF16) for n in (3 * pairs // 4, pairs // 4)]
    keep = SDS((pairs, per, hidden), BF16)
    if not fast:
        keep = SDS((width // 2, hidden), BF16)
        send = [keep] if last else [keep, SDS((8, LANES), BF16)]
    outs += send + [keep, SDS((1, hidden), F32)]
    if last:
        outs += [SDS((tokens // 2, width), F32), SDS((tokens // 2, width), BF16)]
        outs += [SDS((tokens, width), F32), SDS((tokens, width), BF16)]
    else:
        outs += [SDS((tokens, width), F32)] * 2
    return call(
        functools.partial(feed_kernel, last, fast),
        outs,
        (sidx, bidx, normed2, gb2, fc1, bias, fc2) + tuple(prev),
        [pltpu.VMEM((width, hidden), F32), pltpu.VMEM((hidden // 2, width), F32)],
        flops=12 * tokens * width * hidden,
        scalars=2,
    )


def by_batch_bit(arr, per):
    arr = arr.reshape(-1, 2, per, arr.shape[-1])
    own = lax.axis_index("batch") & 1
    return [pick(arr, 1 - own, 1), pick(arr, own, 1)]


def middle_back_kernel(
    sref, gn_keep, gn_got, middle, keeps, cp0, cp1, c0, c1, w_out, gain, gb2, gmid_own, gbr_out, gatt_send, sums
):
    s = sref[0]
    rows, width = gmid_own.shape
    cols = gatt_send.shape[1]
    hat, scale = normalize(middle[...])
    g = gn_keep[...] + gn_got[...].astype(F32)
    gout = jnp.concatenate([cots_of(cp0, c0), cots_of(cp1, c1)], axis=0)
    gmid = gout + normalize_back(g * gain[1:2, :], hat, scale)
    gbr = (keeps[:, 0:1] * gmid).astype(BF16)
    gbr_out[...] = gbr
    w_oth = w_out[pl.ds(pl.multiple_of((s ^ 2) * cols, HEAD), cols), :]
    gatt_send[...] = dot_t(gbr, w_oth).astype(BF16)
    gmid_own[...] = gmid[:rows]
    own = slice(0, rows)
    lines = [
        jnp.sum(g[own] * hat[own], axis=0, keepdims=True),
        jnp.sum(g[own], axis=0, keepdims=True),
        jnp.sum(gb2[own, :].astype(F32), axis=0, keepdims=True),
        jnp.sum(gbr[own].astype(F32), axis=0, keepdims=True),
        jnp.zeros((4, width), F32),
    ]
    sums[...] = jnp.concatenate(lines, axis=0)


def branch_back_kernel(
    per, sref, bref, gbr, w_out, a0, a2, middle, keeps, b2_keep, b2_got, bias, gain1, shift1, sums, fb_own, fb_oth,
    gatt, go_send, go_keep, early, opat, ospe, fcol, wide,
):
    s = sref[0]
    cols = a0.shape[1]
    rows, width = b2_keep.shape
    w_own = w_out[pl.ds(pl.multiple_of(s * cols, HEAD), cols), :]
    gatt[...] = dot_t(gbr[...], w_own).astype(BF16)
    for j, a in enumerate((a0, a2)):
        split_rows(dot_lt(a[...], gbr[...]), wide, bref[0] & 1, go_send.at[j], go_keep.at[j])
    res = middle[:rows, :] + keeps[:rows, 1:2] * (b2_keep[...] + b2_got[...].astype(F32) + bias[3:4, :])
    res = res.astype(BF16)
    opat[...] = res[: opat.shape[0]]
    ospe[...] = res[opat.shape[0] : opat.shape[0] + ospe.shape[0]]
    blank = functools.partial(jnp.zeros, dtype=F32)
    lines = [gain1[0:1, :], shift1[0:1, :], blank((HEAD + 2, width)), sums[:4, :], blank((LANES - HEAD - 8, width))]
    early[...] = jnp.concatenate(lines, axis=0).T
    lane = lane_of(cols)
    for j, ref in ((0, fb_own), (2, fb_oth)):
        fcol[...] = jnp.broadcast_to(ref[...], (LANES, ref.shape[1])).T
        at = pl.ds(pl.multiple_of((s ^ j) * cols, HEAD), cols)
        val = early[at, :]
        for k in range(4):
            lines = [fcol[(4 * b + k) * per : (4 * b + k + 1) * per, :] for b in range(cols // per)]
            val = jnp.where(lane == HEAD + 8 + k, jnp.concatenate(lines, axis=0), val)
        early[at, :] = val


def attend_back_kernel(first, heads, unroll, qa, ka, va, lse, ga, gx, out, sums, goa, dq, dk, dv):
    whole = qa.shape[1]
    half = ga.shape[0]
    lane = lane_of(half)
    for i in range(heads):
        h = first + i
        for ref, start in ((ga, 0), (gx, half)):
            if h < 2:
                t = ref[:, :LANES].astype(F32)
                t = jnp.where(lane < HEAD, t if h == 0 else pltpu.roll(t, HEAD, 1), 0.0)
            else:
                t = ref[:, LANES:].astype(F32)
                t = jnp.concatenate([t, jnp.zeros_like(t)], axis=1)
            goa[i, pl.ds(start, half), :] = t.astype(BF16)
    step = whole // 3

    def block(n, carry):
        i, b = n // 3, n % 3
        h = first + i
        at = pl.ds(pl.multiple_of(b * step, step), step)
        q, go = qa[h, at, :], goa[i, at, :]
        prob = jnp.exp(dot_t(ka[h], q) - lse[h, b][0:1, :])
        gp = dot_t(va[h], go)
        inner = jnp.sum(gp * prob, axis=0, keepdims=True)
        gs = (prob * (gp - inner)).astype(BF16)
        pv = dot(prob.astype(BF16), go)
        pk = dot(gs, q)
        dq[i, at, :] = dot_lt(gs, ka[h])

        dv[i] = jnp.where(b == 0, pv, dv[i] + pv)
        dk[i] = jnp.where(b == 0, pk, dk[i] + pk)
        return carry

    lax.fori_loop(0, 3 * heads, block, 0, unroll=unroll)
    for i in range(heads):
        out[i, :, :LANES] = pack_pair(dq[i] * HEAD**-0.5, dk[i]).astype(BF16)
        out[i, :, LANES:] = dv[i, :, :HEAD].astype(BF16)
        sums[i] = jnp.sum(out[i].astype(F32), axis=0, keepdims=True)


def attend_back(first, heads, qa, ka, va, lse, ga, gx):
    whole = qa.shape[1]
    return call(
        functools.partial(attend_back_kernel, first, heads),
        [SDS((heads, whole, 3 * HEAD), BF16), SDS((heads, 1, 3 * HEAD), F32)],
        (qa, ka, va, lse, ga, gx),
        [pltpu.VMEM((heads, whole, LANES), BF16)] + [pltpu.VMEM((heads, whole, LANES), F32)] * 3,
        flops=10 * heads * whole * whole * LANES,
    )


def norm1_kernel(g01, g2, w, keep, send):
    rows = keep.shape[0] // 2
    cols = g2.shape[2]
    for i in range(4):
        at = pl.ds(i * rows, rows)
        part = dot_t(g01[0, at, :], w[:, :cols])
        part = part + dot_t(g01[1, at, :], w[:, cols : 2 * cols])
        part = part + dot_t(g2[0, at, :], w[:, 2 * cols : 3 * cols])
        to = pl.ds((i // 2) * rows, rows)
        if i % 2 == 0:
            keep[to, :] = part
        else:
            send[to, :] = part.astype(BF16)


def qkv_grad(sref, normed, grads, sums, w, first, tile, bound):
    width, cols = w.shape[0], grads[0].shape[1]
    g = jnp.concatenate([dot_lt(normed[...], v) for v in grads], axis=1)
    w32 = w[:, first * cols : (first + len(grads)) * cols].astype(F32)
    rows = jnp.concatenate(sums, axis=1)
    both = jnp.sum(g * w32, axis=-1, keepdims=True)
    gshift = jnp.sum(w32 * rows, axis=-1, keepdims=True)
    lane = lane_of(width)
    old = bound[...]
    tile[...] = jnp.where(lane == HEAD, old + both, jnp.where(lane == HEAD + 1, old + gshift, old))
    ones = jnp.ones((grads[0].shape[0], LANES), BF16)
    at = pl.multiple_of(sref[0] * cols, HEAD)
    lanes = lane_of(HEAD)
    for i, v in enumerate(grads):
        col = dot_lt(v, ones)
        here = pl.ds(at + (first + i) * HEAD, HEAD)
        row = tile[here, :]
        row = jnp.where(lanes == HEAD + 2, col[:HEAD], row)
        tile[here, :] = jnp.where(lanes == HEAD + 3, col[2 * HEAD :], row)
    return g


def heads_kernel(
    fast, sref, bref, qa, ka, va, lse, ga, gx, normed, w, early, g01, send, keep, tile,
    s01, goa, dq, dk, dv, wide,
):
    attend_back_kernel(0, 2, 2, qa, ka, va, lse, ga, gx, g01, s01, goa, dq, dk, dv)
    g = qkv_grad(sref, normed, (g01[0], g01[1]), (s01[0], s01[1]), w, 0, tile, early)
    if not fast:
        rows = g.shape[0] // 2
        send[...] = g[:rows].astype(BF16)
        keep[...] = g[rows:].astype(BF16)
        return
    wide[...] = g
    y, z1, z2 = bref[0] & 1, (bref[0] >> 1) & 1, bref[0] >> 2
    per, cols = send.shape[1], g.shape[1]
    for m in range(8):
        zz1 = z1 if m & 4 else 1 - z1
        zz2 = z2 if m & 2 else 1 - z2
        for j in range(2):
            base = per * ((2 * (m & 1) + j) * 8 + 4 * zz2 + 2 * zz1)
            to = slice(j * cols, (j + 1) * cols)
            send[m, :, to] = wide[pl.ds(pl.multiple_of(base + (1 - y) * per, 8), per), :].astype(BF16)
            keep[m, :, to] = wide[pl.ds(pl.multiple_of(base + y * per, 8), per), :].astype(BF16)


def tail_kernel(
    sref, bref, qa, ka, va, lse, ga, gx, normed, g01, w, early, gn_keep, gn_send, send, keep,
    g2, s2, goa, dq, dk, dv, tile, wide,
):
    attend_back_kernel(2, 1, 1, qa, ka, va, lse, ga, gx, g2, s2, goa, dq, dk, dv)
    norm1_kernel(g01, g2, w, gn_keep, gn_send)
    g = qkv_grad(sref, normed, (g2[0],), (s2[0],), w, 2, tile, early)
    width = g.shape[0]
    lane = lane_of(width)
    val = tile[...]
    gshift = val[:, HEAD + 1 : HEAD + 2]
    ggain = (val[:, HEAD : HEAD + 1] - val[:, 1:2] * gshift) / val[:, 0:1]
    val = jnp.where(lane == HEAD, ggain, val)
    last = jnp.concatenate([g[:, LANES:], jnp.zeros((width, LANES - HEAD), F32)], axis=1)
    out = jnp.concatenate([g[:, :LANES], jnp.where(lane < HEAD, last, val)], axis=1)
    split_rows(out, wide, bref[0] & 1, send, keep)


def wide_sum(*parts):
    return sum(p.astype(F32) for p in parts[1:]) + parts[0].astype(F32)


def stage0_kernel(own_keep, own_got, oth_keep, oth_got, msg, part):
    for i in range(2):
        msg[i] = wide_sum(own_keep[i], own_got[i]).astype(BF16)
        msg[2 + i] = wide_sum(oth_keep[i], oth_got[i]).astype(BF16)
        part[i] = wide_sum(own_keep[2 + i], own_got[2 + i])
        part[2 + i] = wide_sum(oth_keep[2 + i], oth_got[2 + i])


def stage1_kernel(
    bref, keep_own, keep_oth, y1, y2, fc2, g2a, g2m, out, y3, part_0, got_0, q_send,
    msg_z, msg_y, msg_x, part_f, part_a, part_o, part_p,
):
    y, z1, z2 = bref[0] & 1, (bref[0] >> 1) & 1, bref[0] >> 2
    n = keep_own.shape[0] // 2
    for i in range(n):
        more = n // 2
        msg_z[i] = wide_sum(keep_own[i], y2[more + i]).astype(BF16)
        msg_z[n + i] = wide_sum(keep_oth[i], y1[i]).astype(BF16)
        part_f[i] = wide_sum(keep_own[n + i], y2[more + n + i])
        part_f[n + i] = wide_sum(keep_oth[n + i], y1[n + i] if i < more else y2[i - more])
        msg_y[8 + i] = q_send[i]
    rows = g2a.shape[1]
    for i in range(4):
        zz1 = z1 if i >> 1 else 1 - z1
        zz2 = z2 if i & 1 else 1 - z2
        m = 2 * zz2 + zz1
        msg_x[i] = wide_sum(out[1, m], y3[1, m]).astype(BF16)
        part_o[i] = wide_sum(out[0, m], y3[0, m])
        for k, got in enumerate((g2a, g2m)):
            at = slice(k * rows, (k + 1) * rows)
            b = 2 * m + 1 - y
            msg_y[2 * i + k] = wide_sum(fc2[b, at], got[b]).astype(BF16)
            b = 2 * m + y
            part_a[2 * i + k] = wide_sum(fc2[b, at], got[b])
    for i in range(2):
        for k in range(2):
            at = slice(k * rows, (k + 1) * rows)
            msg_x[4 + 2 * i + k] = wide_sum(part_0[2 + i, at], got_0[2 + i, at]).astype(BF16)
            part_p[2 * i + k] = wide_sum(part_0[i, at], got_0[i, at])


def stage2_kernel(
    part_f, got_z, part_a, got_y, part_o, got_x, part_p, q_keep, q2_send, msg_x, msg_z, msg_y, part_g, part_c, part_q
):
    n, _, cols = q2_send.shape
    for i in range(n):
        msg_y[i] = q2_send[i]
    for half in range(2):
        for i in range(4):
            k = 8 * half + i
            msg_x[4 * half + i] = wide_sum(part_f[k], got_z[k]).astype(BF16)
            part_g[4 * half + i] = wide_sum(part_f[k + 4], got_z[k + 4])
    for i in range(4):
        msg_z[i] = wide_sum(part_a[i], got_y[i]).astype(BF16)
        part_c[i] = wide_sum(part_a[4 + i], got_y[4 + i])
        msg_z[6 + i] = wide_sum(q_keep[i], got_y[8 + i]).astype(BF16)
        part_c[6 + i] = wide_sum(q_keep[4 + i], got_y[12 + i])
    for i in range(2):
        msg_z[4 + i] = wide_sum(part_o[i], got_x[i]).astype(BF16)
        part_c[4 + i] = wide_sum(part_o[2 + i], got_x[2 + i])
        rest = wide_sum(part_p[i], got_x[4 + i]).astype(BF16)
        for k in range(3):
            msg_y[n + 3 * i + k] = rest[:, k * cols : (k + 1) * cols]
        part_q[i] = wide_sum(part_p[2 + i], got_x[6 + i])


def stage3_kernel(bref, part_g, got_x, part_c, got_z, q_keep, got_y, msg, kept, z1, z2, z3, q_kept):
    for half in range(2):
        for i in range(2):
            k, other = 4 * half + i, 4 * (1 - half) + i
            msg[2 * half + i] = wide_sum(part_g[k], got_x[other]).astype(BF16)
            kept[2 * half + i] = wide_sum(part_g[k + 2], got_x[other + 2])
    for to, a, b in ((4, 0, 2), (5, 1, 3), (6, 4, 5), (7, 6, 8), (8, 7, 9)):
        msg[to] = wide_sum(part_c[a], got_z[a]).astype(BF16)
        kept[to] = wide_sum(part_c[b], got_z[b])
    q = bref[0] >> 1
    for r in range(4):
        for k, ref in enumerate((q_kept, z1, z2, z3)):
            m = r * 4 + (q ^ k)
            ref[r] = wide_sum(q_keep[m], got_y[m]).astype(ref.dtype)


def shift_kernel(keep, got, send):
    rows = send.shape[0]
    send[...] = wide_sum(keep[rows:, :], got[rows:, :]).astype(BF16)


def sums_kernel(kept, got, part_q, got_q, swap_send, swap_keep, fc2, out):
    per = out.shape[0]
    for half in range(2):
        at = pl.ds(half * per, per)
        swap_send[at, :] = wide_sum(kept[2 * half], got[2 * half]).astype(BF16)
        swap_keep[at, :] = wide_sum(kept[2 * half + 1], got[2 * half + 1])
        fc2[at, :] = wide_sum(kept[4 + half], got[4 + half])
        cols = got_q.shape[2]
        for k in range(3):
            at3 = slice(k * cols, (k + 1) * cols)
            fc2[pl.ds((2 + half) * per, per), at3] = wide_sum(part_q[half, :, at3], got_q[16 + 3 * half + k])
    out[...] = wide_sum(kept[6], got[6])


def owner_kernel(sref, most, got, kept, z1, z2, z3, s1, s2, s3, own, every):
    s = sref[0]
    cols = most.shape[2] // 2
    for m in range(4):
        at = slice((m % 2) * cols, (m % 2 + 1) * cols)
        every[m, :, :cols] = wide_sum(most[7 + m // 2, :, at], got[7 + m // 2, :, at])
        every[m, :, cols:] = wide_sum(kept[m], z1[m], z2[m], z3[m])
    for k, ref in enumerate((own, s1, s2, s3)):
        ref[...] = every[s ^ k].astype(ref.dtype)


def final_kernel(k0, c0, x0, p0, s0, gmid, gain, gpat, gspe):
    rows, width = x0.shape
    count = gpat.shape[0]
    hat, scale = normalize(tokens_of(p0, s0))
    g = wide_sum(k0[:rows], c0[:rows], x0[...])
    res = gmid[...] + normalize_back(g * gain[0:1, :], hat, scale)
    gpat[...] = res[:count]
    gspe[...] = res[count : count + gspe.shape[0]]


def collect_kernel(
    sref, own, g1, g2, g3, swap_keep, swap_got, out, gains, shifts, biases, fc1_bias, fc1, every
):
    s = sref[0]
    per, hidden = swap_keep.shape[0] // 2, swap_keep.shape[1]
    for j, value in ((0, swap_keep[:per]), (2, swap_keep[per:]), (1, swap_got[:per]), (3, swap_got[per:])):
        fc1[:, pl.ds(pl.multiple_of((s ^ j) * hidden, LANES), hidden)] = value.astype(F32)
    for k, ref in enumerate((own, g1, g2, g3)):
        every[k] = ref[...].astype(F32)
    pieces = [every[s ^ a] for a in range(4)]

    def part(u):
        j, a, h = u // 12, (u // 3) % 4, u % 3
        e = 3 * h + j
        return pieces[a][:, (e // 2) * LANES : (e // 2 + 1) * LANES], e % 2

    lane = lane_of(out.shape[0])
    for t in range(out.shape[1] // LANES):
        (low, lo), (high, hi) = part(2 * t), part(2 * t + 1)
        low = pltpu.roll(low, HEAD, 1) if lo else low
        high = high if hi else pltpu.roll(high, HEAD, 1)
        out[:, t * LANES : (t + 1) * LANES] = jnp.where(lane < HEAD, low, high)
    tail = 4 * LANES
    vec = wide_sum(*[every[k, :, tail:] for k in range(4)])
    vec = jnp.concatenate([vec, jnp.zeros((LANES - per, LANES), F32)], axis=0).T
    for ref, lines in ((gains, (0, 4)), (shifts, (1, 5)), (biases, (2, 3, 7, 6))):
        for i, k in enumerate(lines):
            ref[i : i + 1, :] = vec[HEAD + k : HEAD + k + 1, :per]
    flat = jnp.zeros((8, LANES), F32)
    for k in range(4):
        line = jnp.broadcast_to(vec[HEAD + 8 + k : HEAD + 9 + k], (8, LANES))
        flat = flat + (pltpu.roll(line, k * per, 1) if k else line)
    fc1_bias[...] = flat[:1, : 4 * per]


def pick(arr, index, axis):
    return lax.dynamic_index_in_dim(arr, index, axis, keepdims=False)


def total(parts):
    out = parts[0].astype(F32)
    for part in parts[1:]:
        out = out + part.astype(F32)
    return out


def swap(kind, v, mask):
    return lax.ppermute(v, kind, [(i, i ^ mask) for i in range(lax.axis_size(kind))])


def swap_seq(v, mask):
    return swap("seq", v, mask)


def after(value, *first):
    return lax.optimization_barrier((value, first))[0]


def bits_of(kind):
    return lax.axis_size(kind).bit_length() - 1


def split_bits(arr, axis, count):
    shape = arr.shape
    return arr.reshape(shape[:axis] + (2,) * count + shape[axis + 1 :])


def to_send(parts, axis, bit, kind):
    own = (lax.axis_index(kind) >> bit) & 1
    send = total([pick(p, 1 - own, axis) for p in parts]).astype(BF16)
    return send, [pick(p, own, axis) for p in parts]


def send_four(parts, axis, low):
    own = (lax.axis_index("batch") >> low) & 3

    def quarter(p, k):
        return pick(pick(p, k >> 1, axis), k & 1, axis)

    sends = [total([quarter(p, own ^ k) for p in parts]).astype(BF16) for k in (1, 2, 3)]
    return sends, [quarter(p, own) for p in parts]


def swap_four(sends, low):
    return [swap("batch", v, k << low) for k, v in zip((1, 2, 3), sends)]


def sum_rest(parts, axis, low):
    top = bits_of("batch")
    while low < top:
        if low + 1 < top:
            sends, kept = send_four(parts, axis + top - low - 2, low)
            parts, low = kept + swap_four(sends, low), low + 2
        else:
            send, kept = to_send(parts, axis, low, "batch")
            parts, low = kept + [swap("batch", send, 1 << low)], low + 1
    return total(parts)


def body(
    patches,
    specials,
    segment_ids,
    special_order,
    keep_mask,
    norm_gains,
    norm_shifts,
    w_qkv,
    biases,
    w_out,
    w_fc1,
    fc1_bias,
    w_fc2,
    cot_patches,
    cot_specials,
):
    count, width = patches.shape[1:]
    extra = specials.shape[1]
    images = keep_mask.shape[1] // 2
    block = count + PAD
    chip = 2 * block
    whole = 4 * block
    cols = OWN * HEAD
    hidden = w_fc1.shape[1] // 4
    s = lax.axis_index("seq")
    sidx = s.astype(jnp.int32).reshape(1)
    bidx = lax.axis_index("batch").astype(jnp.int32).reshape(1)
    nb = lax.axis_size("batch")
    nbits = bits_of("batch")

    own_p, own_cot = patches[0], cot_patches[0]
    got_px = swap_seq(own_p, 2)
    got_pc = swap_seq(own_p, 1)
    (small,) = call(
        small_kernel,
        [SDS((32, width), BF16)],
        (specials[0], segment_ids, special_order, cot_specials[0]),
        [pltpu.VMEM((extra, width), BF16), pltpu.VMEM((1, count), jnp.int32), pltpu.VMEM((1, extra), jnp.int32)]
        + [pltpu.VMEM((extra, width), BF16), pltpu.VMEM((32, width), F32), pltpu.SemaphoreType.DMA((4,))],
        far=(0, 1, 2, 3),
    )
    got_sx = swap_seq(small, 2)
    got_sc = swap_seq(small, 1)
    cot_c = swap_seq(own_cot, 1)
    fb = fc1_bias.reshape(1, -1)
    sidx, bidx, small = lax.optimization_barrier((sidx, bidx, small))
    w_own, bias_own = call(
        prep_kernel,
        [SDS((width, 5 * LANES), BF16), SDS((1, 5 * LANES), F32)],
        (sidx, w_qkv, biases),
        [pltpu.VMEM((3 * OWN, width, LANES), BF16), pltpu.VMEM(biases.shape, F32)]
        + [pltpu.SemaphoreType.DMA((3 * OWN + 1,))],
        scalars=1,
        far=(1, 2),
    )
    headed = SDS((OWN, chip, LANES), BF16)
    q0, k0, v0, n0, toks, keeps = call(
        project_kernel,
        [headed] * 3 + [SDS((chip, width), BF16), SDS((chip, width), BF16), SDS((chip, LANES), F32)],
        (keep_mask, own_p, small, got_pc, got_sc, norm_gains, norm_shifts, w_own, bias_own),
        flops=2 * chip * width * 3 * cols,
        scalars=1,
    )
    got_px, got_sx, n0 = lax.optimization_barrier((got_px, got_sx, n0))
    got_pd = swap_seq(got_px, 1)
    got_sd = swap_seq(got_sx, 1)

    headed = SDS((OWN, whole, LANES), BF16)
    heads32 = SDS((OWN, chip, LANES), F32)
    qa, ka, va, att_send, other, normed = call(
        attend_first_kernel,
        [headed] * 3 + [SDS((chip, cols), BF16), heads32, SDS((whole, width), BF16)],
        (q0, k0, v0, n0, got_px, got_sx, got_pd, got_sd, norm_gains, norm_shifts, w_own, bias_own),
        flops=2 * chip * width * 3 * cols + 2 * OWN * whole * whole * LANES,
    )
    a2 = swap_seq(att_send, 2)
    a0, lse = call(
        attend_second_kernel,
        [SDS((chip, cols), BF16), SDS((OWN, 3, 8, whole // 3), F32)],
        (qa, ka, va, other),
        [pltpu.VMEM((OWN, chip, LANES), F32)],
        flops=2 * OWN * whole * whole * LANES,
    )
    a1 = swap_seq(a0, 1)
    a3 = swap_seq(a2, 1)

    middle, normed2, gb2, w1, w2, w3, w4 = call(
        middle_kernel,
        [SDS((chip, width), F32), SDS((chip, width), BF16), SDS((chip, width), BF16)]
        + [SDS((width, hidden), BF16), SDS((hidden, width), BF16)] * 2,
        (sidx, a0, a1, a2, a3, toks, keeps, own_cot, cot_c, small, got_sc, w_out, biases, norm_gains, norm_shifts)
        + (w_fc1, w_fc2),
        [pltpu.SemaphoreType.DMA((2, 2))],
        flops=2 * chip * width * width,
        scalars=1,
        far=(15, 16),
    )
    per = width // (4 * nb)
    fast = nb == 8
    fc2_a, fc2_m, zo_send, zo_keep, y1, y_rest, keep_oth, fb_oth, b2, gn = feed(
        False, fast, per, sidx, bidx, normed2, gb2, w1, fb, w2
    )
    got2a = swap_seq(fc2_a, 2)
    if not fast:
        y1, keep_oth = by_batch_bit(jnp.concatenate([y1, keep_oth], axis=0), per)
    got_y1 = swap("batch", y1, 1)
    got_zo = swap("batch", zo_send, 2) if fast else zo_send
    ahead = (got2a, got_y1, got_zo)
    fc2_keep, zn_send, zn_keep, y2, keep_own, fb_own, b2_keep, b2_send, gn_keep, gn_send = feed(
        True, fast, per, sidx, bidx, normed2, gb2, w3, fb, w4, (b2, gn, y_rest)
    )
    if not fast:
        y2, keep_own = by_batch_bit(jnp.concatenate([y2, keep_own], axis=0), per)
    gn_send, b2_send, zn_send, y2, (got2a, got_y1, got_zo) = lax.optimization_barrier(
        (gn_send, b2_send, zn_send, y2, ahead)
    )
    gn_got = swap_seq(gn_send, 1)
    b2_got = swap_seq(b2_send, 1)
    got_zn = swap("batch", zn_send, 2) if fast else zn_send
    got_y2 = swap("batch", y2, 1)

    gmid, gbr, gatt_send, line_sums = call(
        middle_back_kernel,
        [SDS((block, width), F32), SDS((chip, width), BF16), SDS((chip, cols), BF16), SDS((8, width), F32)],
        (sidx, gn_keep, gn_got, middle, keeps, own_cot, cot_c, small, got_sc, w_out, norm_gains, gb2),
        flops=2 * chip * width * cols,
        scalars=1,
    )
    gatt_x = swap_seq(gatt_send, 2)
    if fast:
        split = SDS((2, cols // (2 * per), per, width), BF16)
    else:
        split = SDS((2, cols // 2, width), BF16)
    gatt, go_send, go_keep, early, opat, ospe = call(
        functools.partial(branch_back_kernel, per),
        [SDS((chip, cols), BF16), split, split, SDS((width, LANES), F32)]
        + [SDS((count, width), BF16), SDS((extra, width), BF16)],
        (sidx, bidx, gbr, w_out, a0, a2, middle, keeps, b2_keep, b2_got, biases, norm_gains, norm_shifts)
        + (line_sums, fb_own, fb_oth),
        [pltpu.VMEM((hidden, LANES), F32), pltpu.VMEM((cols, width), F32)],
        flops=6 * chip * width * cols,
        scalars=2,
    )
    if not fast:
        halves = [by_batch_bit(jnp.concatenate([go_send[j], go_keep[j]], axis=0), per) for j in range(2)]
        go_send, go_keep = [jnp.stack([halves[j][k] for j in range(2)]) for k in range(2)]
    got_o = swap("batch", go_send, 1)
    msg_0, part_0 = None, None
    if fast:
        msg_0, part_0 = call(
            stage0_kernel,
            [SDS(zn_keep.shape, BF16), SDS(zn_keep.shape, F32)],
            (zn_keep, after(got_zn, go_send), zo_keep, got_zo),
        )
        gatt_x = after(gatt_x, msg_0)
    gatt_x, fc2_m = lax.optimization_barrier((after(gatt_x, go_send), fc2_m))
    got2m = swap_seq(fc2_m, 2)
    pairs = (keep_own, keep_oth, got_y1, got_y2)

    def heads_scratch(heads):
        return [pltpu.VMEM((heads, whole, LANES), BF16)] + [pltpu.VMEM((heads, whole, LANES), F32)] * 3

    def first_heads(lse):
        if fast:
            split = [SDS((8, per, 4 * cols), BF16)] * 2
        else:
            split = [SDS((width // 2, 2 * cols), BF16)] * 2
        return call(
            functools.partial(heads_kernel, fast),
            [SDS((2, whole, cols), BF16)] + split + [SDS((width, LANES), F32)],
            (sidx, bidx, qa, ka, va, lse, gatt, gatt_x, normed, w_own, early),
            [pltpu.VMEM((2, 1, cols), F32)] + heads_scratch(2) + [pltpu.VMEM((width, 2 * cols), F32)],
            flops=20 * whole * whole * LANES,
            scalars=2,
            room=20,
        )

    def tail_part(lse, g01, tile):
        wide = cols + HEAD
        if fast:
            outs = [SDS((width // (2 * per), per, wide), BF16)] * 2
        else:
            outs = [SDS((width // 2, wide), BF16)] * 2
        return call(
            tail_kernel,
            [SDS((chip, width), F32), SDS((chip, width), BF16)] + outs,
            (sidx, bidx, qa, ka, va, lse, gatt, gatt_x, normed, g01, w_own, tile),
            [pltpu.VMEM((1, whole, cols), BF16), pltpu.VMEM((1, 1, cols), F32)]
            + heads_scratch(1)
            + [pltpu.VMEM((width, LANES), F32), pltpu.VMEM((width, wide), F32)],
            flops=10 * whole * whole * LANES,
            scalars=2,
            room=20,
        )

    rest = (sidx, bidx, per, block, chip, hidden, cols, count, extra, width)
    zs = (zn_send, zn_keep, zo_send, zo_keep, msg_0, part_0)
    reduce_all = reduce_eight if fast else reduce_any
    out_fc2, out_out, out_fc1, out_qkv, smalls, gpat, gspe = reduce_all(
        rest, pairs, (fc2_keep, got2a, got2m, zs), (go_keep, got_o), lse, gatt_x,
        first_heads, tail_part, (own_p, small), gmid, norm_gains,
    )
    grad_gains, grad_shifts, grad_biases, grad_fc1_bias = smalls
    return (
        opat[None],
        ospe[None],
        gpat[None],
        gspe[None],
        grad_gains,
        grad_shifts,
        out_qkv,
        grad_biases,
        out_out,
        out_fc1,
        grad_fc1_bias.reshape(-1),
        out_fc2,
    )


def reduce_eight(
    rest, pairs, twos, outs, lse, gatt_x, first_heads, tail_part, pay, gmid, gains
):
    sidx, bidx, per, block, chip, hidden, cols, count, extra, width = rest
    fc2_keep, got2a, got2m, zs = twos
    go_keep, got_o = outs
    deep = hidden // 8
    got_0 = swap("batch", zs[4], 4)
    part_0 = zs[5]
    g01, q01_send, q01_keep, tile = first_heads(after(lse, gatt_x))
    g01, got_y2, got2m, got_o, got_0 = lax.optimization_barrier((g01, pairs[3], got2m, got_o, got_0))
    keep_own, keep_oth, got_y1 = pairs[:3]

    def blocks(n, dtype=BF16):
        return SDS((n, per, width), dtype)

    msg_z, msg_y, msg_x, part_f, part_a, part_o, part_p = call(
        stage1_kernel,
        [blocks(16), blocks(16), blocks(8), blocks(16, F32), blocks(8, F32), blocks(4, F32), blocks(4, F32)],
        (bidx, keep_own, keep_oth, got_y1, got_y2, fc2_keep, got2a, got2m, go_keep, got_o, part_0, got_0)
        + (q01_send,),
        scalars=1,
    )
    msg_z, msg_y, msg_x, lse = lax.optimization_barrier((msg_z, msg_y, msg_x, after(lse, g01)))
    got_z = swap("batch", msg_z, 2)
    got_y = swap("batch", msg_y, 1)
    got_x = swap_seq(msg_x, 2)
    gn1_keep, gn1_send, q_send, q_keep = tail_part(lse, g01, tile)
    gn1_send, got_x, got_y, got_z = lax.optimization_barrier((gn1_send, got_x, got_y, got_z))
    gn1_c = swap_seq(gn1_send, 1)
    part = SDS((22, per, cols + HEAD), BF16)
    msg_x, msg_z, msg_y, part_g, part_c, part_q = call(
        stage2_kernel,
        [blocks(8), blocks(10), part, blocks(8, F32), blocks(10, F32), blocks(2, F32)],
        (part_f, got_z, part_a, got_y, part_o, got_x, part_p, q01_keep, q_send),
    )
    got_x = swap_seq(msg_x, 2)
    got_z = swap("batch", msg_z, 2)
    got_y = swap("batch", msg_y, 1)
    (xsend,) = call(shift_kernel, [SDS((block, width), BF16)], (after(gn1_keep, msg_x), gn1_c))
    gn1_x = swap_seq(xsend, 2)
    quarter = SDS((4, per, cols + HEAD), BF16)
    msg, kept, q1, q2, q3, q_kept = call(
        stage3_kernel,
        [blocks(9), blocks(9, F32), quarter, quarter, quarter, SDS(quarter.shape, F32)],
        (bidx, part_g, after(got_x, xsend), part_c, got_z, q_keep, got_y),
        scalars=1,
    )
    got_last = swap("batch", msg, 4)
    got_qz = swap_four((q1, q2, q3), 1)
    gpat, gspe = call(
        final_kernel,
        [SDS((count, width), F32), SDS((extra, width), F32)],
        (gn1_keep, gn1_c, after(gn1_x, q1), *pay, gmid, gains),
    )
    got_last = after(got_last, gpat)
    row = SDS((per, 5 * LANES), BF16)
    s1, s2, s3, own = call(
        owner_kernel,
        [row, row, row, SDS(row.shape, F32)],
        (sidx, kept, got_last, q_kept, *got_qz),
        [pltpu.VMEM((4, per, 5 * LANES), F32)],
        scalars=1,
    )
    swap_send, swap_keep, out_fc2, out_out = call(
        sums_kernel,
        [SDS((2 * per, width), BF16), SDS((2 * per, width), F32), SDS((deep, width), F32), SDS((per, width), F32)],
        (kept, after(got_last, s1), part_q, got_y),
    )
    swap_got = swap_seq(swap_send, 1)
    gots = [swap_seq(v, k) for k, v in ((1, s1), (2, s2), (3, s3))]
    lines = [SDS((2, per), F32), SDS((2, per), F32), SDS((4, per), F32), SDS((1, 4 * per), F32)]
    out_qkv, *smalls, out_fc1 = call(
        collect_kernel,
        [SDS((per, 3 * width), F32), *lines, SDS((per, 4 * hidden), F32)],
        (sidx, own, *gots, swap_keep, swap_got),
        [pltpu.VMEM((4, per, 5 * LANES), F32)],
        scalars=1,
    )
    return out_fc2, out_out, out_fc1, out_qkv, smalls, gpat, gspe


def reduce_any(
    rest, pairs, twos, outs, lse, gatt_x, first_heads, tail_part, pay, gmid, gains
):
    sidx, bidx, per, block, chip, hidden, cols, count, extra, width = rest
    s = lax.axis_index("seq")
    nb = lax.axis_size("batch")
    nbits = bits_of("batch")
    low = nbits - 1
    fc2_keep, got2a, got2m, zs = twos
    go_keep, got_o = outs
    keep_own, keep_oth, got_oth, got_own = [
        split_bits(p.reshape(2, 2, nb // 2, per, hidden), 2, low) for p in pairs
    ]
    g01, q01_top, q01_low, tile = first_heads(lse)
    send_own, parts_own = to_send([keep_own, got_own], 0, 1, "seq")
    send_oth, parts_oth = to_send([keep_oth, got_oth], 0, 1, "seq")
    got_b = swap_seq(jnp.concatenate([send_own, send_oth], axis=-1), 2)
    sum_own = sum_rest(parts_own + [got_b[..., hidden:]], 1, 1)
    sum_oth = sum_rest(parts_oth + [got_b[..., :hidden]], 1, 1)
    own_c = s & 1
    other = jnp.concatenate([pick(sum_own, 1 - own_c, 0), pick(sum_oth, 1 - own_c, 0)], axis=-1)
    got = swap_seq(other.astype(BF16), 1).astype(F32)
    rel = jnp.stack([pick(sum_own, own_c, 0), got[:, :hidden], pick(sum_oth, own_c, 0), got[:, hidden:]])
    out_fc1 = jnp.concatenate([pick(rel, s ^ a, 0) for a in range(4)], axis=1)
    zn_send, zn_keep, zo_send, zo_keep = zs[:4]
    got2 = jnp.concatenate([got2a, got2m, swap_seq(jnp.concatenate([zo_send, zo_keep], axis=0), 2)], axis=0)
    fc2_keep = jnp.concatenate([fc2_keep, zn_send, zn_keep], axis=0)
    parts = [split_bits(p.reshape(nb, -1, width), 0, nbits) for p in (fc2_keep, got2)]
    out_fc2 = sum_rest(parts, 0, 0)
    parts = [split_bits(p.reshape(2, nb // 2, per, width), 1, low) for p in (go_keep, got_o)]
    parts = [p[0] for p in parts] + [swap_seq(total([p[1] for p in parts]).astype(BF16), 2)]
    out_out = sum_rest(parts, 0, 1)
    gn1_keep, gn1_send, q2_top, q2_low = tail_part(lse, g01, tile)
    q_all = [jnp.concatenate(v, axis=1) for v in ((q01_top, q2_top), (q01_low, q2_low))]
    q_send, q_keep = by_batch_bit(jnp.concatenate(q_all, axis=0), per)
    gn1_c = swap_seq(gn1_send, 1)
    gn1_x = swap_seq((gn1_keep[block:] + gn1_c[block:].astype(F32)).astype(BF16), 2)
    gpat, gspe = call(
        final_kernel,
        [SDS((count, width), F32), SDS((extra, width), F32)],
        (gn1_keep, gn1_c, gn1_x, *pay, gmid, gains),
    )
    wide = 5 * LANES
    parts = [split_bits(p.reshape(4, nb // 2, per, wide), 1, low) for p in (q_keep, swap("batch", q_send, 1))]
    sum_q = sum_rest(parts, 1, 1)
    pieces = [pick(sum_q, s, 0)] + [
        swap_seq(pick(sum_q, s ^ j, 0).astype(BF16), j).astype(F32) for j in (1, 2, 3)
    ]
    rel = jnp.stack([p[:, : 3 * cols] for p in pieces])
    absolute = jnp.stack([pick(rel, s ^ a, 0) for a in range(4)], axis=1)
    out_qkv = absolute.reshape(-1, 4, OWN, 3, HEAD).transpose(0, 3, 1, 2, 4).reshape(-1, 3 * width)
    vec = total([p[:, 3 * cols :] for p in pieces]).T
    smalls = [vec[jnp.array(k)] for k in ((0, 4), (1, 5), (2, 3, 7, 6), (8, 9, 10, 11))]
    return out_fc2, out_out, out_fc1, out_qkv, smalls, gpat, gspe


def solution(mesh):
    tok = P("batch", "seq", None)
    ids = P("batch", "seq")
    split = P(None, ("seq", "batch"))
    rows = P(("seq", "batch"), None)
    return jax.shard_map(
        body,
        mesh=mesh,
        in_specs=(tok, tok, ids, ids, P("batch", None)) + (P(),) * 8 + (tok, tok),
        out_specs=(tok, tok, tok, tok, split, split, rows, split, rows, rows, P(("seq", "batch")), rows),
        check_vma=False,
    )
```

```python
import functools

import jax
import jax.numpy as jnp
from jax import lax
from jax.experimental import pallas as pl
from jax.experimental.pallas import tpu as pltpu
from jax.sharding import PartitionSpec as P

HEADS = 12
HEAD = 64
PAD = 32
SPECIAL = 4
LANES = 128
OWN = 3
FAR = -(2.0**100)
F32 = jnp.float32
BF16 = jnp.bfloat16
SDS = jax.ShapeDtypeStruct


def dot(a, b):
    return jnp.dot(a, b, preferred_element_type=F32)


def dot_t(a, b):
    return lax.dot_general(a, b, (((1,), (1,)), ((), ())), preferred_element_type=F32)


def dot_lt(a, b):
    return lax.dot_general(a, b, (((0,), (0,)), ((), ())), preferred_element_type=F32)


def normalize(v):
    center = v - jnp.mean(v, axis=-1, keepdims=True)
    spread = jnp.mean(center * center, axis=-1, keepdims=True)
    scale = lax.rsqrt(spread + 1e-06)
    return center * scale, scale


def normalize_back(grad_hat, hat, scale):
    mean_g = jnp.mean(grad_hat, axis=-1, keepdims=True)
    mean_gh = jnp.mean(grad_hat * hat, axis=-1, keepdims=True)
    return scale * (grad_hat - mean_g - hat * mean_gh)


def gelu_pair(v):
    half = 0.5 * (1.0 + lax.erf(v * 0.5**0.5))
    slope = half + v * jnp.exp(-0.5 * v * v) * 0.3989422804014327
    return v * half, slope


def lane_of(rows):
    return lax.broadcasted_iota(jnp.int32, (rows, LANES), 1)


def unpack_head(tiles, e):
    tile = tiles[:, (e // 2) * LANES : (e // 2 + 1) * LANES]
    return tile if e % 2 == 0 else pltpu.roll(tile, HEAD, 1)


def pack_pair(low, high):
    return jnp.where(lane_of(low.shape[0]) < HEAD, low, pltpu.roll(high, HEAD, 1))


def vmem():
    return pl.BlockSpec(memory_space=pltpu.VMEM)


def smem():
    return pl.BlockSpec(memory_space=pltpu.SMEM)


def call(kernel, outs, args, scratch=(), flops=0, scalars=0, room=16, far=()):
    args = [pltpu.with_memory_space_constraint(a, pltpu.HBM) if i in far else a for i, a in enumerate(args)]
    nbytes = sum(a.size * a.dtype.itemsize for a in args)
    nbytes += sum(o.size * o.dtype.itemsize for o in outs)
    return pl.pallas_call(
        kernel,
        out_shape=outs,
        in_specs=[
            smem() if i < scalars else pl.BlockSpec(memory_space=pltpu.HBM) if i in far else vmem()
            for i in range(len(args))
        ],
        out_specs=[vmem()] * len(outs),
        scratch_shapes=list(scratch),
        compiler_params=pltpu.CompilerParams(vmem_limit_bytes=room << 20),
        cost_estimate=pl.CostEstimate(flops=flops, bytes_accessed=nbytes, transcendentals=0),
    )(*args)


def prep_kernel(sref, w, biases, w_own, bias_own, tiles, lines, sems):
    width = w.shape[0]
    per = width // HEAD
    spots = [per * (e % 3) + OWN * sref[0] + e // 3 for e in range(3 * OWN)]
    copies = [pltpu.make_async_copy(biases, lines, sems.at[3 * OWN])]
    for e, u in enumerate(spots):
        tile = w.at[:, pl.ds(pl.multiple_of((u >> 1) * LANES, LANES), LANES)]
        copies.append(pltpu.make_async_copy(tile, tiles.at[e], sems.at[e]))
    for copy in copies:
        copy.start()
    copies[0].wait()
    line = lax.broadcasted_iota(jnp.int32, (1, LANES), 1)
    for t in range((3 * OWN + 1) // 2):
        out, bias = jnp.zeros((width, LANES), F32), jnp.zeros((1, LANES), F32)
        for dest in range(2):
            e = 2 * t + dest
            if e == 3 * OWN:
                continue
            copies[1 + e].wait()
            u, j = spots[e], e % 3
            side = (lane_of(width) >= HEAD) == (dest == 1)
            moved = jnp.broadcast_to((u & 1) != dest, (1, LANES))
            tile = tiles[e].astype(F32)
            tile = jnp.where(moved, pltpu.roll(tile, HEAD, 1), tile)
            out = jnp.where(side, tile, out)
            if j != 1:
                v = OWN * sref[0] + e // 3
                tile = lines[j // 2 : j // 2 + 1, pl.ds(pl.multiple_of((v >> 1) * LANES, LANES), LANES)]
                tile = jnp.broadcast_to(tile, (8, LANES))
                away = jnp.broadcast_to((v & 1) != dest, (8, LANES))
                tile = jnp.where(away, pltpu.roll(tile, HEAD, 1), tile)[:1]
                bias = jnp.where((line >= HEAD) == (dest == 1), tile, bias)
        w_own[:, t * LANES : (t + 1) * LANES] = out.astype(BF16)
        bias_own[:, t * LANES : (t + 1) * LANES] = bias


def small_kernel(specials_in, segments_in, order_in, cots_in, small, specials, segments, order, cots, wide, sems):
    pairs = ((specials_in, specials), (segments_in, segments), (order_in, order), (cots_in, cots))
    copies = [pltpu.make_async_copy(src, dst, sems.at[i]) for i, (src, dst) in enumerate(pairs)]
    for copy in copies:
        copy.start()
    extra, width = specials.shape
    count = segments.shape[1]
    wide[...] = jnp.zeros_like(wide)
    wide[extra : extra + 1, :] = jnp.full((1, width), -1.0, F32)
    for copy in copies:
        copy.wait()
    wide[:extra, :] = specials[...].astype(F32)
    wide[16 : 16 + extra, :] = cots[...].astype(F32)
    wide[extra : extra + 1, :count] = segments[...].astype(F32)
    wide[extra : extra + 1, count : count + extra] = (order[...] >> 1).astype(F32)
    small[...] = wide[...].astype(BF16)


def tokens_of(patches, small):
    parts = [patches[...].astype(F32), small[:16, :].astype(F32)]
    return jnp.concatenate(parts + [jnp.zeros((PAD - 16, patches.shape[1]), F32)], axis=0)


def cots_of(patches, small):
    parts = [patches[...].astype(F32), small[16:, :].astype(F32)]
    return jnp.concatenate(parts + [jnp.zeros((PAD - 16, patches.shape[1]), F32)], axis=0)


def images_of(small, rows):
    size = -(-rows // LANES) * LANES
    line = small[:16, :size].astype(F32)[SPECIAL : SPECIAL + 1]
    return jnp.broadcast_to(line, (LANES, size)).T[:rows]


def project(patches, small, gain, shift, w, bias, at, qa, ka, va, normed):
    tok = tokens_of(patches, small)
    rows = tok.shape[0]
    lane = lane_of(rows)
    hat, _ = normalize(tok)
    nrm = (hat * gain[0:1, :] + shift[0:1, :]).astype(BF16)
    normed[at, :] = nrm
    qkv = dot(nrm, w[...]) + bias[...]
    image = images_of(small, rows)
    hot = jnp.where((lane >= HEAD) & (image == (lane - HEAD).astype(F32)), 1.0, 0.0)
    far = jnp.where((lane >= HEAD) & (lane < HEAD + 8) & (hot == 0.0), FAR, 0.0)
    one = jnp.where(lane == HEAD, 1.0, 0.0)
    for h in range(OWN):
        q = unpack_head(qkv, 3 * h) * HEAD**-0.5
        qa[h, at, :] = jnp.where(lane < HEAD, q, hot).astype(BF16)
        ka[h, at, :] = jnp.where(lane < HEAD, unpack_head(qkv, 3 * h + 1), far).astype(BF16)
        va[h, at, :] = jnp.where(lane < HEAD, unpack_head(qkv, 3 * h + 2), one).astype(BF16)
    return tok, image


def project_kernel(flags, p0, s0, p1, s1, gain, shift, w, bias, qa, ka, va, normed, toks, keeps):
    rows = normed.shape[0] // 2
    lane = lane_of(rows)
    for i, (p, small) in enumerate(((p0, s0), (p1, s1))):
        at = pl.ds(i * rows, rows)
        tok, image = project(p, small, gain, shift, w, bias, at, qa, ka, va, normed)
        toks[at, :] = tok.astype(BF16)
        keep = jnp.zeros((rows, LANES), F32)
        half = flags.shape[1] // 2
        for j in range(half):
            first = flags[0, j].astype(F32) / 0.75
            second = flags[0, half + j].astype(F32) / 0.75
            keep = jnp.where(image == float(j), jnp.where(lane == 0, first, second), keep)
        keeps[at, :] = keep


def attend_block(h, at, keys, values, queries, oacc):
    sc = dot_t(queries[h, at, :], keys[h])
    top = jnp.max(sc, axis=-1, keepdims=True)
    e = jnp.exp(sc - top).astype(BF16)
    o = dot(e, values[h])
    tot = o[:, HEAD : HEAD + 1]
    mark = jnp.where(lane_of(o.shape[0]) == HEAD + 1, top + jnp.log(tot), o * (1.0 / tot))
    return mark


def attend_first_kernel(
    q0, k0, v0, n0, p2, s2, p3, s3, gain, shift, w, bias, qa, ka, va, send, oacc, normed
):
    half = n0.shape[0]
    rows = half // 2
    own = pl.ds(0, half)
    for h in range(OWN):
        qa[h, own, :] = q0[h]
        ka[h, own, :] = k0[h]
        va[h, own, :] = v0[h]
    normed[own, :] = n0[...]
    for i, (p, small) in enumerate(((p2, s2), (p3, s3))):
        project(p, small, gain, shift, w, bias, pl.ds(half + i * rows, rows), qa, ka, va, normed)

    def block(i, carry):
        h, b = i // 2, i % 2
        at = pl.ds(pl.multiple_of(half + b * rows, 16), rows)
        oacc[h, pl.ds(pl.multiple_of(b * rows, 16), rows), :] = attend_block(h, at, ka, va, qa, oacc)
        return carry

    lax.fori_loop(0, 2 * OWN, block, 0, unroll=3)
    gather_heads(oacc, send)


def gather_heads(oacc, out):
    out[:, :LANES] = pack_pair(oacc[0], oacc[1]).astype(BF16)
    out[:, LANES:] = oacc[2, :, :HEAD].astype(BF16)


def attend_second_kernel(
    sref, qa, ka, va, other, w_fc1, w_fc2, keep, lse, w1, w2, w3, w4, oacc, sems
):
    s = sref[0]
    copies = fetch(s ^ 2, w_fc1, w_fc2, w1, w2, sems.at[0]) + fetch(s, w_fc1, w_fc2, w3, w4, sems.at[1])
    half = oacc.shape[1]
    rows = half // 2

    def block(i, carry):
        h, b = i // 2, i % 2
        at = pl.ds(pl.multiple_of(b * rows, 16), rows)
        oacc[h, at, :] = attend_block(h, at, ka, va, qa, oacc)
        return carry

    lax.fori_loop(0, 2 * OWN, block, 0, unroll=3)
    gather_heads(oacc, keep)
    step = 2 * half // 3
    for h in range(OWN):
        parts = [
            oacc[h, :step, :],
            jnp.concatenate([oacc[h, step:, :], other[h, : step - (half - step), :]], axis=0),
            other[h, half - step :, :],
        ]
        for b in range(3):
            lse[h, b] = jnp.broadcast_to(parts[b].T[HEAD + 1 : HEAD + 2], (8, step))
    for copy in copies:
        copy.wait()


def middle_kernel(
    sref, a0, a1, a2, a3, toks, keeps, cp0, cp1, c0, c1, w_out, bias, gain, shift,
    middle, normed2, gb2,
):
    s = sref[0]
    chip, width = toks.shape
    rows = chip // 2
    cols = a0.shape[1]
    acc = jnp.zeros((chip, width), F32) + bias[2:3, :]
    for j, a in ((0, a0), (2, a2)):
        w = w_out[pl.ds(pl.multiple_of((s ^ j) * cols, HEAD), cols), :]
        acc = acc + dot(a[...], w)
    for j, a in ((1, a1), (3, a3)):
        w = w_out[pl.ds(pl.multiple_of((s ^ j) * cols, HEAD), cols), :]
        part = dot(a[...], w)
        acc = acc + jnp.concatenate([part[rows:], part[:rows]], axis=0)
    mid = toks[...].astype(F32) + keeps[:, 0:1] * acc
    middle[...] = mid
    hat, _ = normalize(mid)
    normed2[...] = (hat * gain[1:2, :] + shift[1:2, :]).astype(BF16)
    gout = jnp.concatenate([cots_of(cp0, c0), cots_of(cp1, c1)], axis=0)
    gb2[...] = (keeps[:, 1:2] * gout).astype(BF16)


def fetch(block, w_fc1, w_fc2, w1, w2, sems):
    size = w1.shape[1]
    at = pl.ds(pl.multiple_of(block * size, LANES), size)
    copies = [
        pltpu.make_async_copy(w_fc1.at[:, at], w1, sems.at[0]),
        pltpu.make_async_copy(w_fc2.at[at, :], w2, sems.at[1]),
    ]
    for copy in copies:
        copy.start()
    return copies


def feed_kernel(last, fast, sref, bref, normed2, gb2, fc1, bias, fc2, *refs):
    if last:
        b2_in, gn_in, y_in, g2, zb_send, zb_keep, y_send, g1_keep, gb, b2_keep, b2_send, gn_keep, gn_send, wide, wide2 = refs
    else:
        g2a, g2m, zb_send, zb_keep, y_first, y_second, g1_keep, gb, b2, gn, wide, wide2 = refs
    tokens = normed2.shape[0]
    half = tokens // 2
    block = sref[0] if last else sref[0] ^ 2
    pre = dot(normed2[...], fc1[...]) + bias[:, pl.ds(pl.multiple_of(block * fc1.shape[1], LANES), fc1.shape[1])]
    gact = dot_t(gb2[...], fc2[...])
    act, slope = gelu_pair(pre)
    act = act.astype(BF16)
    gh = (gact * slope).astype(BF16)
    grad1 = dot_lt(normed2[...], gh)
    if not fast:
        rows = grad1.shape[0] // 2
        (y_send if last else y_first)[...] = grad1[:rows].astype(BF16)
        g1_keep[...] = grad1[rows:].astype(BF16)
    else:
        x, c = sref[0] >> 1, sref[0] & 1
        y, z1, z2 = bref[0] & 1, (bref[0] >> 1) & 1, bref[0] >> 2
        wide[...] = grad1
        n, rows = g1_keep.shape[:2]
        for m in range(2 * n):
            near = [(m >> k) & 1 for k in (4, 3, 2, 1, 0)]
            yy, zz1, xx, zz2, cc = [own if r else 1 - own for own, r in zip((y, z1, x, z2, c), near)]
            base = rows * (16 * xx + 8 * cc + 4 * zz2 + 2 * zz1 + yy)
            piece = wide[pl.ds(pl.multiple_of(base, 8), rows), :].astype(BF16)
            if m >= n:
                g1_keep[m - n] = piece
            elif last:
                y_send[n // 4 + m] = piece
            elif m < 3 * n // 4:
                y_first[m] = piece
            else:
                y_second[m - 3 * n // 4] = piece
        if last:
            for m in range(n // 4):
                y_send[m] = y_in[m]
    gb[...] = jnp.sum(gh.astype(F32), axis=0, keepdims=True)
    partn = dot_t(gh, fc1[...])
    part2 = dot(act, fc2[...])
    if last:
        partn = partn + gn_in[...]
        part2 = part2 + b2_in[...]
        b2_keep[...] = part2[:half]
        b2_send[...] = part2[half:].astype(BF16)
        gn_keep[...] = partn
        gn_send[:half] = partn[half:].astype(BF16)
        gn_send[half:] = partn[:half].astype(BF16)
    else:
        b2[...] = part2
        gn[...] = partn
    grad2 = dot_lt(act, gb2[...])
    if not fast:
        rows = zb_send.shape[0]
        if last:
            g2[...] = grad2[: 2 * rows].astype(BF16)
        else:
            g2a[...] = grad2[:rows].astype(BF16)
            g2m[...] = grad2[rows : 2 * rows].astype(BF16)
        zb_send[...] = grad2[2 * rows : 3 * rows].astype(BF16)
        zb_keep[...] = grad2[3 * rows :].astype(BF16)
    else:
        deep = grad2.shape[0] // 8
        half = deep // 2
        for m in range(8):
            if last:
                g2[m] = grad2[m * deep : m * deep + half].astype(BF16)
            else:
                mid = m * deep + half // 2
                g2a[m] = grad2[m * deep : mid].astype(BF16)
                g2m[m] = grad2[mid : mid + half // 2].astype(BF16)
            wide2[pl.ds(m * half, half), :] = grad2[m * deep + half : (m + 1) * deep]
        for m in range(8):
            near = [(m >> k) & 1 for k in (2, 1, 0)]
            zz1, zz2, yy = [own if r else 1 - own for own, r in zip((z1, z2, y), near)]
            base = half * (4 * zz2 + 2 * zz1 + yy)
            piece = wide2[pl.ds(pl.multiple_of(base, 8), half), :].astype(BF16)
            (zb_keep if m >= 4 else zb_send)[m % 4] = piece


def split_rows(value, wide, bit, send, keep):
    if len(send.shape) == 2:
        rows = value.shape[0] // 2
        send[...] = value[:rows].astype(BF16)
        keep[...] = value[rows:].astype(BF16)
        return
    wide[...] = value
    rows = send.shape[1]
    for m in range(send.shape[0]):
        base = 2 * m * rows
        send[m] = wide[pl.ds(pl.multiple_of(base + (1 - bit) * rows, 8), rows), :].astype(BF16)
        keep[m] = wide[pl.ds(pl.multiple_of(base + bit * rows, 8), rows), :].astype(BF16)


def feed(last, fast, per, sidx, bidx, normed2, gb2, fc1, bias, fc2, prev=()):
    tokens, width = normed2.shape
    hidden = fc1.shape[1]
    pairs = width // (2 * per)
    deep = hidden // 8
    if fast:
        outs = [SDS((8, deep // 2, width), BF16)] if last else [SDS((8, deep // 4, width), BF16)] * 2
        outs += [SDS((4, deep // 2, width), BF16)] * 2
    else:
        outs = [SDS((hidden // 2, width), BF16)] if last else [SDS((hidden // 4, width), BF16)] * 2
        outs += [SDS((hidden // 4, width), BF16)] * 2
    if last:
        send = [SDS((5 * pairs // 4, per, hidden), BF16)]
    else:
        send = [SDS((n, per, hidden), BF16) for n in (3 * pairs // 4, pairs // 4)]
    keep = SDS((pairs, per, hidden), BF16)
    if not fast:
        keep = SDS((width // 2, hidden), BF16)
        send = [keep] if last else [keep, SDS((8, LANES), BF16)]
    outs += send + [keep, SDS((1, hidden), F32)]
    if last:
        outs += [SDS((tokens // 2, width), F32), SDS((tokens // 2, width), BF16)]
        outs += [SDS((tokens, width), F32), SDS((tokens, width), BF16)]
    else:
        outs += [SDS((tokens, width), F32)] * 2
    return call(
        functools.partial(feed_kernel, last, fast),
        outs,
        (sidx, bidx, normed2, gb2, fc1, bias, fc2) + tuple(prev),
        [pltpu.VMEM((width, hidden), F32), pltpu.VMEM((hidden // 2, width), F32)],
        flops=12 * tokens * width * hidden,
        scalars=2,
    )


def by_batch_bit(arr, per):
    arr = arr.reshape(-1, 2, per, arr.shape[-1])
    own = lax.axis_index("batch") & 1
    return [pick(arr, 1 - own, 1), pick(arr, own, 1)]


def middle_back_kernel(
    sref, gn_keep, gn_got, middle, keeps, cp0, cp1, c0, c1, w_out, gain, gb2, gmid_own, gbr_out, gatt_send, sums
):
    s = sref[0]
    rows, width = gmid_own.shape
    cols = gatt_send.shape[1]
    hat, scale = normalize(middle[...])
    g = gn_keep[...] + gn_got[...].astype(F32)
    gout = jnp.concatenate([cots_of(cp0, c0), cots_of(cp1, c1)], axis=0)
    gmid = gout + normalize_back(g * gain[1:2, :], hat, scale)
    gbr = (keeps[:, 0:1] * gmid).astype(BF16)
    gbr_out[...] = gbr
    w_oth = w_out[pl.ds(pl.multiple_of((s ^ 2) * cols, HEAD), cols), :]
    gatt_send[...] = dot_t(gbr, w_oth).astype(BF16)
    gmid_own[...] = gmid[:rows]
    own = slice(0, rows)
    lines = [
        jnp.sum(g[own] * hat[own], axis=0, keepdims=True),
        jnp.sum(g[own], axis=0, keepdims=True),
        jnp.sum(gb2[own, :].astype(F32), axis=0, keepdims=True),
        jnp.sum(gbr[own].astype(F32), axis=0, keepdims=True),
        jnp.zeros((4, width), F32),
    ]
    sums[...] = jnp.concatenate(lines, axis=0)


def branch_back_kernel(
    per, sref, bref, gbr, w_out, a0, a2, middle, keeps, b2_keep, b2_got, bias, gain1, shift1, sums, fb_own, fb_oth,
    gatt, go_send, go_keep, early, opat, ospe, fcol, wide,
):
    s = sref[0]
    cols = a0.shape[1]
    rows, width = b2_keep.shape
    w_own = w_out[pl.ds(pl.multiple_of(s * cols, HEAD), cols), :]
    gatt[...] = dot_t(gbr[...], w_own).astype(BF16)
    for j, a in enumerate((a0, a2)):
        split_rows(dot_lt(a[...], gbr[...]), wide, bref[0] & 1, go_send.at[j], go_keep.at[j])
    res = middle[:rows, :] + keeps[:rows, 1:2] * (b2_keep[...] + b2_got[...].astype(F32) + bias[3:4, :])
    res = res.astype(BF16)
    opat[...] = res[: opat.shape[0]]
    ospe[...] = res[opat.shape[0] : opat.shape[0] + ospe.shape[0]]
    blank = functools.partial(jnp.zeros, dtype=F32)
    lines = [gain1[0:1, :], shift1[0:1, :], blank((HEAD + 2, width)), sums[:4, :], blank((LANES - HEAD - 8, width))]
    early[...] = jnp.concatenate(lines, axis=0).T
    lane = lane_of(cols)
    for j, ref in ((0, fb_own), (2, fb_oth)):
        fcol[...] = jnp.broadcast_to(ref[...], (LANES, ref.shape[1])).T
        at = pl.ds(pl.multiple_of((s ^ j) * cols, HEAD), cols)
        val = early[at, :]
        for k in range(4):
            lines = [fcol[(4 * b + k) * per : (4 * b + k + 1) * per, :] for b in range(cols // per)]
            val = jnp.where(lane == HEAD + 8 + k, jnp.concatenate(lines, axis=0), val)
        early[at, :] = val


def attend_back_kernel(first, heads, unroll, qa, ka, va, lse, ga, gx, out, sums, goa, dq, dk, dv):
    whole = qa.shape[1]
    half = ga.shape[0]
    lane = lane_of(half)
    for i in range(heads):
        h = first + i
        for ref, start in ((ga, 0), (gx, half)):
            if h < 2:
                t = ref[:, :LANES].astype(F32)
                t = jnp.where(lane < HEAD, t if h == 0 else pltpu.roll(t, HEAD, 1), 0.0)
            else:
                t = ref[:, LANES:].astype(F32)
                t = jnp.concatenate([t, jnp.zeros_like(t)], axis=1)
            goa[i, pl.ds(start, half), :] = t.astype(BF16)
    step = whole // 3

    def block(n, carry):
        i, b = n // 3, n % 3
        h = first + i
        at = pl.ds(pl.multiple_of(b * step, step), step)
        q, go = qa[h, at, :], goa[i, at, :]
        prob = jnp.exp(dot_t(ka[h], q) - lse[h, b][0:1, :])
        gp = dot_t(va[h], go)
        inner = jnp.sum(gp * prob, axis=0, keepdims=True)
        gs = (prob * (gp - inner)).astype(BF16)
        pv = dot(prob.astype(BF16), go)
        pk = dot(gs, q)
        dq[i, at, :] = dot_lt(gs, ka[h])

        dv[i] = jnp.where(b == 0, pv, dv[i] + pv)
        dk[i] = jnp.where(b == 0, pk, dk[i] + pk)
        return carry

    lax.fori_loop(0, 3 * heads, block, 0, unroll=unroll)
    for i in range(heads):
        out[i, :, :LANES] = pack_pair(dq[i] * HEAD**-0.5, dk[i]).astype(BF16)
        out[i, :, LANES:] = dv[i, :, :HEAD].astype(BF16)
        sums[i] = jnp.sum(out[i].astype(F32), axis=0, keepdims=True)


def attend_back(first, heads, qa, ka, va, lse, ga, gx):
    whole = qa.shape[1]
    return call(
        functools.partial(attend_back_kernel, first, heads),
        [SDS((heads, whole, 3 * HEAD), BF16), SDS((heads, 1, 3 * HEAD), F32)],
        (qa, ka, va, lse, ga, gx),
        [pltpu.VMEM((heads, whole, LANES), BF16)] + [pltpu.VMEM((heads, whole, LANES), F32)] * 3,
        flops=10 * heads * whole * whole * LANES,
    )


def norm1_kernel(g01, g2, w, keep, send):
    rows = keep.shape[0] // 2
    cols = g2.shape[2]
    for i in range(4):
        at = pl.ds(i * rows, rows)
        part = dot_t(g01[0, at, :], w[:, :cols])
        part = part + dot_t(g01[1, at, :], w[:, cols : 2 * cols])
        part = part + dot_t(g2[0, at, :], w[:, 2 * cols : 3 * cols])
        to = pl.ds((i // 2) * rows, rows)
        if i % 2 == 0:
            keep[to, :] = part
        else:
            send[to, :] = part.astype(BF16)


def qkv_grad(sref, normed, grads, sums, w, first, tile, bound):
    width, cols = w.shape[0], grads[0].shape[1]
    g = jnp.concatenate([dot_lt(normed[...], v) for v in grads], axis=1)
    w32 = w[:, first * cols : (first + len(grads)) * cols].astype(F32)
    rows = jnp.concatenate(sums, axis=1)
    both = jnp.sum(g * w32, axis=-1, keepdims=True)
    gshift = jnp.sum(w32 * rows, axis=-1, keepdims=True)
    lane = lane_of(width)
    old = bound[...]
    tile[...] = jnp.where(lane == HEAD, old + both, jnp.where(lane == HEAD + 1, old + gshift, old))
    ones = jnp.ones((grads[0].shape[0], LANES), BF16)
    at = pl.multiple_of(sref[0] * cols, HEAD)
    lanes = lane_of(HEAD)
    for i, v in enumerate(grads):
        col = dot_lt(v, ones)
        here = pl.ds(at + (first + i) * HEAD, HEAD)
        row = tile[here, :]
        row = jnp.where(lanes == HEAD + 2, col[:HEAD], row)
        tile[here, :] = jnp.where(lanes == HEAD + 3, col[2 * HEAD :], row)
    return g


def heads_kernel(
    fast, sref, bref, qa, ka, va, lse, ga, gx, normed, w, early, g01, send, keep, tile,
    s01, goa, dq, dk, dv, wide,
):
    attend_back_kernel(0, 2, 2, qa, ka, va, lse, ga, gx, g01, s01, goa, dq, dk, dv)
    g = qkv_grad(sref, normed, (g01[0], g01[1]), (s01[0], s01[1]), w, 0, tile, early)
    if not fast:
        rows = g.shape[0] // 2
        send[...] = g[:rows].astype(BF16)
        keep[...] = g[rows:].astype(BF16)
        return
    wide[...] = g
    y, z1, z2 = bref[0] & 1, (bref[0] >> 1) & 1, bref[0] >> 2
    per, cols = send.shape[1], g.shape[1]
    for m in range(8):
        zz1 = z1 if m & 4 else 1 - z1
        zz2 = z2 if m & 2 else 1 - z2
        for j in range(2):
            base = per * ((2 * (m & 1) + j) * 8 + 4 * zz2 + 2 * zz1)
            to = slice(j * cols, (j + 1) * cols)
            send[m, :, to] = wide[pl.ds(pl.multiple_of(base + (1 - y) * per, 8), per), :].astype(BF16)
            keep[m, :, to] = wide[pl.ds(pl.multiple_of(base + y * per, 8), per), :].astype(BF16)


def tail_kernel(
    sref, bref, qa, ka, va, lse, ga, gx, normed, g01, w, early, gn_keep, gn_send, send, keep,
    g2, s2, goa, dq, dk, dv, tile, wide,
):
    attend_back_kernel(2, 1, 1, qa, ka, va, lse, ga, gx, g2, s2, goa, dq, dk, dv)
    norm1_kernel(g01, g2, w, gn_keep, gn_send)
    g = qkv_grad(sref, normed, (g2[0],), (s2[0],), w, 2, tile, early)
    width = g.shape[0]
    lane = lane_of(width)
    val = tile[...]
    gshift = val[:, HEAD + 1 : HEAD + 2]
    ggain = (val[:, HEAD : HEAD + 1] - val[:, 1:2] * gshift) / val[:, 0:1]
    val = jnp.where(lane == HEAD, ggain, val)
    last = jnp.concatenate([g[:, LANES:], jnp.zeros((width, LANES - HEAD), F32)], axis=1)
    out = jnp.concatenate([g[:, :LANES], jnp.where(lane < HEAD, last, val)], axis=1)
    split_rows(out, wide, bref[0] & 1, send, keep)


def wide_sum(*parts):
    return sum(p.astype(F32) for p in parts[1:]) + parts[0].astype(F32)


def stage0_kernel(own_keep, own_got, oth_keep, oth_got, msg, part):
    for i in range(2):
        msg[i] = wide_sum(own_keep[i], own_got[i]).astype(BF16)
        msg[2 + i] = wide_sum(oth_keep[i], oth_got[i]).astype(BF16)
        part[i] = wide_sum(own_keep[2 + i], own_got[2 + i])
        part[2 + i] = wide_sum(oth_keep[2 + i], oth_got[2 + i])


def stage1_kernel(
    bref, keep_own, keep_oth, y1, y2, fc2, g2a, g2m, out, y3, part_0, got_0, q_send,
    msg_z, msg_y, msg_x, part_f, part_a, part_o, part_p,
):
    y, z1, z2 = bref[0] & 1, (bref[0] >> 1) & 1, bref[0] >> 2
    n = keep_own.shape[0] // 2
    for i in range(n):
        more = n // 2
        msg_z[i] = wide_sum(keep_own[i], y2[more + i]).astype(BF16)
        msg_z[n + i] = wide_sum(keep_oth[i], y1[i]).astype(BF16)
        part_f[i] = wide_sum(keep_own[n + i], y2[more + n + i])
        part_f[n + i] = wide_sum(keep_oth[n + i], y1[n + i] if i < more else y2[i - more])
        msg_y[8 + i] = q_send[i]
    rows = g2a.shape[1]
    for i in range(4):
        zz1 = z1 if i >> 1 else 1 - z1
        zz2 = z2 if i & 1 else 1 - z2
        m = 2 * zz2 + zz1
        msg_x[i] = wide_sum(out[1, m], y3[1, m]).astype(BF16)
        part_o[i] = wide_sum(out[0, m], y3[0, m])
        for k, got in enumerate((g2a, g2m)):
            at = slice(k * rows, (k + 1) * rows)
            b = 2 * m + 1 - y
            msg_y[2 * i + k] = wide_sum(fc2[b, at], got[b]).astype(BF16)
            b = 2 * m + y
            part_a[2 * i + k] = wide_sum(fc2[b, at], got[b])
    for i in range(2):
        for k in range(2):
            at = slice(k * rows, (k + 1) * rows)
            msg_x[4 + 2 * i + k] = wide_sum(part_0[2 + i, at], got_0[2 + i, at]).astype(BF16)
            part_p[2 * i + k] = wide_sum(part_0[i, at], got_0[i, at])


def stage2_kernel(
    part_f, got_z, part_a, got_y, part_o, got_x, part_p, q_keep, q2_send, msg_x, msg_z, msg_y, part_g, part_c, part_q
):
    n, _, cols = q2_send.shape
    for i in range(n):
        msg_y[i] = q2_send[i]
    for half in range(2):
        for i in range(4):
            k = 8 * half + i
            msg_x[4 * half + i] = wide_sum(part_f[k], got_z[k]).astype(BF16)
            part_g[4 * half + i] = wide_sum(part_f[k + 4], got_z[k + 4])
    for i in range(4):
        msg_z[i] = wide_sum(part_a[i], got_y[i]).astype(BF16)
        part_c[i] = wide_sum(part_a[4 + i], got_y[4 + i])
        msg_z[6 + i] = wide_sum(q_keep[i], got_y[8 + i]).astype(BF16)
        part_c[6 + i] = wide_sum(q_keep[4 + i], got_y[12 + i])
    for i in range(2):
        msg_z[4 + i] = wide_sum(part_o[i], got_x[i]).astype(BF16)
        part_c[4 + i] = wide_sum(part_o[2 + i], got_x[2 + i])
        rest = wide_sum(part_p[i], got_x[4 + i]).astype(BF16)
        for k in range(3):
            msg_y[n + 3 * i + k] = rest[:, k * cols : (k + 1) * cols]
        part_q[i] = wide_sum(part_p[2 + i], got_x[6 + i])


def stage3_kernel(bref, part_g, got_x, part_c, got_z, q_keep, got_y, msg, kept, z1, z2, z3, q_kept):
    for half in range(2):
        for i in range(2):
            k, other = 4 * half + i, 4 * (1 - half) + i
            msg[2 * half + i] = wide_sum(part_g[k], got_x[other]).astype(BF16)
            kept[2 * half + i] = wide_sum(part_g[k + 2], got_x[other + 2])
    for to, a, b in ((4, 0, 2), (5, 1, 3), (6, 4, 5), (7, 6, 8), (8, 7, 9)):
        msg[to] = wide_sum(part_c[a], got_z[a]).astype(BF16)
        kept[to] = wide_sum(part_c[b], got_z[b])
    q = bref[0] >> 1
    for r in range(4):
        for k, ref in enumerate((q_kept, z1, z2, z3)):
            m = r * 4 + (q ^ k)
            ref[r] = wide_sum(q_keep[m], got_y[m]).astype(ref.dtype)


def shift_kernel(keep, got, send):
    rows = send.shape[0]
    send[...] = wide_sum(keep[rows:, :], got[rows:, :]).astype(BF16)


def sums_kernel(kept, got, part_q, got_q, swap_send, swap_keep, fc2, out):
    per = out.shape[0]
    for half in range(2):
        at = pl.ds(half * per, per)
        swap_send[at, :] = wide_sum(kept[2 * half], got[2 * half]).astype(BF16)
        swap_keep[at, :] = wide_sum(kept[2 * half + 1], got[2 * half + 1])
        fc2[at, :] = wide_sum(kept[4 + half], got[4 + half])
        cols = got_q.shape[2]
        for k in range(3):
            at3 = slice(k * cols, (k + 1) * cols)
            fc2[pl.ds((2 + half) * per, per), at3] = wide_sum(part_q[half, :, at3], got_q[16 + 3 * half + k])
    out[...] = wide_sum(kept[6], got[6])


def owner_kernel(sref, most, got, kept, z1, z2, z3, s1, s2, s3, own, every):
    s = sref[0]
    cols = most.shape[2] // 2
    for m in range(4):
        at = slice((m % 2) * cols, (m % 2 + 1) * cols)
        every[m, :, :cols] = wide_sum(most[7 + m // 2, :, at], got[7 + m // 2, :, at])
        every[m, :, cols:] = wide_sum(kept[m], z1[m], z2[m], z3[m])
    for k, ref in enumerate((own, s1, s2, s3)):
        ref[...] = every[s ^ k].astype(ref.dtype)


def final_kernel(k0, c0, x0, p0, s0, gmid, gain, gpat, gspe):
    rows, width = x0.shape
    count = gpat.shape[0]
    hat, scale = normalize(tokens_of(p0, s0))
    g = wide_sum(k0[:rows], c0[:rows], x0[...])
    res = gmid[...] + normalize_back(g * gain[0:1, :], hat, scale)
    gpat[...] = res[:count]
    gspe[...] = res[count : count + gspe.shape[0]]


def collect_kernel(
    sref, own, g1, g2, g3, swap_keep, swap_got, out, gains, shifts, biases, fc1_bias, fc1, every
):
    s = sref[0]
    per, hidden = swap_keep.shape[0] // 2, swap_keep.shape[1]
    for j, value in ((0, swap_keep[:per]), (2, swap_keep[per:]), (1, swap_got[:per]), (3, swap_got[per:])):
        fc1[:, pl.ds(pl.multiple_of((s ^ j) * hidden, LANES), hidden)] = value.astype(F32)
    for k, ref in enumerate((own, g1, g2, g3)):
        every[k] = ref[...].astype(F32)
    pieces = [every[s ^ a] for a in range(4)]

    def part(u):
        j, a, h = u // 12, (u // 3) % 4, u % 3
        e = 3 * h + j
        return pieces[a][:, (e // 2) * LANES : (e // 2 + 1) * LANES], e % 2

    lane = lane_of(out.shape[0])
    for t in range(out.shape[1] // LANES):
        (low, lo), (high, hi) = part(2 * t), part(2 * t + 1)
        low = pltpu.roll(low, HEAD, 1) if lo else low
        high = high if hi else pltpu.roll(high, HEAD, 1)
        out[:, t * LANES : (t + 1) * LANES] = jnp.where(lane < HEAD, low, high)
    tail = 4 * LANES
    vec = wide_sum(*[every[k, :, tail:] for k in range(4)])
    vec = jnp.concatenate([vec, jnp.zeros((LANES - per, LANES), F32)], axis=0).T
    for ref, lines in ((gains, (0, 4)), (shifts, (1, 5)), (biases, (2, 3, 7, 6))):
        for i, k in enumerate(lines):
            ref[i : i + 1, :] = vec[HEAD + k : HEAD + k + 1, :per]
    flat = jnp.zeros((8, LANES), F32)
    for k in range(4):
        line = jnp.broadcast_to(vec[HEAD + 8 + k : HEAD + 9 + k], (8, LANES))
        flat = flat + (pltpu.roll(line, k * per, 1) if k else line)
    fc1_bias[...] = flat[:1, : 4 * per]


def pick(arr, index, axis):
    return lax.dynamic_index_in_dim(arr, index, axis, keepdims=False)


def total(parts):
    out = parts[0].astype(F32)
    for part in parts[1:]:
        out = out + part.astype(F32)
    return out


def swap(kind, v, mask):
    return lax.ppermute(v, kind, [(i, i ^ mask) for i in range(lax.axis_size(kind))])


def swap_seq(v, mask):
    return swap("seq", v, mask)


def after(value, *first):
    return lax.optimization_barrier((value, first))[0]


def bits_of(kind):
    return lax.axis_size(kind).bit_length() - 1


def split_bits(arr, axis, count):
    shape = arr.shape
    return arr.reshape(shape[:axis] + (2,) * count + shape[axis + 1 :])


def to_send(parts, axis, bit, kind):
    own = (lax.axis_index(kind) >> bit) & 1
    send = total([pick(p, 1 - own, axis) for p in parts]).astype(BF16)
    return send, [pick(p, own, axis) for p in parts]


def send_four(parts, axis, low):
    own = (lax.axis_index("batch") >> low) & 3

    def quarter(p, k):
        return pick(pick(p, k >> 1, axis), k & 1, axis)

    sends = [total([quarter(p, own ^ k) for p in parts]).astype(BF16) for k in (1, 2, 3)]
    return sends, [quarter(p, own) for p in parts]


def swap_four(sends, low):
    return [swap("batch", v, k << low) for k, v in zip((1, 2, 3), sends)]


def sum_rest(parts, axis, low):
    top = bits_of("batch")
    while low < top:
        if low + 1 < top:
            sends, kept = send_four(parts, axis + top - low - 2, low)
            parts, low = kept + swap_four(sends, low), low + 2
        else:
            send, kept = to_send(parts, axis, low, "batch")
            parts, low = kept + [swap("batch", send, 1 << low)], low + 1
    return total(parts)


def body(
    patches,
    specials,
    segment_ids,
    special_order,
    keep_mask,
    norm_gains,
    norm_shifts,
    w_qkv,
    biases,
    w_out,
    w_fc1,
    fc1_bias,
    w_fc2,
    cot_patches,
    cot_specials,
):
    count, width = patches.shape[1:]
    extra = specials.shape[1]
    images = keep_mask.shape[1] // 2
    block = count + PAD
    chip = 2 * block
    whole = 4 * block
    cols = OWN * HEAD
    hidden = w_fc1.shape[1] // 4
    s = lax.axis_index("seq")
    sidx = s.astype(jnp.int32).reshape(1)
    bidx = lax.axis_index("batch").astype(jnp.int32).reshape(1)
    nb = lax.axis_size("batch")
    nbits = bits_of("batch")

    own_p, own_cot = patches[0], cot_patches[0]
    got_px = swap_seq(own_p, 2)
    got_pc = swap_seq(own_p, 1)
    (small,) = call(
        small_kernel,
        [SDS((32, width), BF16)],
        (specials[0], segment_ids, special_order, cot_specials[0]),
        [pltpu.VMEM((extra, width), BF16), pltpu.VMEM((1, count), jnp.int32), pltpu.VMEM((1, extra), jnp.int32)]
        + [pltpu.VMEM((extra, width), BF16), pltpu.VMEM((32, width), F32), pltpu.SemaphoreType.DMA((4,))],
        far=(0, 1, 2, 3),
    )
    got_sx = swap_seq(small, 2)
    got_sc = swap_seq(small, 1)
    cot_c = swap_seq(own_cot, 1)
    fb = fc1_bias.reshape(1, -1)
    sidx, bidx, small = lax.optimization_barrier((sidx, bidx, small))
    w_own, bias_own = call(
        prep_kernel,
        [SDS((width, 5 * LANES), BF16), SDS((1, 5 * LANES), F32)],
        (sidx, w_qkv, biases),
        [pltpu.VMEM((3 * OWN, width, LANES), BF16), pltpu.VMEM(biases.shape, F32)]
        + [pltpu.SemaphoreType.DMA((3 * OWN + 1,))],
        scalars=1,
        far=(1, 2),
    )
    headed = SDS((OWN, chip, LANES), BF16)
    q0, k0, v0, n0, toks, keeps = call(
        project_kernel,
        [headed] * 3 + [SDS((chip, width), BF16), SDS((chip, width), BF16), SDS((chip, LANES), F32)],
        (keep_mask, own_p, small, got_pc, got_sc, norm_gains, norm_shifts, w_own, bias_own),
        flops=2 * chip * width * 3 * cols,
        scalars=1,
    )
    got_px, got_sx, n0 = lax.optimization_barrier((got_px, got_sx, n0))
    got_pd = swap_seq(got_px, 1)
    got_sd = swap_seq(got_sx, 1)

    headed = SDS((OWN, whole, LANES), BF16)
    heads32 = SDS((OWN, chip, LANES), F32)
    qa, ka, va, att_send, other, normed = call(
        attend_first_kernel,
        [headed] * 3 + [SDS((chip, cols), BF16), heads32, SDS((whole, width), BF16)],
        (q0, k0, v0, n0, got_px, got_sx, got_pd, got_sd, norm_gains, norm_shifts, w_own, bias_own),
        flops=2 * chip * width * 3 * cols + 2 * OWN * whole * whole * LANES,
    )
    a2 = swap_seq(att_send, 2)
    a0, lse, w1, w2, w3, w4 = call(
        attend_second_kernel,
        [SDS((chip, cols), BF16), SDS((OWN, 3, 8, whole // 3), F32)]
        + [SDS((width, hidden), BF16), SDS((hidden, width), BF16)] * 2,
        (sidx, qa, ka, va, other, w_fc1, w_fc2),
        [pltpu.VMEM((OWN, chip, LANES), F32), pltpu.SemaphoreType.DMA((2, 2))],
        flops=2 * OWN * whole * whole * LANES,
        scalars=1,
        far=(5, 6),
    )
    a1 = swap_seq(a0, 1)
    a3 = swap_seq(a2, 1)

    middle, normed2, gb2 = call(
        middle_kernel,
        [SDS((chip, width), F32), SDS((chip, width), BF16), SDS((chip, width), BF16)],
        (sidx, a0, a1, a2, a3, toks, keeps, own_cot, cot_c, small, got_sc, w_out, biases, norm_gains, norm_shifts),
        flops=2 * chip * width * width,
        scalars=1,
    )
    per = width // (4 * nb)
    fast = nb == 8
    fc2_a, fc2_m, zo_send, zo_keep, y1, y_rest, keep_oth, fb_oth, b2, gn = feed(
        False, fast, per, sidx, bidx, normed2, gb2, w1, fb, w2
    )
    got2a = swap_seq(fc2_a, 2)
    if not fast:
        y1, keep_oth = by_batch_bit(jnp.concatenate([y1, keep_oth], axis=0), per)
    got_y1 = swap("batch", y1, 1)
    got_zo = swap("batch", zo_send, 2) if fast else zo_send
    ahead = (got2a, got_y1, got_zo)
    fc2_keep, zn_send, zn_keep, y2, keep_own, fb_own, b2_keep, b2_send, gn_keep, gn_send = feed(
        True, fast, per, sidx, bidx, normed2, gb2, w3, fb, w4, (b2, gn, y_rest)
    )
    if not fast:
        y2, keep_own = by_batch_bit(jnp.concatenate([y2, keep_own], axis=0), per)
    gn_send, b2_send, zn_send, y2, (got2a, got_y1, got_zo) = lax.optimization_barrier(
        (gn_send, b2_send, zn_send, y2, ahead)
    )
    gn_got = swap_seq(gn_send, 1)
    b2_got = swap_seq(b2_send, 1)
    got_zn = swap("batch", zn_send, 2) if fast else zn_send
    got_y2 = swap("batch", y2, 1)

    gmid, gbr, gatt_send, line_sums = call(
        middle_back_kernel,
        [SDS((block, width), F32), SDS((chip, width), BF16), SDS((chip, cols), BF16), SDS((8, width), F32)],
        (sidx, gn_keep, gn_got, middle, keeps, own_cot, cot_c, small, got_sc, w_out, norm_gains, gb2),
        flops=2 * chip * width * cols,
        scalars=1,
    )
    gatt_x = swap_seq(gatt_send, 2)
    if fast:
        split = SDS((2, cols // (2 * per), per, width), BF16)
    else:
        split = SDS((2, cols // 2, width), BF16)
    gatt, go_send, go_keep, early, opat, ospe = call(
        functools.partial(branch_back_kernel, per),
        [SDS((chip, cols), BF16), split, split, SDS((width, LANES), F32)]
        + [SDS((count, width), BF16), SDS((extra, width), BF16)],
        (sidx, bidx, gbr, w_out, a0, a2, middle, keeps, b2_keep, b2_got, biases, norm_gains, norm_shifts)
        + (line_sums, fb_own, fb_oth),
        [pltpu.VMEM((hidden, LANES), F32), pltpu.VMEM((cols, width), F32)],
        flops=6 * chip * width * cols,
        scalars=2,
    )
    if not fast:
        halves = [by_batch_bit(jnp.concatenate([go_send[j], go_keep[j]], axis=0), per) for j in range(2)]
        go_send, go_keep = [jnp.stack([halves[j][k] for j in range(2)]) for k in range(2)]
    got_o = swap("batch", go_send, 1)
    msg_0, part_0 = None, None
    if fast:
        msg_0, part_0 = call(
            stage0_kernel,
            [SDS(zn_keep.shape, BF16), SDS(zn_keep.shape, F32)],
            (zn_keep, after(got_zn, go_send), zo_keep, got_zo),
        )
        gatt_x = after(gatt_x, msg_0)
    gatt_x, fc2_m = lax.optimization_barrier((after(gatt_x, go_send), fc2_m))
    got2m = swap_seq(fc2_m, 2)
    pairs = (keep_own, keep_oth, got_y1, got_y2)

    def heads_scratch(heads):
        return [pltpu.VMEM((heads, whole, LANES), BF16)] + [pltpu.VMEM((heads, whole, LANES), F32)] * 3

    def first_heads(lse):
        if fast:
            split = [SDS((8, per, 4 * cols), BF16)] * 2
        else:
            split = [SDS((width // 2, 2 * cols), BF16)] * 2
        return call(
            functools.partial(heads_kernel, fast),
            [SDS((2, whole, cols), BF16)] + split + [SDS((width, LANES), F32)],
            (sidx, bidx, qa, ka, va, lse, gatt, gatt_x, normed, w_own, early),
            [pltpu.VMEM((2, 1, cols), F32)] + heads_scratch(2) + [pltpu.VMEM((width, 2 * cols), F32)],
            flops=20 * whole * whole * LANES,
            scalars=2,
            room=20,
        )

    def tail_part(lse, g01, tile):
        wide = cols + HEAD
        if fast:
            outs = [SDS((width // (2 * per), per, wide), BF16)] * 2
        else:
            outs = [SDS((width // 2, wide), BF16)] * 2
        return call(
            tail_kernel,
            [SDS((chip, width), F32), SDS((chip, width), BF16)] + outs,
            (sidx, bidx, qa, ka, va, lse, gatt, gatt_x, normed, g01, w_own, tile),
            [pltpu.VMEM((1, whole, cols), BF16), pltpu.VMEM((1, 1, cols), F32)]
            + heads_scratch(1)
            + [pltpu.VMEM((width, LANES), F32), pltpu.VMEM((width, wide), F32)],
            flops=10 * whole * whole * LANES,
            scalars=2,
            room=20,
        )

    rest = (sidx, bidx, per, block, chip, hidden, cols, count, extra, width)
    zs = (zn_send, zn_keep, zo_send, zo_keep, msg_0, part_0)
    reduce_all = reduce_eight if fast else reduce_any
    out_fc2, out_out, out_fc1, out_qkv, smalls, gpat, gspe = reduce_all(
        rest, pairs, (fc2_keep, got2a, got2m, zs), (go_keep, got_o), lse, gatt_x,
        first_heads, tail_part, (own_p, small), gmid, norm_gains,
    )
    grad_gains, grad_shifts, grad_biases, grad_fc1_bias = smalls
    return (
        opat[None],
        ospe[None],
        gpat[None],
        gspe[None],
        grad_gains,
        grad_shifts,
        out_qkv,
        grad_biases,
        out_out,
        out_fc1,
        grad_fc1_bias.reshape(-1),
        out_fc2,
    )


def reduce_eight(
    rest, pairs, twos, outs, lse, gatt_x, first_heads, tail_part, pay, gmid, gains
):
    sidx, bidx, per, block, chip, hidden, cols, count, extra, width = rest
    fc2_keep, got2a, got2m, zs = twos
    go_keep, got_o = outs
    deep = hidden // 8
    got_0 = swap("batch", zs[4], 4)
    part_0 = zs[5]
    g01, q01_send, q01_keep, tile = first_heads(after(lse, gatt_x))
    g01, got_y2, got2m, got_o, got_0 = lax.optimization_barrier((g01, pairs[3], got2m, got_o, got_0))
    keep_own, keep_oth, got_y1 = pairs[:3]

    def blocks(n, dtype=BF16):
        return SDS((n, per, width), dtype)

    msg_z, msg_y, msg_x, part_f, part_a, part_o, part_p = call(
        stage1_kernel,
        [blocks(16), blocks(16), blocks(8), blocks(16, F32), blocks(8, F32), blocks(4, F32), blocks(4, F32)],
        (bidx, keep_own, keep_oth, got_y1, got_y2, fc2_keep, got2a, got2m, go_keep, got_o, part_0, got_0)
        + (q01_send,),
        scalars=1,
    )
    msg_z, msg_y, msg_x, lse = lax.optimization_barrier((msg_z, msg_y, msg_x, after(lse, g01)))
    got_z = swap("batch", msg_z, 2)
    got_y = swap("batch", msg_y, 1)
    got_x = swap_seq(msg_x, 2)
    gn1_keep, gn1_send, q_send, q_keep = tail_part(lse, g01, tile)
    gn1_send, got_x, got_y, got_z = lax.optimization_barrier((gn1_send, got_x, got_y, got_z))
    gn1_c = swap_seq(gn1_send, 1)
    part = SDS((22, per, cols + HEAD), BF16)
    msg_x, msg_z, msg_y, part_g, part_c, part_q = call(
        stage2_kernel,
        [blocks(8), blocks(10), part, blocks(8, F32), blocks(10, F32), blocks(2, F32)],
        (part_f, got_z, part_a, got_y, part_o, got_x, part_p, q01_keep, q_send),
    )
    got_x = swap_seq(msg_x, 2)
    got_z = swap("batch", msg_z, 2)
    got_y = swap("batch", msg_y, 1)
    (xsend,) = call(shift_kernel, [SDS((block, width), BF16)], (after(gn1_keep, msg_x), gn1_c))
    gn1_x = swap_seq(xsend, 2)
    quarter = SDS((4, per, cols + HEAD), BF16)
    msg, kept, q1, q2, q3, q_kept = call(
        stage3_kernel,
        [blocks(9), blocks(9, F32), quarter, quarter, quarter, SDS(quarter.shape, F32)],
        (bidx, part_g, after(got_x, xsend), part_c, got_z, q_keep, got_y),
        scalars=1,
    )
    got_last = swap("batch", msg, 4)
    got_qz = swap_four((q1, q2, q3), 1)
    gpat, gspe = call(
        final_kernel,
        [SDS((count, width), F32), SDS((extra, width), F32)],
        (gn1_keep, gn1_c, after(gn1_x, q1), *pay, gmid, gains),
    )
    got_last = after(got_last, gpat)
    row = SDS((per, 5 * LANES), BF16)
    s1, s2, s3, own = call(
        owner_kernel,
        [row, row, row, SDS(row.shape, F32)],
        (sidx, kept, got_last, q_kept, *got_qz),
        [pltpu.VMEM((4, per, 5 * LANES), F32)],
        scalars=1,
    )
    swap_send, swap_keep, out_fc2, out_out = call(
        sums_kernel,
        [SDS((2 * per, width), BF16), SDS((2 * per, width), F32), SDS((deep, width), F32), SDS((per, width), F32)],
        (kept, after(got_last, s1), part_q, got_y),
    )
    swap_got = swap_seq(swap_send, 1)
    gots = [swap_seq(v, k) for k, v in ((1, s1), (2, s2), (3, s3))]
    lines = [SDS((2, per), F32), SDS((2, per), F32), SDS((4, per), F32), SDS((1, 4 * per), F32)]
    out_qkv, *smalls, out_fc1 = call(
        collect_kernel,
        [SDS((per, 3 * width), F32), *lines, SDS((per, 4 * hidden), F32)],
        (sidx, own, *gots, swap_keep, swap_got),
        [pltpu.VMEM((4, per, 5 * LANES), F32)],
        scalars=1,
    )
    return out_fc2, out_out, out_fc1, out_qkv, smalls, gpat, gspe


def reduce_any(
    rest, pairs, twos, outs, lse, gatt_x, first_heads, tail_part, pay, gmid, gains
):
    sidx, bidx, per, block, chip, hidden, cols, count, extra, width = rest
    s = lax.axis_index("seq")
    nb = lax.axis_size("batch")
    nbits = bits_of("batch")
    low = nbits - 1
    fc2_keep, got2a, got2m, zs = twos
    go_keep, got_o = outs
    keep_own, keep_oth, got_oth, got_own = [
        split_bits(p.reshape(2, 2, nb // 2, per, hidden), 2, low) for p in pairs
    ]
    g01, q01_top, q01_low, tile = first_heads(lse)
    send_own, parts_own = to_send([keep_own, got_own], 0, 1, "seq")
    send_oth, parts_oth = to_send([keep_oth, got_oth], 0, 1, "seq")
    got_b = swap_seq(jnp.concatenate([send_own, send_oth], axis=-1), 2)
    sum_own = sum_rest(parts_own + [got_b[..., hidden:]], 1, 1)
    sum_oth = sum_rest(parts_oth + [got_b[..., :hidden]], 1, 1)
    own_c = s & 1
    other = jnp.concatenate([pick(sum_own, 1 - own_c, 0), pick(sum_oth, 1 - own_c, 0)], axis=-1)
    got = swap_seq(other.astype(BF16), 1).astype(F32)
    rel = jnp.stack([pick(sum_own, own_c, 0), got[:, :hidden], pick(sum_oth, own_c, 0), got[:, hidden:]])
    out_fc1 = jnp.concatenate([pick(rel, s ^ a, 0) for a in range(4)], axis=1)
    zn_send, zn_keep, zo_send, zo_keep = zs[:4]
    got2 = jnp.concatenate([got2a, got2m, swap_seq(jnp.concatenate([zo_send, zo_keep], axis=0), 2)], axis=0)
    fc2_keep = jnp.concatenate([fc2_keep, zn_send, zn_keep], axis=0)
    parts = [split_bits(p.reshape(nb, -1, width), 0, nbits) for p in (fc2_keep, got2)]
    out_fc2 = sum_rest(parts, 0, 0)
    parts = [split_bits(p.reshape(2, nb // 2, per, width), 1, low) for p in (go_keep, got_o)]
    parts = [p[0] for p in parts] + [swap_seq(total([p[1] for p in parts]).astype(BF16), 2)]
    out_out = sum_rest(parts, 0, 1)
    gn1_keep, gn1_send, q2_top, q2_low = tail_part(lse, g01, tile)
    q_all = [jnp.concatenate(v, axis=1) for v in ((q01_top, q2_top), (q01_low, q2_low))]
    q_send, q_keep = by_batch_bit(jnp.concatenate(q_all, axis=0), per)
    gn1_c = swap_seq(gn1_send, 1)
    gn1_x = swap_seq((gn1_keep[block:] + gn1_c[block:].astype(F32)).astype(BF16), 2)
    gpat, gspe = call(
        final_kernel,
        [SDS((count, width), F32), SDS((extra, width), F32)],
        (gn1_keep, gn1_c, gn1_x, *pay, gmid, gains),
    )
    wide = 5 * LANES
    parts = [split_bits(p.reshape(4, nb // 2, per, wide), 1, low) for p in (q_keep, swap("batch", q_send, 1))]
    sum_q = sum_rest(parts, 1, 1)
    pieces = [pick(sum_q, s, 0)] + [
        swap_seq(pick(sum_q, s ^ j, 0).astype(BF16), j).astype(F32) for j in (1, 2, 3)
    ]
    rel = jnp.stack([p[:, : 3 * cols] for p in pieces])
    absolute = jnp.stack([pick(rel, s ^ a, 0) for a in range(4)], axis=1)
    out_qkv = absolute.reshape(-1, 4, OWN, 3, HEAD).transpose(0, 3, 1, 2, 4).reshape(-1, 3 * width)
    vec = total([p[:, 3 * cols :] for p in pieces]).T
    smalls = [vec[jnp.array(k)] for k in ((0, 4), (1, 5), (2, 3, 7, 6), (8, 9, 10, 11))]
    return out_fc2, out_out, out_fc1, out_qkv, smalls, gpat, gspe


def solution(mesh):
    tok = P("batch", "seq", None)
    ids = P("batch", "seq")
    split = P(None, ("seq", "batch"))
    rows = P(("seq", "batch"), None)
    return jax.shard_map(
        body,
        mesh=mesh,
        in_specs=(tok, tok, ids, ids, P("batch", None)) + (P(),) * 8 + (tok, tok),
        out_specs=(tok, tok, tok, tok, split, split, rows, split, rows, rows, P(("seq", "batch")), rows),
        check_vma=False,
    )
```

```python
import functools

import jax
import jax.numpy as jnp
from jax import lax
from jax.experimental import pallas as pl
from jax.experimental.pallas import tpu as pltpu
from jax.sharding import PartitionSpec as P

HEADS = 12
HEAD = 64
PAD = 32
SPECIAL = 4
LANES = 128
OWN = 3
FAR = -(2.0**100)
F32 = jnp.float32
BF16 = jnp.bfloat16
SDS = jax.ShapeDtypeStruct


def dot(a, b):
    return jnp.dot(a, b, preferred_element_type=F32)


def dot_t(a, b):
    return lax.dot_general(a, b, (((1,), (1,)), ((), ())), preferred_element_type=F32)


def dot_lt(a, b):
    return lax.dot_general(a, b, (((0,), (0,)), ((), ())), preferred_element_type=F32)


def normalize(v):
    center = v - jnp.mean(v, axis=-1, keepdims=True)
    spread = jnp.mean(center * center, axis=-1, keepdims=True)
    scale = lax.rsqrt(spread + 1e-06)
    return center * scale, scale


def normalize_back(grad_hat, hat, scale):
    mean_g = jnp.mean(grad_hat, axis=-1, keepdims=True)
    mean_gh = jnp.mean(grad_hat * hat, axis=-1, keepdims=True)
    return scale * (grad_hat - mean_g - hat * mean_gh)


def gelu_pair(v):
    half = 0.5 * (1.0 + lax.erf(v * 0.5**0.5))
    slope = half + v * jnp.exp(-0.5 * v * v) * 0.3989422804014327
    return v * half, slope


def lane_of(rows):
    return lax.broadcasted_iota(jnp.int32, (rows, LANES), 1)


def unpack_head(tiles, e):
    tile = tiles[:, (e // 2) * LANES : (e // 2 + 1) * LANES]
    return tile if e % 2 == 0 else pltpu.roll(tile, HEAD, 1)


def pack_pair(low, high):
    return jnp.where(lane_of(low.shape[0]) < HEAD, low, pltpu.roll(high, HEAD, 1))


def vmem():
    return pl.BlockSpec(memory_space=pltpu.VMEM)


def smem():
    return pl.BlockSpec(memory_space=pltpu.SMEM)


def call(kernel, outs, args, scratch=(), flops=0, scalars=0, room=16, far=()):
    args = [pltpu.with_memory_space_constraint(a, pltpu.HBM) if i in far else a for i, a in enumerate(args)]
    nbytes = sum(a.size * a.dtype.itemsize for a in args)
    nbytes += sum(o.size * o.dtype.itemsize for o in outs)
    return pl.pallas_call(
        kernel,
        out_shape=outs,
        in_specs=[
            smem() if i < scalars else pl.BlockSpec(memory_space=pltpu.HBM) if i in far else vmem()
            for i in range(len(args))
        ],
        out_specs=[vmem()] * len(outs),
        scratch_shapes=list(scratch),
        compiler_params=pltpu.CompilerParams(vmem_limit_bytes=room << 20),
        cost_estimate=pl.CostEstimate(flops=flops, bytes_accessed=nbytes, transcendentals=0),
    )(*args)


def prep_kernel(sref, w, biases, w_own, bias_own, tiles, lines, sems):
    width = w.shape[0]
    per = width // HEAD
    spots = [per * (e % 3) + OWN * sref[0] + e // 3 for e in range(3 * OWN)]
    copies = [pltpu.make_async_copy(biases, lines, sems.at[3 * OWN])]
    for e, u in enumerate(spots):
        tile = w.at[:, pl.ds(pl.multiple_of((u >> 1) * LANES, LANES), LANES)]
        copies.append(pltpu.make_async_copy(tile, tiles.at[e], sems.at[e]))
    for copy in copies:
        copy.start()
    copies[0].wait()
    line = lax.broadcasted_iota(jnp.int32, (1, LANES), 1)
    for t in range((3 * OWN + 1) // 2):
        out, bias = jnp.zeros((width, LANES), F32), jnp.zeros((1, LANES), F32)
        for dest in range(2):
            e = 2 * t + dest
            if e == 3 * OWN:
                continue
            copies[1 + e].wait()
            u, j = spots[e], e % 3
            side = (lane_of(width) >= HEAD) == (dest == 1)
            moved = jnp.broadcast_to((u & 1) != dest, (1, LANES))
            tile = tiles[e].astype(F32)
            tile = jnp.where(moved, pltpu.roll(tile, HEAD, 1), tile)
            out = jnp.where(side, tile, out)
            if j != 1:
                v = OWN * sref[0] + e // 3
                tile = lines[j // 2 : j // 2 + 1, pl.ds(pl.multiple_of((v >> 1) * LANES, LANES), LANES)]
                tile = jnp.broadcast_to(tile, (8, LANES))
                away = jnp.broadcast_to((v & 1) != dest, (8, LANES))
                tile = jnp.where(away, pltpu.roll(tile, HEAD, 1), tile)[:1]
                bias = jnp.where((line >= HEAD) == (dest == 1), tile, bias)
        w_own[:, t * LANES : (t + 1) * LANES] = out.astype(BF16)
        bias_own[:, t * LANES : (t + 1) * LANES] = bias


def small_kernel(specials_in, segments_in, order_in, cots_in, small, head, specials, segments, order, cots, wide, sems):
    pairs = ((specials_in, specials), (segments_in, segments), (order_in, order), (cots_in, cots))
    copies = [pltpu.make_async_copy(src, dst, sems.at[i]) for i, (src, dst) in enumerate(pairs)]
    for copy in copies:
        copy.start()
    extra, width = specials.shape
    count = segments.shape[1]
    wide[...] = jnp.zeros_like(wide)
    wide[extra : extra + 1, :] = jnp.full((1, width), -1.0, F32)
    for copy in copies:
        copy.wait()
    wide[:extra, :] = specials[...].astype(F32)
    wide[16 : 16 + extra, :] = cots[...].astype(F32)
    wide[extra : extra + 1, :count] = segments[...].astype(F32)
    wide[extra : extra + 1, count : count + extra] = (order[...] >> 1).astype(F32)
    small[...] = wide[...].astype(BF16)
    head[...] = wide[:16, :].astype(BF16)


def tokens_of(patches, small):
    parts = [patches[...].astype(F32), small[:16, :].astype(F32)]
    return jnp.concatenate(parts + [jnp.zeros((PAD - 16, patches.shape[1]), F32)], axis=0)


def cots_of(patches, small):
    parts = [patches[...].astype(F32), small[16:, :].astype(F32)]
    return jnp.concatenate(parts + [jnp.zeros((PAD - 16, patches.shape[1]), F32)], axis=0)


def images_of(small, rows):
    size = -(-rows // LANES) * LANES
    line = small[:16, :size].astype(F32)[SPECIAL : SPECIAL + 1]
    return jnp.broadcast_to(line, (LANES, size)).T[:rows]


def project(patches, small, gain, shift, w, bias, at, qa, ka, va, normed):
    tok = tokens_of(patches, small)
    rows = tok.shape[0]
    lane = lane_of(rows)
    hat, _ = normalize(tok)
    nrm = (hat * gain[0:1, :] + shift[0:1, :]).astype(BF16)
    normed[at, :] = nrm
    qkv = dot(nrm, w[...]) + bias[...]
    image = images_of(small, rows)
    hot = jnp.where((lane >= HEAD) & (image == (lane - HEAD).astype(F32)), 1.0, 0.0)
    far = jnp.where((lane >= HEAD) & (lane < HEAD + 8) & (hot == 0.0), FAR, 0.0)
    one = jnp.where(lane == HEAD, 1.0, 0.0)
    for h in range(OWN):
        q = unpack_head(qkv, 3 * h) * HEAD**-0.5
        qa[h, at, :] = jnp.where(lane < HEAD, q, hot).astype(BF16)
        ka[h, at, :] = jnp.where(lane < HEAD, unpack_head(qkv, 3 * h + 1), far).astype(BF16)
        va[h, at, :] = jnp.where(lane < HEAD, unpack_head(qkv, 3 * h + 2), one).astype(BF16)
    return tok, image


def project_kernel(flags, p0, s0, p1, s1, gain, shift, w, bias, qa, ka, va, normed, toks, keeps):
    rows = normed.shape[0] // 2
    lane = lane_of(rows)
    for i, (p, small) in enumerate(((p0, s0), (p1, s1))):
        at = pl.ds(i * rows, rows)
        tok, image = project(p, small, gain, shift, w, bias, at, qa, ka, va, normed)
        toks[at, :] = tok.astype(BF16)
        keep = jnp.zeros((rows, LANES), F32)
        half = flags.shape[1] // 2
        for j in range(half):
            first = flags[0, j].astype(F32) / 0.75
            second = flags[0, half + j].astype(F32) / 0.75
            keep = jnp.where(image == float(j), jnp.where(lane == 0, first, second), keep)
        keeps[at, :] = keep


def attend_block(h, at, keys, values, queries, oacc):
    sc = dot_t(queries[h, at, :], keys[h])
    top = jnp.max(sc, axis=-1, keepdims=True)
    e = jnp.exp(sc - top).astype(BF16)
    o = dot(e, values[h])
    tot = o[:, HEAD : HEAD + 1]
    mark = jnp.where(lane_of(o.shape[0]) == HEAD + 1, top + jnp.log(tot), o * (1.0 / tot))
    return mark


def project_one_kernel(p, small, gain, shift, w, bias, qa, ka, va, normed):
    project(p, small, gain, shift, w, bias, pl.ds(0, normed.shape[0]), qa, ka, va, normed)


def attend_first_kernel(
    q0, k0, v0, n0, q2, k2, v2, n2, p3, s3, gain, shift, w, bias, qa, ka, va, send, oacc, normed
):
    half = n0.shape[0]
    rows = half // 2
    for at, qs, ks, vs, ns in ((pl.ds(0, half), q0, k0, v0, n0), (pl.ds(half, rows), q2, k2, v2, n2)):
        for h in range(OWN):
            qa[h, at, :] = qs[h]
            ka[h, at, :] = ks[h]
            va[h, at, :] = vs[h]
        normed[at, :] = ns[...]
    project(p3, s3, gain, shift, w, bias, pl.ds(half + rows, rows), qa, ka, va, normed)

    def block(i, carry):
        h, b = i // 2, i % 2
        at = pl.ds(pl.multiple_of(half + b * rows, 16), rows)
        oacc[h, pl.ds(pl.multiple_of(b * rows, 16), rows), :] = attend_block(h, at, ka, va, qa, oacc)
        return carry

    lax.fori_loop(0, 2 * OWN, block, 0, unroll=3)
    gather_heads(oacc, send)


def gather_heads(oacc, out):
    out[:, :LANES] = pack_pair(oacc[0], oacc[1]).astype(BF16)
    out[:, LANES:] = oacc[2, :, :HEAD].astype(BF16)


def attend_second_kernel(
    sref, qa, ka, va, other, w_fc1, w_fc2, keep, lse, w1, w2, w3, w4, oacc, sems
):
    s = sref[0]
    copies = fetch(s ^ 2, w_fc1, w_fc2, w1, w2, sems.at[0]) + fetch(s, w_fc1, w_fc2, w3, w4, sems.at[1])
    half = oacc.shape[1]
    rows = half // 2

    def block(i, carry):
        h, b = i // 2, i % 2
        at = pl.ds(pl.multiple_of(b * rows, 16), rows)
        oacc[h, at, :] = attend_block(h, at, ka, va, qa, oacc)
        return carry

    lax.fori_loop(0, 2 * OWN, block, 0, unroll=3)
    gather_heads(oacc, keep)
    step = 2 * half // 3
    for h in range(OWN):
        parts = [
            oacc[h, :step, :],
            jnp.concatenate([oacc[h, step:, :], other[h, : step - (half - step), :]], axis=0),
            other[h, half - step :, :],
        ]
        for b in range(3):
            lse[h, b] = jnp.broadcast_to(parts[b].T[HEAD + 1 : HEAD + 2], (8, step))
    for copy in copies:
        copy.wait()


def middle_kernel(
    sref, a0, a1, a2, a3, toks, keeps, cp0, cp1, c0, c1, w_out, bias, gain, shift,
    middle, normed2, gb2,
):
    s = sref[0]
    chip, width = toks.shape
    rows = chip // 2
    cols = a0.shape[1]
    acc = jnp.zeros((chip, width), F32) + bias[2:3, :]
    for j, a in ((0, a0), (2, a2)):
        w = w_out[pl.ds(pl.multiple_of((s ^ j) * cols, HEAD), cols), :]
        acc = acc + dot(a[...], w)
    for j, a in ((1, a1), (3, a3)):
        w = w_out[pl.ds(pl.multiple_of((s ^ j) * cols, HEAD), cols), :]
        part = dot(a[...], w)
        acc = acc + jnp.concatenate([part[rows:], part[:rows]], axis=0)
    mid = toks[...].astype(F32) + keeps[:, 0:1] * acc
    middle[...] = mid
    hat, _ = normalize(mid)
    normed2[...] = (hat * gain[1:2, :] + shift[1:2, :]).astype(BF16)
    gout = jnp.concatenate([cots_of(cp0, c0), cots_of(cp1, c1)], axis=0)
    gb2[...] = (keeps[:, 1:2] * gout).astype(BF16)


def fetch(block, w_fc1, w_fc2, w1, w2, sems):
    size = w1.shape[1]
    at = pl.ds(pl.multiple_of(block * size, LANES), size)
    copies = [
        pltpu.make_async_copy(w_fc1.at[:, at], w1, sems.at[0]),
        pltpu.make_async_copy(w_fc2.at[at, :], w2, sems.at[1]),
    ]
    for copy in copies:
        copy.start()
    return copies


def feed_kernel(last, fast, sref, bref, normed2, gb2, fc1, bias, fc2, *refs):
    if last:
        b2_in, gn_in, y_in, g2, zb_send, zb_keep, y_send, g1_keep, gb, b2_keep, b2_send, gn_keep, gn_send, wide, wide2 = refs
    else:
        g2a, g2m, zb_send, zb_keep, y_first, y_second, g1_keep, gb, b2, gn, wide, wide2 = refs
    tokens = normed2.shape[0]
    half = tokens // 2
    block = sref[0] if last else sref[0] ^ 2
    pre = dot(normed2[...], fc1[...]) + bias[:, pl.ds(pl.multiple_of(block * fc1.shape[1], LANES), fc1.shape[1])]
    gact = dot_t(gb2[...], fc2[...])
    act, slope = gelu_pair(pre)
    act = act.astype(BF16)
    gh = (gact * slope).astype(BF16)
    grad1 = dot_lt(normed2[...], gh)
    if not fast:
        rows = grad1.shape[0] // 2
        (y_send if last else y_first)[...] = grad1[:rows].astype(BF16)
        g1_keep[...] = grad1[rows:].astype(BF16)
    else:
        x, c = sref[0] >> 1, sref[0] & 1
        y, z1, z2 = bref[0] & 1, (bref[0] >> 1) & 1, bref[0] >> 2
        wide[...] = grad1
        n, rows = g1_keep.shape[:2]
        for m in range(2 * n):
            near = [(m >> k) & 1 for k in (4, 3, 2, 1, 0)]
            yy, zz1, xx, zz2, cc = [own if r else 1 - own for own, r in zip((y, z1, x, z2, c), near)]
            base = rows * (16 * xx + 8 * cc + 4 * zz2 + 2 * zz1 + yy)
            piece = wide[pl.ds(pl.multiple_of(base, 8), rows), :].astype(BF16)
            if m >= n:
                g1_keep[m - n] = piece
            elif last:
                y_send[n // 4 + m] = piece
            elif m < 3 * n // 4:
                y_first[m] = piece
            else:
                y_second[m - 3 * n // 4] = piece
        if last:
            for m in range(n // 4):
                y_send[m] = y_in[m]
    gb[...] = jnp.sum(gh.astype(F32), axis=0, keepdims=True)
    partn = dot_t(gh, fc1[...])
    part2 = dot(act, fc2[...])
    if last:
        partn = partn + gn_in[...]
        part2 = part2 + b2_in[...]
        b2_keep[...] = part2[:half]
        b2_send[...] = part2[half:].astype(BF16)
        gn_keep[...] = partn
        gn_send[:half] = partn[half:].astype(BF16)
        gn_send[half:] = partn[:half].astype(BF16)
    else:
        b2[...] = part2
        gn[...] = partn
    grad2 = dot_lt(act, gb2[...])
    if not fast:
        rows = zb_send.shape[0]
        if last:
            g2[...] = grad2[: 2 * rows].astype(BF16)
        else:
            g2a[...] = grad2[:rows].astype(BF16)
            g2m[...] = grad2[rows : 2 * rows].astype(BF16)
        zb_send[...] = grad2[2 * rows : 3 * rows].astype(BF16)
        zb_keep[...] = grad2[3 * rows :].astype(BF16)
    else:
        deep = grad2.shape[0] // 8
        half = deep // 2
        for m in range(8):
            if last:
                g2[m] = grad2[m * deep : m * deep + half].astype(BF16)
            else:
                mid = m * deep + half // 2
                g2a[m] = grad2[m * deep : mid].astype(BF16)
                g2m[m] = grad2[mid : mid + half // 2].astype(BF16)
            wide2[pl.ds(m * half, half), :] = grad2[m * deep + half : (m + 1) * deep]
        for m in range(8):
            near = [(m >> k) & 1 for k in (2, 1, 0)]
            zz1, zz2, yy = [own if r else 1 - own for own, r in zip((z1, z2, y), near)]
            base = half * (4 * zz2 + 2 * zz1 + yy)
            piece = wide2[pl.ds(pl.multiple_of(base, 8), half), :].astype(BF16)
            (zb_keep if m >= 4 else zb_send)[m % 4] = piece


def split_rows(value, wide, bit, send, keep):
    if len(send.shape) == 2:
        rows = value.shape[0] // 2
        send[...] = value[:rows].astype(BF16)
        keep[...] = value[rows:].astype(BF16)
        return
    wide[...] = value
    rows = send.shape[1]
    for m in range(send.shape[0]):
        base = 2 * m * rows
        send[m] = wide[pl.ds(pl.multiple_of(base + (1 - bit) * rows, 8), rows), :].astype(BF16)
        keep[m] = wide[pl.ds(pl.multiple_of(base + bit * rows, 8), rows), :].astype(BF16)


def feed(last, fast, per, sidx, bidx, normed2, gb2, fc1, bias, fc2, prev=()):
    tokens, width = normed2.shape
    hidden = fc1.shape[1]
    pairs = width // (2 * per)
    deep = hidden // 8
    if fast:
        outs = [SDS((8, deep // 2, width), BF16)] if last else [SDS((8, deep // 4, width), BF16)] * 2
        outs += [SDS((4, deep // 2, width), BF16)] * 2
    else:
        outs = [SDS((hidden // 2, width), BF16)] if last else [SDS((hidden // 4, width), BF16)] * 2
        outs += [SDS((hidden // 4, width), BF16)] * 2
    if last:
        send = [SDS((5 * pairs // 4, per, hidden), BF16)]
    else:
        send = [SDS((n, per, hidden), BF16) for n in (3 * pairs // 4, pairs // 4)]
    keep = SDS((pairs, per, hidden), BF16)
    if not fast:
        keep = SDS((width // 2, hidden), BF16)
        send = [keep] if last else [keep, SDS((8, LANES), BF16)]
    outs += send + [keep, SDS((1, hidden), F32)]
    if last:
        outs += [SDS((tokens // 2, width), F32), SDS((tokens // 2, width), BF16)]
        outs += [SDS((tokens, width), F32), SDS((tokens, width), BF16)]
    else:
        outs += [SDS((tokens, width), F32)] * 2
    return call(
        functools.partial(feed_kernel, last, fast),
        outs,
        (sidx, bidx, normed2, gb2, fc1, bias, fc2) + tuple(prev),
        [pltpu.VMEM((width, hidden), F32), pltpu.VMEM((hidden // 2, width), F32)],
        flops=12 * tokens * width * hidden,
        scalars=2,
    )


def by_batch_bit(arr, per):
    arr = arr.reshape(-1, 2, per, arr.shape[-1])
    own = lax.axis_index("batch") & 1
    return [pick(arr, 1 - own, 1), pick(arr, own, 1)]


def middle_back_kernel(
    sref, gn_keep, gn_got, middle, keeps, cp0, cp1, c0, c1, w_out, gain, gb2, gmid_own, gbr_out, gatt_send, sums
):
    s = sref[0]
    rows, width = gmid_own.shape
    cols = gatt_send.shape[1]
    hat, scale = normalize(middle[...])
    g = gn_keep[...] + gn_got[...].astype(F32)
    gout = jnp.concatenate([cots_of(cp0, c0), cots_of(cp1, c1)], axis=0)
    gmid = gout + normalize_back(g * gain[1:2, :], hat, scale)
    gbr = (keeps[:, 0:1] * gmid).astype(BF16)
    gbr_out[...] = gbr
    w_oth = w_out[pl.ds(pl.multiple_of((s ^ 2) * cols, HEAD), cols), :]
    gatt_send[...] = dot_t(gbr, w_oth).astype(BF16)
    gmid_own[...] = gmid[:rows]
    own = slice(0, rows)
    lines = [
        jnp.sum(g[own] * hat[own], axis=0, keepdims=True),
        jnp.sum(g[own], axis=0, keepdims=True),
        jnp.sum(gb2[own, :].astype(F32), axis=0, keepdims=True),
        jnp.sum(gbr[own].astype(F32), axis=0, keepdims=True),
        jnp.zeros((4, width), F32),
    ]
    sums[...] = jnp.concatenate(lines, axis=0)


def branch_back_kernel(
    per, sref, bref, gbr, w_out, a0, a2, middle, keeps, b2_keep, b2_got, bias, gain1, shift1, sums, fb_own, fb_oth,
    gatt, go_send, go_keep, early, opat, ospe, fcol, wide,
):
    s = sref[0]
    cols = a0.shape[1]
    rows, width = b2_keep.shape
    w_own = w_out[pl.ds(pl.multiple_of(s * cols, HEAD), cols), :]
    gatt[...] = dot_t(gbr[...], w_own).astype(BF16)
    for j, a in enumerate((a0, a2)):
        split_rows(dot_lt(a[...], gbr[...]), wide, bref[0] & 1, go_send.at[j], go_keep.at[j])
    res = middle[:rows, :] + keeps[:rows, 1:2] * (b2_keep[...] + b2_got[...].astype(F32) + bias[3:4, :])
    res = res.astype(BF16)
    opat[...] = res[: opat.shape[0]]
    ospe[...] = res[opat.shape[0] : opat.shape[0] + ospe.shape[0]]
    blank = functools.partial(jnp.zeros, dtype=F32)
    lines = [gain1[0:1, :], shift1[0:1, :], blank((HEAD + 2, width)), sums[:4, :], blank((LANES - HEAD - 8, width))]
    early[...] = jnp.concatenate(lines, axis=0).T
    lane = lane_of(cols)
    for j, ref in ((0, fb_own), (2, fb_oth)):
        fcol[...] = jnp.broadcast_to(ref[...], (LANES, ref.shape[1])).T
        at = pl.ds(pl.multiple_of((s ^ j) * cols, HEAD), cols)
        val = early[at, :]
        for k in range(4):
            lines = [fcol[(4 * b + k) * per : (4 * b + k + 1) * per, :] for b in range(cols // per)]
            val = jnp.where(lane == HEAD + 8 + k, jnp.concatenate(lines, axis=0), val)
        early[at, :] = val


def attend_back_kernel(first, heads, unroll, qa, ka, va, lse, ga, gx, out, sums, goa, dq, dk, dv):
    whole = qa.shape[1]
    half = ga.shape[0]
    lane = lane_of(half)
    for i in range(heads):
        h = first + i
        for ref, start in ((ga, 0), (gx, half)):
            if h < 2:
                t = ref[:, :LANES].astype(F32)
                t = jnp.where(lane < HEAD, t if h == 0 else pltpu.roll(t, HEAD, 1), 0.0)
            else:
                t = ref[:, LANES:].astype(F32)
                t = jnp.concatenate([t, jnp.zeros_like(t)], axis=1)
            goa[i, pl.ds(start, half), :] = t.astype(BF16)
    step = whole // 3

    def block(n, carry):
        i, b = n // 3, n % 3
        h = first + i
        at = pl.ds(pl.multiple_of(b * step, step), step)
        q, go = qa[h, at, :], goa[i, at, :]
        prob = jnp.exp(dot_t(ka[h], q) - lse[h, b][0:1, :])
        gp = dot_t(va[h], go)
        inner = jnp.sum(gp * prob, axis=0, keepdims=True)
        gs = (prob * (gp - inner)).astype(BF16)
        pv = dot(prob.astype(BF16), go)
        pk = dot(gs, q)
        dq[i, at, :] = dot_lt(gs, ka[h])

        dv[i] = jnp.where(b == 0, pv, dv[i] + pv)
        dk[i] = jnp.where(b == 0, pk, dk[i] + pk)
        return carry

    lax.fori_loop(0, 3 * heads, block, 0, unroll=unroll)
    for i in range(heads):
        out[i, :, :LANES] = pack_pair(dq[i] * HEAD**-0.5, dk[i]).astype(BF16)
        out[i, :, LANES:] = dv[i, :, :HEAD].astype(BF16)
        sums[i] = jnp.sum(out[i].astype(F32), axis=0, keepdims=True)


def attend_back(first, heads, qa, ka, va, lse, ga, gx):
    whole = qa.shape[1]
    return call(
        functools.partial(attend_back_kernel, first, heads),
        [SDS((heads, whole, 3 * HEAD), BF16), SDS((heads, 1, 3 * HEAD), F32)],
        (qa, ka, va, lse, ga, gx),
        [pltpu.VMEM((heads, whole, LANES), BF16)] + [pltpu.VMEM((heads, whole, LANES), F32)] * 3,
        flops=10 * heads * whole * whole * LANES,
    )


def norm1_kernel(g01, g2, w, keep, send):
    rows = keep.shape[0] // 2
    cols = g2.shape[2]
    for i in range(4):
        at = pl.ds(i * rows, rows)
        part = dot_t(g01[0, at, :], w[:, :cols])
        part = part + dot_t(g01[1, at, :], w[:, cols : 2 * cols])
        part = part + dot_t(g2[0, at, :], w[:, 2 * cols : 3 * cols])
        to = pl.ds((i // 2) * rows, rows)
        if i % 2 == 0:
            keep[to, :] = part
        else:
            send[to, :] = part.astype(BF16)


def qkv_grad(sref, normed, grads, sums, w, first, tile, bound):
    width, cols = w.shape[0], grads[0].shape[1]
    g = jnp.concatenate([dot_lt(normed[...], v) for v in grads], axis=1)
    w32 = w[:, first * cols : (first + len(grads)) * cols].astype(F32)
    rows = jnp.concatenate(sums, axis=1)
    both = jnp.sum(g * w32, axis=-1, keepdims=True)
    gshift = jnp.sum(w32 * rows, axis=-1, keepdims=True)
    lane = lane_of(width)
    old = bound[...]
    tile[...] = jnp.where(lane == HEAD, old + both, jnp.where(lane == HEAD + 1, old + gshift, old))
    ones = jnp.ones((grads[0].shape[0], LANES), BF16)
    at = pl.multiple_of(sref[0] * cols, HEAD)
    lanes = lane_of(HEAD)
    for i, v in enumerate(grads):
        col = dot_lt(v, ones)
        here = pl.ds(at + (first + i) * HEAD, HEAD)
        row = tile[here, :]
        row = jnp.where(lanes == HEAD + 2, col[:HEAD], row)
        tile[here, :] = jnp.where(lanes == HEAD + 3, col[2 * HEAD :], row)
    return g


def heads_kernel(
    fast, sref, bref, qa, ka, va, lse, ga, gx, normed, w, early, g01, send, keep, tile,
    s01, goa, dq, dk, dv, wide,
):
    attend_back_kernel(0, 2, 2, qa, ka, va, lse, ga, gx, g01, s01, goa, dq, dk, dv)
    g = qkv_grad(sref, normed, (g01[0], g01[1]), (s01[0], s01[1]), w, 0, tile, early)
    if not fast:
        rows = g.shape[0] // 2
        send[...] = g[:rows].astype(BF16)
        keep[...] = g[rows:].astype(BF16)
        return
    wide[...] = g
    y, z1, z2 = bref[0] & 1, (bref[0] >> 1) & 1, bref[0] >> 2
    per, cols = send.shape[1], g.shape[1]
    for m in range(8):
        zz1 = z1 if m & 4 else 1 - z1
        zz2 = z2 if m & 2 else 1 - z2
        for j in range(2):
            base = per * ((2 * (m & 1) + j) * 8 + 4 * zz2 + 2 * zz1)
            to = slice(j * cols, (j + 1) * cols)
            send[m, :, to] = wide[pl.ds(pl.multiple_of(base + (1 - y) * per, 8), per), :].astype(BF16)
            keep[m, :, to] = wide[pl.ds(pl.multiple_of(base + y * per, 8), per), :].astype(BF16)


def tail_kernel(
    sref, bref, qa, ka, va, lse, ga, gx, normed, g01, w, early, gn_keep, gn_send, send, keep,
    g2, s2, goa, dq, dk, dv, tile, wide,
):
    attend_back_kernel(2, 1, 1, qa, ka, va, lse, ga, gx, g2, s2, goa, dq, dk, dv)
    norm1_kernel(g01, g2, w, gn_keep, gn_send)
    g = qkv_grad(sref, normed, (g2[0],), (s2[0],), w, 2, tile, early)
    width = g.shape[0]
    lane = lane_of(width)
    val = tile[...]
    gshift = val[:, HEAD + 1 : HEAD + 2]
    ggain = (val[:, HEAD : HEAD + 1] - val[:, 1:2] * gshift) / val[:, 0:1]
    val = jnp.where(lane == HEAD, ggain, val)
    last = jnp.concatenate([g[:, LANES:], jnp.zeros((width, LANES - HEAD), F32)], axis=1)
    out = jnp.concatenate([g[:, :LANES], jnp.where(lane < HEAD, last, val)], axis=1)
    split_rows(out, wide, bref[0] & 1, send, keep)


def wide_sum(*parts):
    return sum(p.astype(F32) for p in parts[1:]) + parts[0].astype(F32)


def stage0_kernel(own_keep, own_got, oth_keep, oth_got, msg, part):
    for i in range(2):
        msg[i] = wide_sum(own_keep[i], own_got[i]).astype(BF16)
        msg[2 + i] = wide_sum(oth_keep[i], oth_got[i]).astype(BF16)
        part[i] = wide_sum(own_keep[2 + i], own_got[2 + i])
        part[2 + i] = wide_sum(oth_keep[2 + i], oth_got[2 + i])


def stage1_kernel(
    bref, keep_own, keep_oth, y1, y2, fc2, g2a, g2m, out, y3, part_0, got_0, q_send,
    msg_z, msg_y, msg_x, part_f, part_a, part_o, part_p,
):
    y, z1, z2 = bref[0] & 1, (bref[0] >> 1) & 1, bref[0] >> 2
    n = keep_own.shape[0] // 2
    for i in range(n):
        more = n // 2
        msg_z[i] = wide_sum(keep_own[i], y2[more + i]).astype(BF16)
        msg_z[n + i] = wide_sum(keep_oth[i], y1[i]).astype(BF16)
        part_f[i] = wide_sum(keep_own[n + i], y2[more + n + i])
        part_f[n + i] = wide_sum(keep_oth[n + i], y1[n + i] if i < more else y2[i - more])
        msg_y[8 + i] = q_send[i]
    rows = g2a.shape[1]
    for i in range(4):
        zz1 = z1 if i >> 1 else 1 - z1
        zz2 = z2 if i & 1 else 1 - z2
        m = 2 * zz2 + zz1
        msg_x[i] = wide_sum(out[1, m], y3[1, m]).astype(BF16)
        part_o[i] = wide_sum(out[0, m], y3[0, m])
        for k, got in enumerate((g2a, g2m)):
            at = slice(k * rows, (k + 1) * rows)
            b = 2 * m + 1 - y
            msg_y[2 * i + k] = wide_sum(fc2[b, at], got[b]).astype(BF16)
            b = 2 * m + y
            part_a[2 * i + k] = wide_sum(fc2[b, at], got[b])
    for i in range(2):
        for k in range(2):
            at = slice(k * rows, (k + 1) * rows)
            msg_x[4 + 2 * i + k] = wide_sum(part_0[2 + i, at], got_0[2 + i, at]).astype(BF16)
            part_p[2 * i + k] = wide_sum(part_0[i, at], got_0[i, at])


def stage2_kernel(
    part_f, got_z, part_a, got_y, part_o, got_x, part_p, q_keep, q2_send, msg_x, msg_z, msg_y, part_g, part_c, part_q
):
    n, _, cols = q2_send.shape
    for i in range(n):
        msg_y[i] = q2_send[i]
    for half in range(2):
        for i in range(4):
            k = 8 * half + i
            msg_x[4 * half + i] = wide_sum(part_f[k], got_z[k]).astype(BF16)
            part_g[4 * half + i] = wide_sum(part_f[k + 4], got_z[k + 4])
    for i in range(4):
        msg_z[i] = wide_sum(part_a[i], got_y[i]).astype(BF16)
        part_c[i] = wide_sum(part_a[4 + i], got_y[4 + i])
        msg_z[6 + i] = wide_sum(q_keep[i], got_y[8 + i]).astype(BF16)
        part_c[6 + i] = wide_sum(q_keep[4 + i], got_y[12 + i])
    for i in range(2):
        msg_z[4 + i] = wide_sum(part_o[i], got_x[i]).astype(BF16)
        part_c[4 + i] = wide_sum(part_o[2 + i], got_x[2 + i])
        rest = wide_sum(part_p[i], got_x[4 + i]).astype(BF16)
        for k in range(3):
            msg_y[n + 3 * i + k] = rest[:, k * cols : (k + 1) * cols]
        part_q[i] = wide_sum(part_p[2 + i], got_x[6 + i])


def stage3_kernel(bref, part_g, got_x, part_c, got_z, q_keep, got_y, msg, kept, z1, z2, z3, q_kept):
    for half in range(2):
        for i in range(2):
            k, other = 4 * half + i, 4 * (1 - half) + i
            msg[2 * half + i] = wide_sum(part_g[k], got_x[other]).astype(BF16)
            kept[2 * half + i] = wide_sum(part_g[k + 2], got_x[other + 2])
    for to, a, b in ((4, 0, 2), (5, 1, 3), (6, 4, 5), (7, 6, 8), (8, 7, 9)):
        msg[to] = wide_sum(part_c[a], got_z[a]).astype(BF16)
        kept[to] = wide_sum(part_c[b], got_z[b])
    q = bref[0] >> 1
    for r in range(4):
        for k, ref in enumerate((q_kept, z1, z2, z3)):
            m = r * 4 + (q ^ k)
            ref[r] = wide_sum(q_keep[m], got_y[m]).astype(ref.dtype)


def shift_kernel(keep, got, send):
    rows = send.shape[0]
    send[...] = wide_sum(keep[rows:, :], got[rows:, :]).astype(BF16)


def sums_kernel(kept, got, part_q, got_q, swap_send, swap_keep, fc2, out):
    per = out.shape[0]
    for half in range(2):
        at = pl.ds(half * per, per)
        swap_send[at, :] = wide_sum(kept[2 * half], got[2 * half]).astype(BF16)
        swap_keep[at, :] = wide_sum(kept[2 * half + 1], got[2 * half + 1])
        fc2[at, :] = wide_sum(kept[4 + half], got[4 + half])
        cols = got_q.shape[2]
        for k in range(3):
            at3 = slice(k * cols, (k + 1) * cols)
            fc2[pl.ds((2 + half) * per, per), at3] = wide_sum(part_q[half, :, at3], got_q[16 + 3 * half + k])
    out[...] = wide_sum(kept[6], got[6])


def owner_kernel(sref, most, got, kept, z1, z2, z3, s1, s2, s3, own, every):
    s = sref[0]
    cols = most.shape[2] // 2
    for m in range(4):
        at = slice((m % 2) * cols, (m % 2 + 1) * cols)
        every[m, :, :cols] = wide_sum(most[7 + m // 2, :, at], got[7 + m // 2, :, at])
        every[m, :, cols:] = wide_sum(kept[m], z1[m], z2[m], z3[m])
    for k, ref in enumerate((own, s1, s2, s3)):
        ref[...] = every[s ^ k].astype(ref.dtype)


def final_kernel(k0, c0, x0, p0, s0, gmid, gain, gpat, gspe):
    rows, width = x0.shape
    count = gpat.shape[0]
    hat, scale = normalize(tokens_of(p0, s0))
    g = wide_sum(k0[:rows], c0[:rows], x0[...])
    res = gmid[...] + normalize_back(g * gain[0:1, :], hat, scale)
    gpat[...] = res[:count]
    gspe[...] = res[count : count + gspe.shape[0]]


def collect_kernel(
    sref, own, g1, g2, g3, swap_keep, swap_got, out, gains, shifts, biases, fc1_bias, fc1, every
):
    s = sref[0]
    per, hidden = swap_keep.shape[0] // 2, swap_keep.shape[1]
    for j, value in ((0, swap_keep[:per]), (2, swap_keep[per:]), (1, swap_got[:per]), (3, swap_got[per:])):
        fc1[:, pl.ds(pl.multiple_of((s ^ j) * hidden, LANES), hidden)] = value.astype(F32)
    for k, ref in enumerate((own, g1, g2, g3)):
        every[k] = ref[...].astype(F32)
    pieces = [every[s ^ a] for a in range(4)]

    def part(u):
        j, a, h = u // 12, (u // 3) % 4, u % 3
        e = 3 * h + j
        return pieces[a][:, (e // 2) * LANES : (e // 2 + 1) * LANES], e % 2

    lane = lane_of(out.shape[0])
    for t in range(out.shape[1] // LANES):
        (low, lo), (high, hi) = part(2 * t), part(2 * t + 1)
        low = pltpu.roll(low, HEAD, 1) if lo else low
        high = high if hi else pltpu.roll(high, HEAD, 1)
        out[:, t * LANES : (t + 1) * LANES] = jnp.where(lane < HEAD, low, high)
    tail = 4 * LANES
    vec = wide_sum(*[every[k, :, tail:] for k in range(4)])
    vec = jnp.concatenate([vec, jnp.zeros((LANES - per, LANES), F32)], axis=0).T
    for ref, lines in ((gains, (0, 4)), (shifts, (1, 5)), (biases, (2, 3, 7, 6))):
        for i, k in enumerate(lines):
            ref[i : i + 1, :] = vec[HEAD + k : HEAD + k + 1, :per]
    flat = jnp.zeros((8, LANES), F32)
    for k in range(4):
        line = jnp.broadcast_to(vec[HEAD + 8 + k : HEAD + 9 + k], (8, LANES))
        flat = flat + (pltpu.roll(line, k * per, 1) if k else line)
    fc1_bias[...] = flat[:1, : 4 * per]


def pick(arr, index, axis):
    return lax.dynamic_index_in_dim(arr, index, axis, keepdims=False)


def total(parts):
    out = parts[0].astype(F32)
    for part in parts[1:]:
        out = out + part.astype(F32)
    return out


def swap(kind, v, mask):
    return lax.ppermute(v, kind, [(i, i ^ mask) for i in range(lax.axis_size(kind))])


def swap_seq(v, mask):
    return swap("seq", v, mask)


def after(value, *first):
    return lax.optimization_barrier((value, first))[0]


def bits_of(kind):
    return lax.axis_size(kind).bit_length() - 1


def split_bits(arr, axis, count):
    shape = arr.shape
    return arr.reshape(shape[:axis] + (2,) * count + shape[axis + 1 :])


def to_send(parts, axis, bit, kind):
    own = (lax.axis_index(kind) >> bit) & 1
    send = total([pick(p, 1 - own, axis) for p in parts]).astype(BF16)
    return send, [pick(p, own, axis) for p in parts]


def send_four(parts, axis, low):
    own = (lax.axis_index("batch") >> low) & 3

    def quarter(p, k):
        return pick(pick(p, k >> 1, axis), k & 1, axis)

    sends = [total([quarter(p, own ^ k) for p in parts]).astype(BF16) for k in (1, 2, 3)]
    return sends, [quarter(p, own) for p in parts]


def swap_four(sends, low):
    return [swap("batch", v, k << low) for k, v in zip((1, 2, 3), sends)]


def sum_rest(parts, axis, low):
    top = bits_of("batch")
    while low < top:
        if low + 1 < top:
            sends, kept = send_four(parts, axis + top - low - 2, low)
            parts, low = kept + swap_four(sends, low), low + 2
        else:
            send, kept = to_send(parts, axis, low, "batch")
            parts, low = kept + [swap("batch", send, 1 << low)], low + 1
    return total(parts)


def body(
    patches,
    specials,
    segment_ids,
    special_order,
    keep_mask,
    norm_gains,
    norm_shifts,
    w_qkv,
    biases,
    w_out,
    w_fc1,
    fc1_bias,
    w_fc2,
    cot_patches,
    cot_specials,
):
    count, width = patches.shape[1:]
    extra = specials.shape[1]
    images = keep_mask.shape[1] // 2
    block = count + PAD
    chip = 2 * block
    whole = 4 * block
    cols = OWN * HEAD
    hidden = w_fc1.shape[1] // 4
    s = lax.axis_index("seq")
    sidx = s.astype(jnp.int32).reshape(1)
    bidx = lax.axis_index("batch").astype(jnp.int32).reshape(1)
    nb = lax.axis_size("batch")
    nbits = bits_of("batch")

    own_p, own_cot = patches[0], cot_patches[0]
    got_px = swap_seq(own_p, 2)
    got_pc = swap_seq(own_p, 1)
    small, small_head = call(
        small_kernel,
        [SDS((32, width), BF16), SDS((16, width), BF16)],
        (specials[0], segment_ids, special_order, cot_specials[0]),
        [pltpu.VMEM((extra, width), BF16), pltpu.VMEM((1, count), jnp.int32), pltpu.VMEM((1, extra), jnp.int32)]
        + [pltpu.VMEM((extra, width), BF16), pltpu.VMEM((32, width), F32), pltpu.SemaphoreType.DMA((4,))],
        far=(0, 1, 2, 3),
    )
    got_sx = swap_seq(small_head, 2)
    got_sc = swap_seq(small, 1)
    cot_c = swap_seq(own_cot, 1)
    fb = fc1_bias.reshape(1, -1)
    sidx, bidx, small = lax.optimization_barrier((sidx, bidx, small))
    w_own, bias_own = call(
        prep_kernel,
        [SDS((width, 5 * LANES), BF16), SDS((1, 5 * LANES), F32)],
        (sidx, w_qkv, biases),
        [pltpu.VMEM((3 * OWN, width, LANES), BF16), pltpu.VMEM(biases.shape, F32)]
        + [pltpu.SemaphoreType.DMA((3 * OWN + 1,))],
        scalars=1,
        far=(1, 2),
    )
    headed = SDS((OWN, chip, LANES), BF16)
    q0, k0, v0, n0, toks, keeps = call(
        project_kernel,
        [headed] * 3 + [SDS((chip, width), BF16), SDS((chip, width), BF16), SDS((chip, LANES), F32)],
        (keep_mask, own_p, small, got_pc, got_sc, norm_gains, norm_shifts, w_own, bias_own),
        flops=2 * chip * width * 3 * cols,
        scalars=1,
    )
    got_px, got_sx, n0 = lax.optimization_barrier((got_px, got_sx, n0))
    got_pd = swap_seq(got_px, 1)
    got_sd = swap_seq(got_sx, 1)

    headed = SDS((OWN, block, LANES), BF16)
    q2, k2, v2, n2 = call(
        project_one_kernel,
        [headed] * 3 + [SDS((block, width), BF16)],
        (got_px, got_sx, norm_gains, norm_shifts, w_own, bias_own),
        flops=2 * block * width * 3 * cols,
    )
    headed = SDS((OWN, whole, LANES), BF16)
    heads32 = SDS((OWN, chip, LANES), F32)
    qa, ka, va, att_send, other, normed = call(
        attend_first_kernel,
        [headed] * 3 + [SDS((chip, cols), BF16), heads32, SDS((whole, width), BF16)],
        (q0, k0, v0, n0, q2, k2, v2, n2, got_pd, got_sd, norm_gains, norm_shifts, w_own, bias_own),
        flops=2 * chip * width * 3 * cols + 2 * OWN * whole * whole * LANES,
    )
    a2 = swap_seq(att_send, 2)
    a0, lse, w1, w2, w3, w4 = call(
        attend_second_kernel,
        [SDS((chip, cols), BF16), SDS((OWN, 3, 8, whole // 3), F32)]
        + [SDS((width, hidden), BF16), SDS((hidden, width), BF16)] * 2,
        (sidx, qa, ka, va, other, w_fc1, w_fc2),
        [pltpu.VMEM((OWN, chip, LANES), F32), pltpu.SemaphoreType.DMA((2, 2))],
        flops=2 * OWN * whole * whole * LANES,
        scalars=1,
        far=(5, 6),
    )
    a1 = swap_seq(a0, 1)
    a3 = swap_seq(a2, 1)

    middle, normed2, gb2 = call(
        middle_kernel,
        [SDS((chip, width), F32), SDS((chip, width), BF16), SDS((chip, width), BF16)],
        (sidx, a0, a1, a2, a3, toks, keeps, own_cot, cot_c, small, got_sc, w_out, biases, norm_gains, norm_shifts),
        flops=2 * chip * width * width,
        scalars=1,
    )
    per = width // (4 * nb)
    fast = nb == 8
    fc2_a, fc2_m, zo_send, zo_keep, y1, y_rest, keep_oth, fb_oth, b2, gn = feed(
        False, fast, per, sidx, bidx, normed2, gb2, w1, fb, w2
    )
    got2a = swap_seq(fc2_a, 2)
    if not fast:
        y1, keep_oth = by_batch_bit(jnp.concatenate([y1, keep_oth], axis=0), per)
    got_y1 = swap("batch", y1, 1)
    got_zo = swap("batch", zo_send, 2) if fast else zo_send
    ahead = (got2a, got_y1, got_zo)
    fc2_keep, zn_send, zn_keep, y2, keep_own, fb_own, b2_keep, b2_send, gn_keep, gn_send = feed(
        True, fast, per, sidx, bidx, normed2, gb2, w3, fb, w4, (b2, gn, y_rest)
    )
    if not fast:
        y2, keep_own = by_batch_bit(jnp.concatenate([y2, keep_own], axis=0), per)
    gn_send, b2_send, zn_send, y2, (got2a, got_y1, got_zo) = lax.optimization_barrier(
        (gn_send, b2_send, zn_send, y2, ahead)
    )
    gn_got = swap_seq(gn_send, 1)
    b2_got = swap_seq(b2_send, 1)
    got_zn = swap("batch", zn_send, 2) if fast else zn_send
    got_y2 = swap("batch", y2, 1)

    gmid, gbr, gatt_send, line_sums = call(
        middle_back_kernel,
        [SDS((block, width), F32), SDS((chip, width), BF16), SDS((chip, cols), BF16), SDS((8, width), F32)],
        (sidx, gn_keep, gn_got, middle, keeps, own_cot, cot_c, small, got_sc, w_out, norm_gains, gb2),
        flops=2 * chip * width * cols,
        scalars=1,
    )
    gatt_x = swap_seq(gatt_send, 2)
    if fast:
        split = SDS((2, cols // (2 * per), per, width), BF16)
    else:
        split = SDS((2, cols // 2, width), BF16)
    gatt, go_send, go_keep, early, opat, ospe = call(
        functools.partial(branch_back_kernel, per),
        [SDS((chip, cols), BF16), split, split, SDS((width, LANES), F32)]
        + [SDS((count, width), BF16), SDS((extra, width), BF16)],
        (sidx, bidx, gbr, w_out, a0, a2, middle, keeps, b2_keep, b2_got, biases, norm_gains, norm_shifts)
        + (line_sums, fb_own, fb_oth),
        [pltpu.VMEM((hidden, LANES), F32), pltpu.VMEM((cols, width), F32)],
        flops=6 * chip * width * cols,
        scalars=2,
    )
    if not fast:
        halves = [by_batch_bit(jnp.concatenate([go_send[j], go_keep[j]], axis=0), per) for j in range(2)]
        go_send, go_keep = [jnp.stack([halves[j][k] for j in range(2)]) for k in range(2)]
    got_o = swap("batch", go_send, 1)
    msg_0, part_0 = None, None
    if fast:
        msg_0, part_0 = call(
            stage0_kernel,
            [SDS(zn_keep.shape, BF16), SDS(zn_keep.shape, F32)],
            (zn_keep, after(got_zn, go_send), zo_keep, got_zo),
        )
        gatt_x = after(gatt_x, msg_0)
    gatt_x, fc2_m = lax.optimization_barrier((after(gatt_x, go_send), fc2_m))
    got2m = swap_seq(fc2_m, 2)
    pairs = (keep_own, keep_oth, got_y1, got_y2)

    def heads_scratch(heads):
        return [pltpu.VMEM((heads, whole, LANES), BF16)] + [pltpu.VMEM((heads, whole, LANES), F32)] * 3

    def first_heads(lse):
        if fast:
            split = [SDS((8, per, 4 * cols), BF16)] * 2
        else:
            split = [SDS((width // 2, 2 * cols), BF16)] * 2
        return call(
            functools.partial(heads_kernel, fast),
            [SDS((2, whole, cols), BF16)] + split + [SDS((width, LANES), F32)],
            (sidx, bidx, qa, ka, va, lse, gatt, gatt_x, normed, w_own, early),
            [pltpu.VMEM((2, 1, cols), F32)] + heads_scratch(2) + [pltpu.VMEM((width, 2 * cols), F32)],
            flops=20 * whole * whole * LANES,
            scalars=2,
            room=20,
        )

    def tail_part(lse, g01, tile):
        wide = cols + HEAD
        if fast:
            outs = [SDS((width // (2 * per), per, wide), BF16)] * 2
        else:
            outs = [SDS((width // 2, wide), BF16)] * 2
        return call(
            tail_kernel,
            [SDS((chip, width), F32), SDS((chip, width), BF16)] + outs,
            (sidx, bidx, qa, ka, va, lse, gatt, gatt_x, normed, g01, w_own, tile),
            [pltpu.VMEM((1, whole, cols), BF16), pltpu.VMEM((1, 1, cols), F32)]
            + heads_scratch(1)
            + [pltpu.VMEM((width, LANES), F32), pltpu.VMEM((width, wide), F32)],
            flops=10 * whole * whole * LANES,
            scalars=2,
            room=20,
        )

    rest = (sidx, bidx, per, block, chip, hidden, cols, count, extra, width)
    zs = (zn_send, zn_keep, zo_send, zo_keep, msg_0, part_0)
    reduce_all = reduce_eight if fast else reduce_any
    out_fc2, out_out, out_fc1, out_qkv, smalls, gpat, gspe = reduce_all(
        rest, pairs, (fc2_keep, got2a, got2m, zs), (go_keep, got_o), lse, gatt_x,
        first_heads, tail_part, (own_p, small), gmid, norm_gains,
    )
    grad_gains, grad_shifts, grad_biases, grad_fc1_bias = smalls
    return (
        opat[None],
        ospe[None],
        gpat[None],
        gspe[None],
        grad_gains,
        grad_shifts,
        out_qkv,
        grad_biases,
        out_out,
        out_fc1,
        grad_fc1_bias.reshape(-1),
        out_fc2,
    )


def reduce_eight(
    rest, pairs, twos, outs, lse, gatt_x, first_heads, tail_part, pay, gmid, gains
):
    sidx, bidx, per, block, chip, hidden, cols, count, extra, width = rest
    fc2_keep, got2a, got2m, zs = twos
    go_keep, got_o = outs
    deep = hidden // 8
    got_0 = swap("batch", zs[4], 4)
    part_0 = zs[5]
    g01, q01_send, q01_keep, tile = first_heads(after(lse, gatt_x))
    g01, got_y2, got2m, got_o, got_0 = lax.optimization_barrier((g01, pairs[3], got2m, got_o, got_0))
    keep_own, keep_oth, got_y1 = pairs[:3]

    def blocks(n, dtype=BF16):
        return SDS((n, per, width), dtype)

    msg_z, msg_y, msg_x, part_f, part_a, part_o, part_p = call(
        stage1_kernel,
        [blocks(16), blocks(16), blocks(8), blocks(16, F32), blocks(8, F32), blocks(4, F32), blocks(4, F32)],
        (bidx, keep_own, keep_oth, got_y1, got_y2, fc2_keep, got2a, got2m, go_keep, got_o, part_0, got_0)
        + (q01_send,),
        scalars=1,
    )
    msg_z, msg_y, msg_x, lse = lax.optimization_barrier((msg_z, msg_y, msg_x, after(lse, g01)))
    got_z = swap("batch", msg_z, 2)
    got_y = swap("batch", msg_y, 1)
    got_x = swap_seq(msg_x, 2)
    gn1_keep, gn1_send, q_send, q_keep = tail_part(lse, g01, tile)
    gn1_send, got_x, got_y, got_z = lax.optimization_barrier((gn1_send, got_x, got_y, got_z))
    gn1_c = swap_seq(gn1_send, 1)
    part = SDS((22, per, cols + HEAD), BF16)
    msg_x, msg_z, msg_y, part_g, part_c, part_q = call(
        stage2_kernel,
        [blocks(8), blocks(10), part, blocks(8, F32), blocks(10, F32), blocks(2, F32)],
        (part_f, got_z, part_a, got_y, part_o, got_x, part_p, q01_keep, q_send),
    )
    got_x = swap_seq(msg_x, 2)
    got_z = swap("batch", msg_z, 2)
    got_y = swap("batch", msg_y, 1)
    (xsend,) = call(shift_kernel, [SDS((block, width), BF16)], (after(gn1_keep, msg_x), gn1_c))
    gn1_x = swap_seq(xsend, 2)
    quarter = SDS((4, per, cols + HEAD), BF16)
    msg, kept, q1, q2, q3, q_kept = call(
        stage3_kernel,
        [blocks(9), blocks(9, F32), quarter, quarter, quarter, SDS(quarter.shape, F32)],
        (bidx, part_g, after(got_x, xsend), part_c, got_z, q_keep, got_y),
        scalars=1,
    )
    got_last = swap("batch", msg, 4)
    got_qz = swap_four((q1, q2, q3), 1)
    gpat, gspe = call(
        final_kernel,
        [SDS((count, width), F32), SDS((extra, width), F32)],
        (gn1_keep, gn1_c, after(gn1_x, q1), *pay, gmid, gains),
    )
    got_last = after(got_last, gpat)
    row = SDS((per, 5 * LANES), BF16)
    s1, s2, s3, own = call(
        owner_kernel,
        [row, row, row, SDS(row.shape, F32)],
        (sidx, kept, got_last, q_kept, *got_qz),
        [pltpu.VMEM((4, per, 5 * LANES), F32)],
        scalars=1,
    )
    swap_send, swap_keep, out_fc2, out_out = call(
        sums_kernel,
        [SDS((2 * per, width), BF16), SDS((2 * per, width), F32), SDS((deep, width), F32), SDS((per, width), F32)],
        (kept, after(got_last, s1), part_q, got_y),
    )
    swap_got = swap_seq(swap_send, 1)
    gots = [swap_seq(v, k) for k, v in ((1, s1), (2, s2), (3, s3))]
    lines = [SDS((2, per), F32), SDS((2, per), F32), SDS((4, per), F32), SDS((1, 4 * per), F32)]
    out_qkv, *smalls, out_fc1 = call(
        collect_kernel,
        [SDS((per, 3 * width), F32), *lines, SDS((per, 4 * hidden), F32)],
        (sidx, own, *gots, swap_keep, swap_got),
        [pltpu.VMEM((4, per, 5 * LANES), F32)],
        scalars=1,
    )
    return out_fc2, out_out, out_fc1, out_qkv, smalls, gpat, gspe


def reduce_any(
    rest, pairs, twos, outs, lse, gatt_x, first_heads, tail_part, pay, gmid, gains
):
    sidx, bidx, per, block, chip, hidden, cols, count, extra, width = rest
    s = lax.axis_index("seq")
    nb = lax.axis_size("batch")
    nbits = bits_of("batch")
    low = nbits - 1
    fc2_keep, got2a, got2m, zs = twos
    go_keep, got_o = outs
    keep_own, keep_oth, got_oth, got_own = [
        split_bits(p.reshape(2, 2, nb // 2, per, hidden), 2, low) for p in pairs
    ]
    g01, q01_top, q01_low, tile = first_heads(lse)
    send_own, parts_own = to_send([keep_own, got_own], 0, 1, "seq")
    send_oth, parts_oth = to_send([keep_oth, got_oth], 0, 1, "seq")
    got_b = swap_seq(jnp.concatenate([send_own, send_oth], axis=-1), 2)
    sum_own = sum_rest(parts_own + [got_b[..., hidden:]], 1, 1)
    sum_oth = sum_rest(parts_oth + [got_b[..., :hidden]], 1, 1)
    own_c = s & 1
    other = jnp.concatenate([pick(sum_own, 1 - own_c, 0), pick(sum_oth, 1 - own_c, 0)], axis=-1)
    got = swap_seq(other.astype(BF16), 1).astype(F32)
    rel = jnp.stack([pick(sum_own, own_c, 0), got[:, :hidden], pick(sum_oth, own_c, 0), got[:, hidden:]])
    out_fc1 = jnp.concatenate([pick(rel, s ^ a, 0) for a in range(4)], axis=1)
    zn_send, zn_keep, zo_send, zo_keep = zs[:4]
    got2 = jnp.concatenate([got2a, got2m, swap_seq(jnp.concatenate([zo_send, zo_keep], axis=0), 2)], axis=0)
    fc2_keep = jnp.concatenate([fc2_keep, zn_send, zn_keep], axis=0)
    parts = [split_bits(p.reshape(nb, -1, width), 0, nbits) for p in (fc2_keep, got2)]
    out_fc2 = sum_rest(parts, 0, 0)
    parts = [split_bits(p.reshape(2, nb // 2, per, width), 1, low) for p in (go_keep, got_o)]
    parts = [p[0] for p in parts] + [swap_seq(total([p[1] for p in parts]).astype(BF16), 2)]
    out_out = sum_rest(parts, 0, 1)
    gn1_keep, gn1_send, q2_top, q2_low = tail_part(lse, g01, tile)
    q_all = [jnp.concatenate(v, axis=1) for v in ((q01_top, q2_top), (q01_low, q2_low))]
    q_send, q_keep = by_batch_bit(jnp.concatenate(q_all, axis=0), per)
    gn1_c = swap_seq(gn1_send, 1)
    gn1_x = swap_seq((gn1_keep[block:] + gn1_c[block:].astype(F32)).astype(BF16), 2)
    gpat, gspe = call(
        final_kernel,
        [SDS((count, width), F32), SDS((extra, width), F32)],
        (gn1_keep, gn1_c, gn1_x, *pay, gmid, gains),
    )
    wide = 5 * LANES
    parts = [split_bits(p.reshape(4, nb // 2, per, wide), 1, low) for p in (q_keep, swap("batch", q_send, 1))]
    sum_q = sum_rest(parts, 1, 1)
    pieces = [pick(sum_q, s, 0)] + [
        swap_seq(pick(sum_q, s ^ j, 0).astype(BF16), j).astype(F32) for j in (1, 2, 3)
    ]
    rel = jnp.stack([p[:, : 3 * cols] for p in pieces])
    absolute = jnp.stack([pick(rel, s ^ a, 0) for a in range(4)], axis=1)
    out_qkv = absolute.reshape(-1, 4, OWN, 3, HEAD).transpose(0, 3, 1, 2, 4).reshape(-1, 3 * width)
    vec = total([p[:, 3 * cols :] for p in pieces]).T
    smalls = [vec[jnp.array(k)] for k in ((0, 4), (1, 5), (2, 3, 7, 6), (8, 9, 10, 11))]
    return out_fc2, out_out, out_fc1, out_qkv, smalls, gpat, gspe


def solution(mesh):
    tok = P("batch", "seq", None)
    ids = P("batch", "seq")
    split = P(None, ("seq", "batch"))
    rows = P(("seq", "batch"), None)
    return jax.shard_map(
        body,
        mesh=mesh,
        in_specs=(tok, tok, ids, ids, P("batch", None)) + (P(),) * 8 + (tok, tok),
        out_specs=(tok, tok, tok, tok, split, split, rows, split, rows, rows, P(("seq", "batch")), rows),
        check_vma=False,
    )
```
